256 devices in a mesh: sx: 32 (over x_hi, z, core), sy: 8 (over y, x_lo).
Axes of the slice: x: 4 (x_hi: 2, x_lo: 2; x = x_hi * 2 + x_lo), y: 4, z: 8, core: 2. Of those that a mesh axis runs over, the one named last changes fastest.
Arguments:
- object_field: float32 [2, 4096, 4096], P(None, 'sx', 'sy'), may hold values from -6 to 6
- probe_field: float32 [2, 256, 256], replicated, may hold values from -4.2 to 4.2
- amplitudes: float32 [32, 8, 2, 256, 256], P('sx', 'sy'), may hold values from 0 to 2
- centres: int32 [32, 8, 2, 2], P('sx', 'sy'), may hold values from 0 to 511, as said below
- counts: int32 [32, 8], P(None, 'sy'), may hold values from 1 to 2, as said below
Outputs:
- object_next: float32 [2, 4096, 4096], P(None, 'sx', 'sy')
The draws below stay inside these ranges and needn't reach their ends.
Inputs may be any that keep to these rules, and one draw needn't show every extreme that they name: centres[s, t, k, 0] is below 128 and centres[s, t, k, 1] below 512; slots from counts[s, t] on are unused. A device's live positions are its first counts[s, t] slots; 2 is reached in every draw.
All inputs are finite; a program needn't handle non-finite values.
Results may differ from the reference program's by a relative error of at most 0.0003.
Values sent between devices are 32-bit elements; how exact they have to be, the bound alone decides.
A program may use at most 128 MiB of HBM per device.

```python
import math
import jax
import jax.numpy as jnp
from jax import lax

PS = 256
BR = 128
BC = 512
CAP = 2
ITERS = 2
NR = 4096
NC = 4096
N_SX = 32
N_SY = 8


def draw_counts(key, part):
    band_start = jax.random.randint(jax.random.fold_in(key, 11), (), 0, N_SX)
    band_width = max(N_SX // 4, 1)
    row_index = jnp.arange(N_SX, dtype=jnp.int32)
    dense_rows = (row_index - band_start) % N_SX < band_width
    light_counts = jax.random.randint(jax.random.fold_in(key, 12), (N_SX, N_SY), 1, 3)
    return jnp.where(dense_rows[:, None], CAP, light_counts).astype(jnp.int32)


def draw_centres(key, part):
    row_values = jax.random.randint(jax.random.fold_in(key, 21), (N_SX, N_SY, CAP), 0, BR)
    col_values = jax.random.randint(jax.random.fold_in(key, 22), (N_SX, N_SY, CAP), 0, BC)
    chosen_row = jax.random.randint(jax.random.fold_in(key, 23), (), 0, N_SX)
    chosen_col = jax.random.randint(jax.random.fold_in(key, 24), (), 0, N_SY)
    col_values = col_values.at[chosen_row, chosen_col, 0].set(BC - 1)
    return jnp.stack([row_values, col_values], axis=-1).astype(jnp.int32)


def shard_levels(key, extent, pieces, low, high):
    def one(position, parts):
        draws = jax.random.uniform(jax.random.fold_in(jax.random.fold_in(key, 6), position), (parts,), jnp.float32, low / len(pieces), high / len(pieces))
        return jnp.repeat(jnp.exp(draws), extent[position] // parts).reshape((-1,) + (1,) * (len(extent) - position - 1))

    gain = one(*pieces[0])
    for cut in pieces[1:]:
        gain = gain * one(*cut)
    return gain


def centred(own_key, extent, deviation, most, shards=(), kind=jnp.bfloat16):
    loudness = shard_levels(own_key, extent, shards, -0.22, 0.18) if shards else 1.0
    result = jax.random.normal(own_key, extent, jnp.float32) * deviation * loudness
    return jnp.minimum(jnp.maximum(result, -most), most).astype(kind)


def setup_inputs(seed: int = 0) -> dict:
    seeds = jax.random.split(jax.random.key(seed), 6)
    return {
        "object_field": centred(seeds[0], (2, NR, NC), 1.0, 6.0, ((1, 32), (2, 8)), jnp.float32),
        "probe_field": centred(seeds[1], (2, PS, PS), 0.7, 4.2, (), jnp.float32),
        "amplitudes": jnp.clip(2.0 * jax.random.uniform(seeds[2], (N_SX, N_SY, CAP, PS, PS), jnp.float32) ** shard_levels(seeds[2], (N_SX, N_SY, CAP, PS, PS), ((0, 32), (1, 8)), -0.2, 0.2), 0.0, 2.0),
        "centres": draw_centres(jax.random.fold_in(seeds[5], 71), 0),
        "counts": draw_counts(jax.random.fold_in(seeds[5], 71), 0),
    }


SMOOTH = 1.0
DAMPING = 1.0

def dft_tables(length):
    index_values = jnp.arange(length, dtype=jnp.int32)
    product_mod = index_values[:, None] * index_values[None, :] % length
    angles = product_mod.astype(jnp.float32) * (2.0 * math.pi / length)
    scaling = 1.0 / math.sqrt(length)
    return (jnp.cos(angles) * scaling, -jnp.sin(angles) * scaling)

def matmul_exact(left_side, right_side):
    return jnp.dot(left_side, right_side, precision=lax.Precision.HIGHEST)

def complex_left(table_real, table_imag, field_real, field_imag):
    out_real = matmul_exact(table_real, field_real) - matmul_exact(table_imag, field_imag)
    out_imag = matmul_exact(table_real, field_imag) + matmul_exact(table_imag, field_real)
    return (out_real, out_imag)

def complex_right(field_real, field_imag, table_real, table_imag):
    out_real = matmul_exact(field_real, table_real) - matmul_exact(field_imag, table_imag)
    out_imag = matmul_exact(field_real, table_imag) + matmul_exact(field_imag, table_real)
    return (out_real, out_imag)

def position_gradient(object_patch, probe_field, amplitude, table_real, table_imag):
    probe_real = probe_field[0]
    probe_imag = probe_field[1]
    exit_real = probe_real * object_patch[0] - probe_imag * object_patch[1]
    exit_imag = probe_real * object_patch[1] + probe_imag * object_patch[0]
    half_real, half_imag = complex_left(table_real, table_imag, exit_real, exit_imag)
    far_real, far_imag = complex_right(half_real, half_imag, table_real, table_imag)
    factor = 1.0 - amplitude / jnp.sqrt(far_real * far_real + far_imag * far_imag + SMOOTH)
    miss_real = far_real * factor
    miss_imag = far_imag * factor
    back_real, back_imag = complex_left(table_real, -table_imag, miss_real, miss_imag)
    near_real, near_imag = complex_right(back_real, back_imag, table_real, -table_imag)
    return jnp.stack([probe_real * near_real + probe_imag * near_imag, probe_real * near_imag - probe_imag * near_real])

def add_patch(canvas, patch_values, corner_row, corner_col):
    zero_index = jnp.zeros((), jnp.int32)
    starts = (zero_index, corner_row, corner_col)
    present = lax.dynamic_slice(canvas, starts, patch_values.shape)
    return lax.dynamic_update_slice(canvas, present + patch_values, starts)

def reference(object_field, probe_field, amplitudes, centres, counts):
    table_real, table_imag = dft_tables(PS)
    half_probe = PS // 2
    total_devices = N_SX * N_SY
    flat_centres = centres.reshape(total_devices, CAP, 2)
    flat_counts = counts.reshape(total_devices)
    flat_amps = amplitudes.reshape(total_devices, CAP, PS, PS)
    padding = ((0, 0), (half_probe, half_probe), (half_probe, half_probe))
    spot_power = (probe_field[0] * probe_field[0] + probe_field[1] * probe_field[1])[None]

    def corner_of(device, slot_index):
        corner_row = device // N_SY * BR + flat_centres[device, slot_index, 0]
        corner_col = device % N_SY * BC + flat_centres[device, slot_index, 1]
        return (corner_row.astype(jnp.int32), corner_col.astype(jnp.int32))

    def over_positions(device_step):

        def outer_step(device, state_carry):

            def inner_step(slot_index, inner_carry):
                return device_step(device, slot_index, inner_carry)
            return lax.fori_loop(0, flat_counts[device], inner_step, state_carry)
        return outer_step

    def add_power(device, slot_index, canvas):
        corner_row, corner_col = corner_of(device, slot_index)
        return add_patch(canvas, spot_power, corner_row, corner_col)
    blank_power = jnp.zeros((1, NR + PS, NC + PS), jnp.float32)
    power_canvas = lax.fori_loop(0, total_devices, over_positions(add_power), blank_power)
    illumination = power_canvas[:, half_probe:half_probe + NR, half_probe:half_probe + NC]
    current = object_field
    for sweep_index in range(ITERS):
        padded = jnp.pad(current, padding)

        def add_gradient(device, slot_index, canvas, padded=padded):
            corner_row, corner_col = corner_of(device, slot_index)
            zero_index = jnp.zeros((), jnp.int32)
            object_patch = lax.dynamic_slice(padded, (zero_index, corner_row, corner_col), (2, PS, PS))
            update = position_gradient(object_patch, probe_field, flat_amps[device, slot_index], table_real, table_imag)
            return add_patch(canvas, update, corner_row, corner_col)
        blank_grad = jnp.zeros((2, NR + PS, NC + PS), jnp.float32)
        grad_canvas = lax.fori_loop(0, total_devices, over_positions(add_gradient), blank_grad)
        gradient = grad_canvas[:, half_probe:half_probe + NR, half_probe:half_probe + NC]
        current = current - gradient / (illumination + DAMPING)
    return current
```

```python
import math

import jax
import jax.numpy as jnp
from jax import lax
from jax.sharding import PartitionSpec as P
from jax.experimental import pallas as pl
from jax.experimental.pallas import tpu as pltpu

ITERS = 2


SMOOTH = 1.0
DAMPING = 1.0


def with_halo(cells, sides, width):
    for axis, dim in sides:
        count = lax.axis_size(axis)
        ends = count - 1
        head = lax.slice_in_dim(cells, 0, width, axis=dim)
        tail = lax.slice_in_dim(cells, cells.shape[dim] - width, cells.shape[dim], axis=dim)
        cells = jnp.concatenate(
            [
                lax.ppermute(tail, axis, [(i, (i + 1) % count) for i in range(ends)]),
                cells,
                lax.ppermute(head, axis, [((i + 1) % count, i) for i in range(ends)]),
            ],
            axis=dim,
        )
    return cells


def dft_tables(length):
    index_values = jnp.arange(length, dtype=jnp.int32)
    product_mod = index_values[:, None] * index_values[None, :] % length
    angles = product_mod.astype(jnp.float32) * (2.0 * math.pi / length)
    scaling = 1.0 / math.sqrt(length)
    return (jnp.cos(angles) * scaling, -jnp.sin(angles) * scaling)


def matmul_exact(left_side, right_side):
    return jnp.dot(left_side, right_side, precision=lax.Precision.HIGHEST)


def complex_left(table_real, table_imag, field_real, field_imag):
    out_real = matmul_exact(table_real, field_real) - matmul_exact(table_imag, field_imag)
    out_imag = matmul_exact(table_real, field_imag) + matmul_exact(table_imag, field_real)
    return (out_real, out_imag)


def complex_right(field_real, field_imag, table_real, table_imag):
    out_real = matmul_exact(field_real, table_real) - matmul_exact(field_imag, table_imag)
    out_imag = matmul_exact(field_real, table_imag) + matmul_exact(field_imag, table_real)
    return (out_real, out_imag)


def position_gradient(object_patch, probe_field, amplitude, table_real, table_imag):
    probe_real = probe_field[0]
    probe_imag = probe_field[1]
    exit_real = probe_real * object_patch[0] - probe_imag * object_patch[1]
    exit_imag = probe_real * object_patch[1] + probe_imag * object_patch[0]
    half_real, half_imag = complex_left(table_real, table_imag, exit_real, exit_imag)
    far_real, far_imag = complex_right(half_real, half_imag, table_real, table_imag)
    factor = 1.0 - amplitude / jnp.sqrt(far_real * far_real + far_imag * far_imag + SMOOTH)
    miss_real = far_real * factor
    miss_imag = far_imag * factor
    back_real, back_imag = complex_left(table_real, -table_imag, miss_real, miss_imag)
    near_real, near_imag = complex_right(back_real, back_imag, table_real, -table_imag)
    return jnp.stack(
        [
            probe_real * near_real + probe_imag * near_imag,
            probe_real * near_imag - probe_imag * near_real,
        ]
    )


def add_patch(canvas, patch_values, corner_row, corner_col):
    zero_index = jnp.zeros((), jnp.int32)
    starts = (zero_index, corner_row, corner_col)
    present = lax.dynamic_slice(canvas, starts, patch_values.shape)
    return lax.dynamic_update_slice(canvas, present + patch_values, starts)


def fold_rows(extended, margin, length):
    middle_part = extended[:, 2 * margin : 2 * margin + length]
    upper_rim = extended[:, :margin]
    lower_rim = extended[:, extended.shape[1] - margin :]
    middle_part = middle_part.at[:, :margin].add(upper_rim)
    return middle_part.at[:, length - margin :].add(lower_rim)


def fold_cols(extended, margin, length):
    middle_part = extended[:, :, 2 * margin : 2 * margin + length]
    left_rim = extended[:, :, :margin]
    right_rim = extended[:, :, extended.shape[2] - margin :]
    middle_part = middle_part.at[:, :, :margin].add(left_rim)
    return middle_part.at[:, :, length - margin :].add(right_rim)


def settle(stacked, margin, block_rows, block_cols):
    full_ext = with_halo(stacked, (("sx", 1), ("sy", 2)), margin)
    return fold_cols(fold_rows(full_ext, margin, block_rows), margin, block_cols)


def local_pass(canvas, extended, spots, own_amps, probe_field, table_real, table_imag, upper_bound):
    size_probe = probe_field.shape[1]

    def local_step(slot_index, canvas_state):
        row_start = spots[slot_index, 0]
        col_start = spots[slot_index, 1]
        zero_index = jnp.zeros((), jnp.int32)
        object_patch = lax.dynamic_slice(
            extended, (zero_index, row_start, col_start), (2, size_probe, size_probe)
        )
        update = position_gradient(
            object_patch, probe_field, own_amps[slot_index], table_real, table_imag
        )
        return add_patch(canvas_state, update, row_start, col_start)

    return lax.fori_loop(0, upper_bound, local_step, canvas)


def dot_exact(left_side, right_side):
    return jnp.dot(
        left_side, right_side, precision=lax.Precision.HIGHEST, preferred_element_type=jnp.float32
    )


def gradient_kernel(spots_ref, count_ref, ext_ref, probe_ref, amps_ref, fr_ref, fi_ref, out_ref):
    size = probe_ref.shape[1]
    lanes = 128
    sublanes = 8
    wide = size + lanes
    tall = size + sublanes
    out_ref[...] = jnp.zeros(out_ref.shape, jnp.float32)
    with_power = out_ref.shape[0] > 2
    for slot in range(amps_ref.shape[0]):

        @pl.when(slot < count_ref[0])
        def _():
            row = spots_ref[slot, 0]
            col = spots_ref[slot, 1]
            row_base = pl.multiple_of((row // sublanes) * sublanes, sublanes)
            col_base = pl.multiple_of((col // lanes) * lanes, lanes)
            row_shift = row % sublanes
            col_shift = col % lanes
            rows = pl.ds(row_base, tall)
            cols = pl.ds(col_base, wide)

            def take(channel):
                block = ext_ref[channel, rows, cols]
                block = pltpu.roll(block, (tall - row_shift) % tall, 0)
                return pltpu.roll(block, (wide - col_shift) % wide, 1)[:size, :size]

            def put(channel, values):
                block = jnp.concatenate([values, jnp.zeros((size, lanes), jnp.float32)], axis=1)
                block = jnp.concatenate([block, jnp.zeros((sublanes, wide), jnp.float32)], axis=0)
                block = pltpu.roll(pltpu.roll(block, col_shift, 1), row_shift, 0)
                out_ref[channel, rows, cols] += block

            probe_real = probe_ref[0]
            probe_imag = probe_ref[1]
            table_real = fr_ref[...]
            table_imag = fi_ref[...]
            obj_real = take(0)
            obj_imag = take(1)
            exit_real = probe_real * obj_real - probe_imag * obj_imag
            exit_imag = probe_real * obj_imag + probe_imag * obj_real
            half_real = dot_exact(table_real, exit_real) - dot_exact(table_imag, exit_imag)
            half_imag = dot_exact(table_real, exit_imag) + dot_exact(table_imag, exit_real)
            far_real = dot_exact(half_real, table_real) - dot_exact(half_imag, table_imag)
            far_imag = dot_exact(half_real, table_imag) + dot_exact(half_imag, table_real)
            factor = 1.0 - amps_ref[slot] / jnp.sqrt(far_real * far_real + far_imag * far_imag + SMOOTH)
            miss_real = far_real * factor
            miss_imag = far_imag * factor
            back_real = dot_exact(table_real, miss_real) + dot_exact(table_imag, miss_imag)
            back_imag = dot_exact(table_real, miss_imag) - dot_exact(table_imag, miss_real)
            near_real = dot_exact(back_real, table_real) + dot_exact(back_imag, table_imag)
            near_imag = dot_exact(back_imag, table_real) - dot_exact(back_real, table_imag)
            put(0, probe_real * near_real + probe_imag * near_imag)
            put(1, probe_real * near_imag - probe_imag * near_real)
            if with_power:
                put(2, probe_real * probe_real + probe_imag * probe_imag)


def gradient_canvas(channels, ext_shape, spots, count, extended, probe_field, own_amps, tables):
    vmem = pl.BlockSpec(memory_space=pltpu.VMEM)
    smem = pl.BlockSpec(memory_space=pltpu.SMEM)
    return pl.pallas_call(
        gradient_kernel,
        out_shape=jax.ShapeDtypeStruct((channels,) + ext_shape, jnp.float32),
        in_specs=[smem, smem, vmem, vmem, vmem, vmem, vmem],
        out_specs=vmem,
        compiler_params=pltpu.CompilerParams(vmem_limit_bytes=60 * 1024 * 1024),
    )(spots, count.reshape(1), extended, probe_field, own_amps, tables[0], tables[1])


def on_device(object_field, probe_field, amplitudes, centres, counts):
    size_probe = probe_field.shape[1]
    margin = size_probe // 2
    block_rows = object_field.shape[1]
    block_cols = object_field.shape[2]
    tables = dft_tables(size_probe)
    spots = centres[0, 0]
    own_amps = amplitudes[0, 0]
    sx_size = lax.axis_size("sx")
    sx_index = lax.axis_index("sx")
    column_counts = counts[:, 0]
    sx_positions = jnp.arange(sx_size, dtype=jnp.int32)
    own_count = jnp.sum(jnp.where(sx_positions == sx_index, column_counts, 0))
    ext_shape = (block_rows + size_probe, block_cols + size_probe)
    current = object_field
    for sweep_index in range(ITERS):
        extended = with_halo(current, (("sx", 1), ("sy", 2)), margin)
        channels = 3 if sweep_index == 0 else 2
        canvas = gradient_canvas(
            channels, ext_shape, spots, own_count, extended, probe_field, own_amps, tables
        )
        settled = settle(canvas, margin, block_rows, block_cols)
        if sweep_index == 0:
            illumination = settled[2]
        gradient = settled[0:2]
        current = current - gradient / (illumination + DAMPING)
    return current


def solution(mesh):
    return jax.shard_map(
        on_device,
        mesh=mesh,
        in_specs=(
            P(None, "sx", "sy"),
            P(),
            P("sx", "sy", None, None, None),
            P("sx", "sy", None, None),
            P(None, "sy"),
        ),
        out_specs=P(None, "sx", "sy"),
        check_vma=False,
    )
```

```python
import math

import jax
import jax.numpy as jnp
from jax import lax
from jax.sharding import PartitionSpec as P
from jax.experimental import pallas as pl
from jax.experimental.pallas import tpu as pltpu

ITERS = 2


SMOOTH = 1.0
DAMPING = 1.0


def with_halo(cells, sides, width):
    for axis, dim in sides:
        count = lax.axis_size(axis)
        ends = count - 1
        head = lax.slice_in_dim(cells, 0, width, axis=dim)
        tail = lax.slice_in_dim(cells, cells.shape[dim] - width, cells.shape[dim], axis=dim)
        cells = jnp.concatenate(
            [
                lax.ppermute(tail, axis, [(i, (i + 1) % count) for i in range(ends)]),
                cells,
                lax.ppermute(head, axis, [((i + 1) % count, i) for i in range(ends)]),
            ],
            axis=dim,
        )
    return cells


def dft_tables(length):
    index_values = jnp.arange(length, dtype=jnp.int32)
    product_mod = index_values[:, None] * index_values[None, :] % length
    angles = product_mod.astype(jnp.float32) * (2.0 * math.pi / length)
    scaling = 1.0 / math.sqrt(length)
    return (jnp.cos(angles) * scaling, -jnp.sin(angles) * scaling)


def matmul_exact(left_side, right_side):
    return jnp.dot(left_side, right_side, precision=lax.Precision.HIGHEST)


def complex_left(table_real, table_imag, field_real, field_imag):
    out_real = matmul_exact(table_real, field_real) - matmul_exact(table_imag, field_imag)
    out_imag = matmul_exact(table_real, field_imag) + matmul_exact(table_imag, field_real)
    return (out_real, out_imag)


def complex_right(field_real, field_imag, table_real, table_imag):
    out_real = matmul_exact(field_real, table_real) - matmul_exact(field_imag, table_imag)
    out_imag = matmul_exact(field_real, table_imag) + matmul_exact(field_imag, table_real)
    return (out_real, out_imag)


def position_gradient(object_patch, probe_field, amplitude, table_real, table_imag):
    probe_real = probe_field[0]
    probe_imag = probe_field[1]
    exit_real = probe_real * object_patch[0] - probe_imag * object_patch[1]
    exit_imag = probe_real * object_patch[1] + probe_imag * object_patch[0]
    half_real, half_imag = complex_left(table_real, table_imag, exit_real, exit_imag)
    far_real, far_imag = complex_right(half_real, half_imag, table_real, table_imag)
    factor = 1.0 - amplitude / jnp.sqrt(far_real * far_real + far_imag * far_imag + SMOOTH)
    miss_real = far_real * factor
    miss_imag = far_imag * factor
    back_real, back_imag = complex_left(table_real, -table_imag, miss_real, miss_imag)
    near_real, near_imag = complex_right(back_real, back_imag, table_real, -table_imag)
    return jnp.stack(
        [
            probe_real * near_real + probe_imag * near_imag,
            probe_real * near_imag - probe_imag * near_real,
        ]
    )


def add_patch(canvas, patch_values, corner_row, corner_col):
    zero_index = jnp.zeros((), jnp.int32)
    starts = (zero_index, corner_row, corner_col)
    present = lax.dynamic_slice(canvas, starts, patch_values.shape)
    return lax.dynamic_update_slice(canvas, present + patch_values, starts)


def fold_rows(extended, margin, length):
    middle_part = extended[:, 2 * margin : 2 * margin + length]
    upper_rim = extended[:, :margin]
    lower_rim = extended[:, extended.shape[1] - margin :]
    middle_part = middle_part.at[:, :margin].add(upper_rim)
    return middle_part.at[:, length - margin :].add(lower_rim)


def fold_cols(extended, margin, length):
    middle_part = extended[:, :, 2 * margin : 2 * margin + length]
    left_rim = extended[:, :, :margin]
    right_rim = extended[:, :, extended.shape[2] - margin :]
    middle_part = middle_part.at[:, :, :margin].add(left_rim)
    return middle_part.at[:, :, length - margin :].add(right_rim)


def settle(stacked, margin, block_rows, block_cols):
    full_ext = with_halo(stacked, (("sx", 1), ("sy", 2)), margin)
    return fold_cols(fold_rows(full_ext, margin, block_rows), margin, block_cols)


def local_pass(canvas, extended, spots, own_amps, probe_field, table_real, table_imag, upper_bound):
    size_probe = probe_field.shape[1]

    def local_step(slot_index, canvas_state):
        row_start = spots[slot_index, 0]
        col_start = spots[slot_index, 1]
        zero_index = jnp.zeros((), jnp.int32)
        object_patch = lax.dynamic_slice(
            extended, (zero_index, row_start, col_start), (2, size_probe, size_probe)
        )
        update = position_gradient(
            object_patch, probe_field, own_amps[slot_index], table_real, table_imag
        )
        return add_patch(canvas_state, update, row_start, col_start)

    return lax.fori_loop(0, upper_bound, local_step, canvas)


def dot_exact(left_side, right_side):
    return jnp.dot(
        left_side, right_side, precision=lax.Precision.HIGHEST, preferred_element_type=jnp.float32
    )


def window_tools(size, row, col):
    lanes = 128
    sublanes = 8
    wide = size + lanes
    tall = size + sublanes
    row_base = pl.multiple_of((row // sublanes) * sublanes, sublanes)
    col_base = pl.multiple_of((col // lanes) * lanes, lanes)
    row_shift = row % sublanes
    col_shift = col % lanes
    rows = pl.ds(row_base, tall)
    cols = pl.ds(col_base, wide)

    def take(ref, channel):
        block = ref[channel, rows, cols]
        block = pltpu.roll(block, (tall - row_shift) % tall, 0)
        return pltpu.roll(block, (wide - col_shift) % wide, 1)[:size, :size]

    def put(ref, channel, values):
        block = jnp.concatenate([values, jnp.zeros((size, lanes), jnp.float32)], axis=1)
        block = jnp.concatenate([block, jnp.zeros((sublanes, wide), jnp.float32)], axis=0)
        block = pltpu.roll(pltpu.roll(block, col_shift, 1), row_shift, 0)
        ref[channel, rows, cols] += block

    return take, put


def gradient_kernel(spots_ref, count_ref, ext_ref, probe_ref, amps_ref, fr_ref, fi_ref, out_ref):
    size = probe_ref.shape[1]
    out_ref[...] = jnp.zeros(out_ref.shape, jnp.float32)
    for slot in range(amps_ref.shape[0]):

        @pl.when(slot < count_ref[0])
        def _():
            take, put = window_tools(size, spots_ref[slot, 0], spots_ref[slot, 1])
            probe_real = probe_ref[0]
            probe_imag = probe_ref[1]
            table_real = fr_ref[...]
            table_imag = fi_ref[...]
            obj_real = take(ext_ref, 0)
            obj_imag = take(ext_ref, 1)
            exit_real = probe_real * obj_real - probe_imag * obj_imag
            exit_imag = probe_real * obj_imag + probe_imag * obj_real
            half_real = dot_exact(table_real, exit_real) - dot_exact(table_imag, exit_imag)
            half_imag = dot_exact(table_real, exit_imag) + dot_exact(table_imag, exit_real)
            far_real = dot_exact(half_real, table_real) - dot_exact(half_imag, table_imag)
            far_imag = dot_exact(half_real, table_imag) + dot_exact(half_imag, table_real)
            factor = 1.0 - amps_ref[slot] / jnp.sqrt(far_real * far_real + far_imag * far_imag + SMOOTH)
            miss_real = far_real * factor
            miss_imag = far_imag * factor
            back_real = dot_exact(table_real, miss_real) + dot_exact(table_imag, miss_imag)
            back_imag = dot_exact(table_real, miss_imag) - dot_exact(table_imag, miss_real)
            near_real = dot_exact(back_real, table_real) + dot_exact(back_imag, table_imag)
            near_imag = dot_exact(back_imag, table_real) - dot_exact(back_real, table_imag)
            put(out_ref, 0, probe_real * near_real + probe_imag * near_imag)
            put(out_ref, 1, probe_real * near_imag - probe_imag * near_real)


def power_kernel(spots_ref, count_ref, probe_ref, out_ref):
    size = probe_ref.shape[1]
    out_ref[...] = jnp.zeros(out_ref.shape, jnp.float32)
    power = probe_ref[0] * probe_ref[0] + probe_ref[1] * probe_ref[1]
    for slot in range(spots_ref.shape[0]):

        @pl.when(slot < count_ref[0])
        def _():
            _, put = window_tools(size, spots_ref[slot, 0], spots_ref[slot, 1])
            put(out_ref, 0, power)


VMEM_SPEC = pl.BlockSpec(memory_space=pltpu.VMEM)
SMEM_SPEC = pl.BlockSpec(memory_space=pltpu.SMEM)
KERNEL_PARAMS = pltpu.CompilerParams(vmem_limit_bytes=60 * 1024 * 1024)


def gradient_canvas(ext_shape, spots, count, extended, probe_field, own_amps, tables):
    return pl.pallas_call(
        gradient_kernel,
        out_shape=jax.ShapeDtypeStruct((2,) + ext_shape, jnp.float32),
        in_specs=[SMEM_SPEC, SMEM_SPEC] + [VMEM_SPEC] * 5,
        out_specs=VMEM_SPEC,
        compiler_params=KERNEL_PARAMS,
    )(spots, count.reshape(1), extended, probe_field, own_amps, tables[0], tables[1])


def power_canvas(ext_shape, spots, count, probe_field):
    return pl.pallas_call(
        power_kernel,
        out_shape=jax.ShapeDtypeStruct((1,) + ext_shape, jnp.float32),
        in_specs=[SMEM_SPEC, SMEM_SPEC, VMEM_SPEC],
        out_specs=VMEM_SPEC,
        compiler_params=KERNEL_PARAMS,
    )(spots, count.reshape(1), probe_field)


def from_prev(cells, axis):
    count = lax.axis_size(axis)
    return lax.ppermute(cells, axis, [(i, i + 1) for i in range(count - 1)])


def from_next(cells, axis):
    count = lax.axis_size(axis)
    return lax.ppermute(cells, axis, [(i + 1, i) for i in range(count - 1)])


def fold_canvas(canvas, margin, with_halo_cols):
    rows = canvas.shape[1]
    cols = canvas.shape[2]
    upper = canvas[:, :margin]
    lower = canvas[:, rows - margin :]
    folded = canvas[:, margin : rows - margin] + from_prev(lower, "sx") + from_next(upper, "sx")
    left_rim = folded[..., :margin]
    left_edge = folded[..., margin : 2 * margin]
    right_edge = folded[..., cols - 2 * margin : cols - margin]
    right_rim = folded[..., cols - margin :]
    inner = folded[..., 2 * margin : cols - 2 * margin]
    if with_halo_cols:
        got_prev = from_prev(jnp.concatenate([right_rim, right_edge], axis=0), "sy")
        got_next = from_next(jnp.concatenate([left_rim, left_edge], axis=0), "sy")
        depth = canvas.shape[0]
        return jnp.concatenate(
            [
                left_rim + got_prev[depth:],
                left_edge + got_prev[:depth],
                inner,
                right_edge + got_next[:depth],
                right_rim + got_next[depth:],
            ],
            axis=2,
        )
    return jnp.concatenate(
        [left_edge + from_prev(right_rim, "sy"), inner, right_edge + from_next(left_rim, "sy")],
        axis=2,
    )


def on_device(object_field, probe_field, amplitudes, centres, counts):
    size_probe = probe_field.shape[1]
    margin = size_probe // 2
    block_rows = object_field.shape[1]
    block_cols = object_field.shape[2]
    tables = dft_tables(size_probe)
    spots = centres[0, 0]
    own_amps = amplitudes[0, 0]
    sx_size = lax.axis_size("sx")
    sx_index = lax.axis_index("sx")
    sy_size = lax.axis_size("sy")
    sy_index = lax.axis_index("sy")
    column_counts = counts[:, 0]
    sx_positions = jnp.arange(sx_size, dtype=jnp.int32)
    own_count = jnp.sum(jnp.where(sx_positions == sx_index, column_counts, 0))
    ext_shape = (block_rows + size_probe, block_cols + size_probe)

    illumination = fold_canvas(power_canvas(ext_shape, spots, own_count, probe_field), margin, True)[0]
    current = object_field
    wide = jnp.concatenate(
        [
            from_prev(current[..., block_cols - margin :], "sy"),
            current,
            from_next(current[..., :margin], "sy"),
        ],
        axis=2,
    )
    col_index = jnp.arange(block_cols + size_probe, dtype=jnp.int32)
    inside = ((col_index >= margin) | (sy_index > 0)) & (
        (col_index < block_cols + margin) | (sy_index < sy_size - 1)
    )
    for sweep_index in range(ITERS):
        extended = jnp.concatenate([from_prev(wide, "sx"), wide, from_next(wide, "sx")], axis=1)
        canvas = gradient_canvas(ext_shape, spots, own_count, extended, probe_field, own_amps, tables)
        last = sweep_index == ITERS - 1
        gradient = fold_canvas(canvas, margin, not last)
        if last:
            current = wide[..., margin : margin + block_cols] - gradient / (
                illumination[:, margin : margin + block_cols] + DAMPING
            )
        else:
            wide = jnp.where(inside, wide - gradient / (illumination + DAMPING), 0.0)
    return current


def solution(mesh):
    return jax.shard_map(
        on_device,
        mesh=mesh,
        in_specs=(
            P(None, "sx", "sy"),
            P(),
            P("sx", "sy", None, None, None),
            P("sx", "sy", None, None),
            P(None, "sy"),
        ),
        out_specs=P(None, "sx", "sy"),
        check_vma=False,
    )
```

```python
import math

import jax
import jax.numpy as jnp
from jax import lax
from jax.sharding import PartitionSpec as P
from jax.experimental import pallas as pl
from jax.experimental.pallas import tpu as pltpu

ITERS = 2


SMOOTH = 1.0
DAMPING = 1.0


def with_halo(cells, sides, width):
    for axis, dim in sides:
        count = lax.axis_size(axis)
        ends = count - 1
        head = lax.slice_in_dim(cells, 0, width, axis=dim)
        tail = lax.slice_in_dim(cells, cells.shape[dim] - width, cells.shape[dim], axis=dim)
        cells = jnp.concatenate(
            [
                lax.ppermute(tail, axis, [(i, (i + 1) % count) for i in range(ends)]),
                cells,
                lax.ppermute(head, axis, [((i + 1) % count, i) for i in range(ends)]),
            ],
            axis=dim,
        )
    return cells


def dft_tables(length):
    index_values = jnp.arange(length, dtype=jnp.int32)
    product_mod = index_values[:, None] * index_values[None, :] % length
    angles = product_mod.astype(jnp.float32) * (2.0 * math.pi / length)
    scaling = 1.0 / math.sqrt(length)
    return (jnp.cos(angles) * scaling, -jnp.sin(angles) * scaling)


def matmul_exact(left_side, right_side):
    return jnp.dot(left_side, right_side, precision=lax.Precision.HIGHEST)


def complex_left(table_real, table_imag, field_real, field_imag):
    out_real = matmul_exact(table_real, field_real) - matmul_exact(table_imag, field_imag)
    out_imag = matmul_exact(table_real, field_imag) + matmul_exact(table_imag, field_real)
    return (out_real, out_imag)


def complex_right(field_real, field_imag, table_real, table_imag):
    out_real = matmul_exact(field_real, table_real) - matmul_exact(field_imag, table_imag)
    out_imag = matmul_exact(field_real, table_imag) + matmul_exact(field_imag, table_real)
    return (out_real, out_imag)


def position_gradient(object_patch, probe_field, amplitude, table_real, table_imag):
    probe_real = probe_field[0]
    probe_imag = probe_field[1]
    exit_real = probe_real * object_patch[0] - probe_imag * object_patch[1]
    exit_imag = probe_real * object_patch[1] + probe_imag * object_patch[0]
    half_real, half_imag = complex_left(table_real, table_imag, exit_real, exit_imag)
    far_real, far_imag = complex_right(half_real, half_imag, table_real, table_imag)
    factor = 1.0 - amplitude / jnp.sqrt(far_real * far_real + far_imag * far_imag + SMOOTH)
    miss_real = far_real * factor
    miss_imag = far_imag * factor
    back_real, back_imag = complex_left(table_real, -table_imag, miss_real, miss_imag)
    near_real, near_imag = complex_right(back_real, back_imag, table_real, -table_imag)
    return jnp.stack(
        [
            probe_real * near_real + probe_imag * near_imag,
            probe_real * near_imag - probe_imag * near_real,
        ]
    )


def add_patch(canvas, patch_values, corner_row, corner_col):
    zero_index = jnp.zeros((), jnp.int32)
    starts = (zero_index, corner_row, corner_col)
    present = lax.dynamic_slice(canvas, starts, patch_values.shape)
    return lax.dynamic_update_slice(canvas, present + patch_values, starts)


def fold_rows(extended, margin, length):
    middle_part = extended[:, 2 * margin : 2 * margin + length]
    upper_rim = extended[:, :margin]
    lower_rim = extended[:, extended.shape[1] - margin :]
    middle_part = middle_part.at[:, :margin].add(upper_rim)
    return middle_part.at[:, length - margin :].add(lower_rim)


def fold_cols(extended, margin, length):
    middle_part = extended[:, :, 2 * margin : 2 * margin + length]
    left_rim = extended[:, :, :margin]
    right_rim = extended[:, :, extended.shape[2] - margin :]
    middle_part = middle_part.at[:, :, :margin].add(left_rim)
    return middle_part.at[:, :, length - margin :].add(right_rim)


def settle(stacked, margin, block_rows, block_cols):
    full_ext = with_halo(stacked, (("sx", 1), ("sy", 2)), margin)
    return fold_cols(fold_rows(full_ext, margin, block_rows), margin, block_cols)


def local_pass(canvas, extended, spots, own_amps, probe_field, table_real, table_imag, upper_bound):
    size_probe = probe_field.shape[1]

    def local_step(slot_index, canvas_state):
        row_start = spots[slot_index, 0]
        col_start = spots[slot_index, 1]
        zero_index = jnp.zeros((), jnp.int32)
        object_patch = lax.dynamic_slice(
            extended, (zero_index, row_start, col_start), (2, size_probe, size_probe)
        )
        update = position_gradient(
            object_patch, probe_field, own_amps[slot_index], table_real, table_imag
        )
        return add_patch(canvas_state, update, row_start, col_start)

    return lax.fori_loop(0, upper_bound, local_step, canvas)


def dot_exact(left_side, right_side):
    return jnp.dot(
        left_side, right_side, precision=lax.Precision.HIGHEST, preferred_element_type=jnp.float32
    )


def window_tools(size, row, col):
    lanes = 128
    sublanes = 8
    wide = size + lanes
    tall = size + sublanes
    row_base = pl.multiple_of((row // sublanes) * sublanes, sublanes)
    col_base = pl.multiple_of((col // lanes) * lanes, lanes)
    row_shift = row % sublanes
    col_shift = col % lanes
    rows = pl.ds(row_base, tall)
    cols = pl.ds(col_base, wide)

    def take(ref, channel):
        block = ref[channel, rows, cols]
        block = pltpu.roll(block, (tall - row_shift) % tall, 0)
        return pltpu.roll(block, (wide - col_shift) % wide, 1)[:size, :size]

    def put(ref, channel, values):
        block = jnp.concatenate([values, jnp.zeros((size, lanes), jnp.float32)], axis=1)
        block = jnp.concatenate([block, jnp.zeros((sublanes, wide), jnp.float32)], axis=0)
        block = pltpu.roll(pltpu.roll(block, col_shift, 1), row_shift, 0)
        ref[channel, rows, cols] += block

    return take, put


def gradient_kernel(spots_ref, count_ref, ext_ref, probe_ref, amps_ref, fr_ref, fi_ref, out_ref):
    size = probe_ref.shape[1]
    out_ref[...] = jnp.zeros(out_ref.shape, jnp.float32)
    for slot in range(amps_ref.shape[0]):

        @pl.when(slot < count_ref[0])
        def _():
            take, put = window_tools(size, spots_ref[slot, 0], spots_ref[slot, 1])
            probe_real = probe_ref[0]
            probe_imag = probe_ref[1]
            table_real = fr_ref[...]
            table_imag = fi_ref[...]
            obj_real = take(ext_ref, 0)
            obj_imag = take(ext_ref, 1)
            exit_real = probe_real * obj_real - probe_imag * obj_imag
            exit_imag = probe_real * obj_imag + probe_imag * obj_real
            half_real = dot_exact(table_real, exit_real) - dot_exact(table_imag, exit_imag)
            half_imag = dot_exact(table_real, exit_imag) + dot_exact(table_imag, exit_real)
            far_real = dot_exact(half_real, table_real) - dot_exact(half_imag, table_imag)
            far_imag = dot_exact(half_real, table_imag) + dot_exact(half_imag, table_real)
            factor = 1.0 - amps_ref[slot] / jnp.sqrt(far_real * far_real + far_imag * far_imag + SMOOTH)
            miss_real = far_real * factor
            miss_imag = far_imag * factor
            back_real = dot_exact(table_real, miss_real) + dot_exact(table_imag, miss_imag)
            back_imag = dot_exact(table_real, miss_imag) - dot_exact(table_imag, miss_real)
            near_real = dot_exact(back_real, table_real) + dot_exact(back_imag, table_imag)
            near_imag = dot_exact(back_imag, table_real) - dot_exact(back_real, table_imag)
            put(out_ref, 0, probe_real * near_real + probe_imag * near_imag)
            put(out_ref, 1, probe_real * near_imag - probe_imag * near_real)


def power_kernel(spots_ref, count_ref, probe_ref, out_ref):
    size = probe_ref.shape[1]
    out_ref[...] = jnp.zeros(out_ref.shape, jnp.float32)
    power = probe_ref[0] * probe_ref[0] + probe_ref[1] * probe_ref[1]
    for slot in range(spots_ref.shape[0]):

        @pl.when(slot < count_ref[0])
        def _():
            _, put = window_tools(size, spots_ref[slot, 0], spots_ref[slot, 1])
            put(out_ref, 0, power)


VMEM_SPEC = pl.BlockSpec(memory_space=pltpu.VMEM)
SMEM_SPEC = pl.BlockSpec(memory_space=pltpu.SMEM)
KERNEL_PARAMS = pltpu.CompilerParams(vmem_limit_bytes=60 * 1024 * 1024)


def gradient_canvas(ext_shape, spots, count, extended, probe_field, own_amps, tables):
    return pl.pallas_call(
        gradient_kernel,
        out_shape=jax.ShapeDtypeStruct((2,) + ext_shape, jnp.float32),
        in_specs=[SMEM_SPEC, SMEM_SPEC] + [VMEM_SPEC] * 5,
        out_specs=VMEM_SPEC,
        compiler_params=KERNEL_PARAMS,
    )(spots, count.reshape(1), extended, probe_field, own_amps, tables[0], tables[1])


def power_canvas(ext_shape, spots, count, probe_field):
    return pl.pallas_call(
        power_kernel,
        out_shape=jax.ShapeDtypeStruct((1,) + ext_shape, jnp.float32),
        in_specs=[SMEM_SPEC, SMEM_SPEC, VMEM_SPEC],
        out_specs=VMEM_SPEC,
        compiler_params=KERNEL_PARAMS,
    )(spots, count.reshape(1), probe_field)


NEIGHBOURS = [(-1, -1), (-1, 0), (-1, 1), (0, -1), (0, 1), (1, -1), (1, 0), (1, 1)]


def mesh_place():
    return (
        lax.axis_index("sx"),
        lax.axis_index("sy"),
        lax.axis_size("sx"),
        lax.axis_size("sy"),
    )


def exists(row_dev, col_dev, row_count, col_count):
    return (row_dev >= 0) & (row_dev < row_count) & (col_dev >= 0) & (col_dev < col_count)


def halo_kernel(cur_ref, ext_ref, send_sems, recv_sems):
    rows = cur_ref.shape[1]
    cols = cur_ref.shape[2]
    margin = (ext_ref.shape[2] - cols) // 2
    me_r, me_c, n_r, n_c = mesh_place()
    ext_ref[:, margin : margin + rows, margin : margin + cols] = cur_ref[...]
    src_cols = {-1: slice(0, margin), 0: slice(0, cols), 1: slice(cols - margin, cols)}
    dst_rows = {-1: slice(margin + rows, 2 * margin + rows), 0: slice(margin, margin + rows), 1: slice(0, margin)}
    dst_cols = {-1: slice(margin + cols, 2 * margin + cols), 0: slice(margin, margin + cols), 1: slice(0, margin)}
    copies = []
    for index, (dr, dc) in enumerate(NEIGHBOURS):
        copy = pltpu.make_async_remote_copy(
            src_ref=cur_ref.at[:, :, src_cols[dc]],
            dst_ref=ext_ref.at[:, dst_rows[dr], dst_cols[dc]],
            send_sem=send_sems.at[index],
            recv_sem=recv_sems.at[index],
            device_id=(me_r + dr, me_c + dc),
            device_id_type=pl.DeviceIdType.MESH,
        )
        copies.append(copy)

        @pl.when(exists(me_r + dr, me_c + dc, n_r, n_c))
        def _():
            copy.start()

        @pl.when(jnp.logical_not(exists(me_r - dr, me_c - dc, n_r, n_c)))
        def _():
            region = (slice(None), dst_rows[dr], dst_cols[dc])
            ext_ref[region] = jnp.zeros(ext_ref[region].shape, jnp.float32)

    for index, (dr, dc) in enumerate(NEIGHBOURS):
        copy = copies[index]

        @pl.when(exists(me_r + dr, me_c + dc, n_r, n_c))
        def _():
            copy.wait_send()

        @pl.when(exists(me_r - dr, me_c - dc, n_r, n_c))
        def _():
            copy.wait_recv()


def fold_kernel(canvas_ref, out_ref, wide_bufs, narrow_bufs, send_sems, recv_sems):
    rows = out_ref.shape[1]
    cols = out_ref.shape[2]
    margin = (canvas_ref.shape[2] - cols) // 2
    me_r, me_c, n_r, n_c = mesh_place()
    src_rows = {-1: slice(0, margin), 0: slice(margin, margin + rows), 1: slice(margin + rows, 2 * margin + rows)}
    src_cols = {-1: slice(0, margin), 0: slice(margin, margin + cols), 1: slice(margin + cols, 2 * margin + cols)}
    dst_cols = {-1: slice(cols - margin, cols), 0: slice(0, cols), 1: slice(0, margin)}
    copies = []
    wide_index = 0
    narrow_index = 0
    for index, (dr, dc) in enumerate(NEIGHBOURS):
        if dc == 0:
            buffer = wide_bufs.at[wide_index]
            wide_index += 1
        else:
            buffer = narrow_bufs.at[narrow_index]
            narrow_index += 1
        copy = pltpu.make_async_remote_copy(
            src_ref=canvas_ref.at[:, src_rows[dr], src_cols[dc]],
            dst_ref=buffer,
            send_sem=send_sems.at[index],
            recv_sem=recv_sems.at[index],
            device_id=(me_r + dr, me_c + dc),
            device_id_type=pl.DeviceIdType.MESH,
        )
        copies.append((copy, buffer))

        @pl.when(exists(me_r + dr, me_c + dc, n_r, n_c))
        def _():
            copy.start()

    out_ref[...] = canvas_ref[:, margin : margin + rows, margin : margin + cols]
    for index, (dr, dc) in enumerate(NEIGHBOURS):
        copy, buffer = copies[index]

        @pl.when(exists(me_r + dr, me_c + dc, n_r, n_c))
        def _():
            copy.wait_send()

        @pl.when(exists(me_r - dr, me_c - dc, n_r, n_c))
        def _():
            copy.wait_recv()
            out_ref[:, :, dst_cols[dc]] += buffer[...]


def exchange_halo(current, margin):
    depth, rows, cols = current.shape
    return pl.pallas_call(
        halo_kernel,
        out_shape=jax.ShapeDtypeStruct((depth, rows + 2 * margin, cols + 2 * margin), jnp.float32),
        in_specs=[VMEM_SPEC],
        out_specs=VMEM_SPEC,
        scratch_shapes=[pltpu.SemaphoreType.DMA((8,)), pltpu.SemaphoreType.DMA((8,))],
        compiler_params=pltpu.CompilerParams(vmem_limit_bytes=60 * 1024 * 1024, has_side_effects=True),
    )(current)


def exchange_fold(canvas, margin):
    depth, ext_rows, ext_cols = canvas.shape
    rows = ext_rows - 2 * margin
    cols = ext_cols - 2 * margin
    return pl.pallas_call(
        fold_kernel,
        out_shape=jax.ShapeDtypeStruct((depth, rows, cols), jnp.float32),
        in_specs=[VMEM_SPEC],
        out_specs=VMEM_SPEC,
        scratch_shapes=[
            pltpu.VMEM((2, depth, margin, cols), jnp.float32),
            pltpu.VMEM((6, depth, margin, margin), jnp.float32),
            pltpu.SemaphoreType.DMA((8,)),
            pltpu.SemaphoreType.DMA((8,)),
        ],
        compiler_params=pltpu.CompilerParams(vmem_limit_bytes=60 * 1024 * 1024, has_side_effects=True),
    )(canvas)


def on_device(object_field, probe_field, amplitudes, centres, counts):
    size_probe = probe_field.shape[1]
    margin = size_probe // 2
    block_rows = object_field.shape[1]
    block_cols = object_field.shape[2]
    tables = dft_tables(size_probe)
    spots = centres[0, 0]
    own_amps = amplitudes[0, 0]
    sx_size = lax.axis_size("sx")
    sx_index = lax.axis_index("sx")
    column_counts = counts[:, 0]
    sx_positions = jnp.arange(sx_size, dtype=jnp.int32)
    own_count = jnp.sum(jnp.where(sx_positions == sx_index, column_counts, 0))
    ext_shape = (block_rows + size_probe, block_cols + size_probe)

    power = power_canvas(ext_shape, spots, own_count, probe_field)
    current = object_field
    for sweep_index in range(ITERS):
        extended = exchange_halo(current, margin)
        canvas = gradient_canvas(ext_shape, spots, own_count, extended, probe_field, own_amps, tables)
        if sweep_index == 0:
            folded = exchange_fold(jnp.concatenate([canvas, power], axis=0), margin)
            illumination = folded[2]
            gradient = folded[0:2]
        else:
            gradient = exchange_fold(canvas, margin)
        current = current - gradient / (illumination + DAMPING)
    return current


def solution(mesh):
    return jax.shard_map(
        on_device,
        mesh=mesh,
        in_specs=(
            P(None, "sx", "sy"),
            P(),
            P("sx", "sy", None, None, None),
            P("sx", "sy", None, None),
            P(None, "sy"),
        ),
        out_specs=P(None, "sx", "sy"),
        check_vma=False,
    )
```

```python
import math

import jax
import jax.numpy as jnp
from jax import lax
from jax.sharding import PartitionSpec as P
from jax.experimental import pallas as pl
from jax.experimental.pallas import tpu as pltpu

ITERS = 2


SMOOTH = 1.0
DAMPING = 1.0


def with_halo(cells, sides, width):
    for axis, dim in sides:
        count = lax.axis_size(axis)
        ends = count - 1
        head = lax.slice_in_dim(cells, 0, width, axis=dim)
        tail = lax.slice_in_dim(cells, cells.shape[dim] - width, cells.shape[dim], axis=dim)
        cells = jnp.concatenate(
            [
                lax.ppermute(tail, axis, [(i, (i + 1) % count) for i in range(ends)]),
                cells,
                lax.ppermute(head, axis, [((i + 1) % count, i) for i in range(ends)]),
            ],
            axis=dim,
        )
    return cells


def dft_tables(length):
    index_values = jnp.arange(length, dtype=jnp.int32)
    product_mod = index_values[:, None] * index_values[None, :] % length
    angles = product_mod.astype(jnp.float32) * (2.0 * math.pi / length)
    scaling = 1.0 / math.sqrt(length)
    return (jnp.cos(angles) * scaling, -jnp.sin(angles) * scaling)


def matmul_exact(left_side, right_side):
    return jnp.dot(left_side, right_side, precision=lax.Precision.HIGHEST)


def complex_left(table_real, table_imag, field_real, field_imag):
    out_real = matmul_exact(table_real, field_real) - matmul_exact(table_imag, field_imag)
    out_imag = matmul_exact(table_real, field_imag) + matmul_exact(table_imag, field_real)
    return (out_real, out_imag)


def complex_right(field_real, field_imag, table_real, table_imag):
    out_real = matmul_exact(field_real, table_real) - matmul_exact(field_imag, table_imag)
    out_imag = matmul_exact(field_real, table_imag) + matmul_exact(field_imag, table_real)
    return (out_real, out_imag)


def position_gradient(object_patch, probe_field, amplitude, table_real, table_imag):
    probe_real = probe_field[0]
    probe_imag = probe_field[1]
    exit_real = probe_real * object_patch[0] - probe_imag * object_patch[1]
    exit_imag = probe_real * object_patch[1] + probe_imag * object_patch[0]
    half_real, half_imag = complex_left(table_real, table_imag, exit_real, exit_imag)
    far_real, far_imag = complex_right(half_real, half_imag, table_real, table_imag)
    factor = 1.0 - amplitude / jnp.sqrt(far_real * far_real + far_imag * far_imag + SMOOTH)
    miss_real = far_real * factor
    miss_imag = far_imag * factor
    back_real, back_imag = complex_left(table_real, -table_imag, miss_real, miss_imag)
    near_real, near_imag = complex_right(back_real, back_imag, table_real, -table_imag)
    return jnp.stack(
        [
            probe_real * near_real + probe_imag * near_imag,
            probe_real * near_imag - probe_imag * near_real,
        ]
    )


def add_patch(canvas, patch_values, corner_row, corner_col):
    zero_index = jnp.zeros((), jnp.int32)
    starts = (zero_index, corner_row, corner_col)
    present = lax.dynamic_slice(canvas, starts, patch_values.shape)
    return lax.dynamic_update_slice(canvas, present + patch_values, starts)


def fold_rows(extended, margin, length):
    middle_part = extended[:, 2 * margin : 2 * margin + length]
    upper_rim = extended[:, :margin]
    lower_rim = extended[:, extended.shape[1] - margin :]
    middle_part = middle_part.at[:, :margin].add(upper_rim)
    return middle_part.at[:, length - margin :].add(lower_rim)


def fold_cols(extended, margin, length):
    middle_part = extended[:, :, 2 * margin : 2 * margin + length]
    left_rim = extended[:, :, :margin]
    right_rim = extended[:, :, extended.shape[2] - margin :]
    middle_part = middle_part.at[:, :, :margin].add(left_rim)
    return middle_part.at[:, :, length - margin :].add(right_rim)


def settle(stacked, margin, block_rows, block_cols):
    full_ext = with_halo(stacked, (("sx", 1), ("sy", 2)), margin)
    return fold_cols(fold_rows(full_ext, margin, block_rows), margin, block_cols)


def local_pass(canvas, extended, spots, own_amps, probe_field, table_real, table_imag, upper_bound):
    size_probe = probe_field.shape[1]

    def local_step(slot_index, canvas_state):
        row_start = spots[slot_index, 0]
        col_start = spots[slot_index, 1]
        zero_index = jnp.zeros((), jnp.int32)
        object_patch = lax.dynamic_slice(
            extended, (zero_index, row_start, col_start), (2, size_probe, size_probe)
        )
        update = position_gradient(
            object_patch, probe_field, own_amps[slot_index], table_real, table_imag
        )
        return add_patch(canvas_state, update, row_start, col_start)

    return lax.fori_loop(0, upper_bound, local_step, canvas)


def dot_exact(left_side, right_side):
    return jnp.dot(
        left_side, right_side, precision=lax.Precision.HIGHEST, preferred_element_type=jnp.float32
    )


def window_tools(size, row, col):
    lanes = 128
    sublanes = 8
    wide = size + lanes
    tall = size + sublanes
    row_base = pl.multiple_of((row // sublanes) * sublanes, sublanes)
    col_base = pl.multiple_of((col // lanes) * lanes, lanes)
    row_shift = row % sublanes
    col_shift = col % lanes
    rows = pl.ds(row_base, tall)
    cols = pl.ds(col_base, wide)

    def take(ref, channel):
        block = ref[channel, rows, cols]
        block = pltpu.roll(block, (tall - row_shift) % tall, 0)
        return pltpu.roll(block, (wide - col_shift) % wide, 1)[:size, :size]

    def put(ref, channel, values):
        block = jnp.concatenate([values, jnp.zeros((size, lanes), jnp.float32)], axis=1)
        block = jnp.concatenate([block, jnp.zeros((sublanes, wide), jnp.float32)], axis=0)
        block = pltpu.roll(pltpu.roll(block, col_shift, 1), row_shift, 0)
        ref[channel, rows, cols] += block

    return take, put


def gradient_kernel(spots_ref, count_ref, ext_ref, probe_ref, amps_ref, fr_ref, fi_ref, out_ref):
    size = probe_ref.shape[1]
    out_ref[...] = jnp.zeros(out_ref.shape, jnp.float32)
    for slot in range(amps_ref.shape[0]):

        @pl.when(slot < count_ref[0])
        def _():
            take, put = window_tools(size, spots_ref[slot, 0], spots_ref[slot, 1])
            probe_real = probe_ref[0]
            probe_imag = probe_ref[1]
            table_real = fr_ref[...]
            table_imag = fi_ref[...]
            obj_real = take(ext_ref, 0)
            obj_imag = take(ext_ref, 1)
            exit_real = probe_real * obj_real - probe_imag * obj_imag
            exit_imag = probe_real * obj_imag + probe_imag * obj_real
            half_real = dot_exact(table_real, exit_real) - dot_exact(table_imag, exit_imag)
            half_imag = dot_exact(table_real, exit_imag) + dot_exact(table_imag, exit_real)
            far_real = dot_exact(half_real, table_real) - dot_exact(half_imag, table_imag)
            far_imag = dot_exact(half_real, table_imag) + dot_exact(half_imag, table_real)
            factor = 1.0 - amps_ref[slot] / jnp.sqrt(far_real * far_real + far_imag * far_imag + SMOOTH)
            miss_real = far_real * factor
            miss_imag = far_imag * factor
            back_real = dot_exact(table_real, miss_real) + dot_exact(table_imag, miss_imag)
            back_imag = dot_exact(table_real, miss_imag) - dot_exact(table_imag, miss_real)
            near_real = dot_exact(back_real, table_real) + dot_exact(back_imag, table_imag)
            near_imag = dot_exact(back_imag, table_real) - dot_exact(back_real, table_imag)
            put(out_ref, 0, probe_real * near_real + probe_imag * near_imag)
            put(out_ref, 1, probe_real * near_imag - probe_imag * near_real)


def power_kernel(spots_ref, count_ref, probe_ref, out_ref):
    size = probe_ref.shape[1]
    out_ref[...] = jnp.zeros(out_ref.shape, jnp.float32)
    power = probe_ref[0] * probe_ref[0] + probe_ref[1] * probe_ref[1]
    for slot in range(spots_ref.shape[0]):

        @pl.when(slot < count_ref[0])
        def _():
            _, put = window_tools(size, spots_ref[slot, 0], spots_ref[slot, 1])
            put(out_ref, 0, power)


VMEM_SPEC = pl.BlockSpec(memory_space=pltpu.VMEM)
SMEM_SPEC = pl.BlockSpec(memory_space=pltpu.SMEM)
KERNEL_PARAMS = pltpu.CompilerParams(vmem_limit_bytes=60 * 1024 * 1024)


def gradient_canvas(ext_shape, spots, count, extended, probe_field, own_amps, tables):
    return pl.pallas_call(
        gradient_kernel,
        out_shape=jax.ShapeDtypeStruct((2,) + ext_shape, jnp.float32),
        in_specs=[SMEM_SPEC, SMEM_SPEC] + [VMEM_SPEC] * 5,
        out_specs=VMEM_SPEC,
        compiler_params=KERNEL_PARAMS,
    )(spots, count.reshape(1), extended, probe_field, own_amps, tables[0], tables[1])


def power_canvas(ext_shape, spots, count, probe_field):
    return pl.pallas_call(
        power_kernel,
        out_shape=jax.ShapeDtypeStruct((1,) + ext_shape, jnp.float32),
        in_specs=[SMEM_SPEC, SMEM_SPEC, VMEM_SPEC],
        out_specs=VMEM_SPEC,
        compiler_params=KERNEL_PARAMS,
    )(spots, count.reshape(1), probe_field)


NEIGHBOURS = [(-1, -1), (-1, 0), (-1, 1), (0, -1), (0, 1), (1, -1), (1, 0), (1, 1)]


def mesh_place():
    return (
        lax.axis_index("sx"),
        lax.axis_index("sy"),
        lax.axis_size("sx"),
        lax.axis_size("sy"),
    )


def exists(row_dev, col_dev, row_count, col_count):
    return (row_dev >= 0) & (row_dev < row_count) & (col_dev >= 0) & (col_dev < col_count)


def neighbour_barrier(me_r, me_c, n_r, n_c):
    barrier = pltpu.get_barrier_semaphore()
    greeted = jnp.int32(0)
    for dr, dc in NEIGHBOURS:
        present = exists(me_r + dr, me_c + dc, n_r, n_c)

        @pl.when(present)
        def _():
            pl.semaphore_signal(
                barrier, inc=1, device_id=(me_r + dr, me_c + dc), device_id_type=pl.DeviceIdType.MESH
            )

        greeted = greeted + present.astype(jnp.int32)
    pl.semaphore_wait(barrier, greeted)


def halo_kernel(cur_ref, ext_ref, send_sems, recv_sems):
    rows = cur_ref.shape[1]
    cols = cur_ref.shape[2]
    margin = (ext_ref.shape[2] - cols) // 2
    me_r, me_c, n_r, n_c = mesh_place()
    ext_ref[:, margin : margin + rows, margin : margin + cols] = cur_ref[...]
    neighbour_barrier(me_r, me_c, n_r, n_c)
    src_cols = {-1: slice(0, margin), 0: slice(0, cols), 1: slice(cols - margin, cols)}
    dst_rows = {-1: slice(margin + rows, 2 * margin + rows), 0: slice(margin, margin + rows), 1: slice(0, margin)}
    dst_cols = {-1: slice(margin + cols, 2 * margin + cols), 0: slice(margin, margin + cols), 1: slice(0, margin)}
    copies = []
    for index, (dr, dc) in enumerate(NEIGHBOURS):
        copy = pltpu.make_async_remote_copy(
            src_ref=cur_ref.at[:, :, src_cols[dc]],
            dst_ref=ext_ref.at[:, dst_rows[dr], dst_cols[dc]],
            send_sem=send_sems.at[index],
            recv_sem=recv_sems.at[index],
            device_id=(me_r + dr, me_c + dc),
            device_id_type=pl.DeviceIdType.MESH,
        )
        copies.append(copy)

        @pl.when(exists(me_r + dr, me_c + dc, n_r, n_c))
        def _():
            copy.start()

        @pl.when(jnp.logical_not(exists(me_r - dr, me_c - dc, n_r, n_c)))
        def _():
            region = (slice(None), dst_rows[dr], dst_cols[dc])
            ext_ref[region] = jnp.zeros(ext_ref[region].shape, jnp.float32)

    for index, (dr, dc) in enumerate(NEIGHBOURS):
        copy = copies[index]

        @pl.when(exists(me_r + dr, me_c + dc, n_r, n_c))
        def _():
            copy.wait_send()

        @pl.when(exists(me_r - dr, me_c - dc, n_r, n_c))
        def _():
            copy.wait_recv()


def fold_kernel(canvas_ref, out_ref, wide_bufs, narrow_bufs, send_sems, recv_sems):
    rows = out_ref.shape[1]
    cols = out_ref.shape[2]
    margin = (canvas_ref.shape[2] - cols) // 2
    me_r, me_c, n_r, n_c = mesh_place()
    src_rows = {-1: slice(0, margin), 0: slice(margin, margin + rows), 1: slice(margin + rows, 2 * margin + rows)}
    src_cols = {-1: slice(0, margin), 0: slice(margin, margin + cols), 1: slice(margin + cols, 2 * margin + cols)}
    dst_cols = {-1: slice(cols - margin, cols), 0: slice(0, cols), 1: slice(0, margin)}
    neighbour_barrier(me_r, me_c, n_r, n_c)
    copies = []
    wide_index = 0
    narrow_index = 0
    for index, (dr, dc) in enumerate(NEIGHBOURS):
        if dc == 0:
            buffer = wide_bufs.at[wide_index]
            wide_index += 1
        else:
            buffer = narrow_bufs.at[narrow_index]
            narrow_index += 1
        copy = pltpu.make_async_remote_copy(
            src_ref=canvas_ref.at[:, src_rows[dr], src_cols[dc]],
            dst_ref=buffer,
            send_sem=send_sems.at[index],
            recv_sem=recv_sems.at[index],
            device_id=(me_r + dr, me_c + dc),
            device_id_type=pl.DeviceIdType.MESH,
        )
        copies.append((copy, buffer))

        @pl.when(exists(me_r + dr, me_c + dc, n_r, n_c))
        def _():
            copy.start()

    out_ref[...] = canvas_ref[:, margin : margin + rows, margin : margin + cols]
    for index, (dr, dc) in enumerate(NEIGHBOURS):
        copy, buffer = copies[index]

        @pl.when(exists(me_r + dr, me_c + dc, n_r, n_c))
        def _():
            copy.wait_send()

        @pl.when(exists(me_r - dr, me_c - dc, n_r, n_c))
        def _():
            copy.wait_recv()
            out_ref[:, :, dst_cols[dc]] += buffer[...]


def exchange_halo(current, margin):
    depth, rows, cols = current.shape
    return pl.pallas_call(
        halo_kernel,
        out_shape=jax.ShapeDtypeStruct((depth, rows + 2 * margin, cols + 2 * margin), jnp.float32),
        in_specs=[VMEM_SPEC],
        out_specs=VMEM_SPEC,
        scratch_shapes=[pltpu.SemaphoreType.DMA((8,)), pltpu.SemaphoreType.DMA((8,))],
        compiler_params=pltpu.CompilerParams(
            vmem_limit_bytes=60 * 1024 * 1024, has_side_effects=True, collective_id=0
        ),
    )(current)


def exchange_fold(canvas, margin):
    depth, ext_rows, ext_cols = canvas.shape
    rows = ext_rows - 2 * margin
    cols = ext_cols - 2 * margin
    return pl.pallas_call(
        fold_kernel,
        out_shape=jax.ShapeDtypeStruct((depth, rows, cols), jnp.float32),
        in_specs=[VMEM_SPEC],
        out_specs=VMEM_SPEC,
        scratch_shapes=[
            pltpu.VMEM((2, depth, margin, cols), jnp.float32),
            pltpu.VMEM((6, depth, margin, margin), jnp.float32),
            pltpu.SemaphoreType.DMA((8,)),
            pltpu.SemaphoreType.DMA((8,)),
        ],
        compiler_params=pltpu.CompilerParams(
            vmem_limit_bytes=60 * 1024 * 1024, has_side_effects=True, collective_id=depth
        ),
    )(canvas)


def on_device(object_field, probe_field, amplitudes, centres, counts):
    size_probe = probe_field.shape[1]
    margin = size_probe // 2
    block_rows = object_field.shape[1]
    block_cols = object_field.shape[2]
    tables = dft_tables(size_probe)
    spots = centres[0, 0]
    own_amps = amplitudes[0, 0]
    sx_size = lax.axis_size("sx")
    sx_index = lax.axis_index("sx")
    column_counts = counts[:, 0]
    sx_positions = jnp.arange(sx_size, dtype=jnp.int32)
    own_count = jnp.sum(jnp.where(sx_positions == sx_index, column_counts, 0))
    ext_shape = (block_rows + size_probe, block_cols + size_probe)

    power = power_canvas(ext_shape, spots, own_count, probe_field)
    current = object_field
    for sweep_index in range(ITERS):
        extended = exchange_halo(current, margin)
        canvas = gradient_canvas(ext_shape, spots, own_count, extended, probe_field, own_amps, tables)
        if sweep_index == 0:
            folded = exchange_fold(jnp.concatenate([canvas, power], axis=0), margin)
            illumination = folded[2]
            gradient = folded[0:2]
        else:
            gradient = exchange_fold(canvas, margin)
        current = current - gradient / (illumination + DAMPING)
    return current


def solution(mesh):
    return jax.shard_map(
        on_device,
        mesh=mesh,
        in_specs=(
            P(None, "sx", "sy"),
            P(),
            P("sx", "sy", None, None, None),
            P("sx", "sy", None, None),
            P(None, "sy"),
        ),
        out_specs=P(None, "sx", "sy"),
        check_vma=False,
    )
```

```python
import math

import jax
import jax.numpy as jnp
from jax import lax
from jax.sharding import PartitionSpec as P
from jax.experimental import pallas as pl
from jax.experimental.pallas import tpu as pltpu

ITERS = 2


SMOOTH = 1.0
DAMPING = 1.0


def with_halo(cells, sides, width):
    for axis, dim in sides:
        count = lax.axis_size(axis)
        ends = count - 1
        head = lax.slice_in_dim(cells, 0, width, axis=dim)
        tail = lax.slice_in_dim(cells, cells.shape[dim] - width, cells.shape[dim], axis=dim)
        cells = jnp.concatenate(
            [
                lax.ppermute(tail, axis, [(i, (i + 1) % count) for i in range(ends)]),
                cells,
                lax.ppermute(head, axis, [((i + 1) % count, i) for i in range(ends)]),
            ],
            axis=dim,
        )
    return cells


def dft_tables(length):
    index_values = jnp.arange(length, dtype=jnp.int32)
    product_mod = index_values[:, None] * index_values[None, :] % length
    angles = product_mod.astype(jnp.float32) * (2.0 * math.pi / length)
    scaling = 1.0 / math.sqrt(length)
    return (jnp.cos(angles) * scaling, -jnp.sin(angles) * scaling)


def matmul_exact(left_side, right_side):
    return jnp.dot(left_side, right_side, precision=lax.Precision.HIGHEST)


def complex_left(table_real, table_imag, field_real, field_imag):
    out_real = matmul_exact(table_real, field_real) - matmul_exact(table_imag, field_imag)
    out_imag = matmul_exact(table_real, field_imag) + matmul_exact(table_imag, field_real)
    return (out_real, out_imag)


def complex_right(field_real, field_imag, table_real, table_imag):
    out_real = matmul_exact(field_real, table_real) - matmul_exact(field_imag, table_imag)
    out_imag = matmul_exact(field_real, table_imag) + matmul_exact(field_imag, table_real)
    return (out_real, out_imag)


def position_gradient(object_patch, probe_field, amplitude, table_real, table_imag):
    probe_real = probe_field[0]
    probe_imag = probe_field[1]
    exit_real = probe_real * object_patch[0] - probe_imag * object_patch[1]
    exit_imag = probe_real * object_patch[1] + probe_imag * object_patch[0]
    half_real, half_imag = complex_left(table_real, table_imag, exit_real, exit_imag)
    far_real, far_imag = complex_right(half_real, half_imag, table_real, table_imag)
    factor = 1.0 - amplitude / jnp.sqrt(far_real * far_real + far_imag * far_imag + SMOOTH)
    miss_real = far_real * factor
    miss_imag = far_imag * factor
    back_real, back_imag = complex_left(table_real, -table_imag, miss_real, miss_imag)
    near_real, near_imag = complex_right(back_real, back_imag, table_real, -table_imag)
    return jnp.stack(
        [
            probe_real * near_real + probe_imag * near_imag,
            probe_real * near_imag - probe_imag * near_real,
        ]
    )


def add_patch(canvas, patch_values, corner_row, corner_col):
    zero_index = jnp.zeros((), jnp.int32)
    starts = (zero_index, corner_row, corner_col)
    present = lax.dynamic_slice(canvas, starts, patch_values.shape)
    return lax.dynamic_update_slice(canvas, present + patch_values, starts)


def fold_rows(extended, margin, length):
    middle_part = extended[:, 2 * margin : 2 * margin + length]
    upper_rim = extended[:, :margin]
    lower_rim = extended[:, extended.shape[1] - margin :]
    middle_part = middle_part.at[:, :margin].add(upper_rim)
    return middle_part.at[:, length - margin :].add(lower_rim)


def fold_cols(extended, margin, length):
    middle_part = extended[:, :, 2 * margin : 2 * margin + length]
    left_rim = extended[:, :, :margin]
    right_rim = extended[:, :, extended.shape[2] - margin :]
    middle_part = middle_part.at[:, :, :margin].add(left_rim)
    return middle_part.at[:, :, length - margin :].add(right_rim)


def settle(stacked, margin, block_rows, block_cols):
    full_ext = with_halo(stacked, (("sx", 1), ("sy", 2)), margin)
    return fold_cols(fold_rows(full_ext, margin, block_rows), margin, block_cols)


def local_pass(canvas, extended, spots, own_amps, probe_field, table_real, table_imag, upper_bound):
    size_probe = probe_field.shape[1]

    def local_step(slot_index, canvas_state):
        row_start = spots[slot_index, 0]
        col_start = spots[slot_index, 1]
        zero_index = jnp.zeros((), jnp.int32)
        object_patch = lax.dynamic_slice(
            extended, (zero_index, row_start, col_start), (2, size_probe, size_probe)
        )
        update = position_gradient(
            object_patch, probe_field, own_amps[slot_index], table_real, table_imag
        )
        return add_patch(canvas_state, update, row_start, col_start)

    return lax.fori_loop(0, upper_bound, local_step, canvas)


def dot_exact(left_side, right_side):
    return jnp.dot(
        left_side, right_side, precision=lax.Precision.HIGHEST, preferred_element_type=jnp.float32
    )


def window_tools(size, row, col):
    lanes = 128
    sublanes = 8
    wide = size + lanes
    tall = size + sublanes
    row_base = pl.multiple_of((row // sublanes) * sublanes, sublanes)
    col_base = pl.multiple_of((col // lanes) * lanes, lanes)
    row_shift = row % sublanes
    col_shift = col % lanes
    rows = pl.ds(row_base, tall)
    cols = pl.ds(col_base, wide)

    def take(ref, channel):
        block = ref[channel, rows, cols]
        block = pltpu.roll(block, (tall - row_shift) % tall, 0)
        return pltpu.roll(block, (wide - col_shift) % wide, 1)[:size, :size]

    def put(ref, channel, values):
        block = jnp.concatenate([values, jnp.zeros((size, lanes), jnp.float32)], axis=1)
        block = jnp.concatenate([block, jnp.zeros((sublanes, wide), jnp.float32)], axis=0)
        block = pltpu.roll(pltpu.roll(block, col_shift, 1), row_shift, 0)
        ref[channel, rows, cols] += block

    return take, put


def split_bf16(values):
    scaled = values * 65537.0
    high = scaled - (scaled - values)
    return high.astype(jnp.bfloat16), (values - high).astype(jnp.bfloat16)


def dot_split(left_parts, right_parts):
    left_high, left_low = left_parts
    right_high, right_low = right_parts
    total = jnp.dot(left_high, right_high, preferred_element_type=jnp.float32)
    total += jnp.dot(left_high, right_low, preferred_element_type=jnp.float32)
    return total + jnp.dot(left_low, right_high, preferred_element_type=jnp.float32)


def gradient_kernel(spots_ref, count_ref, ext_ref, probe_ref, amps_ref, tables_ref, out_ref):
    size = probe_ref.shape[1]
    out_ref[...] = jnp.zeros(out_ref.shape, jnp.float32)
    with_power = out_ref.shape[0] > 2
    for slot in range(amps_ref.shape[0]):

        @pl.when(slot < count_ref[0])
        def _():
            take, put = window_tools(size, spots_ref[slot, 0], spots_ref[slot, 1])
            probe_real = probe_ref[0]
            probe_imag = probe_ref[1]
            real_parts = (tables_ref[0], tables_ref[1])
            imag_parts = (tables_ref[2], tables_ref[3])

            def left(field_real, field_imag, sign):
                both = split_bf16(jnp.concatenate([field_real, field_imag], axis=1))
                by_real = dot_split(real_parts, both)
                by_imag = dot_split(imag_parts, both)
                out_real = by_real[:, :size] - sign * by_imag[:, size:]
                out_imag = by_real[:, size:] + sign * by_imag[:, :size]
                return out_real, out_imag

            def right(field_real, field_imag, sign):
                both = split_bf16(jnp.concatenate([field_real, field_imag], axis=0))
                by_real = dot_split(both, real_parts)
                by_imag = dot_split(both, imag_parts)
                out_real = by_real[:size] - sign * by_imag[size:]
                out_imag = by_imag[:size] * sign + by_real[size:]
                return out_real, out_imag

            obj_real = take(ext_ref, 0)
            obj_imag = take(ext_ref, 1)
            exit_real = probe_real * obj_real - probe_imag * obj_imag
            exit_imag = probe_real * obj_imag + probe_imag * obj_real
            half_real, half_imag = left(exit_real, exit_imag, 1.0)
            far_real, far_imag = right(half_real, half_imag, 1.0)
            factor = 1.0 - amps_ref[slot] / jnp.sqrt(far_real * far_real + far_imag * far_imag + SMOOTH)
            miss_real = far_real * factor
            miss_imag = far_imag * factor
            back_real, back_imag = left(miss_real, miss_imag, -1.0)
            near_real, near_imag = right(back_real, back_imag, -1.0)
            put(out_ref, 0, probe_real * near_real + probe_imag * near_imag)
            put(out_ref, 1, probe_real * near_imag - probe_imag * near_real)
            if with_power:
                put(out_ref, 2, probe_real * probe_real + probe_imag * probe_imag)


def power_kernel(spots_ref, count_ref, probe_ref, out_ref):
    size = probe_ref.shape[1]
    out_ref[...] = jnp.zeros(out_ref.shape, jnp.float32)
    power = probe_ref[0] * probe_ref[0] + probe_ref[1] * probe_ref[1]
    for slot in range(spots_ref.shape[0]):

        @pl.when(slot < count_ref[0])
        def _():
            _, put = window_tools(size, spots_ref[slot, 0], spots_ref[slot, 1])
            put(out_ref, 0, power)


VMEM_SPEC = pl.BlockSpec(memory_space=pltpu.VMEM)
SMEM_SPEC = pl.BlockSpec(memory_space=pltpu.SMEM)
KERNEL_PARAMS = pltpu.CompilerParams(vmem_limit_bytes=60 * 1024 * 1024)


def gradient_canvas(channels, ext_shape, spots, count, extended, probe_field, own_amps, tables):
    parts = jnp.stack(split_bf16(tables[0]) + split_bf16(tables[1]))
    return pl.pallas_call(
        gradient_kernel,
        out_shape=jax.ShapeDtypeStruct((channels,) + ext_shape, jnp.float32),
        in_specs=[SMEM_SPEC, SMEM_SPEC] + [VMEM_SPEC] * 4,
        out_specs=VMEM_SPEC,
        compiler_params=KERNEL_PARAMS,
    )(spots, count.reshape(1), extended, probe_field, own_amps, parts)


def power_canvas(ext_shape, spots, count, probe_field):
    return pl.pallas_call(
        power_kernel,
        out_shape=jax.ShapeDtypeStruct((1,) + ext_shape, jnp.float32),
        in_specs=[SMEM_SPEC, SMEM_SPEC, VMEM_SPEC],
        out_specs=VMEM_SPEC,
        compiler_params=KERNEL_PARAMS,
    )(spots, count.reshape(1), probe_field)


NEIGHBOURS = [(-1, -1), (-1, 0), (-1, 1), (0, -1), (0, 1), (1, -1), (1, 0), (1, 1)]


def mesh_place():
    return (
        lax.axis_index("sx"),
        lax.axis_index("sy"),
        lax.axis_size("sx"),
        lax.axis_size("sy"),
    )


def exists(row_dev, col_dev, row_count, col_count):
    return (row_dev >= 0) & (row_dev < row_count) & (col_dev >= 0) & (col_dev < col_count)


def neighbour_barrier(me_r, me_c, n_r, n_c):
    barrier = pltpu.get_barrier_semaphore()
    greeted = jnp.int32(0)
    for dr, dc in NEIGHBOURS:
        present = exists(me_r + dr, me_c + dc, n_r, n_c)

        @pl.when(present)
        def _():
            pl.semaphore_signal(
                barrier, inc=1, device_id=(me_r + dr, me_c + dc), device_id_type=pl.DeviceIdType.MESH
            )

        greeted = greeted + present.astype(jnp.int32)
    pl.semaphore_wait(barrier, greeted)


def halo_kernel(cur_ref, ext_ref, send_sems, recv_sems):
    rows = cur_ref.shape[1]
    cols = cur_ref.shape[2]
    margin = (ext_ref.shape[2] - cols) // 2
    me_r, me_c, n_r, n_c = mesh_place()
    ext_ref[:, margin : margin + rows, margin : margin + cols] = cur_ref[...]
    neighbour_barrier(me_r, me_c, n_r, n_c)
    src_cols = {-1: slice(0, margin), 0: slice(0, cols), 1: slice(cols - margin, cols)}
    dst_rows = {-1: slice(margin + rows, 2 * margin + rows), 0: slice(margin, margin + rows), 1: slice(0, margin)}
    dst_cols = {-1: slice(margin + cols, 2 * margin + cols), 0: slice(margin, margin + cols), 1: slice(0, margin)}
    copies = []
    for index, (dr, dc) in enumerate(NEIGHBOURS):
        copy = pltpu.make_async_remote_copy(
            src_ref=cur_ref.at[:, :, src_cols[dc]],
            dst_ref=ext_ref.at[:, dst_rows[dr], dst_cols[dc]],
            send_sem=send_sems.at[index],
            recv_sem=recv_sems.at[index],
            device_id=(me_r + dr, me_c + dc),
            device_id_type=pl.DeviceIdType.MESH,
        )
        copies.append(copy)

        @pl.when(exists(me_r + dr, me_c + dc, n_r, n_c))
        def _():
            copy.start()

        @pl.when(jnp.logical_not(exists(me_r - dr, me_c - dc, n_r, n_c)))
        def _():
            region = (slice(None), dst_rows[dr], dst_cols[dc])
            ext_ref[region] = jnp.zeros(ext_ref[region].shape, jnp.float32)

    for index, (dr, dc) in enumerate(NEIGHBOURS):
        copy = copies[index]

        @pl.when(exists(me_r + dr, me_c + dc, n_r, n_c))
        def _():
            copy.wait_send()

        @pl.when(exists(me_r - dr, me_c - dc, n_r, n_c))
        def _():
            copy.wait_recv()


def fold_kernel(canvas_ref, out_ref, wide_bufs, narrow_bufs, send_sems, recv_sems):
    rows = out_ref.shape[1]
    cols = out_ref.shape[2]
    margin = (canvas_ref.shape[2] - cols) // 2
    me_r, me_c, n_r, n_c = mesh_place()
    src_rows = {-1: slice(0, margin), 0: slice(margin, margin + rows), 1: slice(margin + rows, 2 * margin + rows)}
    src_cols = {-1: slice(0, margin), 0: slice(margin, margin + cols), 1: slice(margin + cols, 2 * margin + cols)}
    dst_cols = {-1: slice(cols - margin, cols), 0: slice(0, cols), 1: slice(0, margin)}
    neighbour_barrier(me_r, me_c, n_r, n_c)
    copies = []
    wide_index = 0
    narrow_index = 0
    for index, (dr, dc) in enumerate(NEIGHBOURS):
        if dc == 0:
            buffer = wide_bufs.at[wide_index]
            wide_index += 1
        else:
            buffer = narrow_bufs.at[narrow_index]
            narrow_index += 1
        copy = pltpu.make_async_remote_copy(
            src_ref=canvas_ref.at[:, src_rows[dr], src_cols[dc]],
            dst_ref=buffer,
            send_sem=send_sems.at[index],
            recv_sem=recv_sems.at[index],
            device_id=(me_r + dr, me_c + dc),
            device_id_type=pl.DeviceIdType.MESH,
        )
        copies.append((copy, buffer))

        @pl.when(exists(me_r + dr, me_c + dc, n_r, n_c))
        def _():
            copy.start()

    out_ref[...] = canvas_ref[:, margin : margin + rows, margin : margin + cols]
    for index, (dr, dc) in enumerate(NEIGHBOURS):
        copy, buffer = copies[index]

        @pl.when(exists(me_r + dr, me_c + dc, n_r, n_c))
        def _():
            copy.wait_send()

        @pl.when(exists(me_r - dr, me_c - dc, n_r, n_c))
        def _():
            copy.wait_recv()
            out_ref[:, :, dst_cols[dc]] += buffer[...]


def exchange_halo(current, margin):
    depth, rows, cols = current.shape
    return pl.pallas_call(
        halo_kernel,
        out_shape=jax.ShapeDtypeStruct((depth, rows + 2 * margin, cols + 2 * margin), jnp.float32),
        in_specs=[VMEM_SPEC],
        out_specs=VMEM_SPEC,
        scratch_shapes=[pltpu.SemaphoreType.DMA((8,)), pltpu.SemaphoreType.DMA((8,))],
        compiler_params=pltpu.CompilerParams(
            vmem_limit_bytes=60 * 1024 * 1024, has_side_effects=True, collective_id=0
        ),
    )(current)


def exchange_fold(canvas, margin):
    depth, ext_rows, ext_cols = canvas.shape
    rows = ext_rows - 2 * margin
    cols = ext_cols - 2 * margin
    return pl.pallas_call(
        fold_kernel,
        out_shape=jax.ShapeDtypeStruct((depth, rows, cols), jnp.float32),
        in_specs=[VMEM_SPEC],
        out_specs=VMEM_SPEC,
        scratch_shapes=[
            pltpu.VMEM((2, depth, margin, cols), jnp.float32),
            pltpu.VMEM((6, depth, margin, margin), jnp.float32),
            pltpu.SemaphoreType.DMA((8,)),
            pltpu.SemaphoreType.DMA((8,)),
        ],
        compiler_params=pltpu.CompilerParams(
            vmem_limit_bytes=60 * 1024 * 1024, has_side_effects=True, collective_id=depth
        ),
    )(canvas)


def on_device(object_field, probe_field, amplitudes, centres, counts):
    size_probe = probe_field.shape[1]
    margin = size_probe // 2
    block_rows = object_field.shape[1]
    block_cols = object_field.shape[2]
    tables = dft_tables(size_probe)
    spots = centres[0, 0]
    own_amps = amplitudes[0, 0]
    sx_size = lax.axis_size("sx")
    sx_index = lax.axis_index("sx")
    column_counts = counts[:, 0]
    sx_positions = jnp.arange(sx_size, dtype=jnp.int32)
    own_count = jnp.sum(jnp.where(sx_positions == sx_index, column_counts, 0))
    ext_shape = (block_rows + size_probe, block_cols + size_probe)

    current = object_field
    for sweep_index in range(ITERS):
        extended = exchange_halo(current, margin)
        channels = 3 if sweep_index == 0 else 2
        canvas = gradient_canvas(
            channels, ext_shape, spots, own_count, extended, probe_field, own_amps, tables
        )
        folded = exchange_fold(canvas, margin)
        if sweep_index == 0:
            illumination = folded[2]
        current = current - folded[0:2] / (illumination + DAMPING)
    return current


def solution(mesh):
    return jax.shard_map(
        on_device,
        mesh=mesh,
        in_specs=(
            P(None, "sx", "sy"),
            P(),
            P("sx", "sy", None, None, None),
            P("sx", "sy", None, None),
            P(None, "sy"),
        ),
        out_specs=P(None, "sx", "sy"),
        check_vma=False,
    )
```

```python
import math

import jax
import jax.numpy as jnp
from jax import lax
from jax.sharding import PartitionSpec as P
from jax.experimental import pallas as pl
from jax.experimental.pallas import tpu as pltpu

ITERS = 2


SMOOTH = 1.0
DAMPING = 1.0


def with_halo(cells, sides, width):
    for axis, dim in sides:
        count = lax.axis_size(axis)
        ends = count - 1
        head = lax.slice_in_dim(cells, 0, width, axis=dim)
        tail = lax.slice_in_dim(cells, cells.shape[dim] - width, cells.shape[dim], axis=dim)
        cells = jnp.concatenate(
            [
                lax.ppermute(tail, axis, [(i, (i + 1) % count) for i in range(ends)]),
                cells,
                lax.ppermute(head, axis, [((i + 1) % count, i) for i in range(ends)]),
            ],
            axis=dim,
        )
    return cells


def dft_tables(length):
    index_values = jnp.arange(length, dtype=jnp.int32)
    product_mod = index_values[:, None] * index_values[None, :] % length
    angles = product_mod.astype(jnp.float32) * (2.0 * math.pi / length)
    scaling = 1.0 / math.sqrt(length)
    return (jnp.cos(angles) * scaling, -jnp.sin(angles) * scaling)


def matmul_exact(left_side, right_side):
    return jnp.dot(left_side, right_side, precision=lax.Precision.HIGHEST)


def complex_left(table_real, table_imag, field_real, field_imag):
    out_real = matmul_exact(table_real, field_real) - matmul_exact(table_imag, field_imag)
    out_imag = matmul_exact(table_real, field_imag) + matmul_exact(table_imag, field_real)
    return (out_real, out_imag)


def complex_right(field_real, field_imag, table_real, table_imag):
    out_real = matmul_exact(field_real, table_real) - matmul_exact(field_imag, table_imag)
    out_imag = matmul_exact(field_real, table_imag) + matmul_exact(field_imag, table_real)
    return (out_real, out_imag)


def position_gradient(object_patch, probe_field, amplitude, table_real, table_imag):
    probe_real = probe_field[0]
    probe_imag = probe_field[1]
    exit_real = probe_real * object_patch[0] - probe_imag * object_patch[1]
    exit_imag = probe_real * object_patch[1] + probe_imag * object_patch[0]
    half_real, half_imag = complex_left(table_real, table_imag, exit_real, exit_imag)
    far_real, far_imag = complex_right(half_real, half_imag, table_real, table_imag)
    factor = 1.0 - amplitude / jnp.sqrt(far_real * far_real + far_imag * far_imag + SMOOTH)
    miss_real = far_real * factor
    miss_imag = far_imag * factor
    back_real, back_imag = complex_left(table_real, -table_imag, miss_real, miss_imag)
    near_real, near_imag = complex_right(back_real, back_imag, table_real, -table_imag)
    return jnp.stack(
        [
            probe_real * near_real + probe_imag * near_imag,
            probe_real * near_imag - probe_imag * near_real,
        ]
    )


def add_patch(canvas, patch_values, corner_row, corner_col):
    zero_index = jnp.zeros((), jnp.int32)
    starts = (zero_index, corner_row, corner_col)
    present = lax.dynamic_slice(canvas, starts, patch_values.shape)
    return lax.dynamic_update_slice(canvas, present + patch_values, starts)


def fold_rows(extended, margin, length):
    middle_part = extended[:, 2 * margin : 2 * margin + length]
    upper_rim = extended[:, :margin]
    lower_rim = extended[:, extended.shape[1] - margin :]
    middle_part = middle_part.at[:, :margin].add(upper_rim)
    return middle_part.at[:, length - margin :].add(lower_rim)


def fold_cols(extended, margin, length):
    middle_part = extended[:, :, 2 * margin : 2 * margin + length]
    left_rim = extended[:, :, :margin]
    right_rim = extended[:, :, extended.shape[2] - margin :]
    middle_part = middle_part.at[:, :, :margin].add(left_rim)
    return middle_part.at[:, :, length - margin :].add(right_rim)


def settle(stacked, margin, block_rows, block_cols):
    full_ext = with_halo(stacked, (("sx", 1), ("sy", 2)), margin)
    return fold_cols(fold_rows(full_ext, margin, block_rows), margin, block_cols)


def local_pass(canvas, extended, spots, own_amps, probe_field, table_real, table_imag, upper_bound):
    size_probe = probe_field.shape[1]

    def local_step(slot_index, canvas_state):
        row_start = spots[slot_index, 0]
        col_start = spots[slot_index, 1]
        zero_index = jnp.zeros((), jnp.int32)
        object_patch = lax.dynamic_slice(
            extended, (zero_index, row_start, col_start), (2, size_probe, size_probe)
        )
        update = position_gradient(
            object_patch, probe_field, own_amps[slot_index], table_real, table_imag
        )
        return add_patch(canvas_state, update, row_start, col_start)

    return lax.fori_loop(0, upper_bound, local_step, canvas)


def dot_exact(left_side, right_side):
    return jnp.dot(
        left_side, right_side, precision=lax.Precision.HIGHEST, preferred_element_type=jnp.float32
    )


def window_tools(size, row, col):
    lanes = 128
    sublanes = 8
    wide = size + lanes
    tall = size + sublanes
    row_base = pl.multiple_of((row // sublanes) * sublanes, sublanes)
    col_base = pl.multiple_of((col // lanes) * lanes, lanes)
    row_shift = row % sublanes
    col_shift = col % lanes
    rows = pl.ds(row_base, tall)
    cols = pl.ds(col_base, wide)

    def take(ref, channel):
        block = ref[channel, rows, cols]
        block = pltpu.roll(block, (tall - row_shift) % tall, 0)
        return pltpu.roll(block, (wide - col_shift) % wide, 1)[:size, :size]

    def put(ref, channel, values):
        block = jnp.concatenate([values, jnp.zeros((size, lanes), jnp.float32)], axis=1)
        block = jnp.concatenate([block, jnp.zeros((sublanes, wide), jnp.float32)], axis=0)
        block = pltpu.roll(pltpu.roll(block, col_shift, 1), row_shift, 0)
        ref[channel, rows, cols] += block

    return take, put


def split_bf16(values):
    scaled = values * 65537.0
    high = scaled - (scaled - values)
    return high.astype(jnp.bfloat16), (values - high).astype(jnp.bfloat16)


def dot_split(left_parts, right_parts):
    left_high, left_low = left_parts
    right_high, right_low = right_parts
    total = jnp.dot(left_high, right_high, preferred_element_type=jnp.float32)
    total += jnp.dot(left_high, right_low, preferred_element_type=jnp.float32)
    return total + jnp.dot(left_low, right_high, preferred_element_type=jnp.float32)


def gradient_kernel(spots_ref, count_ref, ext_ref, probe_ref, amps_ref, tables_ref, out_ref):
    size = probe_ref.shape[1]
    out_ref[...] = jnp.zeros(out_ref.shape, jnp.float32)
    with_power = out_ref.shape[0] > 2
    for slot in range(amps_ref.shape[0]):

        @pl.when(slot < count_ref[0])
        def _():
            take, put = window_tools(size, spots_ref[slot, 0], spots_ref[slot, 1])
            probe_real = probe_ref[0]
            probe_imag = probe_ref[1]
            real_parts = (tables_ref[0], tables_ref[1])
            imag_parts = (tables_ref[2], tables_ref[3])

            def left(field_real, field_imag, sign):
                both = split_bf16(jnp.concatenate([field_real, field_imag], axis=1))
                by_real = dot_split(real_parts, both)
                by_imag = dot_split(imag_parts, both)
                out_real = by_real[:, :size] - sign * by_imag[:, size:]
                out_imag = by_real[:, size:] + sign * by_imag[:, :size]
                return out_real, out_imag

            def right(field_real, field_imag, sign):
                both = split_bf16(jnp.concatenate([field_real, field_imag], axis=0))
                by_real = dot_split(both, real_parts)
                by_imag = dot_split(both, imag_parts)
                out_real = by_real[:size] - sign * by_imag[size:]
                out_imag = by_imag[:size] * sign + by_real[size:]
                return out_real, out_imag

            obj_real = take(ext_ref, 0)
            obj_imag = take(ext_ref, 1)
            exit_real = probe_real * obj_real - probe_imag * obj_imag
            exit_imag = probe_real * obj_imag + probe_imag * obj_real
            half_real, half_imag = left(exit_real, exit_imag, 1.0)
            far_real, far_imag = right(half_real, half_imag, 1.0)
            factor = 1.0 - amps_ref[slot] / jnp.sqrt(far_real * far_real + far_imag * far_imag + SMOOTH)
            miss_real = far_real * factor
            miss_imag = far_imag * factor
            back_real, back_imag = left(miss_real, miss_imag, -1.0)
            near_real, near_imag = right(back_real, back_imag, -1.0)
            put(out_ref, 0, probe_real * near_real + probe_imag * near_imag)
            put(out_ref, 1, probe_real * near_imag - probe_imag * near_real)
            if with_power:
                put(out_ref, 2, probe_real * probe_real + probe_imag * probe_imag)


def power_kernel(spots_ref, count_ref, probe_ref, out_ref):
    size = probe_ref.shape[1]
    out_ref[...] = jnp.zeros(out_ref.shape, jnp.float32)
    power = probe_ref[0] * probe_ref[0] + probe_ref[1] * probe_ref[1]
    for slot in range(spots_ref.shape[0]):

        @pl.when(slot < count_ref[0])
        def _():
            _, put = window_tools(size, spots_ref[slot, 0], spots_ref[slot, 1])
            put(out_ref, 0, power)


def illumination_kernel(corners_ref, live_ref, probe_ref, out_ref, canvas_ref):
    size = probe_ref.shape[1]
    rows, cols = out_ref.shape
    top = 2 * (size // 2)
    left = cols + size // 2
    canvas_ref[...] = jnp.zeros(canvas_ref.shape, jnp.float32)
    power = probe_ref[0] * probe_ref[0] + probe_ref[1] * probe_ref[1]
    for window in range(live_ref.shape[0]):

        @pl.when(live_ref[window] > 0)
        def _():
            _, put = window_tools(size, corners_ref[window, 0], corners_ref[window, 1])
            put(canvas_ref, 0, power)

    out_ref[...] = canvas_ref[0, top : top + rows, left : left + cols]


VMEM_SPEC = pl.BlockSpec(memory_space=pltpu.VMEM)
SMEM_SPEC = pl.BlockSpec(memory_space=pltpu.SMEM)
KERNEL_PARAMS = pltpu.CompilerParams(vmem_limit_bytes=60 * 1024 * 1024)


def gradient_canvas(channels, ext_shape, spots, count, extended, probe_field, own_amps, tables):
    parts = jnp.stack(split_bf16(tables[0]) + split_bf16(tables[1]))
    return pl.pallas_call(
        gradient_kernel,
        out_shape=jax.ShapeDtypeStruct((channels,) + ext_shape, jnp.float32),
        in_specs=[SMEM_SPEC, SMEM_SPEC] + [VMEM_SPEC] * 4,
        out_specs=VMEM_SPEC,
        compiler_params=KERNEL_PARAMS,
    )(spots, count.reshape(1), extended, probe_field, own_amps, parts)


def illumination_block(block_shape, centres, counts, probe_field):
    rows, cols = block_shape
    size = probe_field.shape[1]
    margin = size // 2
    me_r, me_c, n_r, n_c = mesh_place()
    corners = []
    live = []
    for dr in (-1, 0, 1):
        for dc in (-1, 0, 1):
            row_dev = me_r + dr
            col_dev = me_c + dc
            present = exists(row_dev, col_dev, n_r, n_c)
            safe_r = jnp.clip(row_dev, 0, n_r - 1)
            safe_c = jnp.clip(col_dev, 0, n_c - 1)
            spots = centres[safe_r, safe_c]
            count = jnp.where(present, counts[safe_r, safe_c], 0)
            for slot in range(spots.shape[0]):
                corners.append(
                    jnp.stack(
                        [
                            dr * rows + spots[slot, 0] - margin + 2 * margin,
                            dc * cols + spots[slot, 1] - margin + cols + margin,
                        ]
                    )
                )
                live.append((slot < count).astype(jnp.int32))
    canvas_rows = 2 * rows + margin + size + 8
    canvas_cols = 3 * cols + size
    return pl.pallas_call(
        illumination_kernel,
        out_shape=jax.ShapeDtypeStruct((rows, cols), jnp.float32),
        in_specs=[SMEM_SPEC, SMEM_SPEC, VMEM_SPEC],
        out_specs=VMEM_SPEC,
        scratch_shapes=[pltpu.VMEM((1, canvas_rows, canvas_cols), jnp.float32)],
        compiler_params=KERNEL_PARAMS,
    )(jnp.stack(corners).astype(jnp.int32), jnp.stack(live), probe_field)


def power_canvas(ext_shape, spots, count, probe_field):
    return pl.pallas_call(
        power_kernel,
        out_shape=jax.ShapeDtypeStruct((1,) + ext_shape, jnp.float32),
        in_specs=[SMEM_SPEC, SMEM_SPEC, VMEM_SPEC],
        out_specs=VMEM_SPEC,
        compiler_params=KERNEL_PARAMS,
    )(spots, count.reshape(1), probe_field)


NEIGHBOURS = [(-1, -1), (-1, 0), (-1, 1), (0, -1), (0, 1), (1, -1), (1, 0), (1, 1)]


def mesh_place():
    return (
        lax.axis_index("sx"),
        lax.axis_index("sy"),
        lax.axis_size("sx"),
        lax.axis_size("sy"),
    )


def exists(row_dev, col_dev, row_count, col_count):
    return (row_dev >= 0) & (row_dev < row_count) & (col_dev >= 0) & (col_dev < col_count)


def neighbour_barrier(me_r, me_c, n_r, n_c):
    barrier = pltpu.get_barrier_semaphore()
    greeted = jnp.int32(0)
    for dr, dc in NEIGHBOURS:
        present = exists(me_r + dr, me_c + dc, n_r, n_c)

        @pl.when(present)
        def _():
            pl.semaphore_signal(
                barrier, inc=1, device_id=(me_r + dr, me_c + dc), device_id_type=pl.DeviceIdType.MESH
            )

        greeted = greeted + present.astype(jnp.int32)
    pl.semaphore_wait(barrier, greeted)


def halo_kernel(cur_ref, ext_ref, send_sems, recv_sems):
    rows = cur_ref.shape[1]
    cols = cur_ref.shape[2]
    margin = (ext_ref.shape[2] - cols) // 2
    me_r, me_c, n_r, n_c = mesh_place()
    ext_ref[:, margin : margin + rows, margin : margin + cols] = cur_ref[...]
    neighbour_barrier(me_r, me_c, n_r, n_c)
    src_cols = {-1: slice(0, margin), 0: slice(0, cols), 1: slice(cols - margin, cols)}
    dst_rows = {-1: slice(margin + rows, 2 * margin + rows), 0: slice(margin, margin + rows), 1: slice(0, margin)}
    dst_cols = {-1: slice(margin + cols, 2 * margin + cols), 0: slice(margin, margin + cols), 1: slice(0, margin)}
    copies = []
    for index, (dr, dc) in enumerate(NEIGHBOURS):
        copy = pltpu.make_async_remote_copy(
            src_ref=cur_ref.at[:, :, src_cols[dc]],
            dst_ref=ext_ref.at[:, dst_rows[dr], dst_cols[dc]],
            send_sem=send_sems.at[index],
            recv_sem=recv_sems.at[index],
            device_id=(me_r + dr, me_c + dc),
            device_id_type=pl.DeviceIdType.MESH,
        )
        copies.append(copy)

        @pl.when(exists(me_r + dr, me_c + dc, n_r, n_c))
        def _():
            copy.start()

        @pl.when(jnp.logical_not(exists(me_r - dr, me_c - dc, n_r, n_c)))
        def _():
            region = (slice(None), dst_rows[dr], dst_cols[dc])
            ext_ref[region] = jnp.zeros(ext_ref[region].shape, jnp.float32)

    for index, (dr, dc) in enumerate(NEIGHBOURS):
        copy = copies[index]

        @pl.when(exists(me_r + dr, me_c + dc, n_r, n_c))
        def _():
            copy.wait_send()

        @pl.when(exists(me_r - dr, me_c - dc, n_r, n_c))
        def _():
            copy.wait_recv()


def fold_kernel(canvas_ref, out_ref, wide_bufs, narrow_bufs, send_sems, recv_sems):
    rows = out_ref.shape[1]
    cols = out_ref.shape[2]
    margin = (canvas_ref.shape[2] - cols) // 2
    me_r, me_c, n_r, n_c = mesh_place()
    src_rows = {-1: slice(0, margin), 0: slice(margin, margin + rows), 1: slice(margin + rows, 2 * margin + rows)}
    src_cols = {-1: slice(0, margin), 0: slice(margin, margin + cols), 1: slice(margin + cols, 2 * margin + cols)}
    dst_cols = {-1: slice(cols - margin, cols), 0: slice(0, cols), 1: slice(0, margin)}
    neighbour_barrier(me_r, me_c, n_r, n_c)
    copies = []
    wide_index = 0
    narrow_index = 0
    for index, (dr, dc) in enumerate(NEIGHBOURS):
        if dc == 0:
            buffer = wide_bufs.at[wide_index]
            wide_index += 1
        else:
            buffer = narrow_bufs.at[narrow_index]
            narrow_index += 1
        copy = pltpu.make_async_remote_copy(
            src_ref=canvas_ref.at[:, src_rows[dr], src_cols[dc]],
            dst_ref=buffer,
            send_sem=send_sems.at[index],
            recv_sem=recv_sems.at[index],
            device_id=(me_r + dr, me_c + dc),
            device_id_type=pl.DeviceIdType.MESH,
        )
        copies.append((copy, buffer))

        @pl.when(exists(me_r + dr, me_c + dc, n_r, n_c))
        def _():
            copy.start()

    out_ref[...] = canvas_ref[:, margin : margin + rows, margin : margin + cols]
    for index, (dr, dc) in enumerate(NEIGHBOURS):
        copy, buffer = copies[index]

        @pl.when(exists(me_r + dr, me_c + dc, n_r, n_c))
        def _():
            copy.wait_send()

        @pl.when(exists(me_r - dr, me_c - dc, n_r, n_c))
        def _():
            copy.wait_recv()
            out_ref[:, :, dst_cols[dc]] += buffer[...]


def exchange_halo(current, margin):
    depth, rows, cols = current.shape
    return pl.pallas_call(
        halo_kernel,
        out_shape=jax.ShapeDtypeStruct((depth, rows + 2 * margin, cols + 2 * margin), jnp.float32),
        in_specs=[VMEM_SPEC],
        out_specs=VMEM_SPEC,
        scratch_shapes=[pltpu.SemaphoreType.DMA((8,)), pltpu.SemaphoreType.DMA((8,))],
        compiler_params=pltpu.CompilerParams(
            vmem_limit_bytes=60 * 1024 * 1024, has_side_effects=True, collective_id=0
        ),
    )(current)


def exchange_fold(canvas, margin):
    depth, ext_rows, ext_cols = canvas.shape
    rows = ext_rows - 2 * margin
    cols = ext_cols - 2 * margin
    return pl.pallas_call(
        fold_kernel,
        out_shape=jax.ShapeDtypeStruct((depth, rows, cols), jnp.float32),
        in_specs=[VMEM_SPEC],
        out_specs=VMEM_SPEC,
        scratch_shapes=[
            pltpu.VMEM((2, depth, margin, cols), jnp.float32),
            pltpu.VMEM((6, depth, margin, margin), jnp.float32),
            pltpu.SemaphoreType.DMA((8,)),
            pltpu.SemaphoreType.DMA((8,)),
        ],
        compiler_params=pltpu.CompilerParams(
            vmem_limit_bytes=60 * 1024 * 1024, has_side_effects=True, collective_id=depth
        ),
    )(canvas)


def on_device(object_field, probe_field, amplitudes, centres, counts):
    size_probe = probe_field.shape[1]
    margin = size_probe // 2
    block_rows = object_field.shape[1]
    block_cols = object_field.shape[2]
    tables = dft_tables(size_probe)
    me_r, me_c, _, _ = mesh_place()
    spots = centres[me_r, me_c]
    own_amps = amplitudes[0, 0]
    own_count = counts[me_r, me_c]
    ext_shape = (block_rows + size_probe, block_cols + size_probe)

    illumination = illumination_block((block_rows, block_cols), centres, counts, probe_field)
    current = object_field
    for sweep_index in range(ITERS):
        extended = exchange_halo(current, margin)
        canvas = gradient_canvas(2, ext_shape, spots, own_count, extended, probe_field, own_amps, tables)
        gradient = exchange_fold(canvas, margin)
        current = current - gradient / (illumination + DAMPING)
    return current


def solution(mesh):
    return jax.shard_map(
        on_device,
        mesh=mesh,
        in_specs=(
            P(None, "sx", "sy"),
            P(),
            P("sx", "sy", None, None, None),
            P(),
            P(),
        ),
        out_specs=P(None, "sx", "sy"),
        check_vma=False,
    )
```

```python
import math

import jax
import jax.numpy as jnp
from jax import lax
from jax.sharding import PartitionSpec as P
from jax.experimental import pallas as pl
from jax.experimental.pallas import tpu as pltpu

ITERS = 2


SMOOTH = 1.0
DAMPING = 1.0


def with_halo(cells, sides, width):
    for axis, dim in sides:
        count = lax.axis_size(axis)
        ends = count - 1
        head = lax.slice_in_dim(cells, 0, width, axis=dim)
        tail = lax.slice_in_dim(cells, cells.shape[dim] - width, cells.shape[dim], axis=dim)
        cells = jnp.concatenate(
            [
                lax.ppermute(tail, axis, [(i, (i + 1) % count) for i in range(ends)]),
                cells,
                lax.ppermute(head, axis, [((i + 1) % count, i) for i in range(ends)]),
            ],
            axis=dim,
        )
    return cells


def dft_tables(length):
    index_values = jnp.arange(length, dtype=jnp.int32)
    product_mod = index_values[:, None] * index_values[None, :] % length
    angles = product_mod.astype(jnp.float32) * (2.0 * math.pi / length)
    scaling = 1.0 / math.sqrt(length)
    return (jnp.cos(angles) * scaling, -jnp.sin(angles) * scaling)


def matmul_exact(left_side, right_side):
    return jnp.dot(left_side, right_side, precision=lax.Precision.HIGHEST)


def complex_left(table_real, table_imag, field_real, field_imag):
    out_real = matmul_exact(table_real, field_real) - matmul_exact(table_imag, field_imag)
    out_imag = matmul_exact(table_real, field_imag) + matmul_exact(table_imag, field_real)
    return (out_real, out_imag)


def complex_right(field_real, field_imag, table_real, table_imag):
    out_real = matmul_exact(field_real, table_real) - matmul_exact(field_imag, table_imag)
    out_imag = matmul_exact(field_real, table_imag) + matmul_exact(field_imag, table_real)
    return (out_real, out_imag)


def position_gradient(object_patch, probe_field, amplitude, table_real, table_imag):
    probe_real = probe_field[0]
    probe_imag = probe_field[1]
    exit_real = probe_real * object_patch[0] - probe_imag * object_patch[1]
    exit_imag = probe_real * object_patch[1] + probe_imag * object_patch[0]
    half_real, half_imag = complex_left(table_real, table_imag, exit_real, exit_imag)
    far_real, far_imag = complex_right(half_real, half_imag, table_real, table_imag)
    factor = 1.0 - amplitude / jnp.sqrt(far_real * far_real + far_imag * far_imag + SMOOTH)
    miss_real = far_real * factor
    miss_imag = far_imag * factor
    back_real, back_imag = complex_left(table_real, -table_imag, miss_real, miss_imag)
    near_real, near_imag = complex_right(back_real, back_imag, table_real, -table_imag)
    return jnp.stack(
        [
            probe_real * near_real + probe_imag * near_imag,
            probe_real * near_imag - probe_imag * near_real,
        ]
    )


def add_patch(canvas, patch_values, corner_row, corner_col):
    zero_index = jnp.zeros((), jnp.int32)
    starts = (zero_index, corner_row, corner_col)
    present = lax.dynamic_slice(canvas, starts, patch_values.shape)
    return lax.dynamic_update_slice(canvas, present + patch_values, starts)


def fold_rows(extended, margin, length):
    middle_part = extended[:, 2 * margin : 2 * margin + length]
    upper_rim = extended[:, :margin]
    lower_rim = extended[:, extended.shape[1] - margin :]
    middle_part = middle_part.at[:, :margin].add(upper_rim)
    return middle_part.at[:, length - margin :].add(lower_rim)


def fold_cols(extended, margin, length):
    middle_part = extended[:, :, 2 * margin : 2 * margin + length]
    left_rim = extended[:, :, :margin]
    right_rim = extended[:, :, extended.shape[2] - margin :]
    middle_part = middle_part.at[:, :, :margin].add(left_rim)
    return middle_part.at[:, :, length - margin :].add(right_rim)


def settle(stacked, margin, block_rows, block_cols):
    full_ext = with_halo(stacked, (("sx", 1), ("sy", 2)), margin)
    return fold_cols(fold_rows(full_ext, margin, block_rows), margin, block_cols)


def local_pass(canvas, extended, spots, own_amps, probe_field, table_real, table_imag, upper_bound):
    size_probe = probe_field.shape[1]

    def local_step(slot_index, canvas_state):
        row_start = spots[slot_index, 0]
        col_start = spots[slot_index, 1]
        zero_index = jnp.zeros((), jnp.int32)
        object_patch = lax.dynamic_slice(
            extended, (zero_index, row_start, col_start), (2, size_probe, size_probe)
        )
        update = position_gradient(
            object_patch, probe_field, own_amps[slot_index], table_real, table_imag
        )
        return add_patch(canvas_state, update, row_start, col_start)

    return lax.fori_loop(0, upper_bound, local_step, canvas)


def dot_exact(left_side, right_side):
    return jnp.dot(
        left_side, right_side, precision=lax.Precision.HIGHEST, preferred_element_type=jnp.float32
    )


def window_tools(size, row, col):
    lanes = 128
    sublanes = 8
    wide = size + lanes
    tall = size + sublanes
    row_base = pl.multiple_of((row // sublanes) * sublanes, sublanes)
    col_base = pl.multiple_of((col // lanes) * lanes, lanes)
    row_shift = row % sublanes
    col_shift = col % lanes
    rows = pl.ds(row_base, tall)
    cols = pl.ds(col_base, wide)

    def take(ref, channel):
        block = ref[channel, rows, cols]
        block = pltpu.roll(block, (tall - row_shift) % tall, 0)
        return pltpu.roll(block, (wide - col_shift) % wide, 1)[:size, :size]

    def put(ref, channel, values):
        block = jnp.concatenate([values, jnp.zeros((size, lanes), jnp.float32)], axis=1)
        block = jnp.concatenate([block, jnp.zeros((sublanes, wide), jnp.float32)], axis=0)
        block = pltpu.roll(pltpu.roll(block, col_shift, 1), row_shift, 0)
        ref[channel, rows, cols] += block

    return take, put


def split_bf16(values):
    scaled = values * 65537.0
    high = scaled - (scaled - values)
    return high.astype(jnp.bfloat16), (values - high).astype(jnp.bfloat16)


def dot_split(left_parts, right_parts):
    left_high, left_low = left_parts
    right_high, right_low = right_parts
    total = jnp.dot(left_high, right_high, preferred_element_type=jnp.float32)
    total += jnp.dot(left_high, right_low, preferred_element_type=jnp.float32)
    return total + jnp.dot(left_low, right_high, preferred_element_type=jnp.float32)


def gradient_kernel(spots_ref, count_ref, ext_ref, probe_ref, amps_ref, tables_ref, out_ref):
    size = probe_ref.shape[1]
    out_ref[...] = jnp.zeros(out_ref.shape, jnp.float32)
    with_power = out_ref.shape[0] > 2
    for slot in range(amps_ref.shape[0]):

        @pl.when(slot < count_ref[0])
        def _():
            take, put = window_tools(size, spots_ref[slot, 0], spots_ref[slot, 1])
            probe_real = probe_ref[0]
            probe_imag = probe_ref[1]
            real_parts = (tables_ref[0], tables_ref[1])
            imag_parts = (tables_ref[2], tables_ref[3])

            def left(field_real, field_imag, sign):
                both = split_bf16(jnp.concatenate([field_real, field_imag], axis=1))
                by_real = dot_split(real_parts, both)
                by_imag = dot_split(imag_parts, both)
                out_real = by_real[:, :size] - sign * by_imag[:, size:]
                out_imag = by_real[:, size:] + sign * by_imag[:, :size]
                return out_real, out_imag

            def right(field_real, field_imag, sign):
                both = split_bf16(jnp.concatenate([field_real, field_imag], axis=0))
                by_real = dot_split(both, real_parts)
                by_imag = dot_split(both, imag_parts)
                out_real = by_real[:size] - sign * by_imag[size:]
                out_imag = by_imag[:size] * sign + by_real[size:]
                return out_real, out_imag

            obj_real = take(ext_ref, 0)
            obj_imag = take(ext_ref, 1)
            exit_real = probe_real * obj_real - probe_imag * obj_imag
            exit_imag = probe_real * obj_imag + probe_imag * obj_real
            half_real, half_imag = left(exit_real, exit_imag, 1.0)
            far_real, far_imag = right(half_real, half_imag, 1.0)
            factor = 1.0 - amps_ref[slot] / jnp.sqrt(far_real * far_real + far_imag * far_imag + SMOOTH)
            miss_real = far_real * factor
            miss_imag = far_imag * factor
            back_real, back_imag = left(miss_real, miss_imag, -1.0)
            near_real, near_imag = right(back_real, back_imag, -1.0)
            put(out_ref, 0, probe_real * near_real + probe_imag * near_imag)
            put(out_ref, 1, probe_real * near_imag - probe_imag * near_real)
            if with_power:
                put(out_ref, 2, probe_real * probe_real + probe_imag * probe_imag)


def power_kernel(spots_ref, count_ref, probe_ref, out_ref):
    size = probe_ref.shape[1]
    out_ref[...] = jnp.zeros(out_ref.shape, jnp.float32)
    power = probe_ref[0] * probe_ref[0] + probe_ref[1] * probe_ref[1]
    for slot in range(spots_ref.shape[0]):

        @pl.when(slot < count_ref[0])
        def _():
            _, put = window_tools(size, spots_ref[slot, 0], spots_ref[slot, 1])
            put(out_ref, 0, power)


VMEM_SPEC = pl.BlockSpec(memory_space=pltpu.VMEM)
SMEM_SPEC = pl.BlockSpec(memory_space=pltpu.SMEM)
KERNEL_PARAMS = pltpu.CompilerParams(vmem_limit_bytes=60 * 1024 * 1024)


def gradient_canvas(channels, ext_shape, spots, count, extended, probe_field, own_amps, tables):
    parts = jnp.stack(split_bf16(tables[0]) + split_bf16(tables[1]))
    return pl.pallas_call(
        gradient_kernel,
        out_shape=jax.ShapeDtypeStruct((channels,) + ext_shape, jnp.float32),
        in_specs=[SMEM_SPEC, SMEM_SPEC] + [VMEM_SPEC] * 4,
        out_specs=VMEM_SPEC,
        compiler_params=KERNEL_PARAMS,
    )(spots, count.reshape(1), extended, probe_field, own_amps, parts)


def power_canvas(ext_shape, spots, count, probe_field):
    return pl.pallas_call(
        power_kernel,
        out_shape=jax.ShapeDtypeStruct((1,) + ext_shape, jnp.float32),
        in_specs=[SMEM_SPEC, SMEM_SPEC, VMEM_SPEC],
        out_specs=VMEM_SPEC,
        compiler_params=KERNEL_PARAMS,
    )(spots, count.reshape(1), probe_field)


def mesh_place():
    return (
        lax.axis_index("sx"),
        lax.axis_index("sy"),
        lax.axis_size("sx"),
        lax.axis_size("sy"),
    )


def exists(row_dev, col_dev, row_count, col_count):
    return (row_dev >= 0) & (row_dev < row_count) & (col_dev >= 0) & (col_dev < col_count)


ROW_NEIGHBOURS = [(-1, 0), (1, 0)]
COL_NEIGHBOURS = [(0, -1), (0, 1)]


def neighbour_barrier(me_r, me_c, n_r, n_c):
    barrier = pltpu.get_barrier_semaphore()
    greeted = jnp.int32(0)
    for dr, dc in ROW_NEIGHBOURS + COL_NEIGHBOURS:
        present = exists(me_r + dr, me_c + dc, n_r, n_c)

        @pl.when(present)
        def _():
            pl.semaphore_signal(
                barrier, inc=1, device_id=(me_r + dr, me_c + dc), device_id_type=pl.DeviceIdType.MESH
            )

        greeted = greeted + present.astype(jnp.int32)
    pl.semaphore_wait(barrier, greeted)


def swap(place, pieces, send_sems, recv_sems):
    me_r, me_c, n_r, n_c = place
    copies = []
    for index, ((dr, dc), source, target) in enumerate(pieces):
        copy = pltpu.make_async_remote_copy(
            src_ref=source,
            dst_ref=target,
            send_sem=send_sems.at[index],
            recv_sem=recv_sems.at[index],
            device_id=(me_r + dr, me_c + dc),
            device_id_type=pl.DeviceIdType.MESH,
        )
        copies.append(copy)

        @pl.when(exists(me_r + dr, me_c + dc, n_r, n_c))
        def _():
            copy.start()

    for index, ((dr, dc), _, _) in enumerate(pieces):
        copy = copies[index]

        @pl.when(exists(me_r + dr, me_c + dc, n_r, n_c))
        def _():
            copy.wait_send()

        @pl.when(exists(me_r - dr, me_c - dc, n_r, n_c))
        def _():
            copy.wait_recv()


def halo_kernel(cur_ref, ext_ref, send_sems, recv_sems):
    rows = cur_ref.shape[1]
    cols = cur_ref.shape[2]
    margin = (ext_ref.shape[2] - cols) // 2
    place = mesh_place()
    me_r, me_c, n_r, n_c = place
    middle = slice(margin, margin + rows)
    ext_ref[:, middle, margin : margin + cols] = cur_ref[...]
    unreached = [
        ((0, 1), (slice(None), middle, slice(0, margin))),
        ((0, -1), (slice(None), middle, slice(margin + cols, 2 * margin + cols))),
        ((1, 0), (slice(None), slice(0, margin), slice(None))),
        ((-1, 0), (slice(None), slice(margin + rows, 2 * margin + rows), slice(None))),
    ]
    for (dr, dc), region in unreached:

        @pl.when(jnp.logical_not(exists(me_r - dr, me_c - dc, n_r, n_c)))
        def _():
            ext_ref[region] = jnp.zeros(ext_ref[region].shape, jnp.float32)

    neighbour_barrier(me_r, me_c, n_r, n_c)
    swap(
        place,
        [
            ((0, -1), cur_ref.at[:, :, 0:margin], ext_ref.at[:, middle, margin + cols : 2 * margin + cols]),
            ((0, 1), cur_ref.at[:, :, cols - margin : cols], ext_ref.at[:, middle, 0:margin]),
        ],
        send_sems.at[0:2],
        recv_sems.at[0:2],
    )
    swap(
        place,
        [
            ((-1, 0), ext_ref.at[:, middle, :], ext_ref.at[:, margin + rows : 2 * margin + rows, :]),
            ((1, 0), ext_ref.at[:, middle, :], ext_ref.at[:, 0:margin, :]),
        ],
        send_sems.at[2:4],
        recv_sems.at[2:4],
    )


def fold_kernel(canvas_ref, out_ref, row_bufs, col_bufs, band_ref, send_sems, recv_sems):
    rows = out_ref.shape[1]
    cols = out_ref.shape[2]
    margin = (canvas_ref.shape[2] - cols) // 2
    place = mesh_place()
    me_r, me_c, n_r, n_c = place
    neighbour_barrier(me_r, me_c, n_r, n_c)
    swap(
        place,
        [
            ((-1, 0), canvas_ref.at[:, 0:margin, :], row_bufs.at[0]),
            ((1, 0), canvas_ref.at[:, margin + rows : 2 * margin + rows, :], row_bufs.at[1]),
        ],
        send_sems.at[0:2],
        recv_sems.at[0:2],
    )
    band_ref[...] = canvas_ref[:, margin : margin + rows, :]

    @pl.when(exists(me_r + 1, me_c, n_r, n_c))
    def _():
        band_ref[...] += row_bufs[0]

    @pl.when(exists(me_r - 1, me_c, n_r, n_c))
    def _():
        band_ref[...] += row_bufs[1]

    swap(
        place,
        [
            ((0, -1), band_ref.at[:, :, 0:margin], col_bufs.at[0]),
            ((0, 1), band_ref.at[:, :, margin + cols : 2 * margin + cols], col_bufs.at[1]),
        ],
        send_sems.at[2:4],
        recv_sems.at[2:4],
    )
    out_ref[...] = band_ref[:, :, margin : margin + cols]

    @pl.when(exists(me_r, me_c + 1, n_r, n_c))
    def _():
        out_ref[:, :, cols - margin : cols] += col_bufs[0]

    @pl.when(exists(me_r, me_c - 1, n_r, n_c))
    def _():
        out_ref[:, :, 0:margin] += col_bufs[1]


def exchange_halo(current, margin):
    depth, rows, cols = current.shape
    return pl.pallas_call(
        halo_kernel,
        out_shape=jax.ShapeDtypeStruct((depth, rows + 2 * margin, cols + 2 * margin), jnp.float32),
        in_specs=[VMEM_SPEC],
        out_specs=VMEM_SPEC,
        scratch_shapes=[pltpu.SemaphoreType.DMA((4,)), pltpu.SemaphoreType.DMA((4,))],
        compiler_params=pltpu.CompilerParams(
            vmem_limit_bytes=60 * 1024 * 1024, has_side_effects=True, collective_id=0
        ),
    )(current)


def exchange_fold(canvas, margin):
    depth, ext_rows, ext_cols = canvas.shape
    rows = ext_rows - 2 * margin
    cols = ext_cols - 2 * margin
    return pl.pallas_call(
        fold_kernel,
        out_shape=jax.ShapeDtypeStruct((depth, rows, cols), jnp.float32),
        in_specs=[VMEM_SPEC],
        out_specs=VMEM_SPEC,
        scratch_shapes=[
            pltpu.VMEM((2, depth, margin, ext_cols), jnp.float32),
            pltpu.VMEM((2, depth, rows, margin), jnp.float32),
            pltpu.VMEM((depth, rows, ext_cols), jnp.float32),
            pltpu.SemaphoreType.DMA((4,)),
            pltpu.SemaphoreType.DMA((4,)),
        ],
        compiler_params=pltpu.CompilerParams(
            vmem_limit_bytes=60 * 1024 * 1024, has_side_effects=True, collective_id=depth
        ),
    )(canvas)


def on_device(object_field, probe_field, amplitudes, centres, counts):
    size_probe = probe_field.shape[1]
    margin = size_probe // 2
    block_rows = object_field.shape[1]
    block_cols = object_field.shape[2]
    tables = dft_tables(size_probe)
    spots = centres[0, 0]
    own_amps = amplitudes[0, 0]
    sx_size = lax.axis_size("sx")
    sx_index = lax.axis_index("sx")
    column_counts = counts[:, 0]
    sx_positions = jnp.arange(sx_size, dtype=jnp.int32)
    own_count = jnp.sum(jnp.where(sx_positions == sx_index, column_counts, 0))
    ext_shape = (block_rows + size_probe, block_cols + size_probe)

    current = object_field
    for sweep_index in range(ITERS):
        extended = exchange_halo(current, margin)
        channels = 3 if sweep_index == 0 else 2
        canvas = gradient_canvas(
            channels, ext_shape, spots, own_count, extended, probe_field, own_amps, tables
        )
        folded = exchange_fold(canvas, margin)
        if sweep_index == 0:
            illumination = folded[2]
        current = current - folded[0:2] / (illumination + DAMPING)
    return current


def solution(mesh):
    return jax.shard_map(
        on_device,
        mesh=mesh,
        in_specs=(
            P(None, "sx", "sy"),
            P(),
            P("sx", "sy", None, None, None),
            P("sx", "sy", None, None),
            P(None, "sy"),
        ),
        out_specs=P(None, "sx", "sy"),
        check_vma=False,
    )
```

```python
import math

import jax
import jax.numpy as jnp
from jax import lax
from jax.sharding import PartitionSpec as P
from jax.experimental import pallas as pl
from jax.experimental.pallas import tpu as pltpu

ITERS = 2


SMOOTH = 1.0
DAMPING = 1.0


def with_halo(cells, sides, width):
    for axis, dim in sides:
        count = lax.axis_size(axis)
        ends = count - 1
        head = lax.slice_in_dim(cells, 0, width, axis=dim)
        tail = lax.slice_in_dim(cells, cells.shape[dim] - width, cells.shape[dim], axis=dim)
        cells = jnp.concatenate(
            [
                lax.ppermute(tail, axis, [(i, (i + 1) % count) for i in range(ends)]),
                cells,
                lax.ppermute(head, axis, [((i + 1) % count, i) for i in range(ends)]),
            ],
            axis=dim,
        )
    return cells


def dft_tables(length):
    index_values = jnp.arange(length, dtype=jnp.int32)
    product_mod = index_values[:, None] * index_values[None, :] % length
    angles = product_mod.astype(jnp.float32) * (2.0 * math.pi / length)
    scaling = 1.0 / math.sqrt(length)
    return (jnp.cos(angles) * scaling, -jnp.sin(angles) * scaling)


def matmul_exact(left_side, right_side):
    return jnp.dot(left_side, right_side, precision=lax.Precision.HIGHEST)


def complex_left(table_real, table_imag, field_real, field_imag):
    out_real = matmul_exact(table_real, field_real) - matmul_exact(table_imag, field_imag)
    out_imag = matmul_exact(table_real, field_imag) + matmul_exact(table_imag, field_real)
    return (out_real, out_imag)


def complex_right(field_real, field_imag, table_real, table_imag):
    out_real = matmul_exact(field_real, table_real) - matmul_exact(field_imag, table_imag)
    out_imag = matmul_exact(field_real, table_imag) + matmul_exact(field_imag, table_real)
    return (out_real, out_imag)


def position_gradient(object_patch, probe_field, amplitude, table_real, table_imag):
    probe_real = probe_field[0]
    probe_imag = probe_field[1]
    exit_real = probe_real * object_patch[0] - probe_imag * object_patch[1]
    exit_imag = probe_real * object_patch[1] + probe_imag * object_patch[0]
    half_real, half_imag = complex_left(table_real, table_imag, exit_real, exit_imag)
    far_real, far_imag = complex_right(half_real, half_imag, table_real, table_imag)
    factor = 1.0 - amplitude / jnp.sqrt(far_real * far_real + far_imag * far_imag + SMOOTH)
    miss_real = far_real * factor
    miss_imag = far_imag * factor
    back_real, back_imag = complex_left(table_real, -table_imag, miss_real, miss_imag)
    near_real, near_imag = complex_right(back_real, back_imag, table_real, -table_imag)
    return jnp.stack(
        [
            probe_real * near_real + probe_imag * near_imag,
            probe_real * near_imag - probe_imag * near_real,
        ]
    )


def add_patch(canvas, patch_values, corner_row, corner_col):
    zero_index = jnp.zeros((), jnp.int32)
    starts = (zero_index, corner_row, corner_col)
    present = lax.dynamic_slice(canvas, starts, patch_values.shape)
    return lax.dynamic_update_slice(canvas, present + patch_values, starts)


def fold_rows(extended, margin, length):
    middle_part = extended[:, 2 * margin : 2 * margin + length]
    upper_rim = extended[:, :margin]
    lower_rim = extended[:, extended.shape[1] - margin :]
    middle_part = middle_part.at[:, :margin].add(upper_rim)
    return middle_part.at[:, length - margin :].add(lower_rim)


def fold_cols(extended, margin, length):
    middle_part = extended[:, :, 2 * margin : 2 * margin + length]
    left_rim = extended[:, :, :margin]
    right_rim = extended[:, :, extended.shape[2] - margin :]
    middle_part = middle_part.at[:, :, :margin].add(left_rim)
    return middle_part.at[:, :, length - margin :].add(right_rim)


def settle(stacked, margin, block_rows, block_cols):
    full_ext = with_halo(stacked, (("sx", 1), ("sy", 2)), margin)
    return fold_cols(fold_rows(full_ext, margin, block_rows), margin, block_cols)


def local_pass(canvas, extended, spots, own_amps, probe_field, table_real, table_imag, upper_bound):
    size_probe = probe_field.shape[1]

    def local_step(slot_index, canvas_state):
        row_start = spots[slot_index, 0]
        col_start = spots[slot_index, 1]
        zero_index = jnp.zeros((), jnp.int32)
        object_patch = lax.dynamic_slice(
            extended, (zero_index, row_start, col_start), (2, size_probe, size_probe)
        )
        update = position_gradient(
            object_patch, probe_field, own_amps[slot_index], table_real, table_imag
        )
        return add_patch(canvas_state, update, row_start, col_start)

    return lax.fori_loop(0, upper_bound, local_step, canvas)


def dot_exact(left_side, right_side):
    return jnp.dot(
        left_side, right_side, precision=lax.Precision.HIGHEST, preferred_element_type=jnp.float32
    )


def window_tools(size, row, col):
    lanes = 128
    sublanes = 8
    wide = size + lanes
    tall = size + sublanes
    row_base = pl.multiple_of((row // sublanes) * sublanes, sublanes)
    col_base = pl.multiple_of((col // lanes) * lanes, lanes)
    row_shift = row % sublanes
    col_shift = col % lanes
    rows = pl.ds(row_base, tall)
    cols = pl.ds(col_base, wide)

    def take(ref, channel):
        block = ref[channel, rows, cols]
        block = pltpu.roll(block, (tall - row_shift) % tall, 0)
        return pltpu.roll(block, (wide - col_shift) % wide, 1)[:size, :size]

    def put(ref, channel, values):
        block = jnp.concatenate([values, jnp.zeros((size, lanes), jnp.float32)], axis=1)
        block = jnp.concatenate([block, jnp.zeros((sublanes, wide), jnp.float32)], axis=0)
        block = pltpu.roll(pltpu.roll(block, col_shift, 1), row_shift, 0)
        ref[channel, rows, cols] += block

    return take, put


def split_bf16(values):
    scaled = values * 65537.0
    high = scaled - (scaled - values)
    return high.astype(jnp.bfloat16), (values - high).astype(jnp.bfloat16)


def dot_split(left_parts, right_parts):
    left_high, left_low = left_parts
    right_high, right_low = right_parts
    total = jnp.dot(left_high, right_high, preferred_element_type=jnp.float32)
    total += jnp.dot(left_high, right_low, preferred_element_type=jnp.float32)
    return total + jnp.dot(left_low, right_high, preferred_element_type=jnp.float32)


def gradient_kernel(spots_ref, count_ref, ext_ref, probe_ref, amps_ref, tables_ref, out_ref):
    size = probe_ref.shape[1]
    out_ref[...] = jnp.zeros(out_ref.shape, jnp.float32)
    with_power = out_ref.shape[0] > 2
    for slot in range(amps_ref.shape[0]):

        @pl.when(slot < count_ref[0])
        def _():
            take, put = window_tools(size, spots_ref[slot, 0], spots_ref[slot, 1])
            probe_real = probe_ref[0]
            probe_imag = probe_ref[1]
            real_parts = (tables_ref[0], tables_ref[1])
            imag_parts = (tables_ref[2], tables_ref[3])

            def left(field_real, field_imag, sign):
                both = split_bf16(jnp.concatenate([field_real, field_imag], axis=1))
                by_real = dot_split(real_parts, both)
                by_imag = dot_split(imag_parts, both)
                out_real = by_real[:, :size] - sign * by_imag[:, size:]
                out_imag = by_real[:, size:] + sign * by_imag[:, :size]
                return out_real, out_imag

            def right(field_real, field_imag, sign):
                both = split_bf16(jnp.concatenate([field_real, field_imag], axis=0))
                by_real = dot_split(both, real_parts)
                by_imag = dot_split(both, imag_parts)
                out_real = by_real[:size] - sign * by_imag[size:]
                out_imag = by_imag[:size] * sign + by_real[size:]
                return out_real, out_imag

            obj_real = take(ext_ref, 0)
            obj_imag = take(ext_ref, 1)
            exit_real = probe_real * obj_real - probe_imag * obj_imag
            exit_imag = probe_real * obj_imag + probe_imag * obj_real
            half_real, half_imag = left(exit_real, exit_imag, 1.0)
            far_real, far_imag = right(half_real, half_imag, 1.0)
            factor = 1.0 - amps_ref[slot] / jnp.sqrt(far_real * far_real + far_imag * far_imag + SMOOTH)
            miss_real = far_real * factor
            miss_imag = far_imag * factor
            back_real, back_imag = left(miss_real, miss_imag, -1.0)
            near_real, near_imag = right(back_real, back_imag, -1.0)
            put(out_ref, 0, probe_real * near_real + probe_imag * near_imag)
            put(out_ref, 1, probe_real * near_imag - probe_imag * near_real)
            if with_power:
                put(out_ref, 2, probe_real * probe_real + probe_imag * probe_imag)


def power_kernel(spots_ref, count_ref, probe_ref, out_ref):
    size = probe_ref.shape[1]
    out_ref[...] = jnp.zeros(out_ref.shape, jnp.float32)
    power = probe_ref[0] * probe_ref[0] + probe_ref[1] * probe_ref[1]
    for slot in range(spots_ref.shape[0]):

        @pl.when(slot < count_ref[0])
        def _():
            _, put = window_tools(size, spots_ref[slot, 0], spots_ref[slot, 1])
            put(out_ref, 0, power)


VMEM_SPEC = pl.BlockSpec(memory_space=pltpu.VMEM)
SMEM_SPEC = pl.BlockSpec(memory_space=pltpu.SMEM)
KERNEL_PARAMS = pltpu.CompilerParams(vmem_limit_bytes=60 * 1024 * 1024)


def gradient_canvas(channels, ext_shape, spots, count, extended, probe_field, own_amps, tables):
    parts = jnp.stack(split_bf16(tables[0]) + split_bf16(tables[1]))
    return pl.pallas_call(
        gradient_kernel,
        out_shape=jax.ShapeDtypeStruct((channels,) + ext_shape, jnp.float32),
        in_specs=[SMEM_SPEC, SMEM_SPEC] + [VMEM_SPEC] * 4,
        out_specs=VMEM_SPEC,
        compiler_params=KERNEL_PARAMS,
    )(spots, count.reshape(1), extended, probe_field, own_amps, parts)


def power_canvas(ext_shape, spots, count, probe_field):
    return pl.pallas_call(
        power_kernel,
        out_shape=jax.ShapeDtypeStruct((1,) + ext_shape, jnp.float32),
        in_specs=[SMEM_SPEC, SMEM_SPEC, VMEM_SPEC],
        out_specs=VMEM_SPEC,
        compiler_params=KERNEL_PARAMS,
    )(spots, count.reshape(1), probe_field)


def mesh_place():
    return (
        lax.axis_index("sx"),
        lax.axis_index("sy"),
        lax.axis_size("sx"),
        lax.axis_size("sy"),
    )


def exists(row_dev, col_dev, row_count, col_count):
    return (row_dev >= 0) & (row_dev < row_count) & (col_dev >= 0) & (col_dev < col_count)


ROW_NEIGHBOURS = [(-1, 0), (1, 0)]
COL_NEIGHBOURS = [(0, -1), (0, 1)]


def neighbour_barrier(me_r, me_c, n_r, n_c):
    barrier = pltpu.get_barrier_semaphore()
    greeted = jnp.int32(0)
    for dr, dc in ROW_NEIGHBOURS + COL_NEIGHBOURS:
        present = exists(me_r + dr, me_c + dc, n_r, n_c)

        @pl.when(present)
        def _():
            pl.semaphore_signal(
                barrier, inc=1, device_id=(me_r + dr, me_c + dc), device_id_type=pl.DeviceIdType.MESH
            )

        greeted = greeted + present.astype(jnp.int32)
    pl.semaphore_wait(barrier, greeted)


def swap(place, pieces, send_sems, recv_sems):
    me_r, me_c, n_r, n_c = place
    copies = []
    for index, ((dr, dc), source, target) in enumerate(pieces):
        copy = pltpu.make_async_remote_copy(
            src_ref=source,
            dst_ref=target,
            send_sem=send_sems.at[index],
            recv_sem=recv_sems.at[index],
            device_id=(me_r + dr, me_c + dc),
            device_id_type=pl.DeviceIdType.MESH,
        )
        copies.append(copy)

        @pl.when(exists(me_r + dr, me_c + dc, n_r, n_c))
        def _():
            copy.start()

    for index, ((dr, dc), _, _) in enumerate(pieces):
        copy = copies[index]

        @pl.when(exists(me_r + dr, me_c + dc, n_r, n_c))
        def _():
            copy.wait_send()

        @pl.when(exists(me_r - dr, me_c - dc, n_r, n_c))
        def _():
            copy.wait_recv()


def halo_kernel(cur_ref, ext_ref, send_sems, recv_sems):
    rows = cur_ref.shape[1]
    cols = cur_ref.shape[2]
    margin = (ext_ref.shape[2] - cols) // 2
    place = mesh_place()
    me_r, me_c, n_r, n_c = place
    middle = slice(margin, margin + rows)
    ext_ref[:, middle, margin : margin + cols] = cur_ref[...]
    unreached = [
        ((0, 1), (slice(None), middle, slice(0, margin))),
        ((0, -1), (slice(None), middle, slice(margin + cols, 2 * margin + cols))),
        ((1, 0), (slice(None), slice(0, margin), slice(None))),
        ((-1, 0), (slice(None), slice(margin + rows, 2 * margin + rows), slice(None))),
    ]
    for (dr, dc), region in unreached:

        @pl.when(jnp.logical_not(exists(me_r - dr, me_c - dc, n_r, n_c)))
        def _():
            ext_ref[region] = jnp.zeros(ext_ref[region].shape, jnp.float32)

    neighbour_barrier(me_r, me_c, n_r, n_c)
    swap(
        place,
        [
            ((0, -1), cur_ref.at[:, :, 0:margin], ext_ref.at[:, middle, margin + cols : 2 * margin + cols]),
            ((0, 1), cur_ref.at[:, :, cols - margin : cols], ext_ref.at[:, middle, 0:margin]),
        ],
        send_sems.at[0:2],
        recv_sems.at[0:2],
    )
    swap(
        place,
        [
            ((-1, 0), ext_ref.at[:, middle, :], ext_ref.at[:, margin + rows : 2 * margin + rows, :]),
            ((1, 0), ext_ref.at[:, middle, :], ext_ref.at[:, 0:margin, :]),
        ],
        send_sems.at[2:4],
        recv_sems.at[2:4],
    )


def fold_kernel(canvas_ref, out_ref, row_bufs, col_bufs, band_ref, send_sems, recv_sems):
    rows = out_ref.shape[1]
    cols = out_ref.shape[2]
    margin = (canvas_ref.shape[2] - cols) // 2
    place = mesh_place()
    me_r, me_c, n_r, n_c = place
    neighbour_barrier(me_r, me_c, n_r, n_c)
    swap(
        place,
        [
            ((-1, 0), canvas_ref.at[:, 0:margin, :], row_bufs.at[0]),
            ((1, 0), canvas_ref.at[:, margin + rows : 2 * margin + rows, :], row_bufs.at[1]),
        ],
        send_sems.at[0:2],
        recv_sems.at[0:2],
    )
    band_ref[...] = canvas_ref[:, margin : margin + rows, :]

    @pl.when(exists(me_r + 1, me_c, n_r, n_c))
    def _():
        band_ref[...] += row_bufs[0]

    @pl.when(exists(me_r - 1, me_c, n_r, n_c))
    def _():
        band_ref[...] += row_bufs[1]

    swap(
        place,
        [
            ((0, -1), band_ref.at[:, :, 0:margin], col_bufs.at[0]),
            ((0, 1), band_ref.at[:, :, margin + cols : 2 * margin + cols], col_bufs.at[1]),
        ],
        send_sems.at[2:4],
        recv_sems.at[2:4],
    )
    out_ref[...] = band_ref[:, :, margin : margin + cols]

    @pl.when(exists(me_r, me_c + 1, n_r, n_c))
    def _():
        out_ref[:, :, cols - margin : cols] += col_bufs[0]

    @pl.when(exists(me_r, me_c - 1, n_r, n_c))
    def _():
        out_ref[:, :, 0:margin] += col_bufs[1]


def fold_step_kernel(canvas_ref, cur_ref, ext_ref, light_ref, row_bufs, col_bufs, edge_bufs, band_ref, send_sems, recv_sems):
    depth = canvas_ref.shape[0]
    rows = cur_ref.shape[1]
    cols = cur_ref.shape[2]
    margin = (canvas_ref.shape[2] - cols) // 2
    place = mesh_place()
    me_r, me_c, n_r, n_c = place
    for dr, region in ((1, slice(0, margin)), (-1, slice(margin + rows, 2 * margin + rows))):

        @pl.when(jnp.logical_not(exists(me_r - dr, me_c, n_r, n_c)))
        def _():
            ext_ref[:, region, :] = jnp.zeros(ext_ref[:, region, :].shape, jnp.float32)

    for side, present in ((0, exists(me_r, me_c + 1, n_r, n_c)), (1, exists(me_r, me_c - 1, n_r, n_c))):

        @pl.when(jnp.logical_not(present))
        def _():
            col_bufs[side] = jnp.zeros(col_bufs.shape[1:], jnp.float32)
            edge_bufs[side] = jnp.zeros(edge_bufs.shape[1:], jnp.float32)

    neighbour_barrier(me_r, me_c, n_r, n_c)
    swap(
        place,
        [
            ((-1, 0), canvas_ref.at[:, 0:margin, :], row_bufs.at[0]),
            ((1, 0), canvas_ref.at[:, margin + rows : 2 * margin + rows, :], row_bufs.at[1]),
        ],
        send_sems.at[0:2],
        recv_sems.at[0:2],
    )
    band_ref[...] = canvas_ref[:, margin : margin + rows, :]

    @pl.when(exists(me_r + 1, me_c, n_r, n_c))
    def _():
        band_ref[...] += row_bufs[0]

    @pl.when(exists(me_r - 1, me_c, n_r, n_c))
    def _():
        band_ref[...] += row_bufs[1]

    ext_cols = cols + 2 * margin
    swap(
        place,
        [
            ((0, -1), band_ref.at[:, :, 0 : 2 * margin], col_bufs.at[0]),
            ((0, 1), band_ref.at[:, :, ext_cols - 2 * margin : ext_cols], col_bufs.at[1]),
            ((0, -1), cur_ref.at[:, :, 0:margin], edge_bufs.at[0]),
            ((0, 1), cur_ref.at[:, :, cols - margin : cols], edge_bufs.at[1]),
        ],
        send_sems.at[2:6],
        recv_sems.at[2:6],
    )
    has_left = exists(me_r, me_c - 1, n_r, n_c)
    has_right = exists(me_r, me_c + 1, n_r, n_c)
    from_right = jnp.where(has_right, col_bufs[0], 0.0)
    from_left = jnp.where(has_left, col_bufs[1], 0.0)
    band = band_ref[...]
    total = jnp.concatenate(
        [
            band[:, :, 0:margin] + from_left[:, :, 0:margin],
            band[:, :, margin : 2 * margin] + from_left[:, :, margin:],
            band[:, :, 2 * margin : ext_cols - 2 * margin],
            band[:, :, ext_cols - 2 * margin : ext_cols - margin] + from_right[:, :, 0:margin],
            band[:, :, ext_cols - margin :] + from_right[:, :, margin:],
        ],
        axis=2,
    )
    light = total[depth - 1]
    values = jnp.concatenate([edge_bufs[1], cur_ref[...], edge_bufs[0]], axis=2)
    updated = values - total[0 : depth - 1] / (light + DAMPING)
    col_index = lax.broadcasted_iota(jnp.int32, updated.shape, 2)
    inside = ((col_index >= margin) | has_left) & ((col_index < margin + cols) | has_right)
    middle = slice(margin, margin + rows)
    ext_ref[:, middle, :] = jnp.where(inside, updated, 0.0)
    light_ref[...] = light[:, margin : margin + cols]
    swap(
        place,
        [
            ((-1, 0), ext_ref.at[:, middle, :], ext_ref.at[:, margin + rows : 2 * margin + rows, :]),
            ((1, 0), ext_ref.at[:, middle, :], ext_ref.at[:, 0:margin, :]),
        ],
        send_sems.at[6:8],
        recv_sems.at[6:8],
    )


def fold_and_step(canvas, current, margin):
    depth, ext_rows, ext_cols = canvas.shape
    rows = ext_rows - 2 * margin
    cols = ext_cols - 2 * margin
    fields = current.shape[0]
    return pl.pallas_call(
        fold_step_kernel,
        out_shape=(
            jax.ShapeDtypeStruct((fields, ext_rows, ext_cols), jnp.float32),
            jax.ShapeDtypeStruct((rows, cols), jnp.float32),
        ),
        in_specs=[VMEM_SPEC, VMEM_SPEC],
        out_specs=(VMEM_SPEC, VMEM_SPEC),
        scratch_shapes=[
            pltpu.VMEM((2, depth, margin, ext_cols), jnp.float32),
            pltpu.VMEM((2, depth, rows, 2 * margin), jnp.float32),
            pltpu.VMEM((2, fields, rows, margin), jnp.float32),
            pltpu.VMEM((depth, rows, ext_cols), jnp.float32),
            pltpu.SemaphoreType.DMA((8,)),
            pltpu.SemaphoreType.DMA((8,)),
        ],
        compiler_params=pltpu.CompilerParams(
            vmem_limit_bytes=60 * 1024 * 1024, has_side_effects=True, collective_id=5
        ),
    )(canvas, current)


def exchange_halo(current, margin):
    depth, rows, cols = current.shape
    return pl.pallas_call(
        halo_kernel,
        out_shape=jax.ShapeDtypeStruct((depth, rows + 2 * margin, cols + 2 * margin), jnp.float32),
        in_specs=[VMEM_SPEC],
        out_specs=VMEM_SPEC,
        scratch_shapes=[pltpu.SemaphoreType.DMA((4,)), pltpu.SemaphoreType.DMA((4,))],
        compiler_params=pltpu.CompilerParams(
            vmem_limit_bytes=60 * 1024 * 1024, has_side_effects=True, collective_id=0
        ),
    )(current)


def exchange_fold(canvas, margin):
    depth, ext_rows, ext_cols = canvas.shape
    rows = ext_rows - 2 * margin
    cols = ext_cols - 2 * margin
    return pl.pallas_call(
        fold_kernel,
        out_shape=jax.ShapeDtypeStruct((depth, rows, cols), jnp.float32),
        in_specs=[VMEM_SPEC],
        out_specs=VMEM_SPEC,
        scratch_shapes=[
            pltpu.VMEM((2, depth, margin, ext_cols), jnp.float32),
            pltpu.VMEM((2, depth, rows, margin), jnp.float32),
            pltpu.VMEM((depth, rows, ext_cols), jnp.float32),
            pltpu.SemaphoreType.DMA((4,)),
            pltpu.SemaphoreType.DMA((4,)),
        ],
        compiler_params=pltpu.CompilerParams(
            vmem_limit_bytes=60 * 1024 * 1024, has_side_effects=True, collective_id=depth
        ),
    )(canvas)


def on_device(object_field, probe_field, amplitudes, centres, counts):
    size_probe = probe_field.shape[1]
    margin = size_probe // 2
    block_rows = object_field.shape[1]
    block_cols = object_field.shape[2]
    tables = dft_tables(size_probe)
    spots = centres[0, 0]
    own_amps = amplitudes[0, 0]
    sx_size = lax.axis_size("sx")
    sx_index = lax.axis_index("sx")
    column_counts = counts[:, 0]
    sx_positions = jnp.arange(sx_size, dtype=jnp.int32)
    own_count = jnp.sum(jnp.where(sx_positions == sx_index, column_counts, 0))
    ext_shape = (block_rows + size_probe, block_cols + size_probe)

    extended = exchange_halo(object_field, margin)
    canvas = gradient_canvas(3, ext_shape, spots, own_count, extended, probe_field, own_amps, tables)
    extended, illumination = fold_and_step(canvas, object_field, margin)
    for sweep_index in range(1, ITERS):
        canvas = gradient_canvas(2, ext_shape, spots, own_count, extended, probe_field, own_amps, tables)
        gradient = exchange_fold(canvas, margin)
        current = extended[:, margin : margin + block_rows, margin : margin + block_cols]
        current = current - gradient / (illumination + DAMPING)
        if sweep_index < ITERS - 1:
            extended = exchange_halo(current, margin)
    return current


def solution(mesh):
    return jax.shard_map(
        on_device,
        mesh=mesh,
        in_specs=(
            P(None, "sx", "sy"),
            P(),
            P("sx", "sy", None, None, None),
            P("sx", "sy", None, None),
            P(None, "sy"),
        ),
        out_specs=P(None, "sx", "sy"),
        check_vma=False,
    )
```

```python
import math

import jax
import jax.numpy as jnp
from jax import lax
from jax.sharding import PartitionSpec as P
from jax.experimental import pallas as pl
from jax.experimental.pallas import tpu as pltpu

ITERS = 2


SMOOTH = 1.0
DAMPING = 1.0


def with_halo(cells, sides, width):
    for axis, dim in sides:
        count = lax.axis_size(axis)
        ends = count - 1
        head = lax.slice_in_dim(cells, 0, width, axis=dim)
        tail = lax.slice_in_dim(cells, cells.shape[dim] - width, cells.shape[dim], axis=dim)
        cells = jnp.concatenate(
            [
                lax.ppermute(tail, axis, [(i, (i + 1) % count) for i in range(ends)]),
                cells,
                lax.ppermute(head, axis, [((i + 1) % count, i) for i in range(ends)]),
            ],
            axis=dim,
        )
    return cells


def dft_tables(length):
    index_values = jnp.arange(length, dtype=jnp.int32)
    product_mod = index_values[:, None] * index_values[None, :] % length
    angles = product_mod.astype(jnp.float32) * (2.0 * math.pi / length)
    scaling = 1.0 / math.sqrt(length)
    return (jnp.cos(angles) * scaling, -jnp.sin(angles) * scaling)


def matmul_exact(left_side, right_side):
    return jnp.dot(left_side, right_side, precision=lax.Precision.HIGHEST)


def complex_left(table_real, table_imag, field_real, field_imag):
    out_real = matmul_exact(table_real, field_real) - matmul_exact(table_imag, field_imag)
    out_imag = matmul_exact(table_real, field_imag) + matmul_exact(table_imag, field_real)
    return (out_real, out_imag)


def complex_right(field_real, field_imag, table_real, table_imag):
    out_real = matmul_exact(field_real, table_real) - matmul_exact(field_imag, table_imag)
    out_imag = matmul_exact(field_real, table_imag) + matmul_exact(field_imag, table_real)
    return (out_real, out_imag)


def position_gradient(object_patch, probe_field, amplitude, table_real, table_imag):
    probe_real = probe_field[0]
    probe_imag = probe_field[1]
    exit_real = probe_real * object_patch[0] - probe_imag * object_patch[1]
    exit_imag = probe_real * object_patch[1] + probe_imag * object_patch[0]
    half_real, half_imag = complex_left(table_real, table_imag, exit_real, exit_imag)
    far_real, far_imag = complex_right(half_real, half_imag, table_real, table_imag)
    factor = 1.0 - amplitude / jnp.sqrt(far_real * far_real + far_imag * far_imag + SMOOTH)
    miss_real = far_real * factor
    miss_imag = far_imag * factor
    back_real, back_imag = complex_left(table_real, -table_imag, miss_real, miss_imag)
    near_real, near_imag = complex_right(back_real, back_imag, table_real, -table_imag)
    return jnp.stack(
        [
            probe_real * near_real + probe_imag * near_imag,
            probe_real * near_imag - probe_imag * near_real,
        ]
    )


def add_patch(canvas, patch_values, corner_row, corner_col):
    zero_index = jnp.zeros((), jnp.int32)
    starts = (zero_index, corner_row, corner_col)
    present = lax.dynamic_slice(canvas, starts, patch_values.shape)
    return lax.dynamic_update_slice(canvas, present + patch_values, starts)


def fold_rows(extended, margin, length):
    middle_part = extended[:, 2 * margin : 2 * margin + length]
    upper_rim = extended[:, :margin]
    lower_rim = extended[:, extended.shape[1] - margin :]
    middle_part = middle_part.at[:, :margin].add(upper_rim)
    return middle_part.at[:, length - margin :].add(lower_rim)


def fold_cols(extended, margin, length):
    middle_part = extended[:, :, 2 * margin : 2 * margin + length]
    left_rim = extended[:, :, :margin]
    right_rim = extended[:, :, extended.shape[2] - margin :]
    middle_part = middle_part.at[:, :, :margin].add(left_rim)
    return middle_part.at[:, :, length - margin :].add(right_rim)


def settle(stacked, margin, block_rows, block_cols):
    full_ext = with_halo(stacked, (("sx", 1), ("sy", 2)), margin)
    return fold_cols(fold_rows(full_ext, margin, block_rows), margin, block_cols)


def local_pass(canvas, extended, spots, own_amps, probe_field, table_real, table_imag, upper_bound):
    size_probe = probe_field.shape[1]

    def local_step(slot_index, canvas_state):
        row_start = spots[slot_index, 0]
        col_start = spots[slot_index, 1]
        zero_index = jnp.zeros((), jnp.int32)
        object_patch = lax.dynamic_slice(
            extended, (zero_index, row_start, col_start), (2, size_probe, size_probe)
        )
        update = position_gradient(
            object_patch, probe_field, own_amps[slot_index], table_real, table_imag
        )
        return add_patch(canvas_state, update, row_start, col_start)

    return lax.fori_loop(0, upper_bound, local_step, canvas)


def dot_exact(left_side, right_side):
    return jnp.dot(
        left_side, right_side, precision=lax.Precision.HIGHEST, preferred_element_type=jnp.float32
    )


def window_tools(size, row, col):
    lanes = 128
    sublanes = 8
    wide = size + lanes
    tall = size + sublanes
    row_base = pl.multiple_of((row // sublanes) * sublanes, sublanes)
    col_base = pl.multiple_of((col // lanes) * lanes, lanes)
    row_shift = row % sublanes
    col_shift = col % lanes
    rows = pl.ds(row_base, tall)
    cols = pl.ds(col_base, wide)

    def take(ref, channel):
        block = ref[channel, rows, cols]
        block = pltpu.roll(block, (tall - row_shift) % tall, 0)
        return pltpu.roll(block, (wide - col_shift) % wide, 1)[:size, :size]

    def put(ref, channel, values):
        block = jnp.concatenate([values, jnp.zeros((size, lanes), jnp.float32)], axis=1)
        block = jnp.concatenate([block, jnp.zeros((sublanes, wide), jnp.float32)], axis=0)
        block = pltpu.roll(pltpu.roll(block, col_shift, 1), row_shift, 0)
        ref[channel, rows, cols] += block

    return take, put


def split_bf16(values):
    scaled = values * 65537.0
    high = scaled - (scaled - values)
    return high.astype(jnp.bfloat16), (values - high).astype(jnp.bfloat16)


def dot_split(left_parts, right_parts):
    left_high, left_low = left_parts
    right_high, right_low = right_parts
    total = jnp.dot(left_high, right_high, preferred_element_type=jnp.float32)
    total += jnp.dot(left_high, right_low, preferred_element_type=jnp.float32)
    return total + jnp.dot(left_low, right_high, preferred_element_type=jnp.float32)


def gradient_kernel(spots_ref, count_ref, ext_ref, probe_ref, amps_ref, tables_ref, out_ref):
    size = probe_ref.shape[1]
    out_ref[...] = jnp.zeros(out_ref.shape, jnp.float32)
    with_power = out_ref.shape[0] > 2
    for slot in range(amps_ref.shape[0]):

        @pl.when(slot < count_ref[0])
        def _():
            take, put = window_tools(size, spots_ref[slot, 0], spots_ref[slot, 1])
            probe_real = probe_ref[0]
            probe_imag = probe_ref[1]
            real_parts = (tables_ref[0], tables_ref[1])
            imag_parts = (tables_ref[2], tables_ref[3])

            def left(field_real, field_imag, sign):
                both = split_bf16(jnp.concatenate([field_real, field_imag], axis=1))
                by_real = dot_split(real_parts, both)
                by_imag = dot_split(imag_parts, both)
                out_real = by_real[:, :size] - sign * by_imag[:, size:]
                out_imag = by_real[:, size:] + sign * by_imag[:, :size]
                return out_real, out_imag

            def right(field_real, field_imag, sign):
                both = split_bf16(jnp.concatenate([field_real, field_imag], axis=0))
                by_real = dot_split(both, real_parts)
                by_imag = dot_split(both, imag_parts)
                out_real = by_real[:size] - sign * by_imag[size:]
                out_imag = by_imag[:size] * sign + by_real[size:]
                return out_real, out_imag

            obj_real = take(ext_ref, 0)
            obj_imag = take(ext_ref, 1)
            exit_real = probe_real * obj_real - probe_imag * obj_imag
            exit_imag = probe_real * obj_imag + probe_imag * obj_real
            half_real, half_imag = left(exit_real, exit_imag, 1.0)
            far_real, far_imag = right(half_real, half_imag, 1.0)
            factor = 1.0 - amps_ref[slot] / jnp.sqrt(far_real * far_real + far_imag * far_imag + SMOOTH)
            miss_real = far_real * factor
            miss_imag = far_imag * factor
            back_real, back_imag = left(miss_real, miss_imag, -1.0)
            near_real, near_imag = right(back_real, back_imag, -1.0)
            put(out_ref, 0, probe_real * near_real + probe_imag * near_imag)
            put(out_ref, 1, probe_real * near_imag - probe_imag * near_real)
            if with_power:
                put(out_ref, 2, probe_real * probe_real + probe_imag * probe_imag)


def power_kernel(spots_ref, count_ref, probe_ref, out_ref):
    size = probe_ref.shape[1]
    out_ref[...] = jnp.zeros(out_ref.shape, jnp.float32)
    power = probe_ref[0] * probe_ref[0] + probe_ref[1] * probe_ref[1]
    for slot in range(spots_ref.shape[0]):

        @pl.when(slot < count_ref[0])
        def _():
            _, put = window_tools(size, spots_ref[slot, 0], spots_ref[slot, 1])
            put(out_ref, 0, power)


VMEM_SPEC = pl.BlockSpec(memory_space=pltpu.VMEM)
SMEM_SPEC = pl.BlockSpec(memory_space=pltpu.SMEM)
KERNEL_PARAMS = pltpu.CompilerParams(vmem_limit_bytes=60 * 1024 * 1024)


def gradient_canvas(channels, ext_shape, spots, count, extended, probe_field, own_amps, tables):
    parts = jnp.stack(split_bf16(tables[0]) + split_bf16(tables[1]))
    return pl.pallas_call(
        gradient_kernel,
        out_shape=jax.ShapeDtypeStruct((channels,) + ext_shape, jnp.float32),
        in_specs=[SMEM_SPEC, SMEM_SPEC] + [VMEM_SPEC] * 4,
        out_specs=VMEM_SPEC,
        compiler_params=KERNEL_PARAMS,
    )(spots, count.reshape(1), extended, probe_field, own_amps, parts)


def power_canvas(ext_shape, spots, count, probe_field):
    return pl.pallas_call(
        power_kernel,
        out_shape=jax.ShapeDtypeStruct((1,) + ext_shape, jnp.float32),
        in_specs=[SMEM_SPEC, SMEM_SPEC, VMEM_SPEC],
        out_specs=VMEM_SPEC,
        compiler_params=KERNEL_PARAMS,
    )(spots, count.reshape(1), probe_field)


def mesh_place():
    return (
        lax.axis_index("sx"),
        lax.axis_index("sy"),
        lax.axis_size("sx"),
        lax.axis_size("sy"),
    )


def exists(row_dev, col_dev, row_count, col_count):
    return (row_dev >= 0) & (row_dev < row_count) & (col_dev >= 0) & (col_dev < col_count)


ROW_NEIGHBOURS = [(-1, 0), (1, 0)]
COL_NEIGHBOURS = [(0, -1), (0, 1)]


def neighbour_barrier(me_r, me_c, n_r, n_c):
    barrier = pltpu.get_barrier_semaphore()
    greeted = jnp.int32(0)
    for dr, dc in ROW_NEIGHBOURS + COL_NEIGHBOURS:
        present = exists(me_r + dr, me_c + dc, n_r, n_c)

        @pl.when(present)
        def _():
            pl.semaphore_signal(
                barrier, inc=1, device_id=(me_r + dr, me_c + dc), device_id_type=pl.DeviceIdType.MESH
            )

        greeted = greeted + present.astype(jnp.int32)
    pl.semaphore_wait(barrier, greeted)


def swap(place, pieces, send_sems, recv_sems):
    me_r, me_c, n_r, n_c = place
    copies = []
    for index, ((dr, dc), source, target) in enumerate(pieces):
        copy = pltpu.make_async_remote_copy(
            src_ref=source,
            dst_ref=target,
            send_sem=send_sems.at[index],
            recv_sem=recv_sems.at[index],
            device_id=(me_r + dr, me_c + dc),
            device_id_type=pl.DeviceIdType.MESH,
        )
        copies.append(copy)

        @pl.when(exists(me_r + dr, me_c + dc, n_r, n_c))
        def _():
            copy.start()

    for index, ((dr, dc), _, _) in enumerate(pieces):
        copy = copies[index]

        @pl.when(exists(me_r + dr, me_c + dc, n_r, n_c))
        def _():
            copy.wait_send()

        @pl.when(exists(me_r - dr, me_c - dc, n_r, n_c))
        def _():
            copy.wait_recv()


def halo_kernel(cur_ref, ext_ref, send_sems, recv_sems):
    rows = cur_ref.shape[1]
    cols = cur_ref.shape[2]
    margin = (ext_ref.shape[2] - cols) // 2
    place = mesh_place()
    me_r, me_c, n_r, n_c = place
    middle = slice(margin, margin + rows)
    ext_ref[:, middle, margin : margin + cols] = cur_ref[...]
    unreached = [
        ((0, 1), (slice(None), middle, slice(0, margin))),
        ((0, -1), (slice(None), middle, slice(margin + cols, 2 * margin + cols))),
        ((1, 0), (slice(None), slice(0, margin), slice(None))),
        ((-1, 0), (slice(None), slice(margin + rows, 2 * margin + rows), slice(None))),
    ]
    for (dr, dc), region in unreached:

        @pl.when(jnp.logical_not(exists(me_r - dr, me_c - dc, n_r, n_c)))
        def _():
            ext_ref[region] = jnp.zeros(ext_ref[region].shape, jnp.float32)

    neighbour_barrier(me_r, me_c, n_r, n_c)
    swap(
        place,
        [
            ((0, -1), cur_ref.at[:, :, 0:margin], ext_ref.at[:, middle, margin + cols : 2 * margin + cols]),
            ((0, 1), cur_ref.at[:, :, cols - margin : cols], ext_ref.at[:, middle, 0:margin]),
        ],
        send_sems.at[0:2],
        recv_sems.at[0:2],
    )
    swap(
        place,
        [
            ((-1, 0), ext_ref.at[:, middle, :], ext_ref.at[:, margin + rows : 2 * margin + rows, :]),
            ((1, 0), ext_ref.at[:, middle, :], ext_ref.at[:, 0:margin, :]),
        ],
        send_sems.at[2:4],
        recv_sems.at[2:4],
    )


def fold_kernel(canvas_ref, out_ref, row_bufs, col_bufs, band_ref, send_sems, recv_sems, band_sem):
    rows = out_ref.shape[1]
    cols = out_ref.shape[2]
    margin = (canvas_ref.shape[2] - cols) // 2
    place = mesh_place()
    me_r, me_c, n_r, n_c = place
    own_band = pltpu.make_async_copy(canvas_ref.at[:, margin : margin + rows, :], band_ref, band_sem)
    own_band.start()
    neighbour_barrier(me_r, me_c, n_r, n_c)
    swap(
        place,
        [
            ((-1, 0), canvas_ref.at[:, 0:margin, :], row_bufs.at[0]),
            ((1, 0), canvas_ref.at[:, margin + rows : 2 * margin + rows, :], row_bufs.at[1]),
        ],
        send_sems.at[0:2],
        recv_sems.at[0:2],
    )
    own_band.wait()

    @pl.when(exists(me_r + 1, me_c, n_r, n_c))
    def _():
        band_ref[...] += row_bufs[0]

    @pl.when(exists(me_r - 1, me_c, n_r, n_c))
    def _():
        band_ref[...] += row_bufs[1]

    swap(
        place,
        [
            ((0, -1), band_ref.at[:, :, 0:margin], col_bufs.at[0]),
            ((0, 1), band_ref.at[:, :, margin + cols : 2 * margin + cols], col_bufs.at[1]),
        ],
        send_sems.at[2:4],
        recv_sems.at[2:4],
    )
    out_ref[...] = band_ref[:, :, margin : margin + cols]

    @pl.when(exists(me_r, me_c + 1, n_r, n_c))
    def _():
        out_ref[:, :, cols - margin : cols] += col_bufs[0]

    @pl.when(exists(me_r, me_c - 1, n_r, n_c))
    def _():
        out_ref[:, :, 0:margin] += col_bufs[1]


def exchange_halo(current, margin):
    depth, rows, cols = current.shape
    return pl.pallas_call(
        halo_kernel,
        out_shape=jax.ShapeDtypeStruct((depth, rows + 2 * margin, cols + 2 * margin), jnp.float32),
        in_specs=[VMEM_SPEC],
        out_specs=VMEM_SPEC,
        scratch_shapes=[pltpu.SemaphoreType.DMA((4,)), pltpu.SemaphoreType.DMA((4,))],
        compiler_params=pltpu.CompilerParams(
            vmem_limit_bytes=60 * 1024 * 1024, has_side_effects=True, collective_id=0
        ),
    )(current)


def exchange_fold(canvas, margin):
    depth, ext_rows, ext_cols = canvas.shape
    rows = ext_rows - 2 * margin
    cols = ext_cols - 2 * margin
    return pl.pallas_call(
        fold_kernel,
        out_shape=jax.ShapeDtypeStruct((depth, rows, cols), jnp.float32),
        in_specs=[pl.BlockSpec(memory_space=pl.ANY)],
        out_specs=VMEM_SPEC,
        scratch_shapes=[
            pltpu.VMEM((2, depth, margin, ext_cols), jnp.float32),
            pltpu.VMEM((2, depth, rows, margin), jnp.float32),
            pltpu.VMEM((depth, rows, ext_cols), jnp.float32),
            pltpu.SemaphoreType.DMA((4,)),
            pltpu.SemaphoreType.DMA((4,)),
            pltpu.SemaphoreType.DMA(()),
        ],
        compiler_params=pltpu.CompilerParams(
            vmem_limit_bytes=60 * 1024 * 1024, has_side_effects=True, collective_id=depth
        ),
    )(canvas)


def on_device(object_field, probe_field, amplitudes, centres, counts):
    size_probe = probe_field.shape[1]
    margin = size_probe // 2
    block_rows = object_field.shape[1]
    block_cols = object_field.shape[2]
    tables = dft_tables(size_probe)
    spots = centres[0, 0]
    own_amps = amplitudes[0, 0]
    sx_size = lax.axis_size("sx")
    sx_index = lax.axis_index("sx")
    column_counts = counts[:, 0]
    sx_positions = jnp.arange(sx_size, dtype=jnp.int32)
    own_count = jnp.sum(jnp.where(sx_positions == sx_index, column_counts, 0))
    ext_shape = (block_rows + size_probe, block_cols + size_probe)

    current = object_field
    for sweep_index in range(ITERS):
        extended = exchange_halo(current, margin)
        channels = 3 if sweep_index == 0 else 2
        canvas = gradient_canvas(
            channels, ext_shape, spots, own_count, extended, probe_field, own_amps, tables
        )
        folded = exchange_fold(canvas, margin)
        if sweep_index == 0:
            illumination = folded[2]
        current = current - folded[0:2] / (illumination + DAMPING)
    return current


def solution(mesh):
    return jax.shard_map(
        on_device,
        mesh=mesh,
        in_specs=(
            P(None, "sx", "sy"),
            P(),
            P("sx", "sy", None, None, None),
            P("sx", "sy", None, None),
            P(None, "sy"),
        ),
        out_specs=P(None, "sx", "sy"),
        check_vma=False,
    )
```

```python
import math

import jax
import jax.numpy as jnp
from jax import lax
from jax.sharding import PartitionSpec as P
from jax.experimental import pallas as pl
from jax.experimental.pallas import tpu as pltpu

ITERS = 2


SMOOTH = 1.0
DAMPING = 1.0


def with_halo(cells, sides, width):
    for axis, dim in sides:
        count = lax.axis_size(axis)
        ends = count - 1
        head = lax.slice_in_dim(cells, 0, width, axis=dim)
        tail = lax.slice_in_dim(cells, cells.shape[dim] - width, cells.shape[dim], axis=dim)
        cells = jnp.concatenate(
            [
                lax.ppermute(tail, axis, [(i, (i + 1) % count) for i in range(ends)]),
                cells,
                lax.ppermute(head, axis, [((i + 1) % count, i) for i in range(ends)]),
            ],
            axis=dim,
        )
    return cells


def dft_tables(length):
    index_values = jnp.arange(length, dtype=jnp.int32)
    product_mod = index_values[:, None] * index_values[None, :] % length
    angles = product_mod.astype(jnp.float32) * (2.0 * math.pi / length)
    scaling = 1.0 / math.sqrt(length)
    return (jnp.cos(angles) * scaling, -jnp.sin(angles) * scaling)


def matmul_exact(left_side, right_side):
    return jnp.dot(left_side, right_side, precision=lax.Precision.HIGHEST)


def complex_left(table_real, table_imag, field_real, field_imag):
    out_real = matmul_exact(table_real, field_real) - matmul_exact(table_imag, field_imag)
    out_imag = matmul_exact(table_real, field_imag) + matmul_exact(table_imag, field_real)
    return (out_real, out_imag)


def complex_right(field_real, field_imag, table_real, table_imag):
    out_real = matmul_exact(field_real, table_real) - matmul_exact(field_imag, table_imag)
    out_imag = matmul_exact(field_real, table_imag) + matmul_exact(field_imag, table_real)
    return (out_real, out_imag)


def position_gradient(object_patch, probe_field, amplitude, table_real, table_imag):
    probe_real = probe_field[0]
    probe_imag = probe_field[1]
    exit_real = probe_real * object_patch[0] - probe_imag * object_patch[1]
    exit_imag = probe_real * object_patch[1] + probe_imag * object_patch[0]
    half_real, half_imag = complex_left(table_real, table_imag, exit_real, exit_imag)
    far_real, far_imag = complex_right(half_real, half_imag, table_real, table_imag)
    factor = 1.0 - amplitude / jnp.sqrt(far_real * far_real + far_imag * far_imag + SMOOTH)
    miss_real = far_real * factor
    miss_imag = far_imag * factor
    back_real, back_imag = complex_left(table_real, -table_imag, miss_real, miss_imag)
    near_real, near_imag = complex_right(back_real, back_imag, table_real, -table_imag)
    return jnp.stack(
        [
            probe_real * near_real + probe_imag * near_imag,
            probe_real * near_imag - probe_imag * near_real,
        ]
    )


def add_patch(canvas, patch_values, corner_row, corner_col):
    zero_index = jnp.zeros((), jnp.int32)
    starts = (zero_index, corner_row, corner_col)
    present = lax.dynamic_slice(canvas, starts, patch_values.shape)
    return lax.dynamic_update_slice(canvas, present + patch_values, starts)


def fold_rows(extended, margin, length):
    middle_part = extended[:, 2 * margin : 2 * margin + length]
    upper_rim = extended[:, :margin]
    lower_rim = extended[:, extended.shape[1] - margin :]
    middle_part = middle_part.at[:, :margin].add(upper_rim)
    return middle_part.at[:, length - margin :].add(lower_rim)


def fold_cols(extended, margin, length):
    middle_part = extended[:, :, 2 * margin : 2 * margin + length]
    left_rim = extended[:, :, :margin]
    right_rim = extended[:, :, extended.shape[2] - margin :]
    middle_part = middle_part.at[:, :, :margin].add(left_rim)
    return middle_part.at[:, :, length - margin :].add(right_rim)


def settle(stacked, margin, block_rows, block_cols):
    full_ext = with_halo(stacked, (("sx", 1), ("sy", 2)), margin)
    return fold_cols(fold_rows(full_ext, margin, block_rows), margin, block_cols)


def local_pass(canvas, extended, spots, own_amps, probe_field, table_real, table_imag, upper_bound):
    size_probe = probe_field.shape[1]

    def local_step(slot_index, canvas_state):
        row_start = spots[slot_index, 0]
        col_start = spots[slot_index, 1]
        zero_index = jnp.zeros((), jnp.int32)
        object_patch = lax.dynamic_slice(
            extended, (zero_index, row_start, col_start), (2, size_probe, size_probe)
        )
        update = position_gradient(
            object_patch, probe_field, own_amps[slot_index], table_real, table_imag
        )
        return add_patch(canvas_state, update, row_start, col_start)

    return lax.fori_loop(0, upper_bound, local_step, canvas)


def dot_exact(left_side, right_side):
    return jnp.dot(
        left_side, right_side, precision=lax.Precision.HIGHEST, preferred_element_type=jnp.float32
    )


def window_tools(size, row, col):
    lanes = 128
    sublanes = 8
    wide = size + lanes
    tall = size + sublanes
    row_base = pl.multiple_of((row // sublanes) * sublanes, sublanes)
    col_base = pl.multiple_of((col // lanes) * lanes, lanes)
    row_shift = row % sublanes
    col_shift = col % lanes
    rows = pl.ds(row_base, tall)
    cols = pl.ds(col_base, wide)

    def take(ref, channel):
        block = ref[channel, rows, cols]
        block = pltpu.roll(block, (tall - row_shift) % tall, 0)
        return pltpu.roll(block, (wide - col_shift) % wide, 1)[:size, :size]

    def put(ref, channel, values):
        block = jnp.concatenate([values, jnp.zeros((size, lanes), jnp.float32)], axis=1)
        block = jnp.concatenate([block, jnp.zeros((sublanes, wide), jnp.float32)], axis=0)
        block = pltpu.roll(pltpu.roll(block, col_shift, 1), row_shift, 0)
        ref[channel, rows, cols] += block

    return take, put


def split_bf16(values):
    scaled = values * 65537.0
    high = scaled - (scaled - values)
    return high.astype(jnp.bfloat16), (values - high).astype(jnp.bfloat16)


def dot_split(left_parts, right_parts):
    left_high, left_low = left_parts
    right_high, right_low = right_parts
    total = jnp.dot(left_high, right_high, preferred_element_type=jnp.float32)
    total += jnp.dot(left_high, right_low, preferred_element_type=jnp.float32)
    return total + jnp.dot(left_low, right_high, preferred_element_type=jnp.float32)


def gradient_kernel(spots_ref, count_ref, ext_ref, probe_ref, amps_ref, tables_ref, out_ref):
    size = probe_ref.shape[1]
    out_ref[...] = jnp.zeros(out_ref.shape, jnp.float32)
    with_power = out_ref.shape[0] > 2
    for slot in range(amps_ref.shape[0]):

        @pl.when(slot < count_ref[0])
        def _():
            take, put = window_tools(size, spots_ref[slot, 0], spots_ref[slot, 1])
            probe_real = probe_ref[0]
            probe_imag = probe_ref[1]
            real_parts = (tables_ref[0], tables_ref[1])
            imag_parts = (tables_ref[2], tables_ref[3])

            def left(field_real, field_imag, sign):
                both = split_bf16(jnp.concatenate([field_real, field_imag], axis=1))
                by_real = dot_split(real_parts, both)
                by_imag = dot_split(imag_parts, both)
                out_real = by_real[:, :size] - sign * by_imag[:, size:]
                out_imag = by_real[:, size:] + sign * by_imag[:, :size]
                return out_real, out_imag

            def right(field_real, field_imag, sign):
                both = split_bf16(jnp.concatenate([field_real, field_imag], axis=0))
                by_real = dot_split(both, real_parts)
                by_imag = dot_split(both, imag_parts)
                out_real = by_real[:size] - sign * by_imag[size:]
                out_imag = by_imag[:size] * sign + by_real[size:]
                return out_real, out_imag

            obj_real = take(ext_ref, 0)
            obj_imag = take(ext_ref, 1)
            exit_real = probe_real * obj_real - probe_imag * obj_imag
            exit_imag = probe_real * obj_imag + probe_imag * obj_real
            half_real, half_imag = left(exit_real, exit_imag, 1.0)
            far_real, far_imag = right(half_real, half_imag, 1.0)
            factor = 1.0 - amps_ref[slot] / jnp.sqrt(far_real * far_real + far_imag * far_imag + SMOOTH)
            miss_real = far_real * factor
            miss_imag = far_imag * factor
            back_real, back_imag = left(miss_real, miss_imag, -1.0)
            near_real, near_imag = right(back_real, back_imag, -1.0)
            put(out_ref, 0, probe_real * near_real + probe_imag * near_imag)
            put(out_ref, 1, probe_real * near_imag - probe_imag * near_real)
            if with_power:
                put(out_ref, 2, probe_real * probe_real + probe_imag * probe_imag)


def power_kernel(spots_ref, count_ref, probe_ref, out_ref):
    size = probe_ref.shape[1]
    out_ref[...] = jnp.zeros(out_ref.shape, jnp.float32)
    power = probe_ref[0] * probe_ref[0] + probe_ref[1] * probe_ref[1]
    for slot in range(spots_ref.shape[0]):

        @pl.when(slot < count_ref[0])
        def _():
            _, put = window_tools(size, spots_ref[slot, 0], spots_ref[slot, 1])
            put(out_ref, 0, power)


VMEM_SPEC = pl.BlockSpec(memory_space=pltpu.VMEM)
SMEM_SPEC = pl.BlockSpec(memory_space=pltpu.SMEM)
KERNEL_PARAMS = pltpu.CompilerParams(vmem_limit_bytes=60 * 1024 * 1024)


def gradient_canvas(channels, ext_shape, spots, count, extended, probe_field, own_amps, tables):
    parts = jnp.stack(split_bf16(tables[0]) + split_bf16(tables[1]))
    return pl.pallas_call(
        gradient_kernel,
        out_shape=jax.ShapeDtypeStruct((channels,) + ext_shape, jnp.float32),
        in_specs=[SMEM_SPEC, SMEM_SPEC] + [VMEM_SPEC] * 4,
        out_specs=VMEM_SPEC,
        compiler_params=KERNEL_PARAMS,
    )(spots, count.reshape(1), extended, probe_field, own_amps, parts)


def power_canvas(ext_shape, spots, count, probe_field):
    return pl.pallas_call(
        power_kernel,
        out_shape=jax.ShapeDtypeStruct((1,) + ext_shape, jnp.float32),
        in_specs=[SMEM_SPEC, SMEM_SPEC, VMEM_SPEC],
        out_specs=VMEM_SPEC,
        compiler_params=KERNEL_PARAMS,
    )(spots, count.reshape(1), probe_field)


def mesh_place():
    return (
        lax.axis_index("sx"),
        lax.axis_index("sy"),
        lax.axis_size("sx"),
        lax.axis_size("sy"),
    )


def exists(row_dev, col_dev, row_count, col_count):
    return (row_dev >= 0) & (row_dev < row_count) & (col_dev >= 0) & (col_dev < col_count)


ROW_NEIGHBOURS = [(-1, 0), (1, 0)]
COL_NEIGHBOURS = [(0, -1), (0, 1)]


def neighbour_barrier(me_r, me_c, n_r, n_c):
    barrier = pltpu.get_barrier_semaphore()
    greeted = jnp.int32(0)
    for dr, dc in ROW_NEIGHBOURS + COL_NEIGHBOURS:
        present = exists(me_r + dr, me_c + dc, n_r, n_c)

        @pl.when(present)
        def _():
            pl.semaphore_signal(
                barrier, inc=1, device_id=(me_r + dr, me_c + dc), device_id_type=pl.DeviceIdType.MESH
            )

        greeted = greeted + present.astype(jnp.int32)
    pl.semaphore_wait(barrier, greeted)


def swap(place, pieces, send_sems, recv_sems):
    me_r, me_c, n_r, n_c = place
    copies = []
    for index, ((dr, dc), source, target) in enumerate(pieces):
        copy = pltpu.make_async_remote_copy(
            src_ref=source,
            dst_ref=target,
            send_sem=send_sems.at[index],
            recv_sem=recv_sems.at[index],
            device_id=(me_r + dr, me_c + dc),
            device_id_type=pl.DeviceIdType.MESH,
        )
        copies.append(copy)

        @pl.when(exists(me_r + dr, me_c + dc, n_r, n_c))
        def _():
            copy.start()

    for index, ((dr, dc), _, _) in enumerate(pieces):
        copy = copies[index]

        @pl.when(exists(me_r + dr, me_c + dc, n_r, n_c))
        def _():
            copy.wait_send()

        @pl.when(exists(me_r - dr, me_c - dc, n_r, n_c))
        def _():
            copy.wait_recv()


def halo_kernel(cur_ref, ext_ref, zeros_ref, send_sems, recv_sems, local_sems):
    rows = cur_ref.shape[1]
    cols = cur_ref.shape[2]
    margin = (ext_ref.shape[2] - cols) // 2
    ext_cols = cols + 2 * margin
    place = mesh_place()
    me_r, me_c, n_r, n_c = place
    middle = slice(margin, margin + rows)
    own = pltpu.make_async_copy(cur_ref, ext_ref.at[:, middle, margin : margin + cols], local_sems.at[0])
    own.start()
    zeros_ref[...] = jnp.zeros(zeros_ref.shape, jnp.float32)
    unreached = [
        ((0, 1), ext_ref.at[:, middle, 0:margin], zeros_ref.at[:, :, 0:margin]),
        ((0, -1), ext_ref.at[:, middle, margin + cols : ext_cols], zeros_ref.at[:, :, 0:margin]),
        ((1, 0), ext_ref.at[:, 0:margin, :], zeros_ref),
        ((-1, 0), ext_ref.at[:, margin + rows : 2 * margin + rows, :], zeros_ref),
    ]
    blanks = []
    for index, ((dr, dc), target, source) in enumerate(unreached):
        blank = pltpu.make_async_copy(source, target, local_sems.at[index + 1])
        missing = jnp.logical_not(exists(me_r - dr, me_c - dc, n_r, n_c))
        blanks.append((blank, missing))

    neighbour_barrier(me_r, me_c, n_r, n_c)
    for blank, missing in blanks:

        @pl.when(missing)
        def _():
            blank.start()

    swap(
        place,
        [
            ((0, -1), cur_ref.at[:, :, 0:margin], ext_ref.at[:, middle, margin + cols : ext_cols]),
            ((0, 1), cur_ref.at[:, :, cols - margin : cols], ext_ref.at[:, middle, 0:margin]),
        ],
        send_sems.at[0:2],
        recv_sems.at[0:2],
    )
    own.wait()
    for blank, missing in blanks:

        @pl.when(missing)
        def _():
            blank.wait()

    swap(
        place,
        [
            ((-1, 0), ext_ref.at[:, middle, :], ext_ref.at[:, margin + rows : 2 * margin + rows, :]),
            ((1, 0), ext_ref.at[:, middle, :], ext_ref.at[:, 0:margin, :]),
        ],
        send_sems.at[2:4],
        recv_sems.at[2:4],
    )


def fold_kernel(canvas_ref, out_ref, row_bufs, col_bufs, band_ref, send_sems, recv_sems, band_sem):
    rows = out_ref.shape[1]
    cols = out_ref.shape[2]
    margin = (canvas_ref.shape[2] - cols) // 2
    place = mesh_place()
    me_r, me_c, n_r, n_c = place
    own_band = pltpu.make_async_copy(canvas_ref.at[:, margin : margin + rows, :], band_ref, band_sem)
    own_band.start()
    neighbour_barrier(me_r, me_c, n_r, n_c)
    swap(
        place,
        [
            ((-1, 0), canvas_ref.at[:, 0:margin, :], row_bufs.at[0]),
            ((1, 0), canvas_ref.at[:, margin + rows : 2 * margin + rows, :], row_bufs.at[1]),
        ],
        send_sems.at[0:2],
        recv_sems.at[0:2],
    )
    own_band.wait()

    @pl.when(exists(me_r + 1, me_c, n_r, n_c))
    def _():
        band_ref[...] += row_bufs[0]

    @pl.when(exists(me_r - 1, me_c, n_r, n_c))
    def _():
        band_ref[...] += row_bufs[1]

    swap(
        place,
        [
            ((0, -1), band_ref.at[:, :, 0:margin], col_bufs.at[0]),
            ((0, 1), band_ref.at[:, :, margin + cols : 2 * margin + cols], col_bufs.at[1]),
        ],
        send_sems.at[2:4],
        recv_sems.at[2:4],
    )
    out_ref[...] = band_ref[:, :, margin : margin + cols]

    @pl.when(exists(me_r, me_c + 1, n_r, n_c))
    def _():
        out_ref[:, :, cols - margin : cols] += col_bufs[0]

    @pl.when(exists(me_r, me_c - 1, n_r, n_c))
    def _():
        out_ref[:, :, 0:margin] += col_bufs[1]


def exchange_halo(current, margin):
    depth, rows, cols = current.shape
    return pl.pallas_call(
        halo_kernel,
        out_shape=jax.ShapeDtypeStruct((depth, rows + 2 * margin, cols + 2 * margin), jnp.float32),
        in_specs=[VMEM_SPEC],
        out_specs=pl.BlockSpec(memory_space=pl.ANY),
        scratch_shapes=[
            pltpu.VMEM((depth, margin, cols + 2 * margin), jnp.float32),
            pltpu.SemaphoreType.DMA((4,)),
            pltpu.SemaphoreType.DMA((4,)),
            pltpu.SemaphoreType.DMA((5,)),
        ],
        compiler_params=pltpu.CompilerParams(
            vmem_limit_bytes=60 * 1024 * 1024, has_side_effects=True, collective_id=0
        ),
    )(current)


def exchange_fold(canvas, margin):
    depth, ext_rows, ext_cols = canvas.shape
    rows = ext_rows - 2 * margin
    cols = ext_cols - 2 * margin
    return pl.pallas_call(
        fold_kernel,
        out_shape=jax.ShapeDtypeStruct((depth, rows, cols), jnp.float32),
        in_specs=[pl.BlockSpec(memory_space=pl.ANY)],
        out_specs=VMEM_SPEC,
        scratch_shapes=[
            pltpu.VMEM((2, depth, margin, ext_cols), jnp.float32),
            pltpu.VMEM((2, depth, rows, margin), jnp.float32),
            pltpu.VMEM((depth, rows, ext_cols), jnp.float32),
            pltpu.SemaphoreType.DMA((4,)),
            pltpu.SemaphoreType.DMA((4,)),
            pltpu.SemaphoreType.DMA(()),
        ],
        compiler_params=pltpu.CompilerParams(
            vmem_limit_bytes=60 * 1024 * 1024, has_side_effects=True, collective_id=depth
        ),
    )(canvas)


def on_device(object_field, probe_field, amplitudes, centres, counts):
    size_probe = probe_field.shape[1]
    margin = size_probe // 2
    block_rows = object_field.shape[1]
    block_cols = object_field.shape[2]
    tables = dft_tables(size_probe)
    spots = centres[0, 0]
    own_amps = amplitudes[0, 0]
    sx_size = lax.axis_size("sx")
    sx_index = lax.axis_index("sx")
    column_counts = counts[:, 0]
    sx_positions = jnp.arange(sx_size, dtype=jnp.int32)
    own_count = jnp.sum(jnp.where(sx_positions == sx_index, column_counts, 0))
    ext_shape = (block_rows + size_probe, block_cols + size_probe)

    current = object_field
    for sweep_index in range(ITERS):
        extended = exchange_halo(current, margin)
        channels = 3 if sweep_index == 0 else 2
        canvas = gradient_canvas(
            channels, ext_shape, spots, own_count, extended, probe_field, own_amps, tables
        )
        folded = exchange_fold(canvas, margin)
        if sweep_index == 0:
            illumination = folded[2]
        current = current - folded[0:2] / (illumination + DAMPING)
    return current


def solution(mesh):
    return jax.shard_map(
        on_device,
        mesh=mesh,
        in_specs=(
            P(None, "sx", "sy"),
            P(),
            P("sx", "sy", None, None, None),
            P("sx", "sy", None, None),
            P(None, "sy"),
        ),
        out_specs=P(None, "sx", "sy"),
        check_vma=False,
    )
```

```python
import math

import jax
import jax.numpy as jnp
from jax import lax
from jax.sharding import PartitionSpec as P
from jax.experimental import pallas as pl
from jax.experimental.pallas import tpu as pltpu

ITERS = 2


SMOOTH = 1.0
DAMPING = 1.0


def with_halo(cells, sides, width):
    for axis, dim in sides:
        count = lax.axis_size(axis)
        ends = count - 1
        head = lax.slice_in_dim(cells, 0, width, axis=dim)
        tail = lax.slice_in_dim(cells, cells.shape[dim] - width, cells.shape[dim], axis=dim)
        cells = jnp.concatenate(
            [
                lax.ppermute(tail, axis, [(i, (i + 1) % count) for i in range(ends)]),
                cells,
                lax.ppermute(head, axis, [((i + 1) % count, i) for i in range(ends)]),
            ],
            axis=dim,
        )
    return cells


def dft_tables(length):
    index_values = jnp.arange(length, dtype=jnp.int32)
    product_mod = index_values[:, None] * index_values[None, :] % length
    angles = product_mod.astype(jnp.float32) * (2.0 * math.pi / length)
    scaling = 1.0 / math.sqrt(length)
    return (jnp.cos(angles) * scaling, -jnp.sin(angles) * scaling)


def matmul_exact(left_side, right_side):
    return jnp.dot(left_side, right_side, precision=lax.Precision.HIGHEST)


def complex_left(table_real, table_imag, field_real, field_imag):
    out_real = matmul_exact(table_real, field_real) - matmul_exact(table_imag, field_imag)
    out_imag = matmul_exact(table_real, field_imag) + matmul_exact(table_imag, field_real)
    return (out_real, out_imag)


def complex_right(field_real, field_imag, table_real, table_imag):
    out_real = matmul_exact(field_real, table_real) - matmul_exact(field_imag, table_imag)
    out_imag = matmul_exact(field_real, table_imag) + matmul_exact(field_imag, table_real)
    return (out_real, out_imag)


def position_gradient(object_patch, probe_field, amplitude, table_real, table_imag):
    probe_real = probe_field[0]
    probe_imag = probe_field[1]
    exit_real = probe_real * object_patch[0] - probe_imag * object_patch[1]
    exit_imag = probe_real * object_patch[1] + probe_imag * object_patch[0]
    half_real, half_imag = complex_left(table_real, table_imag, exit_real, exit_imag)
    far_real, far_imag = complex_right(half_real, half_imag, table_real, table_imag)
    factor = 1.0 - amplitude / jnp.sqrt(far_real * far_real + far_imag * far_imag + SMOOTH)
    miss_real = far_real * factor
    miss_imag = far_imag * factor
    back_real, back_imag = complex_left(table_real, -table_imag, miss_real, miss_imag)
    near_real, near_imag = complex_right(back_real, back_imag, table_real, -table_imag)
    return jnp.stack(
        [
            probe_real * near_real + probe_imag * near_imag,
            probe_real * near_imag - probe_imag * near_real,
        ]
    )


def add_patch(canvas, patch_values, corner_row, corner_col):
    zero_index = jnp.zeros((), jnp.int32)
    starts = (zero_index, corner_row, corner_col)
    present = lax.dynamic_slice(canvas, starts, patch_values.shape)
    return lax.dynamic_update_slice(canvas, present + patch_values, starts)


def fold_rows(extended, margin, length):
    middle_part = extended[:, 2 * margin : 2 * margin + length]
    upper_rim = extended[:, :margin]
    lower_rim = extended[:, extended.shape[1] - margin :]
    middle_part = middle_part.at[:, :margin].add(upper_rim)
    return middle_part.at[:, length - margin :].add(lower_rim)


def fold_cols(extended, margin, length):
    middle_part = extended[:, :, 2 * margin : 2 * margin + length]
    left_rim = extended[:, :, :margin]
    right_rim = extended[:, :, extended.shape[2] - margin :]
    middle_part = middle_part.at[:, :, :margin].add(left_rim)
    return middle_part.at[:, :, length - margin :].add(right_rim)


def settle(stacked, margin, block_rows, block_cols):
    full_ext = with_halo(stacked, (("sx", 1), ("sy", 2)), margin)
    return fold_cols(fold_rows(full_ext, margin, block_rows), margin, block_cols)


def local_pass(canvas, extended, spots, own_amps, probe_field, table_real, table_imag, upper_bound):
    size_probe = probe_field.shape[1]

    def local_step(slot_index, canvas_state):
        row_start = spots[slot_index, 0]
        col_start = spots[slot_index, 1]
        zero_index = jnp.zeros((), jnp.int32)
        object_patch = lax.dynamic_slice(
            extended, (zero_index, row_start, col_start), (2, size_probe, size_probe)
        )
        update = position_gradient(
            object_patch, probe_field, own_amps[slot_index], table_real, table_imag
        )
        return add_patch(canvas_state, update, row_start, col_start)

    return lax.fori_loop(0, upper_bound, local_step, canvas)


def dot_exact(left_side, right_side):
    return jnp.dot(
        left_side, right_side, precision=lax.Precision.HIGHEST, preferred_element_type=jnp.float32
    )


def window_tools(size, row, col):
    lanes = 128
    sublanes = 8
    wide = size + lanes
    tall = size + sublanes
    row_base = pl.multiple_of((row // sublanes) * sublanes, sublanes)
    col_base = pl.multiple_of((col // lanes) * lanes, lanes)
    row_shift = row % sublanes
    col_shift = col % lanes
    rows = pl.ds(row_base, tall)
    cols = pl.ds(col_base, wide)

    def take(ref, channel):
        block = ref[channel, rows, cols]
        block = pltpu.roll(block, (tall - row_shift) % tall, 0)
        return pltpu.roll(block, (wide - col_shift) % wide, 1)[:size, :size]

    def put(ref, channel, values):
        block = jnp.concatenate([values, jnp.zeros((size, lanes), jnp.float32)], axis=1)
        block = jnp.concatenate([block, jnp.zeros((sublanes, wide), jnp.float32)], axis=0)
        block = pltpu.roll(pltpu.roll(block, col_shift, 1), row_shift, 0)
        ref[channel, rows, cols] += block

    return take, put


def split_bf16(values):
    scaled = values * 65537.0
    high = scaled - (scaled - values)
    return high.astype(jnp.bfloat16), (values - high).astype(jnp.bfloat16)


def dot_split(left_parts, right_parts):
    left_high, left_low = left_parts
    right_high, right_low = right_parts
    total = jnp.dot(left_high, right_high, preferred_element_type=jnp.float32)
    total += jnp.dot(left_high, right_low, preferred_element_type=jnp.float32)
    return total + jnp.dot(left_low, right_high, preferred_element_type=jnp.float32)


def gradient_kernel(spots_ref, count_ref, ext_ref, probe_ref, amps_ref, tables_ref, out_ref):
    size = probe_ref.shape[1]
    out_ref[...] = jnp.zeros(out_ref.shape, jnp.float32)
    with_power = out_ref.shape[0] > 2
    for slot in range(amps_ref.shape[0]):

        @pl.when(slot < count_ref[0])
        def _():
            take, put = window_tools(size, spots_ref[slot, 0], spots_ref[slot, 1])
            probe_real = probe_ref[0]
            probe_imag = probe_ref[1]
            real_parts = (tables_ref[0], tables_ref[1])
            imag_parts = (tables_ref[2], tables_ref[3])

            def left(field_real, field_imag, sign):
                both = split_bf16(jnp.concatenate([field_real, field_imag], axis=1))
                by_real = dot_split(real_parts, both)
                by_imag = dot_split(imag_parts, both)
                out_real = by_real[:, :size] - sign * by_imag[:, size:]
                out_imag = by_real[:, size:] + sign * by_imag[:, :size]
                return out_real, out_imag

            def right(field_real, field_imag, sign):
                both = split_bf16(jnp.concatenate([field_real, field_imag], axis=0))
                by_real = dot_split(both, real_parts)
                by_imag = dot_split(both, imag_parts)
                out_real = by_real[:size] - sign * by_imag[size:]
                out_imag = by_imag[:size] * sign + by_real[size:]
                return out_real, out_imag

            obj_real = take(ext_ref, 0)
            obj_imag = take(ext_ref, 1)
            exit_real = probe_real * obj_real - probe_imag * obj_imag
            exit_imag = probe_real * obj_imag + probe_imag * obj_real
            half_real, half_imag = left(exit_real, exit_imag, 1.0)
            far_real, far_imag = right(half_real, half_imag, 1.0)
            factor = 1.0 - amps_ref[slot] / jnp.sqrt(far_real * far_real + far_imag * far_imag + SMOOTH)
            miss_real = far_real * factor
            miss_imag = far_imag * factor
            back_real, back_imag = left(miss_real, miss_imag, -1.0)
            near_real, near_imag = right(back_real, back_imag, -1.0)
            put(out_ref, 0, probe_real * near_real + probe_imag * near_imag)
            put(out_ref, 1, probe_real * near_imag - probe_imag * near_real)
            if with_power:
                put(out_ref, 2, probe_real * probe_real + probe_imag * probe_imag)


def power_kernel(spots_ref, count_ref, probe_ref, out_ref):
    size = probe_ref.shape[1]
    out_ref[...] = jnp.zeros(out_ref.shape, jnp.float32)
    power = probe_ref[0] * probe_ref[0] + probe_ref[1] * probe_ref[1]
    for slot in range(spots_ref.shape[0]):

        @pl.when(slot < count_ref[0])
        def _():
            _, put = window_tools(size, spots_ref[slot, 0], spots_ref[slot, 1])
            put(out_ref, 0, power)


VMEM_SPEC = pl.BlockSpec(memory_space=pltpu.VMEM)
SMEM_SPEC = pl.BlockSpec(memory_space=pltpu.SMEM)
KERNEL_PARAMS = pltpu.CompilerParams(vmem_limit_bytes=60 * 1024 * 1024)


def gradient_canvas(channels, ext_shape, spots, count, extended, probe_field, own_amps, tables):
    parts = jnp.stack(split_bf16(tables[0]) + split_bf16(tables[1]))
    return pl.pallas_call(
        gradient_kernel,
        out_shape=jax.ShapeDtypeStruct((channels,) + ext_shape, jnp.float32),
        in_specs=[SMEM_SPEC, SMEM_SPEC] + [VMEM_SPEC] * 4,
        out_specs=VMEM_SPEC,
        compiler_params=KERNEL_PARAMS,
    )(spots, count.reshape(1), extended, probe_field, own_amps, parts)


def power_canvas(ext_shape, spots, count, probe_field):
    return pl.pallas_call(
        power_kernel,
        out_shape=jax.ShapeDtypeStruct((1,) + ext_shape, jnp.float32),
        in_specs=[SMEM_SPEC, SMEM_SPEC, VMEM_SPEC],
        out_specs=VMEM_SPEC,
        compiler_params=KERNEL_PARAMS,
    )(spots, count.reshape(1), probe_field)


def mesh_place():
    return (
        lax.axis_index("sx"),
        lax.axis_index("sy"),
        lax.axis_size("sx"),
        lax.axis_size("sy"),
    )


def exists(row_dev, col_dev, row_count, col_count):
    return (row_dev >= 0) & (row_dev < row_count) & (col_dev >= 0) & (col_dev < col_count)


ROW_NEIGHBOURS = [(-1, 0), (1, 0)]
COL_NEIGHBOURS = [(0, -1), (0, 1)]


def neighbour_barrier(me_r, me_c, n_r, n_c):
    barrier = pltpu.get_barrier_semaphore()
    greeted = jnp.int32(0)
    for dr, dc in ROW_NEIGHBOURS + COL_NEIGHBOURS:
        present = exists(me_r + dr, me_c + dc, n_r, n_c)

        @pl.when(present)
        def _():
            pl.semaphore_signal(
                barrier, inc=1, device_id=(me_r + dr, me_c + dc), device_id_type=pl.DeviceIdType.MESH
            )

        greeted = greeted + present.astype(jnp.int32)
    pl.semaphore_wait(barrier, greeted)


def swap(place, pieces, send_sems, recv_sems):
    me_r, me_c, n_r, n_c = place
    copies = []
    for index, ((dr, dc), source, target) in enumerate(pieces):
        copy = pltpu.make_async_remote_copy(
            src_ref=source,
            dst_ref=target,
            send_sem=send_sems.at[index],
            recv_sem=recv_sems.at[index],
            device_id=(me_r + dr, me_c + dc),
            device_id_type=pl.DeviceIdType.MESH,
        )
        copies.append(copy)

        @pl.when(exists(me_r + dr, me_c + dc, n_r, n_c))
        def _():
            copy.start()

    for index, ((dr, dc), _, _) in enumerate(pieces):
        copy = copies[index]

        @pl.when(exists(me_r + dr, me_c + dc, n_r, n_c))
        def _():
            copy.wait_send()

        @pl.when(exists(me_r - dr, me_c - dc, n_r, n_c))
        def _():
            copy.wait_recv()


def halo_kernel(cur_ref, ext_ref, zeros_ref, send_sems, recv_sems, local_sems):
    rows = cur_ref.shape[1]
    cols = cur_ref.shape[2]
    margin = (ext_ref.shape[2] - cols) // 2
    ext_cols = cols + 2 * margin
    place = mesh_place()
    me_r, me_c, n_r, n_c = place
    middle = slice(margin, margin + rows)
    own = pltpu.make_async_copy(cur_ref, ext_ref.at[:, middle, margin : margin + cols], local_sems.at[0])
    own.start()
    zeros_ref[...] = jnp.zeros(zeros_ref.shape, jnp.float32)
    unreached = [
        ((0, 1), ext_ref.at[:, middle, 0:margin], zeros_ref.at[:, :, 0:margin]),
        ((0, -1), ext_ref.at[:, middle, margin + cols : ext_cols], zeros_ref.at[:, :, 0:margin]),
        ((1, 0), ext_ref.at[:, 0:margin, :], zeros_ref),
        ((-1, 0), ext_ref.at[:, margin + rows : 2 * margin + rows, :], zeros_ref),
    ]
    blanks = []
    for index, ((dr, dc), target, source) in enumerate(unreached):
        blank = pltpu.make_async_copy(source, target, local_sems.at[index + 1])
        missing = jnp.logical_not(exists(me_r - dr, me_c - dc, n_r, n_c))
        blanks.append((blank, missing))

    neighbour_barrier(me_r, me_c, n_r, n_c)
    for blank, missing in blanks:

        @pl.when(missing)
        def _():
            blank.start()

    swap(
        place,
        [
            ((0, -1), cur_ref.at[:, :, 0:margin], ext_ref.at[:, middle, margin + cols : ext_cols]),
            ((0, 1), cur_ref.at[:, :, cols - margin : cols], ext_ref.at[:, middle, 0:margin]),
        ],
        send_sems.at[0:2],
        recv_sems.at[0:2],
    )
    own.wait()
    for blank, missing in blanks:

        @pl.when(missing)
        def _():
            blank.wait()

    swap(
        place,
        [
            ((-1, 0), ext_ref.at[:, middle, :], ext_ref.at[:, margin + rows : 2 * margin + rows, :]),
            ((1, 0), ext_ref.at[:, middle, :], ext_ref.at[:, 0:margin, :]),
        ],
        send_sems.at[2:4],
        recv_sems.at[2:4],
    )


def fold_kernel(canvas_ref, cur_ref, light_in_ref, out_ref, light_ref, row_bufs, col_bufs, band_ref, total_ref, send_sems, recv_sems, band_sem):
    rows = out_ref.shape[1]
    cols = out_ref.shape[2]
    margin = (canvas_ref.shape[2] - cols) // 2
    place = mesh_place()
    me_r, me_c, n_r, n_c = place
    own_band = pltpu.make_async_copy(canvas_ref.at[:, margin : margin + rows, :], band_ref, band_sem)
    own_band.start()
    neighbour_barrier(me_r, me_c, n_r, n_c)
    swap(
        place,
        [
            ((-1, 0), canvas_ref.at[:, 0:margin, :], row_bufs.at[0]),
            ((1, 0), canvas_ref.at[:, margin + rows : 2 * margin + rows, :], row_bufs.at[1]),
        ],
        send_sems.at[0:2],
        recv_sems.at[0:2],
    )
    own_band.wait()

    @pl.when(exists(me_r + 1, me_c, n_r, n_c))
    def _():
        band_ref[...] += row_bufs[0]

    @pl.when(exists(me_r - 1, me_c, n_r, n_c))
    def _():
        band_ref[...] += row_bufs[1]

    swap(
        place,
        [
            ((0, -1), band_ref.at[:, :, 0:margin], col_bufs.at[0]),
            ((0, 1), band_ref.at[:, :, margin + cols : 2 * margin + cols], col_bufs.at[1]),
        ],
        send_sems.at[2:4],
        recv_sems.at[2:4],
    )
    total_ref[...] = band_ref[:, :, margin : margin + cols]

    @pl.when(exists(me_r, me_c + 1, n_r, n_c))
    def _():
        total_ref[:, :, cols - margin : cols] += col_bufs[0]

    @pl.when(exists(me_r, me_c - 1, n_r, n_c))
    def _():
        total_ref[:, :, 0:margin] += col_bufs[1]

    fields = cur_ref.shape[0]
    if total_ref.shape[0] > fields:
        light_ref[...] = total_ref[fields]
    else:
        light_ref[...] = light_in_ref[...]
    out_ref[...] = cur_ref[...] - total_ref[0:fields] / (light_ref[...] + DAMPING)


def exchange_halo(current, margin):
    depth, rows, cols = current.shape
    return pl.pallas_call(
        halo_kernel,
        out_shape=jax.ShapeDtypeStruct((depth, rows + 2 * margin, cols + 2 * margin), jnp.float32),
        in_specs=[VMEM_SPEC],
        out_specs=pl.BlockSpec(memory_space=pl.ANY),
        scratch_shapes=[
            pltpu.VMEM((depth, margin, cols + 2 * margin), jnp.float32),
            pltpu.SemaphoreType.DMA((4,)),
            pltpu.SemaphoreType.DMA((4,)),
            pltpu.SemaphoreType.DMA((5,)),
        ],
        compiler_params=pltpu.CompilerParams(
            vmem_limit_bytes=60 * 1024 * 1024, has_side_effects=True, collective_id=0
        ),
    )(current)


def fold_and_step(canvas, current, light, margin):
    depth, ext_rows, ext_cols = canvas.shape
    fields, rows, cols = current.shape
    return pl.pallas_call(
        fold_kernel,
        out_shape=(
            jax.ShapeDtypeStruct((fields, rows, cols), jnp.float32),
            jax.ShapeDtypeStruct((rows, cols), jnp.float32),
        ),
        in_specs=[pl.BlockSpec(memory_space=pl.ANY), VMEM_SPEC, VMEM_SPEC],
        out_specs=(VMEM_SPEC, VMEM_SPEC),
        scratch_shapes=[
            pltpu.VMEM((2, depth, margin, ext_cols), jnp.float32),
            pltpu.VMEM((2, depth, rows, margin), jnp.float32),
            pltpu.VMEM((depth, rows, ext_cols), jnp.float32),
            pltpu.VMEM((depth, rows, cols), jnp.float32),
            pltpu.SemaphoreType.DMA((4,)),
            pltpu.SemaphoreType.DMA((4,)),
            pltpu.SemaphoreType.DMA(()),
        ],
        compiler_params=pltpu.CompilerParams(
            vmem_limit_bytes=60 * 1024 * 1024, has_side_effects=True, collective_id=depth
        ),
    )(canvas, current, light)


def on_device(object_field, probe_field, amplitudes, centres, counts):
    size_probe = probe_field.shape[1]
    margin = size_probe // 2
    block_rows = object_field.shape[1]
    block_cols = object_field.shape[2]
    tables = dft_tables(size_probe)
    spots = centres[0, 0]
    own_amps = amplitudes[0, 0]
    sx_size = lax.axis_size("sx")
    sx_index = lax.axis_index("sx")
    column_counts = counts[:, 0]
    sx_positions = jnp.arange(sx_size, dtype=jnp.int32)
    own_count = jnp.sum(jnp.where(sx_positions == sx_index, column_counts, 0))
    ext_shape = (block_rows + size_probe, block_cols + size_probe)

    current = object_field
    illumination = jnp.zeros((block_rows, block_cols), jnp.float32)
    for sweep_index in range(ITERS):
        extended = exchange_halo(current, margin)
        channels = 3 if sweep_index == 0 else 2
        canvas = gradient_canvas(
            channels, ext_shape, spots, own_count, extended, probe_field, own_amps, tables
        )
        current, illumination = fold_and_step(canvas, current, illumination, margin)
    return current


def solution(mesh):
    return jax.shard_map(
        on_device,
        mesh=mesh,
        in_specs=(
            P(None, "sx", "sy"),
            P(),
            P("sx", "sy", None, None, None),
            P("sx", "sy", None, None),
            P(None, "sy"),
        ),
        out_specs=P(None, "sx", "sy"),
        check_vma=False,
    )
```

```python
import math

import jax
import jax.numpy as jnp
from jax import lax
from jax.sharding import PartitionSpec as P
from jax.experimental import pallas as pl
from jax.experimental.pallas import tpu as pltpu

ITERS = 2


SMOOTH = 1.0
DAMPING = 1.0


def with_halo(cells, sides, width):
    for axis, dim in sides:
        count = lax.axis_size(axis)
        ends = count - 1
        head = lax.slice_in_dim(cells, 0, width, axis=dim)
        tail = lax.slice_in_dim(cells, cells.shape[dim] - width, cells.shape[dim], axis=dim)
        cells = jnp.concatenate(
            [
                lax.ppermute(tail, axis, [(i, (i + 1) % count) for i in range(ends)]),
                cells,
                lax.ppermute(head, axis, [((i + 1) % count, i) for i in range(ends)]),
            ],
            axis=dim,
        )
    return cells


def dft_tables(length):
    index_values = jnp.arange(length, dtype=jnp.int32)
    product_mod = index_values[:, None] * index_values[None, :] % length
    angles = product_mod.astype(jnp.float32) * (2.0 * math.pi / length)
    scaling = 1.0 / math.sqrt(length)
    return (jnp.cos(angles) * scaling, -jnp.sin(angles) * scaling)


def matmul_exact(left_side, right_side):
    return jnp.dot(left_side, right_side, precision=lax.Precision.HIGHEST)


def complex_left(table_real, table_imag, field_real, field_imag):
    out_real = matmul_exact(table_real, field_real) - matmul_exact(table_imag, field_imag)
    out_imag = matmul_exact(table_real, field_imag) + matmul_exact(table_imag, field_real)
    return (out_real, out_imag)


def complex_right(field_real, field_imag, table_real, table_imag):
    out_real = matmul_exact(field_real, table_real) - matmul_exact(field_imag, table_imag)
    out_imag = matmul_exact(field_real, table_imag) + matmul_exact(field_imag, table_real)
    return (out_real, out_imag)


def position_gradient(object_patch, probe_field, amplitude, table_real, table_imag):
    probe_real = probe_field[0]
    probe_imag = probe_field[1]
    exit_real = probe_real * object_patch[0] - probe_imag * object_patch[1]
    exit_imag = probe_real * object_patch[1] + probe_imag * object_patch[0]
    half_real, half_imag = complex_left(table_real, table_imag, exit_real, exit_imag)
    far_real, far_imag = complex_right(half_real, half_imag, table_real, table_imag)
    factor = 1.0 - amplitude / jnp.sqrt(far_real * far_real + far_imag * far_imag + SMOOTH)
    miss_real = far_real * factor
    miss_imag = far_imag * factor
    back_real, back_imag = complex_left(table_real, -table_imag, miss_real, miss_imag)
    near_real, near_imag = complex_right(back_real, back_imag, table_real, -table_imag)
    return jnp.stack(
        [
            probe_real * near_real + probe_imag * near_imag,
            probe_real * near_imag - probe_imag * near_real,
        ]
    )


def add_patch(canvas, patch_values, corner_row, corner_col):
    zero_index = jnp.zeros((), jnp.int32)
    starts = (zero_index, corner_row, corner_col)
    present = lax.dynamic_slice(canvas, starts, patch_values.shape)
    return lax.dynamic_update_slice(canvas, present + patch_values, starts)


def fold_rows(extended, margin, length):
    middle_part = extended[:, 2 * margin : 2 * margin + length]
    upper_rim = extended[:, :margin]
    lower_rim = extended[:, extended.shape[1] - margin :]
    middle_part = middle_part.at[:, :margin].add(upper_rim)
    return middle_part.at[:, length - margin :].add(lower_rim)


def fold_cols(extended, margin, length):
    middle_part = extended[:, :, 2 * margin : 2 * margin + length]
    left_rim = extended[:, :, :margin]
    right_rim = extended[:, :, extended.shape[2] - margin :]
    middle_part = middle_part.at[:, :, :margin].add(left_rim)
    return middle_part.at[:, :, length - margin :].add(right_rim)


def settle(stacked, margin, block_rows, block_cols):
    full_ext = with_halo(stacked, (("sx", 1), ("sy", 2)), margin)
    return fold_cols(fold_rows(full_ext, margin, block_rows), margin, block_cols)


def local_pass(canvas, extended, spots, own_amps, probe_field, table_real, table_imag, upper_bound):
    size_probe = probe_field.shape[1]

    def local_step(slot_index, canvas_state):
        row_start = spots[slot_index, 0]
        col_start = spots[slot_index, 1]
        zero_index = jnp.zeros((), jnp.int32)
        object_patch = lax.dynamic_slice(
            extended, (zero_index, row_start, col_start), (2, size_probe, size_probe)
        )
        update = position_gradient(
            object_patch, probe_field, own_amps[slot_index], table_real, table_imag
        )
        return add_patch(canvas_state, update, row_start, col_start)

    return lax.fori_loop(0, upper_bound, local_step, canvas)


def dot_exact(left_side, right_side):
    return jnp.dot(
        left_side, right_side, precision=lax.Precision.HIGHEST, preferred_element_type=jnp.float32
    )


def window_tools(size, row, col):
    lanes = 128
    sublanes = 8
    wide = size + lanes
    tall = size + sublanes
    row_base = pl.multiple_of((row // sublanes) * sublanes, sublanes)
    col_base = pl.multiple_of((col // lanes) * lanes, lanes)
    row_shift = row % sublanes
    col_shift = col % lanes
    rows = pl.ds(row_base, tall)
    cols = pl.ds(col_base, wide)

    def take(ref, channel):
        block = ref[channel, rows, cols]
        block = pltpu.roll(block, (tall - row_shift) % tall, 0)
        return pltpu.roll(block, (wide - col_shift) % wide, 1)[:size, :size]

    def put(ref, channel, values):
        block = jnp.concatenate([values, jnp.zeros((size, lanes), jnp.float32)], axis=1)
        block = jnp.concatenate([block, jnp.zeros((sublanes, wide), jnp.float32)], axis=0)
        block = pltpu.roll(pltpu.roll(block, col_shift, 1), row_shift, 0)
        ref[channel, rows, cols] += block

    return take, put


def split_bf16(values):
    scaled = values * 65537.0
    high = scaled - (scaled - values)
    return high.astype(jnp.bfloat16), (values - high).astype(jnp.bfloat16)


def dot_split(left_parts, right_parts):
    left_high, left_low = left_parts
    right_high, right_low = right_parts
    total = jnp.dot(left_high, right_high, preferred_element_type=jnp.float32)
    total += jnp.dot(left_high, right_low, preferred_element_type=jnp.float32)
    return total + jnp.dot(left_low, right_high, preferred_element_type=jnp.float32)


def gradient_kernel(spots_ref, count_ref, ext_ref, probe_ref, amps_ref, tables_ref, out_ref):
    size = probe_ref.shape[1]
    out_ref[...] = jnp.zeros(out_ref.shape, jnp.float32)
    with_power = out_ref.shape[0] > 2
    for slot in range(amps_ref.shape[0]):

        @pl.when(slot < count_ref[0])
        def _():
            take, put = window_tools(size, spots_ref[slot, 0], spots_ref[slot, 1])
            probe_real = probe_ref[0]
            probe_imag = probe_ref[1]
            real_parts = (tables_ref[0], tables_ref[1])
            imag_parts = (tables_ref[2], tables_ref[3])

            def left(field_real, field_imag, sign):
                both = split_bf16(jnp.concatenate([field_real, field_imag], axis=1))
                by_real = dot_split(real_parts, both)
                by_imag = dot_split(imag_parts, both)
                out_real = by_real[:, :size] - sign * by_imag[:, size:]
                out_imag = by_real[:, size:] + sign * by_imag[:, :size]
                return out_real, out_imag

            def right(field_real, field_imag, sign):
                both = split_bf16(jnp.concatenate([field_real, field_imag], axis=0))
                by_real = dot_split(both, real_parts)
                by_imag = dot_split(both, imag_parts)
                out_real = by_real[:size] - sign * by_imag[size:]
                out_imag = by_imag[:size] * sign + by_real[size:]
                return out_real, out_imag

            obj_real = take(ext_ref, 0)
            obj_imag = take(ext_ref, 1)
            exit_real = probe_real * obj_real - probe_imag * obj_imag
            exit_imag = probe_real * obj_imag + probe_imag * obj_real
            half_real, half_imag = left(exit_real, exit_imag, 1.0)
            far_real, far_imag = right(half_real, half_imag, 1.0)
            factor = 1.0 - amps_ref[slot] / jnp.sqrt(far_real * far_real + far_imag * far_imag + SMOOTH)
            miss_real = far_real * factor
            miss_imag = far_imag * factor
            back_real, back_imag = left(miss_real, miss_imag, -1.0)
            near_real, near_imag = right(back_real, back_imag, -1.0)
            put(out_ref, 0, probe_real * near_real + probe_imag * near_imag)
            put(out_ref, 1, probe_real * near_imag - probe_imag * near_real)
            if with_power:
                put(out_ref, 2, probe_real * probe_real + probe_imag * probe_imag)


def power_kernel(spots_ref, count_ref, probe_ref, out_ref):
    size = probe_ref.shape[1]
    out_ref[...] = jnp.zeros(out_ref.shape, jnp.float32)
    power = probe_ref[0] * probe_ref[0] + probe_ref[1] * probe_ref[1]
    for slot in range(spots_ref.shape[0]):

        @pl.when(slot < count_ref[0])
        def _():
            _, put = window_tools(size, spots_ref[slot, 0], spots_ref[slot, 1])
            put(out_ref, 0, power)


VMEM_SPEC = pl.BlockSpec(memory_space=pltpu.VMEM)
SMEM_SPEC = pl.BlockSpec(memory_space=pltpu.SMEM)
KERNEL_PARAMS = pltpu.CompilerParams(vmem_limit_bytes=60 * 1024 * 1024)


def gradient_canvas(channels, ext_shape, spots, count, extended, probe_field, own_amps, tables):
    parts = jnp.stack(split_bf16(tables[0]) + split_bf16(tables[1]))
    return pl.pallas_call(
        gradient_kernel,
        out_shape=jax.ShapeDtypeStruct((channels,) + ext_shape, jnp.float32),
        in_specs=[SMEM_SPEC, SMEM_SPEC] + [VMEM_SPEC] * 4,
        out_specs=VMEM_SPEC,
        compiler_params=KERNEL_PARAMS,
    )(spots, count.reshape(1), extended, probe_field, own_amps, parts)


def power_canvas(ext_shape, spots, count, probe_field):
    return pl.pallas_call(
        power_kernel,
        out_shape=jax.ShapeDtypeStruct((1,) + ext_shape, jnp.float32),
        in_specs=[SMEM_SPEC, SMEM_SPEC, VMEM_SPEC],
        out_specs=VMEM_SPEC,
        compiler_params=KERNEL_PARAMS,
    )(spots, count.reshape(1), probe_field)


def mesh_place():
    return (
        lax.axis_index("sx"),
        lax.axis_index("sy"),
        lax.axis_size("sx"),
        lax.axis_size("sy"),
    )


def exists(row_dev, col_dev, row_count, col_count):
    return (row_dev >= 0) & (row_dev < row_count) & (col_dev >= 0) & (col_dev < col_count)


ROW_NEIGHBOURS = [(-1, 0), (1, 0)]
COL_NEIGHBOURS = [(0, -1), (0, 1)]


def neighbour_barrier(me_r, me_c, n_r, n_c):
    barrier = pltpu.get_barrier_semaphore()
    greeted = jnp.int32(0)
    for dr, dc in ROW_NEIGHBOURS + COL_NEIGHBOURS:
        present = exists(me_r + dr, me_c + dc, n_r, n_c)

        @pl.when(present)
        def _():
            pl.semaphore_signal(
                barrier, inc=1, device_id=(me_r + dr, me_c + dc), device_id_type=pl.DeviceIdType.MESH
            )

        greeted = greeted + present.astype(jnp.int32)
    pl.semaphore_wait(barrier, greeted)


def start_copies(place, pieces, send_sems, recv_sems):
    me_r, me_c, n_r, n_c = place
    copies = []
    for index, ((dr, dc), source, target) in enumerate(pieces):
        copy = pltpu.make_async_remote_copy(
            src_ref=source,
            dst_ref=target,
            send_sem=send_sems.at[index],
            recv_sem=recv_sems.at[index],
            device_id=(me_r + dr, me_c + dc),
            device_id_type=pl.DeviceIdType.MESH,
        )
        copies.append(((dr, dc), copy))

        @pl.when(exists(me_r + dr, me_c + dc, n_r, n_c))
        def _():
            copy.start()

    return copies


def wait_copies(place, copies):
    me_r, me_c, n_r, n_c = place
    for (dr, dc), copy in copies:

        @pl.when(exists(me_r + dr, me_c + dc, n_r, n_c))
        def _():
            copy.wait_send()

        @pl.when(exists(me_r - dr, me_c - dc, n_r, n_c))
        def _():
            copy.wait_recv()


def swap(place, pieces, send_sems, recv_sems):
    wait_copies(place, start_copies(place, pieces, send_sems, recv_sems))


def halo_kernel(cur_ref, ext_ref, zeros_ref, send_sems, recv_sems, local_sems):
    rows = cur_ref.shape[1]
    cols = cur_ref.shape[2]
    margin = (ext_ref.shape[2] - cols) // 2
    ext_cols = cols + 2 * margin
    place = mesh_place()
    me_r, me_c, n_r, n_c = place
    middle = slice(margin, margin + rows)
    own = pltpu.make_async_copy(cur_ref, ext_ref.at[:, middle, margin : margin + cols], local_sems.at[0])
    own.start()
    zeros_ref[...] = jnp.zeros(zeros_ref.shape, jnp.float32)
    unreached = [
        ((0, 1), ext_ref.at[:, middle, 0:margin], zeros_ref.at[:, :, 0:margin]),
        ((0, -1), ext_ref.at[:, middle, margin + cols : ext_cols], zeros_ref.at[:, :, 0:margin]),
        ((1, 0), ext_ref.at[:, 0:margin, :], zeros_ref),
        ((-1, 0), ext_ref.at[:, margin + rows : 2 * margin + rows, :], zeros_ref),
    ]
    blanks = []
    for index, ((dr, dc), target, source) in enumerate(unreached):
        blank = pltpu.make_async_copy(source, target, local_sems.at[index + 1])
        missing = jnp.logical_not(exists(me_r - dr, me_c - dc, n_r, n_c))
        blanks.append((blank, missing))

    neighbour_barrier(me_r, me_c, n_r, n_c)
    for blank, missing in blanks:

        @pl.when(missing)
        def _():
            blank.start()

    above = slice(0, margin)
    below = slice(margin + rows, 2 * margin + rows)
    inner = slice(margin, margin + cols)
    left = slice(0, margin)
    right = slice(margin + cols, ext_cols)
    bands = start_copies(
        place,
        [
            ((-1, 0), cur_ref, ext_ref.at[:, below, inner]),
            ((1, 0), cur_ref, ext_ref.at[:, above, inner]),
        ],
        send_sems.at[0:2],
        recv_sems.at[0:2],
    )
    swap(
        place,
        [
            ((0, -1), cur_ref.at[:, :, 0:margin], ext_ref.at[:, middle, right]),
            ((0, 1), cur_ref.at[:, :, cols - margin : cols], ext_ref.at[:, middle, left]),
        ],
        send_sems.at[2:4],
        recv_sems.at[2:4],
    )
    own.wait()
    for blank, missing in blanks:

        @pl.when(missing)
        def _():
            blank.wait()

    corners = start_copies(
        place,
        [
            ((-1, 0), ext_ref.at[:, middle, left], ext_ref.at[:, below, left]),
            ((-1, 0), ext_ref.at[:, middle, right], ext_ref.at[:, below, right]),
            ((1, 0), ext_ref.at[:, middle, left], ext_ref.at[:, above, left]),
            ((1, 0), ext_ref.at[:, middle, right], ext_ref.at[:, above, right]),
        ],
        send_sems.at[4:8],
        recv_sems.at[4:8],
    )
    wait_copies(place, bands)
    wait_copies(place, corners)


def fold_kernel(canvas_ref, cur_ref, light_in_ref, out_ref, light_ref, row_bufs, col_bufs, band_ref, total_ref, send_sems, recv_sems, band_sem):
    rows = out_ref.shape[1]
    cols = out_ref.shape[2]
    margin = (canvas_ref.shape[2] - cols) // 2
    place = mesh_place()
    me_r, me_c, n_r, n_c = place
    own_band = pltpu.make_async_copy(canvas_ref.at[:, margin : margin + rows, :], band_ref, band_sem)
    own_band.start()
    neighbour_barrier(me_r, me_c, n_r, n_c)
    swap(
        place,
        [
            ((-1, 0), canvas_ref.at[:, 0:margin, :], row_bufs.at[0]),
            ((1, 0), canvas_ref.at[:, margin + rows : 2 * margin + rows, :], row_bufs.at[1]),
        ],
        send_sems.at[0:2],
        recv_sems.at[0:2],
    )
    own_band.wait()

    @pl.when(exists(me_r + 1, me_c, n_r, n_c))
    def _():
        band_ref[...] += row_bufs[0]

    @pl.when(exists(me_r - 1, me_c, n_r, n_c))
    def _():
        band_ref[...] += row_bufs[1]

    swap(
        place,
        [
            ((0, -1), band_ref.at[:, :, 0:margin], col_bufs.at[0]),
            ((0, 1), band_ref.at[:, :, margin + cols : 2 * margin + cols], col_bufs.at[1]),
        ],
        send_sems.at[2:4],
        recv_sems.at[2:4],
    )
    total_ref[...] = band_ref[:, :, margin : margin + cols]

    @pl.when(exists(me_r, me_c + 1, n_r, n_c))
    def _():
        total_ref[:, :, cols - margin : cols] += col_bufs[0]

    @pl.when(exists(me_r, me_c - 1, n_r, n_c))
    def _():
        total_ref[:, :, 0:margin] += col_bufs[1]

    fields = cur_ref.shape[0]
    if total_ref.shape[0] > fields:
        light_ref[...] = total_ref[fields]
    else:
        light_ref[...] = light_in_ref[...]
    out_ref[...] = cur_ref[...] - total_ref[0:fields] / (light_ref[...] + DAMPING)


def exchange_halo(current, margin):
    depth, rows, cols = current.shape
    return pl.pallas_call(
        halo_kernel,
        out_shape=jax.ShapeDtypeStruct((depth, rows + 2 * margin, cols + 2 * margin), jnp.float32),
        in_specs=[VMEM_SPEC],
        out_specs=pl.BlockSpec(memory_space=pl.ANY),
        scratch_shapes=[
            pltpu.VMEM((depth, margin, cols + 2 * margin), jnp.float32),
            pltpu.SemaphoreType.DMA((8,)),
            pltpu.SemaphoreType.DMA((8,)),
            pltpu.SemaphoreType.DMA((5,)),
        ],
        compiler_params=pltpu.CompilerParams(
            vmem_limit_bytes=60 * 1024 * 1024, has_side_effects=True, collective_id=0
        ),
    )(current)


def fold_and_step(canvas, current, light, margin):
    depth, ext_rows, ext_cols = canvas.shape
    fields, rows, cols = current.shape
    return pl.pallas_call(
        fold_kernel,
        out_shape=(
            jax.ShapeDtypeStruct((fields, rows, cols), jnp.float32),
            jax.ShapeDtypeStruct((rows, cols), jnp.float32),
        ),
        in_specs=[pl.BlockSpec(memory_space=pl.ANY), VMEM_SPEC, VMEM_SPEC],
        out_specs=(VMEM_SPEC, VMEM_SPEC),
        scratch_shapes=[
            pltpu.VMEM((2, depth, margin, ext_cols), jnp.float32),
            pltpu.VMEM((2, depth, rows, margin), jnp.float32),
            pltpu.VMEM((depth, rows, ext_cols), jnp.float32),
            pltpu.VMEM((depth, rows, cols), jnp.float32),
            pltpu.SemaphoreType.DMA((4,)),
            pltpu.SemaphoreType.DMA((4,)),
            pltpu.SemaphoreType.DMA(()),
        ],
        compiler_params=pltpu.CompilerParams(
            vmem_limit_bytes=60 * 1024 * 1024, has_side_effects=True, collective_id=depth
        ),
    )(canvas, current, light)


def on_device(object_field, probe_field, amplitudes, centres, counts):
    size_probe = probe_field.shape[1]
    margin = size_probe // 2
    block_rows = object_field.shape[1]
    block_cols = object_field.shape[2]
    tables = dft_tables(size_probe)
    spots = centres[0, 0]
    own_amps = amplitudes[0, 0]
    sx_size = lax.axis_size("sx")
    sx_index = lax.axis_index("sx")
    column_counts = counts[:, 0]
    sx_positions = jnp.arange(sx_size, dtype=jnp.int32)
    own_count = jnp.sum(jnp.where(sx_positions == sx_index, column_counts, 0))
    ext_shape = (block_rows + size_probe, block_cols + size_probe)

    current = object_field
    illumination = jnp.zeros((block_rows, block_cols), jnp.float32)
    for sweep_index in range(ITERS):
        extended = exchange_halo(current, margin)
        channels = 3 if sweep_index == 0 else 2
        canvas = gradient_canvas(
            channels, ext_shape, spots, own_count, extended, probe_field, own_amps, tables
        )
        current, illumination = fold_and_step(canvas, current, illumination, margin)
    return current


def solution(mesh):
    return jax.shard_map(
        on_device,
        mesh=mesh,
        in_specs=(
            P(None, "sx", "sy"),
            P(),
            P("sx", "sy", None, None, None),
            P("sx", "sy", None, None),
            P(None, "sy"),
        ),
        out_specs=P(None, "sx", "sy"),
        check_vma=False,
    )
```

```python
import math

import jax
import jax.numpy as jnp
from jax import lax
from jax.sharding import PartitionSpec as P
from jax.experimental import pallas as pl
from jax.experimental.pallas import tpu as pltpu

ITERS = 2


SMOOTH = 1.0
DAMPING = 1.0


def with_halo(cells, sides, width):
    for axis, dim in sides:
        count = lax.axis_size(axis)
        ends = count - 1
        head = lax.slice_in_dim(cells, 0, width, axis=dim)
        tail = lax.slice_in_dim(cells, cells.shape[dim] - width, cells.shape[dim], axis=dim)
        cells = jnp.concatenate(
            [
                lax.ppermute(tail, axis, [(i, (i + 1) % count) for i in range(ends)]),
                cells,
                lax.ppermute(head, axis, [((i + 1) % count, i) for i in range(ends)]),
            ],
            axis=dim,
        )
    return cells


def dft_tables(length):
    index_values = jnp.arange(length, dtype=jnp.int32)
    product_mod = index_values[:, None] * index_values[None, :] % length
    angles = product_mod.astype(jnp.float32) * (2.0 * math.pi / length)
    scaling = 1.0 / math.sqrt(length)
    return (jnp.cos(angles) * scaling, -jnp.sin(angles) * scaling)


def matmul_exact(left_side, right_side):
    return jnp.dot(left_side, right_side, precision=lax.Precision.HIGHEST)


def complex_left(table_real, table_imag, field_real, field_imag):
    out_real = matmul_exact(table_real, field_real) - matmul_exact(table_imag, field_imag)
    out_imag = matmul_exact(table_real, field_imag) + matmul_exact(table_imag, field_real)
    return (out_real, out_imag)


def complex_right(field_real, field_imag, table_real, table_imag):
    out_real = matmul_exact(field_real, table_real) - matmul_exact(field_imag, table_imag)
    out_imag = matmul_exact(field_real, table_imag) + matmul_exact(field_imag, table_real)
    return (out_real, out_imag)


def position_gradient(object_patch, probe_field, amplitude, table_real, table_imag):
    probe_real = probe_field[0]
    probe_imag = probe_field[1]
    exit_real = probe_real * object_patch[0] - probe_imag * object_patch[1]
    exit_imag = probe_real * object_patch[1] + probe_imag * object_patch[0]
    half_real, half_imag = complex_left(table_real, table_imag, exit_real, exit_imag)
    far_real, far_imag = complex_right(half_real, half_imag, table_real, table_imag)
    factor = 1.0 - amplitude / jnp.sqrt(far_real * far_real + far_imag * far_imag + SMOOTH)
    miss_real = far_real * factor
    miss_imag = far_imag * factor
    back_real, back_imag = complex_left(table_real, -table_imag, miss_real, miss_imag)
    near_real, near_imag = complex_right(back_real, back_imag, table_real, -table_imag)
    return jnp.stack(
        [
            probe_real * near_real + probe_imag * near_imag,
            probe_real * near_imag - probe_imag * near_real,
        ]
    )


def add_patch(canvas, patch_values, corner_row, corner_col):
    zero_index = jnp.zeros((), jnp.int32)
    starts = (zero_index, corner_row, corner_col)
    present = lax.dynamic_slice(canvas, starts, patch_values.shape)
    return lax.dynamic_update_slice(canvas, present + patch_values, starts)


def fold_rows(extended, margin, length):
    middle_part = extended[:, 2 * margin : 2 * margin + length]
    upper_rim = extended[:, :margin]
    lower_rim = extended[:, extended.shape[1] - margin :]
    middle_part = middle_part.at[:, :margin].add(upper_rim)
    return middle_part.at[:, length - margin :].add(lower_rim)


def fold_cols(extended, margin, length):
    middle_part = extended[:, :, 2 * margin : 2 * margin + length]
    left_rim = extended[:, :, :margin]
    right_rim = extended[:, :, extended.shape[2] - margin :]
    middle_part = middle_part.at[:, :, :margin].add(left_rim)
    return middle_part.at[:, :, length - margin :].add(right_rim)


def settle(stacked, margin, block_rows, block_cols):
    full_ext = with_halo(stacked, (("sx", 1), ("sy", 2)), margin)
    return fold_cols(fold_rows(full_ext, margin, block_rows), margin, block_cols)


def local_pass(canvas, extended, spots, own_amps, probe_field, table_real, table_imag, upper_bound):
    size_probe = probe_field.shape[1]

    def local_step(slot_index, canvas_state):
        row_start = spots[slot_index, 0]
        col_start = spots[slot_index, 1]
        zero_index = jnp.zeros((), jnp.int32)
        object_patch = lax.dynamic_slice(
            extended, (zero_index, row_start, col_start), (2, size_probe, size_probe)
        )
        update = position_gradient(
            object_patch, probe_field, own_amps[slot_index], table_real, table_imag
        )
        return add_patch(canvas_state, update, row_start, col_start)

    return lax.fori_loop(0, upper_bound, local_step, canvas)


def dot_exact(left_side, right_side):
    return jnp.dot(
        left_side, right_side, precision=lax.Precision.HIGHEST, preferred_element_type=jnp.float32
    )


def window_tools(size, row, col):
    lanes = 128
    sublanes = 8
    wide = size + lanes
    tall = size + sublanes
    row_base = pl.multiple_of((row // sublanes) * sublanes, sublanes)
    col_base = pl.multiple_of((col // lanes) * lanes, lanes)
    row_shift = row % sublanes
    col_shift = col % lanes
    rows = pl.ds(row_base, tall)
    cols = pl.ds(col_base, wide)

    def take(ref, channel):
        block = ref[channel, rows, cols]
        block = pltpu.roll(block, (tall - row_shift) % tall, 0)
        return pltpu.roll(block, (wide - col_shift) % wide, 1)[:size, :size]

    def put(ref, channel, values):
        block = jnp.concatenate([values, jnp.zeros((size, lanes), jnp.float32)], axis=1)
        block = jnp.concatenate([block, jnp.zeros((sublanes, wide), jnp.float32)], axis=0)
        block = pltpu.roll(pltpu.roll(block, col_shift, 1), row_shift, 0)
        ref[channel, rows, cols] += block

    return take, put


def split_bf16(values):
    scaled = values * 65537.0
    high = scaled - (scaled - values)
    return high.astype(jnp.bfloat16), (values - high).astype(jnp.bfloat16)


def dot_split(left_parts, right_parts):
    left_high, left_low = left_parts
    right_high, right_low = right_parts
    total = jnp.dot(left_high, right_high, preferred_element_type=jnp.float32)
    total += jnp.dot(left_high, right_low, preferred_element_type=jnp.float32)
    return total + jnp.dot(left_low, right_high, preferred_element_type=jnp.float32)


def gradient_kernel(spots_ref, count_ref, ext_ref, probe_ref, amps_ref, tables_ref, out_ref):
    size = probe_ref.shape[1]
    out_ref[...] = jnp.zeros(out_ref.shape, jnp.float32)
    with_power = out_ref.shape[0] > 2
    for slot in range(amps_ref.shape[0]):

        @pl.when(slot < count_ref[0])
        def _():
            take, put = window_tools(size, spots_ref[slot, 0], spots_ref[slot, 1])
            probe_real = probe_ref[0]
            probe_imag = probe_ref[1]
            real_parts = (tables_ref[0], tables_ref[1])
            imag_parts = (tables_ref[2], tables_ref[3])

            def left(field_real, field_imag, sign):
                both = split_bf16(jnp.concatenate([field_real, field_imag], axis=1))
                by_real = dot_split(real_parts, both)
                by_imag = dot_split(imag_parts, both)
                out_real = by_real[:, :size] - sign * by_imag[:, size:]
                out_imag = by_real[:, size:] + sign * by_imag[:, :size]
                return out_real, out_imag

            def right(field_real, field_imag, sign):
                both = split_bf16(jnp.concatenate([field_real, field_imag], axis=0))
                by_real = dot_split(both, real_parts)
                by_imag = dot_split(both, imag_parts)
                out_real = by_real[:size] - sign * by_imag[size:]
                out_imag = by_imag[:size] * sign + by_real[size:]
                return out_real, out_imag

            obj_real = take(ext_ref, 0)
            obj_imag = take(ext_ref, 1)
            exit_real = probe_real * obj_real - probe_imag * obj_imag
            exit_imag = probe_real * obj_imag + probe_imag * obj_real
            half_real, half_imag = left(exit_real, exit_imag, 1.0)
            far_real, far_imag = right(half_real, half_imag, 1.0)
            factor = 1.0 - amps_ref[slot] / jnp.sqrt(far_real * far_real + far_imag * far_imag + SMOOTH)
            miss_real = far_real * factor
            miss_imag = far_imag * factor
            back_real, back_imag = left(miss_real, miss_imag, -1.0)
            near_real, near_imag = right(back_real, back_imag, -1.0)
            put(out_ref, 0, probe_real * near_real + probe_imag * near_imag)
            put(out_ref, 1, probe_real * near_imag - probe_imag * near_real)
            if with_power:
                put(out_ref, 2, probe_real * probe_real + probe_imag * probe_imag)


def power_kernel(spots_ref, count_ref, probe_ref, out_ref):
    size = probe_ref.shape[1]
    out_ref[...] = jnp.zeros(out_ref.shape, jnp.float32)
    power = probe_ref[0] * probe_ref[0] + probe_ref[1] * probe_ref[1]
    for slot in range(spots_ref.shape[0]):

        @pl.when(slot < count_ref[0])
        def _():
            _, put = window_tools(size, spots_ref[slot, 0], spots_ref[slot, 1])
            put(out_ref, 0, power)


VMEM_SPEC = pl.BlockSpec(memory_space=pltpu.VMEM)
SMEM_SPEC = pl.BlockSpec(memory_space=pltpu.SMEM)
KERNEL_PARAMS = pltpu.CompilerParams(vmem_limit_bytes=60 * 1024 * 1024)


def gradient_canvas(channels, ext_shape, spots, count, extended, probe_field, own_amps, tables):
    parts = jnp.stack(split_bf16(tables[0]) + split_bf16(tables[1]))
    return pl.pallas_call(
        gradient_kernel,
        out_shape=jax.ShapeDtypeStruct((channels,) + ext_shape, jnp.float32),
        in_specs=[SMEM_SPEC, SMEM_SPEC] + [VMEM_SPEC] * 4,
        out_specs=VMEM_SPEC,
        compiler_params=KERNEL_PARAMS,
    )(spots, count.reshape(1), extended, probe_field, own_amps, parts)


def power_canvas(ext_shape, spots, count, probe_field):
    return pl.pallas_call(
        power_kernel,
        out_shape=jax.ShapeDtypeStruct((1,) + ext_shape, jnp.float32),
        in_specs=[SMEM_SPEC, SMEM_SPEC, VMEM_SPEC],
        out_specs=VMEM_SPEC,
        compiler_params=KERNEL_PARAMS,
    )(spots, count.reshape(1), probe_field)


def mesh_place():
    return (
        lax.axis_index("sx"),
        lax.axis_index("sy"),
        lax.axis_size("sx"),
        lax.axis_size("sy"),
    )


def exists(row_dev, col_dev, row_count, col_count):
    return (row_dev >= 0) & (row_dev < row_count) & (col_dev >= 0) & (col_dev < col_count)


ROW_NEIGHBOURS = [(-1, 0), (1, 0)]
COL_NEIGHBOURS = [(0, -1), (0, 1)]


def neighbour_barrier(me_r, me_c, n_r, n_c):
    barrier = pltpu.get_barrier_semaphore()
    greeted = jnp.int32(0)
    for dr, dc in ROW_NEIGHBOURS + COL_NEIGHBOURS:
        present = exists(me_r + dr, me_c + dc, n_r, n_c)

        @pl.when(present)
        def _():
            pl.semaphore_signal(
                barrier, inc=1, device_id=(me_r + dr, me_c + dc), device_id_type=pl.DeviceIdType.MESH
            )

        greeted = greeted + present.astype(jnp.int32)
    pl.semaphore_wait(barrier, greeted)


def start_copies(place, pieces, send_sems, recv_sems):
    me_r, me_c, n_r, n_c = place
    copies = []
    for index, ((dr, dc), source, target) in enumerate(pieces):
        copy = pltpu.make_async_remote_copy(
            src_ref=source,
            dst_ref=target,
            send_sem=send_sems.at[index],
            recv_sem=recv_sems.at[index],
            device_id=(me_r + dr, me_c + dc),
            device_id_type=pl.DeviceIdType.MESH,
        )
        copies.append(((dr, dc), copy))

        @pl.when(exists(me_r + dr, me_c + dc, n_r, n_c))
        def _():
            copy.start()

    return copies


def wait_copies(place, copies):
    me_r, me_c, n_r, n_c = place
    for (dr, dc), copy in copies:

        @pl.when(exists(me_r + dr, me_c + dc, n_r, n_c))
        def _():
            copy.wait_send()

        @pl.when(exists(me_r - dr, me_c - dc, n_r, n_c))
        def _():
            copy.wait_recv()


def swap(place, pieces, send_sems, recv_sems):
    wait_copies(place, start_copies(place, pieces, send_sems, recv_sems))


def halo_kernel(cur_ref, ext_ref, zeros_ref, send_sems, recv_sems, local_sems):
    rows = cur_ref.shape[1]
    cols = cur_ref.shape[2]
    margin = (ext_ref.shape[2] - cols) // 2
    ext_cols = cols + 2 * margin
    place = mesh_place()
    me_r, me_c, n_r, n_c = place
    middle = slice(margin, margin + rows)
    own = pltpu.make_async_copy(cur_ref, ext_ref.at[:, middle, margin : margin + cols], local_sems.at[0])
    own.start()
    zeros_ref[...] = jnp.zeros(zeros_ref.shape, jnp.float32)
    unreached = [
        ((0, 1), ext_ref.at[:, middle, 0:margin], zeros_ref.at[:, :, 0:margin]),
        ((0, -1), ext_ref.at[:, middle, margin + cols : ext_cols], zeros_ref.at[:, :, 0:margin]),
        ((1, 0), ext_ref.at[:, 0:margin, :], zeros_ref),
        ((-1, 0), ext_ref.at[:, margin + rows : 2 * margin + rows, :], zeros_ref),
    ]
    blanks = []
    for index, ((dr, dc), target, source) in enumerate(unreached):
        blank = pltpu.make_async_copy(source, target, local_sems.at[index + 1])
        missing = jnp.logical_not(exists(me_r - dr, me_c - dc, n_r, n_c))
        blanks.append((blank, missing))

    neighbour_barrier(me_r, me_c, n_r, n_c)
    for blank, missing in blanks:

        @pl.when(missing)
        def _():
            blank.start()

    above = slice(0, margin)
    below = slice(margin + rows, 2 * margin + rows)
    inner = slice(margin, margin + cols)
    left = slice(0, margin)
    right = slice(margin + cols, ext_cols)
    bands = start_copies(
        place,
        [
            ((-1, 0), cur_ref, ext_ref.at[:, below, inner]),
            ((1, 0), cur_ref, ext_ref.at[:, above, inner]),
        ],
        send_sems.at[0:2],
        recv_sems.at[0:2],
    )
    swap(
        place,
        [
            ((0, -1), cur_ref.at[:, :, 0:margin], ext_ref.at[:, middle, right]),
            ((0, 1), cur_ref.at[:, :, cols - margin : cols], ext_ref.at[:, middle, left]),
        ],
        send_sems.at[2:4],
        recv_sems.at[2:4],
    )
    own.wait()
    for blank, missing in blanks:

        @pl.when(missing)
        def _():
            blank.wait()

    corners = start_copies(
        place,
        [
            ((-1, 0), ext_ref.at[:, middle, left], ext_ref.at[:, below, left]),
            ((-1, 0), ext_ref.at[:, middle, right], ext_ref.at[:, below, right]),
            ((1, 0), ext_ref.at[:, middle, left], ext_ref.at[:, above, left]),
            ((1, 0), ext_ref.at[:, middle, right], ext_ref.at[:, above, right]),
        ],
        send_sems.at[4:8],
        recv_sems.at[4:8],
    )
    wait_copies(place, bands)
    wait_copies(place, corners)


def fold_kernel(canvas_ref, cur_ref, light_in_ref, out_ref, light_ref, mid_bufs, corner_bufs, col_bufs, band_ref, total_ref, send_sems, recv_sems, band_sem):
    rows = out_ref.shape[1]
    cols = out_ref.shape[2]
    margin = (canvas_ref.shape[2] - cols) // 2
    ext_cols = cols + 2 * margin
    place = mesh_place()
    me_r, me_c, n_r, n_c = place
    own_band = pltpu.make_async_copy(canvas_ref.at[:, margin : margin + rows, :], band_ref, band_sem)
    own_band.start()
    neighbour_barrier(me_r, me_c, n_r, n_c)
    top = slice(0, margin)
    bottom = slice(margin + rows, 2 * margin + rows)
    left = slice(0, margin)
    inner = slice(margin, margin + cols)
    right = slice(margin + cols, ext_cols)
    corners = start_copies(
        place,
        [
            ((-1, 0), canvas_ref.at[:, top, left], corner_bufs.at[0, 0]),
            ((-1, 0), canvas_ref.at[:, top, right], corner_bufs.at[0, 1]),
            ((1, 0), canvas_ref.at[:, bottom, left], corner_bufs.at[1, 0]),
            ((1, 0), canvas_ref.at[:, bottom, right], corner_bufs.at[1, 1]),
        ],
        send_sems.at[0:4],
        recv_sems.at[0:4],
    )
    mids = start_copies(
        place,
        [
            ((-1, 0), canvas_ref.at[:, top, inner], mid_bufs.at[0]),
            ((1, 0), canvas_ref.at[:, bottom, inner], mid_bufs.at[1]),
        ],
        send_sems.at[4:6],
        recv_sems.at[4:6],
    )
    wait_copies(place, corners)
    own_band.wait()
    for slot, source_r in ((0, me_r + 1), (1, me_r - 1)):

        @pl.when(exists(source_r, me_c, n_r, n_c))
        def _():
            band_ref[:, :, left] += corner_bufs[slot, 0]
            band_ref[:, :, right] += corner_bufs[slot, 1]

    strips = start_copies(
        place,
        [
            ((0, -1), band_ref.at[:, :, left], col_bufs.at[0]),
            ((0, 1), band_ref.at[:, :, right], col_bufs.at[1]),
        ],
        send_sems.at[6:8],
        recv_sems.at[6:8],
    )
    wait_copies(place, mids)
    total_ref[...] = band_ref[:, :, inner]
    for slot, source_r in ((0, me_r + 1), (1, me_r - 1)):

        @pl.when(exists(source_r, me_c, n_r, n_c))
        def _():
            total_ref[...] += mid_bufs[slot]

    wait_copies(place, strips)

    @pl.when(exists(me_r, me_c + 1, n_r, n_c))
    def _():
        total_ref[:, :, cols - margin : cols] += col_bufs[0]

    @pl.when(exists(me_r, me_c - 1, n_r, n_c))
    def _():
        total_ref[:, :, 0:margin] += col_bufs[1]

    fields = cur_ref.shape[0]
    if total_ref.shape[0] > fields:
        light_ref[...] = total_ref[fields]
    else:
        light_ref[...] = light_in_ref[...]
    out_ref[...] = cur_ref[...] - total_ref[0:fields] / (light_ref[...] + DAMPING)


def exchange_halo(current, margin):
    depth, rows, cols = current.shape
    return pl.pallas_call(
        halo_kernel,
        out_shape=jax.ShapeDtypeStruct((depth, rows + 2 * margin, cols + 2 * margin), jnp.float32),
        in_specs=[VMEM_SPEC],
        out_specs=pl.BlockSpec(memory_space=pl.ANY),
        scratch_shapes=[
            pltpu.VMEM((depth, margin, cols + 2 * margin), jnp.float32),
            pltpu.SemaphoreType.DMA((8,)),
            pltpu.SemaphoreType.DMA((8,)),
            pltpu.SemaphoreType.DMA((5,)),
        ],
        compiler_params=pltpu.CompilerParams(
            vmem_limit_bytes=60 * 1024 * 1024, has_side_effects=True, collective_id=0
        ),
    )(current)


def fold_and_step(canvas, current, light, margin):
    depth, ext_rows, ext_cols = canvas.shape
    fields, rows, cols = current.shape
    return pl.pallas_call(
        fold_kernel,
        out_shape=(
            jax.ShapeDtypeStruct((fields, rows, cols), jnp.float32),
            jax.ShapeDtypeStruct((rows, cols), jnp.float32),
        ),
        in_specs=[pl.BlockSpec(memory_space=pl.ANY), VMEM_SPEC, VMEM_SPEC],
        out_specs=(VMEM_SPEC, VMEM_SPEC),
        scratch_shapes=[
            pltpu.VMEM((2, depth, margin, cols), jnp.float32),
            pltpu.VMEM((2, 2, depth, margin, margin), jnp.float32),
            pltpu.VMEM((2, depth, rows, margin), jnp.float32),
            pltpu.VMEM((depth, rows, ext_cols), jnp.float32),
            pltpu.VMEM((depth, rows, cols), jnp.float32),
            pltpu.SemaphoreType.DMA((8,)),
            pltpu.SemaphoreType.DMA((8,)),
            pltpu.SemaphoreType.DMA(()),
        ],
        compiler_params=pltpu.CompilerParams(
            vmem_limit_bytes=60 * 1024 * 1024, has_side_effects=True, collective_id=depth
        ),
    )(canvas, current, light)


def on_device(object_field, probe_field, amplitudes, centres, counts):
    size_probe = probe_field.shape[1]
    margin = size_probe // 2
    block_rows = object_field.shape[1]
    block_cols = object_field.shape[2]
    tables = dft_tables(size_probe)
    spots = centres[0, 0]
    own_amps = amplitudes[0, 0]
    sx_size = lax.axis_size("sx")
    sx_index = lax.axis_index("sx")
    column_counts = counts[:, 0]
    sx_positions = jnp.arange(sx_size, dtype=jnp.int32)
    own_count = jnp.sum(jnp.where(sx_positions == sx_index, column_counts, 0))
    ext_shape = (block_rows + size_probe, block_cols + size_probe)

    current = object_field
    illumination = jnp.zeros((block_rows, block_cols), jnp.float32)
    for sweep_index in range(ITERS):
        extended = exchange_halo(current, margin)
        channels = 3 if sweep_index == 0 else 2
        canvas = gradient_canvas(
            channels, ext_shape, spots, own_count, extended, probe_field, own_amps, tables
        )
        current, illumination = fold_and_step(canvas, current, illumination, margin)
    return current


def solution(mesh):
    return jax.shard_map(
        on_device,
        mesh=mesh,
        in_specs=(
            P(None, "sx", "sy"),
            P(),
            P("sx", "sy", None, None, None),
            P("sx", "sy", None, None),
            P(None, "sy"),
        ),
        out_specs=P(None, "sx", "sy"),
        check_vma=False,
    )
```

```python
import math

import jax
import ml_dtypes
import numpy as np
import jax.numpy as jnp
from jax import lax
from jax.sharding import PartitionSpec as P
from jax.experimental import pallas as pl
from jax.experimental.pallas import tpu as pltpu

ITERS = 2


SMOOTH = 1.0
DAMPING = 1.0


def with_halo(cells, sides, width):
    for axis, dim in sides:
        count = lax.axis_size(axis)
        ends = count - 1
        head = lax.slice_in_dim(cells, 0, width, axis=dim)
        tail = lax.slice_in_dim(cells, cells.shape[dim] - width, cells.shape[dim], axis=dim)
        cells = jnp.concatenate(
            [
                lax.ppermute(tail, axis, [(i, (i + 1) % count) for i in range(ends)]),
                cells,
                lax.ppermute(head, axis, [((i + 1) % count, i) for i in range(ends)]),
            ],
            axis=dim,
        )
    return cells


def dft_tables(length):
    index_values = jnp.arange(length, dtype=jnp.int32)
    product_mod = index_values[:, None] * index_values[None, :] % length
    angles = product_mod.astype(jnp.float32) * (2.0 * math.pi / length)
    scaling = 1.0 / math.sqrt(length)
    return (jnp.cos(angles) * scaling, -jnp.sin(angles) * scaling)


def matmul_exact(left_side, right_side):
    return jnp.dot(left_side, right_side, precision=lax.Precision.HIGHEST)


def complex_left(table_real, table_imag, field_real, field_imag):
    out_real = matmul_exact(table_real, field_real) - matmul_exact(table_imag, field_imag)
    out_imag = matmul_exact(table_real, field_imag) + matmul_exact(table_imag, field_real)
    return (out_real, out_imag)


def complex_right(field_real, field_imag, table_real, table_imag):
    out_real = matmul_exact(field_real, table_real) - matmul_exact(field_imag, table_imag)
    out_imag = matmul_exact(field_real, table_imag) + matmul_exact(field_imag, table_real)
    return (out_real, out_imag)


def position_gradient(object_patch, probe_field, amplitude, table_real, table_imag):
    probe_real = probe_field[0]
    probe_imag = probe_field[1]
    exit_real = probe_real * object_patch[0] - probe_imag * object_patch[1]
    exit_imag = probe_real * object_patch[1] + probe_imag * object_patch[0]
    half_real, half_imag = complex_left(table_real, table_imag, exit_real, exit_imag)
    far_real, far_imag = complex_right(half_real, half_imag, table_real, table_imag)
    factor = 1.0 - amplitude / jnp.sqrt(far_real * far_real + far_imag * far_imag + SMOOTH)
    miss_real = far_real * factor
    miss_imag = far_imag * factor
    back_real, back_imag = complex_left(table_real, -table_imag, miss_real, miss_imag)
    near_real, near_imag = complex_right(back_real, back_imag, table_real, -table_imag)
    return jnp.stack(
        [
            probe_real * near_real + probe_imag * near_imag,
            probe_real * near_imag - probe_imag * near_real,
        ]
    )


def add_patch(canvas, patch_values, corner_row, corner_col):
    zero_index = jnp.zeros((), jnp.int32)
    starts = (zero_index, corner_row, corner_col)
    present = lax.dynamic_slice(canvas, starts, patch_values.shape)
    return lax.dynamic_update_slice(canvas, present + patch_values, starts)


def fold_rows(extended, margin, length):
    middle_part = extended[:, 2 * margin : 2 * margin + length]
    upper_rim = extended[:, :margin]
    lower_rim = extended[:, extended.shape[1] - margin :]
    middle_part = middle_part.at[:, :margin].add(upper_rim)
    return middle_part.at[:, length - margin :].add(lower_rim)


def fold_cols(extended, margin, length):
    middle_part = extended[:, :, 2 * margin : 2 * margin + length]
    left_rim = extended[:, :, :margin]
    right_rim = extended[:, :, extended.shape[2] - margin :]
    middle_part = middle_part.at[:, :, :margin].add(left_rim)
    return middle_part.at[:, :, length - margin :].add(right_rim)


def settle(stacked, margin, block_rows, block_cols):
    full_ext = with_halo(stacked, (("sx", 1), ("sy", 2)), margin)
    return fold_cols(fold_rows(full_ext, margin, block_rows), margin, block_cols)


def local_pass(canvas, extended, spots, own_amps, probe_field, table_real, table_imag, upper_bound):
    size_probe = probe_field.shape[1]

    def local_step(slot_index, canvas_state):
        row_start = spots[slot_index, 0]
        col_start = spots[slot_index, 1]
        zero_index = jnp.zeros((), jnp.int32)
        object_patch = lax.dynamic_slice(
            extended, (zero_index, row_start, col_start), (2, size_probe, size_probe)
        )
        update = position_gradient(
            object_patch, probe_field, own_amps[slot_index], table_real, table_imag
        )
        return add_patch(canvas_state, update, row_start, col_start)

    return lax.fori_loop(0, upper_bound, local_step, canvas)


def dot_exact(left_side, right_side):
    return jnp.dot(
        left_side, right_side, precision=lax.Precision.HIGHEST, preferred_element_type=jnp.float32
    )


def window_tools(size, row, col):
    lanes = 128
    sublanes = 8
    wide = size + lanes
    tall = size + sublanes
    row_base = pl.multiple_of((row // sublanes) * sublanes, sublanes)
    col_base = pl.multiple_of((col // lanes) * lanes, lanes)
    row_shift = row % sublanes
    col_shift = col % lanes
    rows = pl.ds(row_base, tall)
    cols = pl.ds(col_base, wide)

    def take(ref, channel):
        block = ref[channel, rows, cols]
        block = pltpu.roll(block, (tall - row_shift) % tall, 0)
        return pltpu.roll(block, (wide - col_shift) % wide, 1)[:size, :size]

    def put(ref, channel, values):
        block = jnp.concatenate([values, jnp.zeros((size, lanes), jnp.float32)], axis=1)
        block = jnp.concatenate([block, jnp.zeros((sublanes, wide), jnp.float32)], axis=0)
        block = pltpu.roll(pltpu.roll(block, col_shift, 1), row_shift, 0)
        ref[channel, rows, cols] += block

    return take, put


def split_bf16(values):
    scaled = values * 65537.0
    high = scaled - (scaled - values)
    return high.astype(jnp.bfloat16), (values - high).astype(jnp.bfloat16)


def dot_split(left_parts, right_parts):
    left_high, left_low = left_parts
    right_high, right_low = right_parts
    total = jnp.dot(left_high, right_high, preferred_element_type=jnp.float32)
    total += jnp.dot(left_high, right_low, preferred_element_type=jnp.float32)
    return total + jnp.dot(left_low, right_high, preferred_element_type=jnp.float32)


def gradient_kernel(spots_ref, count_ref, ext_ref, probe_ref, amps_ref, tables_ref, out_ref):
    size = probe_ref.shape[1]
    out_ref[...] = jnp.zeros(out_ref.shape, jnp.float32)
    with_power = out_ref.shape[0] > 2
    for slot in range(amps_ref.shape[0]):

        @pl.when(slot < count_ref[0])
        def _():
            take, put = window_tools(size, spots_ref[slot, 0], spots_ref[slot, 1])
            probe_real = probe_ref[0]
            probe_imag = probe_ref[1]
            real_parts = (tables_ref[0], tables_ref[1])
            imag_parts = (tables_ref[2], tables_ref[3])

            def left(field_real, field_imag, sign):
                both = split_bf16(jnp.concatenate([field_real, field_imag], axis=1))
                by_real = dot_split(real_parts, both)
                by_imag = dot_split(imag_parts, both)
                out_real = by_real[:, :size] - sign * by_imag[:, size:]
                out_imag = by_real[:, size:] + sign * by_imag[:, :size]
                return out_real, out_imag

            def right(field_real, field_imag, sign):
                both = split_bf16(jnp.concatenate([field_real, field_imag], axis=0))
                by_real = dot_split(both, real_parts)
                by_imag = dot_split(both, imag_parts)
                out_real = by_real[:size] - sign * by_imag[size:]
                out_imag = by_imag[:size] * sign + by_real[size:]
                return out_real, out_imag

            obj_real = take(ext_ref, 0)
            obj_imag = take(ext_ref, 1)
            exit_real = probe_real * obj_real - probe_imag * obj_imag
            exit_imag = probe_real * obj_imag + probe_imag * obj_real
            half_real, half_imag = left(exit_real, exit_imag, 1.0)
            far_real, far_imag = right(half_real, half_imag, 1.0)
            factor = 1.0 - amps_ref[slot] / jnp.sqrt(far_real * far_real + far_imag * far_imag + SMOOTH)
            miss_real = far_real * factor
            miss_imag = far_imag * factor
            back_real, back_imag = left(miss_real, miss_imag, -1.0)
            near_real, near_imag = right(back_real, back_imag, -1.0)
            put(out_ref, 0, probe_real * near_real + probe_imag * near_imag)
            put(out_ref, 1, probe_real * near_imag - probe_imag * near_real)
            if with_power:
                put(out_ref, 2, probe_real * probe_real + probe_imag * probe_imag)


def power_kernel(spots_ref, count_ref, probe_ref, out_ref):
    size = probe_ref.shape[1]
    out_ref[...] = jnp.zeros(out_ref.shape, jnp.float32)
    power = probe_ref[0] * probe_ref[0] + probe_ref[1] * probe_ref[1]
    for slot in range(spots_ref.shape[0]):

        @pl.when(slot < count_ref[0])
        def _():
            _, put = window_tools(size, spots_ref[slot, 0], spots_ref[slot, 1])
            put(out_ref, 0, power)


VMEM_SPEC = pl.BlockSpec(memory_space=pltpu.VMEM)
SMEM_SPEC = pl.BlockSpec(memory_space=pltpu.SMEM)
KERNEL_PARAMS = pltpu.CompilerParams(vmem_limit_bytes=60 * 1024 * 1024)


def split_tables(length):
    index_values = np.arange(length, dtype=np.int32)
    product_mod = index_values[:, None] * index_values[None, :] % length
    angles = product_mod.astype(np.float32) * np.float32(2.0 * math.pi / length)
    scaling = np.float32(1.0 / math.sqrt(length))
    parts = []
    for table in (np.cos(angles) * scaling, -np.sin(angles) * scaling):
        table = table.astype(np.float32)
        scaled = table * np.float32(65537.0)
        high = scaled - (scaled - table)
        parts += [high.astype(ml_dtypes.bfloat16), (table - high).astype(ml_dtypes.bfloat16)]
    return jnp.asarray(np.stack(parts))


def gradient_canvas(channels, ext_shape, spots, count, extended, probe_field, own_amps, tables):
    return pl.pallas_call(
        gradient_kernel,
        out_shape=jax.ShapeDtypeStruct((channels,) + ext_shape, jnp.float32),
        in_specs=[SMEM_SPEC, SMEM_SPEC] + [VMEM_SPEC] * 4,
        out_specs=VMEM_SPEC,
        compiler_params=KERNEL_PARAMS,
    )(spots, count.reshape(1), extended, probe_field, own_amps, tables)


def power_canvas(ext_shape, spots, count, probe_field):
    return pl.pallas_call(
        power_kernel,
        out_shape=jax.ShapeDtypeStruct((1,) + ext_shape, jnp.float32),
        in_specs=[SMEM_SPEC, SMEM_SPEC, VMEM_SPEC],
        out_specs=VMEM_SPEC,
        compiler_params=KERNEL_PARAMS,
    )(spots, count.reshape(1), probe_field)


def mesh_place():
    return (
        lax.axis_index("sx"),
        lax.axis_index("sy"),
        lax.axis_size("sx"),
        lax.axis_size("sy"),
    )


def exists(row_dev, col_dev, row_count, col_count):
    return (row_dev >= 0) & (row_dev < row_count) & (col_dev >= 0) & (col_dev < col_count)


ROW_NEIGHBOURS = [(-1, 0), (1, 0)]
COL_NEIGHBOURS = [(0, -1), (0, 1)]


def neighbour_barrier(me_r, me_c, n_r, n_c):
    barrier = pltpu.get_barrier_semaphore()
    greeted = jnp.int32(0)
    for dr, dc in ROW_NEIGHBOURS + COL_NEIGHBOURS:
        present = exists(me_r + dr, me_c + dc, n_r, n_c)

        @pl.when(present)
        def _():
            pl.semaphore_signal(
                barrier, inc=1, device_id=(me_r + dr, me_c + dc), device_id_type=pl.DeviceIdType.MESH
            )

        greeted = greeted + present.astype(jnp.int32)
    pl.semaphore_wait(barrier, greeted)


def start_copies(place, pieces, send_sems, recv_sems):
    me_r, me_c, n_r, n_c = place
    copies = []
    for index, ((dr, dc), source, target) in enumerate(pieces):
        copy = pltpu.make_async_remote_copy(
            src_ref=source,
            dst_ref=target,
            send_sem=send_sems.at[index],
            recv_sem=recv_sems.at[index],
            device_id=(me_r + dr, me_c + dc),
            device_id_type=pl.DeviceIdType.MESH,
        )
        copies.append(((dr, dc), copy))

        @pl.when(exists(me_r + dr, me_c + dc, n_r, n_c))
        def _():
            copy.start()

    return copies


def wait_copies(place, copies):
    me_r, me_c, n_r, n_c = place
    for (dr, dc), copy in copies:

        @pl.when(exists(me_r + dr, me_c + dc, n_r, n_c))
        def _():
            copy.wait_send()

        @pl.when(exists(me_r - dr, me_c - dc, n_r, n_c))
        def _():
            copy.wait_recv()


def swap(place, pieces, send_sems, recv_sems):
    wait_copies(place, start_copies(place, pieces, send_sems, recv_sems))


def halo_kernel(cur_ref, ext_ref, zeros_ref, send_sems, recv_sems, local_sems):
    rows = cur_ref.shape[1]
    cols = cur_ref.shape[2]
    margin = (ext_ref.shape[2] - cols) // 2
    ext_cols = cols + 2 * margin
    place = mesh_place()
    me_r, me_c, n_r, n_c = place
    middle = slice(margin, margin + rows)
    own = pltpu.make_async_copy(cur_ref, ext_ref.at[:, middle, margin : margin + cols], local_sems.at[0])
    own.start()
    zeros_ref[...] = jnp.zeros(zeros_ref.shape, jnp.float32)
    unreached = [
        ((0, 1), ext_ref.at[:, middle, 0:margin], zeros_ref.at[:, :, 0:margin]),
        ((0, -1), ext_ref.at[:, middle, margin + cols : ext_cols], zeros_ref.at[:, :, 0:margin]),
        ((1, 0), ext_ref.at[:, 0:margin, :], zeros_ref),
        ((-1, 0), ext_ref.at[:, margin + rows : 2 * margin + rows, :], zeros_ref),
    ]
    blanks = []
    for index, ((dr, dc), target, source) in enumerate(unreached):
        blank = pltpu.make_async_copy(source, target, local_sems.at[index + 1])
        missing = jnp.logical_not(exists(me_r - dr, me_c - dc, n_r, n_c))
        blanks.append((blank, missing))

    neighbour_barrier(me_r, me_c, n_r, n_c)
    for blank, missing in blanks:

        @pl.when(missing)
        def _():
            blank.start()

    above = slice(0, margin)
    below = slice(margin + rows, 2 * margin + rows)
    inner = slice(margin, margin + cols)
    left = slice(0, margin)
    right = slice(margin + cols, ext_cols)
    bands = start_copies(
        place,
        [
            ((-1, 0), cur_ref, ext_ref.at[:, below, inner]),
            ((1, 0), cur_ref, ext_ref.at[:, above, inner]),
        ],
        send_sems.at[0:2],
        recv_sems.at[0:2],
    )
    swap(
        place,
        [
            ((0, -1), cur_ref.at[:, :, 0:margin], ext_ref.at[:, middle, right]),
            ((0, 1), cur_ref.at[:, :, cols - margin : cols], ext_ref.at[:, middle, left]),
        ],
        send_sems.at[2:4],
        recv_sems.at[2:4],
    )
    own.wait()
    for blank, missing in blanks:

        @pl.when(missing)
        def _():
            blank.wait()

    corners = start_copies(
        place,
        [
            ((-1, 0), ext_ref.at[:, middle, left], ext_ref.at[:, below, left]),
            ((-1, 0), ext_ref.at[:, middle, right], ext_ref.at[:, below, right]),
            ((1, 0), ext_ref.at[:, middle, left], ext_ref.at[:, above, left]),
            ((1, 0), ext_ref.at[:, middle, right], ext_ref.at[:, above, right]),
        ],
        send_sems.at[4:8],
        recv_sems.at[4:8],
    )
    wait_copies(place, bands)
    wait_copies(place, corners)


def fold_kernel(canvas_ref, cur_ref, *refs):
    if len(refs) == 10:
        light_in_ref, refs = None, refs
    else:
        light_in_ref, refs = refs[0], refs[1:]
    fold_body(canvas_ref, cur_ref, light_in_ref, *refs)


def fold_body(canvas_ref, cur_ref, light_in_ref, out_ref, light_ref, mid_bufs, corner_bufs, col_bufs, band_ref, total_ref, send_sems, recv_sems, band_sem):
    rows = out_ref.shape[1]
    cols = out_ref.shape[2]
    margin = (canvas_ref.shape[2] - cols) // 2
    ext_cols = cols + 2 * margin
    place = mesh_place()
    me_r, me_c, n_r, n_c = place
    own_band = pltpu.make_async_copy(canvas_ref.at[:, margin : margin + rows, :], band_ref, band_sem)
    own_band.start()
    neighbour_barrier(me_r, me_c, n_r, n_c)
    top = slice(0, margin)
    bottom = slice(margin + rows, 2 * margin + rows)
    left = slice(0, margin)
    inner = slice(margin, margin + cols)
    right = slice(margin + cols, ext_cols)
    corners = start_copies(
        place,
        [
            ((-1, 0), canvas_ref.at[:, top, left], corner_bufs.at[0, 0]),
            ((-1, 0), canvas_ref.at[:, top, right], corner_bufs.at[0, 1]),
            ((1, 0), canvas_ref.at[:, bottom, left], corner_bufs.at[1, 0]),
            ((1, 0), canvas_ref.at[:, bottom, right], corner_bufs.at[1, 1]),
        ],
        send_sems.at[0:4],
        recv_sems.at[0:4],
    )
    mids = start_copies(
        place,
        [
            ((-1, 0), canvas_ref.at[:, top, inner], mid_bufs.at[0]),
            ((1, 0), canvas_ref.at[:, bottom, inner], mid_bufs.at[1]),
        ],
        send_sems.at[4:6],
        recv_sems.at[4:6],
    )
    wait_copies(place, corners)
    own_band.wait()
    for slot, source_r in ((0, me_r + 1), (1, me_r - 1)):

        @pl.when(exists(source_r, me_c, n_r, n_c))
        def _():
            band_ref[:, :, left] += corner_bufs[slot, 0]
            band_ref[:, :, right] += corner_bufs[slot, 1]

    strips = start_copies(
        place,
        [
            ((0, -1), band_ref.at[:, :, left], col_bufs.at[0]),
            ((0, 1), band_ref.at[:, :, right], col_bufs.at[1]),
        ],
        send_sems.at[6:8],
        recv_sems.at[6:8],
    )
    wait_copies(place, mids)
    total_ref[...] = band_ref[:, :, inner]
    for slot, source_r in ((0, me_r + 1), (1, me_r - 1)):

        @pl.when(exists(source_r, me_c, n_r, n_c))
        def _():
            total_ref[...] += mid_bufs[slot]

    wait_copies(place, strips)

    @pl.when(exists(me_r, me_c + 1, n_r, n_c))
    def _():
        total_ref[:, :, cols - margin : cols] += col_bufs[0]

    @pl.when(exists(me_r, me_c - 1, n_r, n_c))
    def _():
        total_ref[:, :, 0:margin] += col_bufs[1]

    fields = cur_ref.shape[0]
    if total_ref.shape[0] > fields:
        light_ref[...] = total_ref[fields]
    else:
        light_ref[...] = light_in_ref[...]
    out_ref[...] = cur_ref[...] - total_ref[0:fields] / (light_ref[...] + DAMPING)


def exchange_halo(current, margin):
    depth, rows, cols = current.shape
    return pl.pallas_call(
        halo_kernel,
        out_shape=jax.ShapeDtypeStruct((depth, rows + 2 * margin, cols + 2 * margin), jnp.float32),
        in_specs=[VMEM_SPEC],
        out_specs=pl.BlockSpec(memory_space=pl.ANY),
        scratch_shapes=[
            pltpu.VMEM((depth, margin, cols + 2 * margin), jnp.float32),
            pltpu.SemaphoreType.DMA((8,)),
            pltpu.SemaphoreType.DMA((8,)),
            pltpu.SemaphoreType.DMA((5,)),
        ],
        compiler_params=pltpu.CompilerParams(
            vmem_limit_bytes=60 * 1024 * 1024, has_side_effects=True, collective_id=0
        ),
    )(current)


def fold_and_step(canvas, current, light, margin):
    depth, ext_rows, ext_cols = canvas.shape
    fields, rows, cols = current.shape
    return pl.pallas_call(
        fold_kernel,
        out_shape=(
            jax.ShapeDtypeStruct((fields, rows, cols), jnp.float32),
            jax.ShapeDtypeStruct((rows, cols), jnp.float32),
        ),
        in_specs=[pl.BlockSpec(memory_space=pl.ANY), VMEM_SPEC] + ([] if light is None else [VMEM_SPEC]),
        out_specs=(VMEM_SPEC, VMEM_SPEC),
        scratch_shapes=[
            pltpu.VMEM((2, depth, margin, cols), jnp.float32),
            pltpu.VMEM((2, 2, depth, margin, margin), jnp.float32),
            pltpu.VMEM((2, depth, rows, margin), jnp.float32),
            pltpu.VMEM((depth, rows, ext_cols), jnp.float32),
            pltpu.VMEM((depth, rows, cols), jnp.float32),
            pltpu.SemaphoreType.DMA((8,)),
            pltpu.SemaphoreType.DMA((8,)),
            pltpu.SemaphoreType.DMA(()),
        ],
        compiler_params=pltpu.CompilerParams(
            vmem_limit_bytes=60 * 1024 * 1024, has_side_effects=True, collective_id=depth
        ),
    )(canvas, current, *([] if light is None else [light]))


def on_device(object_field, probe_field, amplitudes, centres, counts):
    size_probe = probe_field.shape[1]
    margin = size_probe // 2
    block_rows = object_field.shape[1]
    block_cols = object_field.shape[2]
    tables = split_tables(size_probe)
    spots = centres[0, 0]
    own_amps = amplitudes[0, 0]
    sx_size = lax.axis_size("sx")
    sx_index = lax.axis_index("sx")
    column_counts = counts[:, 0]
    sx_positions = jnp.arange(sx_size, dtype=jnp.int32)
    own_count = jnp.sum(jnp.where(sx_positions == sx_index, column_counts, 0))
    ext_shape = (block_rows + size_probe, block_cols + size_probe)

    current = object_field
    illumination = None
    for sweep_index in range(ITERS):
        extended = exchange_halo(current, margin)
        channels = 3 if sweep_index == 0 else 2
        canvas = gradient_canvas(
            channels, ext_shape, spots, own_count, extended, probe_field, own_amps, tables
        )
        current, illumination = fold_and_step(canvas, current, illumination, margin)
    return current


def solution(mesh):
    return jax.shard_map(
        on_device,
        mesh=mesh,
        in_specs=(
            P(None, "sx", "sy"),
            P(),
            P("sx", "sy", None, None, None),
            P("sx", "sy", None, None),
            P(None, "sy"),
        ),
        out_specs=P(None, "sx", "sy"),
        check_vma=False,
    )
```

```python
import math

import jax
import ml_dtypes
import numpy as np
import jax.numpy as jnp
from jax import lax
from jax.sharding import PartitionSpec as P
from jax.experimental import pallas as pl
from jax.experimental.pallas import tpu as pltpu

ITERS = 2


SMOOTH = 1.0
DAMPING = 1.0


def with_halo(cells, sides, width):
    for axis, dim in sides:
        count = lax.axis_size(axis)
        ends = count - 1
        head = lax.slice_in_dim(cells, 0, width, axis=dim)
        tail = lax.slice_in_dim(cells, cells.shape[dim] - width, cells.shape[dim], axis=dim)
        cells = jnp.concatenate(
            [
                lax.ppermute(tail, axis, [(i, (i + 1) % count) for i in range(ends)]),
                cells,
                lax.ppermute(head, axis, [((i + 1) % count, i) for i in range(ends)]),
            ],
            axis=dim,
        )
    return cells


def dft_tables(length):
    index_values = jnp.arange(length, dtype=jnp.int32)
    product_mod = index_values[:, None] * index_values[None, :] % length
    angles = product_mod.astype(jnp.float32) * (2.0 * math.pi / length)
    scaling = 1.0 / math.sqrt(length)
    return (jnp.cos(angles) * scaling, -jnp.sin(angles) * scaling)


def matmul_exact(left_side, right_side):
    return jnp.dot(left_side, right_side, precision=lax.Precision.HIGHEST)


def complex_left(table_real, table_imag, field_real, field_imag):
    out_real = matmul_exact(table_real, field_real) - matmul_exact(table_imag, field_imag)
    out_imag = matmul_exact(table_real, field_imag) + matmul_exact(table_imag, field_real)
    return (out_real, out_imag)


def complex_right(field_real, field_imag, table_real, table_imag):
    out_real = matmul_exact(field_real, table_real) - matmul_exact(field_imag, table_imag)
    out_imag = matmul_exact(field_real, table_imag) + matmul_exact(field_imag, table_real)
    return (out_real, out_imag)


def position_gradient(object_patch, probe_field, amplitude, table_real, table_imag):
    probe_real = probe_field[0]
    probe_imag = probe_field[1]
    exit_real = probe_real * object_patch[0] - probe_imag * object_patch[1]
    exit_imag = probe_real * object_patch[1] + probe_imag * object_patch[0]
    half_real, half_imag = complex_left(table_real, table_imag, exit_real, exit_imag)
    far_real, far_imag = complex_right(half_real, half_imag, table_real, table_imag)
    factor = 1.0 - amplitude / jnp.sqrt(far_real * far_real + far_imag * far_imag + SMOOTH)
    miss_real = far_real * factor
    miss_imag = far_imag * factor
    back_real, back_imag = complex_left(table_real, -table_imag, miss_real, miss_imag)
    near_real, near_imag = complex_right(back_real, back_imag, table_real, -table_imag)
    return jnp.stack(
        [
            probe_real * near_real + probe_imag * near_imag,
            probe_real * near_imag - probe_imag * near_real,
        ]
    )


def add_patch(canvas, patch_values, corner_row, corner_col):
    zero_index = jnp.zeros((), jnp.int32)
    starts = (zero_index, corner_row, corner_col)
    present = lax.dynamic_slice(canvas, starts, patch_values.shape)
    return lax.dynamic_update_slice(canvas, present + patch_values, starts)


def fold_rows(extended, margin, length):
    middle_part = extended[:, 2 * margin : 2 * margin + length]
    upper_rim = extended[:, :margin]
    lower_rim = extended[:, extended.shape[1] - margin :]
    middle_part = middle_part.at[:, :margin].add(upper_rim)
    return middle_part.at[:, length - margin :].add(lower_rim)


def fold_cols(extended, margin, length):
    middle_part = extended[:, :, 2 * margin : 2 * margin + length]
    left_rim = extended[:, :, :margin]
    right_rim = extended[:, :, extended.shape[2] - margin :]
    middle_part = middle_part.at[:, :, :margin].add(left_rim)
    return middle_part.at[:, :, length - margin :].add(right_rim)


def settle(stacked, margin, block_rows, block_cols):
    full_ext = with_halo(stacked, (("sx", 1), ("sy", 2)), margin)
    return fold_cols(fold_rows(full_ext, margin, block_rows), margin, block_cols)


def local_pass(canvas, extended, spots, own_amps, probe_field, table_real, table_imag, upper_bound):
    size_probe = probe_field.shape[1]

    def local_step(slot_index, canvas_state):
        row_start = spots[slot_index, 0]
        col_start = spots[slot_index, 1]
        zero_index = jnp.zeros((), jnp.int32)
        object_patch = lax.dynamic_slice(
            extended, (zero_index, row_start, col_start), (2, size_probe, size_probe)
        )
        update = position_gradient(
            object_patch, probe_field, own_amps[slot_index], table_real, table_imag
        )
        return add_patch(canvas_state, update, row_start, col_start)

    return lax.fori_loop(0, upper_bound, local_step, canvas)


def dot_exact(left_side, right_side):
    return jnp.dot(
        left_side, right_side, precision=lax.Precision.HIGHEST, preferred_element_type=jnp.float32
    )


def window_tools(size, row, col):
    lanes = 128
    sublanes = 8
    wide = size + lanes
    tall = size + sublanes
    row_base = pl.multiple_of((row // sublanes) * sublanes, sublanes)
    col_base = pl.multiple_of((col // lanes) * lanes, lanes)
    row_shift = row % sublanes
    col_shift = col % lanes
    rows = pl.ds(row_base, tall)
    cols = pl.ds(col_base, wide)

    def take(ref, channel):
        block = ref[channel, rows, cols]
        block = pltpu.roll(block, (tall - row_shift) % tall, 0)
        return pltpu.roll(block, (wide - col_shift) % wide, 1)[:size, :size]

    def put(ref, channel, values):
        block = jnp.concatenate([values, jnp.zeros((size, lanes), jnp.float32)], axis=1)
        block = jnp.concatenate([block, jnp.zeros((sublanes, wide), jnp.float32)], axis=0)
        block = pltpu.roll(pltpu.roll(block, col_shift, 1), row_shift, 0)
        ref[channel, rows, cols] += block

    return take, put


def split_bf16(values):
    scaled = values * 65537.0
    high = scaled - (scaled - values)
    return high.astype(jnp.bfloat16), (values - high).astype(jnp.bfloat16)


def dot_split(left_parts, right_parts):
    left_high, left_low = left_parts
    right_high, right_low = right_parts
    total = jnp.dot(left_high, right_high, preferred_element_type=jnp.float32)
    total += jnp.dot(left_high, right_low, preferred_element_type=jnp.float32)
    return total + jnp.dot(left_low, right_high, preferred_element_type=jnp.float32)


def gradient_kernel(spots_ref, count_ref, ext_ref, probe_ref, amps_ref, tables_ref, out_ref):
    size = probe_ref.shape[1]
    out_ref[...] = jnp.zeros(out_ref.shape, jnp.float32)
    live = count_ref[lax.axis_index("sx")]
    with_power = out_ref.shape[0] > 2
    for slot in range(amps_ref.shape[0]):

        @pl.when(slot < live)
        def _():
            take, put = window_tools(size, spots_ref[slot, 0], spots_ref[slot, 1])
            probe_real = probe_ref[0]
            probe_imag = probe_ref[1]
            real_parts = (tables_ref[0], tables_ref[1])
            imag_parts = (tables_ref[2], tables_ref[3])

            def left(field_real, field_imag, sign):
                both = split_bf16(jnp.concatenate([field_real, field_imag], axis=1))
                by_real = dot_split(real_parts, both)
                by_imag = dot_split(imag_parts, both)
                out_real = by_real[:, :size] - sign * by_imag[:, size:]
                out_imag = by_real[:, size:] + sign * by_imag[:, :size]
                return out_real, out_imag

            def right(field_real, field_imag, sign):
                both = split_bf16(jnp.concatenate([field_real, field_imag], axis=0))
                by_real = dot_split(both, real_parts)
                by_imag = dot_split(both, imag_parts)
                out_real = by_real[:size] - sign * by_imag[size:]
                out_imag = by_imag[:size] * sign + by_real[size:]
                return out_real, out_imag

            obj_real = take(ext_ref, 0)
            obj_imag = take(ext_ref, 1)
            exit_real = probe_real * obj_real - probe_imag * obj_imag
            exit_imag = probe_real * obj_imag + probe_imag * obj_real
            half_real, half_imag = left(exit_real, exit_imag, 1.0)
            far_real, far_imag = right(half_real, half_imag, 1.0)
            factor = 1.0 - amps_ref[slot] / jnp.sqrt(far_real * far_real + far_imag * far_imag + SMOOTH)
            miss_real = far_real * factor
            miss_imag = far_imag * factor
            back_real, back_imag = left(miss_real, miss_imag, -1.0)
            near_real, near_imag = right(back_real, back_imag, -1.0)
            put(out_ref, 0, probe_real * near_real + probe_imag * near_imag)
            put(out_ref, 1, probe_real * near_imag - probe_imag * near_real)
            if with_power:
                put(out_ref, 2, probe_real * probe_real + probe_imag * probe_imag)


def power_kernel(spots_ref, count_ref, probe_ref, out_ref):
    size = probe_ref.shape[1]
    out_ref[...] = jnp.zeros(out_ref.shape, jnp.float32)
    power = probe_ref[0] * probe_ref[0] + probe_ref[1] * probe_ref[1]
    for slot in range(spots_ref.shape[0]):

        @pl.when(slot < count_ref[0])
        def _():
            _, put = window_tools(size, spots_ref[slot, 0], spots_ref[slot, 1])
            put(out_ref, 0, power)


VMEM_SPEC = pl.BlockSpec(memory_space=pltpu.VMEM)
SMEM_SPEC = pl.BlockSpec(memory_space=pltpu.SMEM)
KERNEL_PARAMS = pltpu.CompilerParams(vmem_limit_bytes=60 * 1024 * 1024)


def split_tables(length):
    index_values = np.arange(length, dtype=np.int32)
    product_mod = index_values[:, None] * index_values[None, :] % length
    angles = product_mod.astype(np.float32) * np.float32(2.0 * math.pi / length)
    scaling = np.float32(1.0 / math.sqrt(length))
    parts = []
    for table in (np.cos(angles) * scaling, -np.sin(angles) * scaling):
        table = table.astype(np.float32)
        scaled = table * np.float32(65537.0)
        high = scaled - (scaled - table)
        parts += [high.astype(ml_dtypes.bfloat16), (table - high).astype(ml_dtypes.bfloat16)]
    return jnp.asarray(np.stack(parts))


def gradient_canvas(channels, ext_shape, spots, count, extended, probe_field, own_amps, tables):
    return pl.pallas_call(
        gradient_kernel,
        out_shape=jax.ShapeDtypeStruct((channels,) + ext_shape, jnp.float32),
        in_specs=[SMEM_SPEC, SMEM_SPEC] + [VMEM_SPEC] * 4,
        out_specs=VMEM_SPEC,
        compiler_params=KERNEL_PARAMS,
    )(spots, count, extended, probe_field, own_amps, tables)


def power_canvas(ext_shape, spots, count, probe_field):
    return pl.pallas_call(
        power_kernel,
        out_shape=jax.ShapeDtypeStruct((1,) + ext_shape, jnp.float32),
        in_specs=[SMEM_SPEC, SMEM_SPEC, VMEM_SPEC],
        out_specs=VMEM_SPEC,
        compiler_params=KERNEL_PARAMS,
    )(spots, count.reshape(1), probe_field)


def mesh_place():
    return (
        lax.axis_index("sx"),
        lax.axis_index("sy"),
        lax.axis_size("sx"),
        lax.axis_size("sy"),
    )


def exists(row_dev, col_dev, row_count, col_count):
    return (row_dev >= 0) & (row_dev < row_count) & (col_dev >= 0) & (col_dev < col_count)


ROW_NEIGHBOURS = [(-1, 0), (1, 0)]
COL_NEIGHBOURS = [(0, -1), (0, 1)]


def neighbour_barrier(me_r, me_c, n_r, n_c):
    barrier = pltpu.get_barrier_semaphore()
    greeted = jnp.int32(0)
    for dr, dc in ROW_NEIGHBOURS + COL_NEIGHBOURS:
        present = exists(me_r + dr, me_c + dc, n_r, n_c)

        @pl.when(present)
        def _():
            pl.semaphore_signal(
                barrier, inc=1, device_id=(me_r + dr, me_c + dc), device_id_type=pl.DeviceIdType.MESH
            )

        greeted = greeted + present.astype(jnp.int32)
    pl.semaphore_wait(barrier, greeted)


def start_copies(place, pieces, send_sems, recv_sems):
    me_r, me_c, n_r, n_c = place
    copies = []
    for index, ((dr, dc), source, target) in enumerate(pieces):
        copy = pltpu.make_async_remote_copy(
            src_ref=source,
            dst_ref=target,
            send_sem=send_sems.at[index],
            recv_sem=recv_sems.at[index],
            device_id=(me_r + dr, me_c + dc),
            device_id_type=pl.DeviceIdType.MESH,
        )
        copies.append(((dr, dc), copy))

        @pl.when(exists(me_r + dr, me_c + dc, n_r, n_c))
        def _():
            copy.start()

    return copies


def wait_copies(place, copies):
    me_r, me_c, n_r, n_c = place
    for (dr, dc), copy in copies:

        @pl.when(exists(me_r + dr, me_c + dc, n_r, n_c))
        def _():
            copy.wait_send()

        @pl.when(exists(me_r - dr, me_c - dc, n_r, n_c))
        def _():
            copy.wait_recv()


def swap(place, pieces, send_sems, recv_sems):
    wait_copies(place, start_copies(place, pieces, send_sems, recv_sems))


def halo_kernel(cur_ref, ext_ref, zeros_ref, send_sems, recv_sems, local_sems):
    rows = cur_ref.shape[1]
    cols = cur_ref.shape[2]
    margin = (ext_ref.shape[2] - cols) // 2
    ext_cols = cols + 2 * margin
    place = mesh_place()
    me_r, me_c, n_r, n_c = place
    middle = slice(margin, margin + rows)
    own = pltpu.make_async_copy(cur_ref, ext_ref.at[:, middle, margin : margin + cols], local_sems.at[0])
    own.start()
    zeros_ref[...] = jnp.zeros(zeros_ref.shape, jnp.float32)
    unreached = [
        ((0, 1), ext_ref.at[:, middle, 0:margin], zeros_ref.at[:, :, 0:margin]),
        ((0, -1), ext_ref.at[:, middle, margin + cols : ext_cols], zeros_ref.at[:, :, 0:margin]),
        ((1, 0), ext_ref.at[:, 0:margin, :], zeros_ref),
        ((-1, 0), ext_ref.at[:, margin + rows : 2 * margin + rows, :], zeros_ref),
    ]
    blanks = []
    for index, ((dr, dc), target, source) in enumerate(unreached):
        blank = pltpu.make_async_copy(source, target, local_sems.at[index + 1])
        missing = jnp.logical_not(exists(me_r - dr, me_c - dc, n_r, n_c))
        blanks.append((blank, missing))

    neighbour_barrier(me_r, me_c, n_r, n_c)
    for blank, missing in blanks:

        @pl.when(missing)
        def _():
            blank.start()

    above = slice(0, margin)
    below = slice(margin + rows, 2 * margin + rows)
    inner = slice(margin, margin + cols)
    left = slice(0, margin)
    right = slice(margin + cols, ext_cols)
    bands = start_copies(
        place,
        [
            ((-1, 0), cur_ref, ext_ref.at[:, below, inner]),
            ((1, 0), cur_ref, ext_ref.at[:, above, inner]),
        ],
        send_sems.at[0:2],
        recv_sems.at[0:2],
    )
    swap(
        place,
        [
            ((0, -1), cur_ref.at[:, :, 0:margin], ext_ref.at[:, middle, right]),
            ((0, 1), cur_ref.at[:, :, cols - margin : cols], ext_ref.at[:, middle, left]),
        ],
        send_sems.at[2:4],
        recv_sems.at[2:4],
    )
    own.wait()
    for blank, missing in blanks:

        @pl.when(missing)
        def _():
            blank.wait()

    corners = start_copies(
        place,
        [
            ((-1, 0), ext_ref.at[:, middle, left], ext_ref.at[:, below, left]),
            ((-1, 0), ext_ref.at[:, middle, right], ext_ref.at[:, below, right]),
            ((1, 0), ext_ref.at[:, middle, left], ext_ref.at[:, above, left]),
            ((1, 0), ext_ref.at[:, middle, right], ext_ref.at[:, above, right]),
        ],
        send_sems.at[4:8],
        recv_sems.at[4:8],
    )
    wait_copies(place, bands)
    wait_copies(place, corners)


def fold_kernel(canvas_ref, cur_ref, *refs):
    if len(refs) == 10:
        light_in_ref, refs = None, refs
    else:
        light_in_ref, refs = refs[0], refs[1:]
    fold_body(canvas_ref, cur_ref, light_in_ref, *refs)


def fold_body(canvas_ref, cur_ref, light_in_ref, out_ref, light_ref, mid_bufs, corner_bufs, col_bufs, band_ref, total_ref, send_sems, recv_sems, band_sem):
    rows = out_ref.shape[1]
    cols = out_ref.shape[2]
    margin = (canvas_ref.shape[2] - cols) // 2
    ext_cols = cols + 2 * margin
    place = mesh_place()
    me_r, me_c, n_r, n_c = place
    own_band = pltpu.make_async_copy(canvas_ref.at[:, margin : margin + rows, :], band_ref, band_sem)
    own_band.start()
    neighbour_barrier(me_r, me_c, n_r, n_c)
    top = slice(0, margin)
    bottom = slice(margin + rows, 2 * margin + rows)
    left = slice(0, margin)
    inner = slice(margin, margin + cols)
    right = slice(margin + cols, ext_cols)
    corners = start_copies(
        place,
        [
            ((-1, 0), canvas_ref.at[:, top, left], corner_bufs.at[0, 0]),
            ((-1, 0), canvas_ref.at[:, top, right], corner_bufs.at[0, 1]),
            ((1, 0), canvas_ref.at[:, bottom, left], corner_bufs.at[1, 0]),
            ((1, 0), canvas_ref.at[:, bottom, right], corner_bufs.at[1, 1]),
        ],
        send_sems.at[0:4],
        recv_sems.at[0:4],
    )
    mids = start_copies(
        place,
        [
            ((-1, 0), canvas_ref.at[:, top, inner], mid_bufs.at[0]),
            ((1, 0), canvas_ref.at[:, bottom, inner], mid_bufs.at[1]),
        ],
        send_sems.at[4:6],
        recv_sems.at[4:6],
    )
    wait_copies(place, corners)
    own_band.wait()
    for slot, source_r in ((0, me_r + 1), (1, me_r - 1)):

        @pl.when(exists(source_r, me_c, n_r, n_c))
        def _():
            band_ref[:, :, left] += corner_bufs[slot, 0]
            band_ref[:, :, right] += corner_bufs[slot, 1]

    strips = start_copies(
        place,
        [
            ((0, -1), band_ref.at[:, :, left], col_bufs.at[0]),
            ((0, 1), band_ref.at[:, :, right], col_bufs.at[1]),
        ],
        send_sems.at[6:8],
        recv_sems.at[6:8],
    )
    wait_copies(place, mids)
    total_ref[...] = band_ref[:, :, inner]
    for slot, source_r in ((0, me_r + 1), (1, me_r - 1)):

        @pl.when(exists(source_r, me_c, n_r, n_c))
        def _():
            total_ref[...] += mid_bufs[slot]

    wait_copies(place, strips)

    @pl.when(exists(me_r, me_c + 1, n_r, n_c))
    def _():
        total_ref[:, :, cols - margin : cols] += col_bufs[0]

    @pl.when(exists(me_r, me_c - 1, n_r, n_c))
    def _():
        total_ref[:, :, 0:margin] += col_bufs[1]

    fields = cur_ref.shape[0]
    if total_ref.shape[0] > fields:
        light_ref[...] = total_ref[fields]
    else:
        light_ref[...] = light_in_ref[...]
    out_ref[...] = cur_ref[...] - total_ref[0:fields] / (light_ref[...] + DAMPING)


def exchange_halo(current, margin):
    depth, rows, cols = current.shape
    return pl.pallas_call(
        halo_kernel,
        out_shape=jax.ShapeDtypeStruct((depth, rows + 2 * margin, cols + 2 * margin), jnp.float32),
        in_specs=[VMEM_SPEC],
        out_specs=pl.BlockSpec(memory_space=pl.ANY),
        scratch_shapes=[
            pltpu.VMEM((depth, margin, cols + 2 * margin), jnp.float32),
            pltpu.SemaphoreType.DMA((8,)),
            pltpu.SemaphoreType.DMA((8,)),
            pltpu.SemaphoreType.DMA((5,)),
        ],
        compiler_params=pltpu.CompilerParams(
            vmem_limit_bytes=60 * 1024 * 1024, has_side_effects=True, collective_id=0
        ),
    )(current)


def fold_and_step(canvas, current, light, margin):
    depth, ext_rows, ext_cols = canvas.shape
    fields, rows, cols = current.shape
    return pl.pallas_call(
        fold_kernel,
        out_shape=(
            jax.ShapeDtypeStruct((fields, rows, cols), jnp.float32),
            jax.ShapeDtypeStruct((rows, cols), jnp.float32),
        ),
        in_specs=[pl.BlockSpec(memory_space=pl.ANY), VMEM_SPEC] + ([] if light is None else [VMEM_SPEC]),
        out_specs=(VMEM_SPEC, VMEM_SPEC),
        scratch_shapes=[
            pltpu.VMEM((2, depth, margin, cols), jnp.float32),
            pltpu.VMEM((2, 2, depth, margin, margin), jnp.float32),
            pltpu.VMEM((2, depth, rows, margin), jnp.float32),
            pltpu.VMEM((depth, rows, ext_cols), jnp.float32),
            pltpu.VMEM((depth, rows, cols), jnp.float32),
            pltpu.SemaphoreType.DMA((8,)),
            pltpu.SemaphoreType.DMA((8,)),
            pltpu.SemaphoreType.DMA(()),
        ],
        compiler_params=pltpu.CompilerParams(
            vmem_limit_bytes=60 * 1024 * 1024, has_side_effects=True, collective_id=depth
        ),
    )(canvas, current, *([] if light is None else [light]))


def on_device(object_field, probe_field, amplitudes, centres, counts):
    size_probe = probe_field.shape[1]
    margin = size_probe // 2
    block_rows = object_field.shape[1]
    block_cols = object_field.shape[2]
    tables = split_tables(size_probe)
    spots = centres[0, 0]
    own_amps = amplitudes[0, 0]
    column_counts = counts[:, 0]
    ext_shape = (block_rows + size_probe, block_cols + size_probe)

    current = object_field
    illumination = None
    for sweep_index in range(ITERS):
        extended = exchange_halo(current, margin)
        channels = 3 if sweep_index == 0 else 2
        canvas = gradient_canvas(
            channels, ext_shape, spots, column_counts, extended, probe_field, own_amps, tables
        )
        current, illumination = fold_and_step(canvas, current, illumination, margin)
    return current


def solution(mesh):
    return jax.shard_map(
        on_device,
        mesh=mesh,
        in_specs=(
            P(None, "sx", "sy"),
            P(),
            P("sx", "sy", None, None, None),
            P("sx", "sy", None, None),
            P(None, "sy"),
        ),
        out_specs=P(None, "sx", "sy"),
        check_vma=False,
    )
```

```python
import math

import jax
import ml_dtypes
import numpy as np
import jax.numpy as jnp
from jax import lax
from jax.sharding import PartitionSpec as P
from jax.experimental import pallas as pl
from jax.experimental.pallas import tpu as pltpu

ITERS = 2


SMOOTH = 1.0
DAMPING = 1.0


def with_halo(cells, sides, width):
    for axis, dim in sides:
        count = lax.axis_size(axis)
        ends = count - 1
        head = lax.slice_in_dim(cells, 0, width, axis=dim)
        tail = lax.slice_in_dim(cells, cells.shape[dim] - width, cells.shape[dim], axis=dim)
        cells = jnp.concatenate(
            [
                lax.ppermute(tail, axis, [(i, (i + 1) % count) for i in range(ends)]),
                cells,
                lax.ppermute(head, axis, [((i + 1) % count, i) for i in range(ends)]),
            ],
            axis=dim,
        )
    return cells


def dft_tables(length):
    index_values = jnp.arange(length, dtype=jnp.int32)
    product_mod = index_values[:, None] * index_values[None, :] % length
    angles = product_mod.astype(jnp.float32) * (2.0 * math.pi / length)
    scaling = 1.0 / math.sqrt(length)
    return (jnp.cos(angles) * scaling, -jnp.sin(angles) * scaling)


def matmul_exact(left_side, right_side):
    return jnp.dot(left_side, right_side, precision=lax.Precision.HIGHEST)


def complex_left(table_real, table_imag, field_real, field_imag):
    out_real = matmul_exact(table_real, field_real) - matmul_exact(table_imag, field_imag)
    out_imag = matmul_exact(table_real, field_imag) + matmul_exact(table_imag, field_real)
    return (out_real, out_imag)


def complex_right(field_real, field_imag, table_real, table_imag):
    out_real = matmul_exact(field_real, table_real) - matmul_exact(field_imag, table_imag)
    out_imag = matmul_exact(field_real, table_imag) + matmul_exact(field_imag, table_real)
    return (out_real, out_imag)


def position_gradient(object_patch, probe_field, amplitude, table_real, table_imag):
    probe_real = probe_field[0]
    probe_imag = probe_field[1]
    exit_real = probe_real * object_patch[0] - probe_imag * object_patch[1]
    exit_imag = probe_real * object_patch[1] + probe_imag * object_patch[0]
    half_real, half_imag = complex_left(table_real, table_imag, exit_real, exit_imag)
    far_real, far_imag = complex_right(half_real, half_imag, table_real, table_imag)
    factor = 1.0 - amplitude / jnp.sqrt(far_real * far_real + far_imag * far_imag + SMOOTH)
    miss_real = far_real * factor
    miss_imag = far_imag * factor
    back_real, back_imag = complex_left(table_real, -table_imag, miss_real, miss_imag)
    near_real, near_imag = complex_right(back_real, back_imag, table_real, -table_imag)
    return jnp.stack(
        [
            probe_real * near_real + probe_imag * near_imag,
            probe_real * near_imag - probe_imag * near_real,
        ]
    )


def add_patch(canvas, patch_values, corner_row, corner_col):
    zero_index = jnp.zeros((), jnp.int32)
    starts = (zero_index, corner_row, corner_col)
    present = lax.dynamic_slice(canvas, starts, patch_values.shape)
    return lax.dynamic_update_slice(canvas, present + patch_values, starts)


def fold_rows(extended, margin, length):
    middle_part = extended[:, 2 * margin : 2 * margin + length]
    upper_rim = extended[:, :margin]
    lower_rim = extended[:, extended.shape[1] - margin :]
    middle_part = middle_part.at[:, :margin].add(upper_rim)
    return middle_part.at[:, length - margin :].add(lower_rim)


def fold_cols(extended, margin, length):
    middle_part = extended[:, :, 2 * margin : 2 * margin + length]
    left_rim = extended[:, :, :margin]
    right_rim = extended[:, :, extended.shape[2] - margin :]
    middle_part = middle_part.at[:, :, :margin].add(left_rim)
    return middle_part.at[:, :, length - margin :].add(right_rim)


def settle(stacked, margin, block_rows, block_cols):
    full_ext = with_halo(stacked, (("sx", 1), ("sy", 2)), margin)
    return fold_cols(fold_rows(full_ext, margin, block_rows), margin, block_cols)


def local_pass(canvas, extended, spots, own_amps, probe_field, table_real, table_imag, upper_bound):
    size_probe = probe_field.shape[1]

    def local_step(slot_index, canvas_state):
        row_start = spots[slot_index, 0]
        col_start = spots[slot_index, 1]
        zero_index = jnp.zeros((), jnp.int32)
        object_patch = lax.dynamic_slice(
            extended, (zero_index, row_start, col_start), (2, size_probe, size_probe)
        )
        update = position_gradient(
            object_patch, probe_field, own_amps[slot_index], table_real, table_imag
        )
        return add_patch(canvas_state, update, row_start, col_start)

    return lax.fori_loop(0, upper_bound, local_step, canvas)


def dot_exact(left_side, right_side):
    return jnp.dot(
        left_side, right_side, precision=lax.Precision.HIGHEST, preferred_element_type=jnp.float32
    )


def window_tools(size, row, col):
    lanes = 128
    sublanes = 8
    wide = size + lanes
    tall = size + sublanes
    row_base = pl.multiple_of((row // sublanes) * sublanes, sublanes)
    col_base = pl.multiple_of((col // lanes) * lanes, lanes)
    row_shift = row % sublanes
    col_shift = col % lanes
    rows = pl.ds(row_base, tall)
    cols = pl.ds(col_base, wide)

    def take(ref, channel):
        block = ref[channel, rows, cols]
        block = pltpu.roll(block, (tall - row_shift) % tall, 0)
        return pltpu.roll(block, (wide - col_shift) % wide, 1)[:size, :size]

    def put(ref, channel, values):
        block = jnp.concatenate([values, jnp.zeros((size, lanes), jnp.float32)], axis=1)
        block = jnp.concatenate([block, jnp.zeros((sublanes, wide), jnp.float32)], axis=0)
        block = pltpu.roll(pltpu.roll(block, col_shift, 1), row_shift, 0)
        ref[channel, rows, cols] += block

    return take, put


def split_bf16(values):
    scaled = values * 65537.0
    high = scaled - (scaled - values)
    return high.astype(jnp.bfloat16), (values - high).astype(jnp.bfloat16)


def dot_split(left_parts, right_parts):
    left_high, left_low = left_parts
    right_high, right_low = right_parts
    total = jnp.dot(left_high, right_high, preferred_element_type=jnp.float32)
    total += jnp.dot(left_high, right_low, preferred_element_type=jnp.float32)
    return total + jnp.dot(left_low, right_high, preferred_element_type=jnp.float32)


def gradient_kernel(spots_ref, count_ref, ext_ref, probe_ref, amps_ref, tables_ref, out_ref):
    size = probe_ref.shape[1]
    out_ref[...] = jnp.zeros(out_ref.shape, jnp.float32)
    live = count_ref[lax.axis_index("sx")]
    with_power = out_ref.shape[0] > 2
    for slot in range(amps_ref.shape[0]):

        @pl.when(slot < live)
        def _():
            take, put = window_tools(size, spots_ref[slot, 0], spots_ref[slot, 1])
            probe_real = probe_ref[0]
            probe_imag = probe_ref[1]
            real_parts = (tables_ref[0], tables_ref[1])
            imag_parts = (tables_ref[2], tables_ref[3])

            def left(field_real, field_imag, conjugate):
                both = split_bf16(jnp.concatenate([field_real, field_imag], axis=1))
                by_real = dot_split(real_parts, both)
                by_imag = dot_split(imag_parts, both)
                if conjugate:
                    return by_real[:, :size] + by_imag[:, size:], by_real[:, size:] - by_imag[:, :size]
                return by_real[:, :size] - by_imag[:, size:], by_real[:, size:] + by_imag[:, :size]

            def right(field_real, field_imag, conjugate):
                both = split_bf16(jnp.concatenate([field_real, field_imag], axis=0))
                by_real = dot_split(both, real_parts)
                by_imag = dot_split(both, imag_parts)
                if conjugate:
                    return by_real[:size] + by_imag[size:], by_real[size:] - by_imag[:size]
                return by_real[:size] - by_imag[size:], by_imag[:size] + by_real[size:]

            obj_real = take(ext_ref, 0)
            obj_imag = take(ext_ref, 1)
            exit_real = probe_real * obj_real - probe_imag * obj_imag
            exit_imag = probe_real * obj_imag + probe_imag * obj_real
            half_real, half_imag = left(exit_real, exit_imag, False)
            far_real, far_imag = right(half_real, half_imag, False)
            factor = 1.0 - amps_ref[slot] * lax.rsqrt(far_real * far_real + far_imag * far_imag + SMOOTH)
            miss_real = far_real * factor
            miss_imag = far_imag * factor
            back_real, back_imag = left(miss_real, miss_imag, True)
            near_real, near_imag = right(back_real, back_imag, True)
            put(out_ref, 0, probe_real * near_real + probe_imag * near_imag)
            put(out_ref, 1, probe_real * near_imag - probe_imag * near_real)
            if with_power:
                put(out_ref, 2, probe_real * probe_real + probe_imag * probe_imag)


def power_kernel(spots_ref, count_ref, probe_ref, out_ref):
    size = probe_ref.shape[1]
    out_ref[...] = jnp.zeros(out_ref.shape, jnp.float32)
    power = probe_ref[0] * probe_ref[0] + probe_ref[1] * probe_ref[1]
    for slot in range(spots_ref.shape[0]):

        @pl.when(slot < count_ref[0])
        def _():
            _, put = window_tools(size, spots_ref[slot, 0], spots_ref[slot, 1])
            put(out_ref, 0, power)


VMEM_SPEC = pl.BlockSpec(memory_space=pltpu.VMEM)
SMEM_SPEC = pl.BlockSpec(memory_space=pltpu.SMEM)
KERNEL_PARAMS = pltpu.CompilerParams(vmem_limit_bytes=60 * 1024 * 1024)


def split_tables(length):
    index_values = np.arange(length, dtype=np.int32)
    product_mod = index_values[:, None] * index_values[None, :] % length
    angles = product_mod.astype(np.float32) * np.float32(2.0 * math.pi / length)
    scaling = np.float32(1.0 / math.sqrt(length))
    parts = []
    for table in (np.cos(angles) * scaling, -np.sin(angles) * scaling):
        table = table.astype(np.float32)
        scaled = table * np.float32(65537.0)
        high = scaled - (scaled - table)
        parts += [high.astype(ml_dtypes.bfloat16), (table - high).astype(ml_dtypes.bfloat16)]
    return jnp.asarray(np.stack(parts))


def gradient_canvas(channels, ext_shape, spots, count, extended, probe_field, own_amps, tables):
    return pl.pallas_call(
        gradient_kernel,
        out_shape=jax.ShapeDtypeStruct((channels,) + ext_shape, jnp.float32),
        in_specs=[SMEM_SPEC, SMEM_SPEC] + [VMEM_SPEC] * 4,
        out_specs=VMEM_SPEC,
        compiler_params=KERNEL_PARAMS,
    )(spots, count, extended, probe_field, own_amps, tables)


def power_canvas(ext_shape, spots, count, probe_field):
    return pl.pallas_call(
        power_kernel,
        out_shape=jax.ShapeDtypeStruct((1,) + ext_shape, jnp.float32),
        in_specs=[SMEM_SPEC, SMEM_SPEC, VMEM_SPEC],
        out_specs=VMEM_SPEC,
        compiler_params=KERNEL_PARAMS,
    )(spots, count.reshape(1), probe_field)


def mesh_place():
    return (
        lax.axis_index("sx"),
        lax.axis_index("sy"),
        lax.axis_size("sx"),
        lax.axis_size("sy"),
    )


def exists(row_dev, col_dev, row_count, col_count):
    return (row_dev >= 0) & (row_dev < row_count) & (col_dev >= 0) & (col_dev < col_count)


ROW_NEIGHBOURS = [(-1, 0), (1, 0)]
COL_NEIGHBOURS = [(0, -1), (0, 1)]


def neighbour_barrier(me_r, me_c, n_r, n_c):
    barrier = pltpu.get_barrier_semaphore()
    greeted = jnp.int32(0)
    for dr, dc in ROW_NEIGHBOURS + COL_NEIGHBOURS:
        present = exists(me_r + dr, me_c + dc, n_r, n_c)

        @pl.when(present)
        def _():
            pl.semaphore_signal(
                barrier, inc=1, device_id=(me_r + dr, me_c + dc), device_id_type=pl.DeviceIdType.MESH
            )

        greeted = greeted + present.astype(jnp.int32)
    pl.semaphore_wait(barrier, greeted)


def start_copies(place, pieces, send_sems, recv_sems):
    me_r, me_c, n_r, n_c = place
    copies = []
    for index, ((dr, dc), source, target) in enumerate(pieces):
        copy = pltpu.make_async_remote_copy(
            src_ref=source,
            dst_ref=target,
            send_sem=send_sems.at[index],
            recv_sem=recv_sems.at[index],
            device_id=(me_r + dr, me_c + dc),
            device_id_type=pl.DeviceIdType.MESH,
        )
        copies.append(((dr, dc), copy))

        @pl.when(exists(me_r + dr, me_c + dc, n_r, n_c))
        def _():
            copy.start()

    return copies


def wait_copies(place, copies):
    me_r, me_c, n_r, n_c = place
    for (dr, dc), copy in copies:

        @pl.when(exists(me_r + dr, me_c + dc, n_r, n_c))
        def _():
            copy.wait_send()

        @pl.when(exists(me_r - dr, me_c - dc, n_r, n_c))
        def _():
            copy.wait_recv()


def swap(place, pieces, send_sems, recv_sems):
    wait_copies(place, start_copies(place, pieces, send_sems, recv_sems))


def halo_kernel(cur_ref, ext_ref, zeros_ref, send_sems, recv_sems, local_sems):
    rows = cur_ref.shape[1]
    cols = cur_ref.shape[2]
    margin = (ext_ref.shape[2] - cols) // 2
    ext_cols = cols + 2 * margin
    place = mesh_place()
    me_r, me_c, n_r, n_c = place
    middle = slice(margin, margin + rows)
    own = pltpu.make_async_copy(cur_ref, ext_ref.at[:, middle, margin : margin + cols], local_sems.at[0])
    own.start()
    zeros_ref[...] = jnp.zeros(zeros_ref.shape, jnp.float32)
    unreached = [
        ((0, 1), ext_ref.at[:, middle, 0:margin], zeros_ref.at[:, :, 0:margin]),
        ((0, -1), ext_ref.at[:, middle, margin + cols : ext_cols], zeros_ref.at[:, :, 0:margin]),
        ((1, 0), ext_ref.at[:, 0:margin, :], zeros_ref),
        ((-1, 0), ext_ref.at[:, margin + rows : 2 * margin + rows, :], zeros_ref),
    ]
    blanks = []
    for index, ((dr, dc), target, source) in enumerate(unreached):
        blank = pltpu.make_async_copy(source, target, local_sems.at[index + 1])
        missing = jnp.logical_not(exists(me_r - dr, me_c - dc, n_r, n_c))
        blanks.append((blank, missing))

    neighbour_barrier(me_r, me_c, n_r, n_c)
    for blank, missing in blanks:

        @pl.when(missing)
        def _():
            blank.start()

    above = slice(0, margin)
    below = slice(margin + rows, 2 * margin + rows)
    inner = slice(margin, margin + cols)
    left = slice(0, margin)
    right = slice(margin + cols, ext_cols)
    bands = start_copies(
        place,
        [
            ((-1, 0), cur_ref, ext_ref.at[:, below, inner]),
            ((1, 0), cur_ref, ext_ref.at[:, above, inner]),
        ],
        send_sems.at[0:2],
        recv_sems.at[0:2],
    )
    swap(
        place,
        [
            ((0, -1), cur_ref.at[:, :, 0:margin], ext_ref.at[:, middle, right]),
            ((0, 1), cur_ref.at[:, :, cols - margin : cols], ext_ref.at[:, middle, left]),
        ],
        send_sems.at[2:4],
        recv_sems.at[2:4],
    )
    own.wait()
    for blank, missing in blanks:

        @pl.when(missing)
        def _():
            blank.wait()

    corners = start_copies(
        place,
        [
            ((-1, 0), ext_ref.at[:, middle, left], ext_ref.at[:, below, left]),
            ((-1, 0), ext_ref.at[:, middle, right], ext_ref.at[:, below, right]),
            ((1, 0), ext_ref.at[:, middle, left], ext_ref.at[:, above, left]),
            ((1, 0), ext_ref.at[:, middle, right], ext_ref.at[:, above, right]),
        ],
        send_sems.at[4:8],
        recv_sems.at[4:8],
    )
    wait_copies(place, bands)
    wait_copies(place, corners)


def fold_kernel(canvas_ref, cur_ref, *refs):
    if len(refs) == 10:
        light_in_ref, refs = None, refs
    else:
        light_in_ref, refs = refs[0], refs[1:]
    fold_body(canvas_ref, cur_ref, light_in_ref, *refs)


def fold_body(canvas_ref, cur_ref, light_in_ref, out_ref, light_ref, mid_bufs, corner_bufs, col_bufs, band_ref, total_ref, send_sems, recv_sems, band_sem):
    rows = out_ref.shape[1]
    cols = out_ref.shape[2]
    margin = (canvas_ref.shape[2] - cols) // 2
    ext_cols = cols + 2 * margin
    place = mesh_place()
    me_r, me_c, n_r, n_c = place
    own_band = pltpu.make_async_copy(canvas_ref.at[:, margin : margin + rows, :], band_ref, band_sem)
    own_band.start()
    neighbour_barrier(me_r, me_c, n_r, n_c)
    top = slice(0, margin)
    bottom = slice(margin + rows, 2 * margin + rows)
    left = slice(0, margin)
    inner = slice(margin, margin + cols)
    right = slice(margin + cols, ext_cols)
    corners = start_copies(
        place,
        [
            ((-1, 0), canvas_ref.at[:, top, left], corner_bufs.at[0, 0]),
            ((-1, 0), canvas_ref.at[:, top, right], corner_bufs.at[0, 1]),
            ((1, 0), canvas_ref.at[:, bottom, left], corner_bufs.at[1, 0]),
            ((1, 0), canvas_ref.at[:, bottom, right], corner_bufs.at[1, 1]),
        ],
        send_sems.at[0:4],
        recv_sems.at[0:4],
    )
    mids = start_copies(
        place,
        [
            ((-1, 0), canvas_ref.at[:, top, inner], mid_bufs.at[0]),
            ((1, 0), canvas_ref.at[:, bottom, inner], mid_bufs.at[1]),
        ],
        send_sems.at[4:6],
        recv_sems.at[4:6],
    )
    wait_copies(place, corners)
    own_band.wait()
    for slot, source_r in ((0, me_r + 1), (1, me_r - 1)):

        @pl.when(exists(source_r, me_c, n_r, n_c))
        def _():
            band_ref[:, :, left] += corner_bufs[slot, 0]
            band_ref[:, :, right] += corner_bufs[slot, 1]

    strips = start_copies(
        place,
        [
            ((0, -1), band_ref.at[:, :, left], col_bufs.at[0]),
            ((0, 1), band_ref.at[:, :, right], col_bufs.at[1]),
        ],
        send_sems.at[6:8],
        recv_sems.at[6:8],
    )
    wait_copies(place, mids)
    total_ref[...] = band_ref[:, :, inner]
    for slot, source_r in ((0, me_r + 1), (1, me_r - 1)):

        @pl.when(exists(source_r, me_c, n_r, n_c))
        def _():
            total_ref[...] += mid_bufs[slot]

    wait_copies(place, strips)

    @pl.when(exists(me_r, me_c + 1, n_r, n_c))
    def _():
        total_ref[:, :, cols - margin : cols] += col_bufs[0]

    @pl.when(exists(me_r, me_c - 1, n_r, n_c))
    def _():
        total_ref[:, :, 0:margin] += col_bufs[1]

    fields = cur_ref.shape[0]
    if total_ref.shape[0] > fields:
        light_ref[...] = total_ref[fields]
    else:
        light_ref[...] = light_in_ref[...]
    out_ref[...] = cur_ref[...] - total_ref[0:fields] / (light_ref[...] + DAMPING)


def exchange_halo(current, margin):
    depth, rows, cols = current.shape
    return pl.pallas_call(
        halo_kernel,
        out_shape=jax.ShapeDtypeStruct((depth, rows + 2 * margin, cols + 2 * margin), jnp.float32),
        in_specs=[VMEM_SPEC],
        out_specs=pl.BlockSpec(memory_space=pl.ANY),
        scratch_shapes=[
            pltpu.VMEM((depth, margin, cols + 2 * margin), jnp.float32),
            pltpu.SemaphoreType.DMA((8,)),
            pltpu.SemaphoreType.DMA((8,)),
            pltpu.SemaphoreType.DMA((5,)),
        ],
        compiler_params=pltpu.CompilerParams(
            vmem_limit_bytes=60 * 1024 * 1024, has_side_effects=True, collective_id=0
        ),
    )(current)


def fold_and_step(canvas, current, light, margin):
    depth, ext_rows, ext_cols = canvas.shape
    fields, rows, cols = current.shape
    return pl.pallas_call(
        fold_kernel,
        out_shape=(
            jax.ShapeDtypeStruct((fields, rows, cols), jnp.float32),
            jax.ShapeDtypeStruct((rows, cols), jnp.float32),
        ),
        in_specs=[pl.BlockSpec(memory_space=pl.ANY), VMEM_SPEC] + ([] if light is None else [VMEM_SPEC]),
        out_specs=(VMEM_SPEC, VMEM_SPEC),
        scratch_shapes=[
            pltpu.VMEM((2, depth, margin, cols), jnp.float32),
            pltpu.VMEM((2, 2, depth, margin, margin), jnp.float32),
            pltpu.VMEM((2, depth, rows, margin), jnp.float32),
            pltpu.VMEM((depth, rows, ext_cols), jnp.float32),
            pltpu.VMEM((depth, rows, cols), jnp.float32),
            pltpu.SemaphoreType.DMA((8,)),
            pltpu.SemaphoreType.DMA((8,)),
            pltpu.SemaphoreType.DMA(()),
        ],
        compiler_params=pltpu.CompilerParams(
            vmem_limit_bytes=60 * 1024 * 1024, has_side_effects=True, collective_id=depth
        ),
    )(canvas, current, *([] if light is None else [light]))


def on_device(object_field, probe_field, amplitudes, centres, counts):
    size_probe = probe_field.shape[1]
    margin = size_probe // 2
    block_rows = object_field.shape[1]
    block_cols = object_field.shape[2]
    tables = split_tables(size_probe)
    spots = centres[0, 0]
    own_amps = amplitudes[0, 0]
    column_counts = counts[:, 0]
    ext_shape = (block_rows + size_probe, block_cols + size_probe)

    current = object_field
    illumination = None
    for sweep_index in range(ITERS):
        extended = exchange_halo(current, margin)
        channels = 3 if sweep_index == 0 else 2
        canvas = gradient_canvas(
            channels, ext_shape, spots, column_counts, extended, probe_field, own_amps, tables
        )
        current, illumination = fold_and_step(canvas, current, illumination, margin)
    return current


def solution(mesh):
    return jax.shard_map(
        on_device,
        mesh=mesh,
        in_specs=(
            P(None, "sx", "sy"),
            P(),
            P("sx", "sy", None, None, None),
            P("sx", "sy", None, None),
            P(None, "sy"),
        ),
        out_specs=P(None, "sx", "sy"),
        check_vma=False,
    )
```

```python
import math

import jax
import ml_dtypes
import numpy as np
import jax.numpy as jnp
from jax import lax
from jax.sharding import PartitionSpec as P
from jax.experimental import pallas as pl
from jax.experimental.pallas import tpu as pltpu

ITERS = 2


SMOOTH = 1.0
DAMPING = 1.0


def with_halo(cells, sides, width):
    for axis, dim in sides:
        count = lax.axis_size(axis)
        ends = count - 1
        head = lax.slice_in_dim(cells, 0, width, axis=dim)
        tail = lax.slice_in_dim(cells, cells.shape[dim] - width, cells.shape[dim], axis=dim)
        cells = jnp.concatenate(
            [
                lax.ppermute(tail, axis, [(i, (i + 1) % count) for i in range(ends)]),
                cells,
                lax.ppermute(head, axis, [((i + 1) % count, i) for i in range(ends)]),
            ],
            axis=dim,
        )
    return cells


def dft_tables(length):
    index_values = jnp.arange(length, dtype=jnp.int32)
    product_mod = index_values[:, None] * index_values[None, :] % length
    angles = product_mod.astype(jnp.float32) * (2.0 * math.pi / length)
    scaling = 1.0 / math.sqrt(length)
    return (jnp.cos(angles) * scaling, -jnp.sin(angles) * scaling)


def matmul_exact(left_side, right_side):
    return jnp.dot(left_side, right_side, precision=lax.Precision.HIGHEST)


def complex_left(table_real, table_imag, field_real, field_imag):
    out_real = matmul_exact(table_real, field_real) - matmul_exact(table_imag, field_imag)
    out_imag = matmul_exact(table_real, field_imag) + matmul_exact(table_imag, field_real)
    return (out_real, out_imag)


def complex_right(field_real, field_imag, table_real, table_imag):
    out_real = matmul_exact(field_real, table_real) - matmul_exact(field_imag, table_imag)
    out_imag = matmul_exact(field_real, table_imag) + matmul_exact(field_imag, table_real)
    return (out_real, out_imag)


def position_gradient(object_patch, probe_field, amplitude, table_real, table_imag):
    probe_real = probe_field[0]
    probe_imag = probe_field[1]
    exit_real = probe_real * object_patch[0] - probe_imag * object_patch[1]
    exit_imag = probe_real * object_patch[1] + probe_imag * object_patch[0]
    half_real, half_imag = complex_left(table_real, table_imag, exit_real, exit_imag)
    far_real, far_imag = complex_right(half_real, half_imag, table_real, table_imag)
    factor = 1.0 - amplitude / jnp.sqrt(far_real * far_real + far_imag * far_imag + SMOOTH)
    miss_real = far_real * factor
    miss_imag = far_imag * factor
    back_real, back_imag = complex_left(table_real, -table_imag, miss_real, miss_imag)
    near_real, near_imag = complex_right(back_real, back_imag, table_real, -table_imag)
    return jnp.stack(
        [
            probe_real * near_real + probe_imag * near_imag,
            probe_real * near_imag - probe_imag * near_real,
        ]
    )


def add_patch(canvas, patch_values, corner_row, corner_col):
    zero_index = jnp.zeros((), jnp.int32)
    starts = (zero_index, corner_row, corner_col)
    present = lax.dynamic_slice(canvas, starts, patch_values.shape)
    return lax.dynamic_update_slice(canvas, present + patch_values, starts)


def fold_rows(extended, margin, length):
    middle_part = extended[:, 2 * margin : 2 * margin + length]
    upper_rim = extended[:, :margin]
    lower_rim = extended[:, extended.shape[1] - margin :]
    middle_part = middle_part.at[:, :margin].add(upper_rim)
    return middle_part.at[:, length - margin :].add(lower_rim)


def fold_cols(extended, margin, length):
    middle_part = extended[:, :, 2 * margin : 2 * margin + length]
    left_rim = extended[:, :, :margin]
    right_rim = extended[:, :, extended.shape[2] - margin :]
    middle_part = middle_part.at[:, :, :margin].add(left_rim)
    return middle_part.at[:, :, length - margin :].add(right_rim)


def settle(stacked, margin, block_rows, block_cols):
    full_ext = with_halo(stacked, (("sx", 1), ("sy", 2)), margin)
    return fold_cols(fold_rows(full_ext, margin, block_rows), margin, block_cols)


def local_pass(canvas, extended, spots, own_amps, probe_field, table_real, table_imag, upper_bound):
    size_probe = probe_field.shape[1]

    def local_step(slot_index, canvas_state):
        row_start = spots[slot_index, 0]
        col_start = spots[slot_index, 1]
        zero_index = jnp.zeros((), jnp.int32)
        object_patch = lax.dynamic_slice(
            extended, (zero_index, row_start, col_start), (2, size_probe, size_probe)
        )
        update = position_gradient(
            object_patch, probe_field, own_amps[slot_index], table_real, table_imag
        )
        return add_patch(canvas_state, update, row_start, col_start)

    return lax.fori_loop(0, upper_bound, local_step, canvas)


def dot_exact(left_side, right_side):
    return jnp.dot(
        left_side, right_side, precision=lax.Precision.HIGHEST, preferred_element_type=jnp.float32
    )


def window_tools(size, row, col):
    lanes = 128
    sublanes = 8
    wide = size + lanes
    tall = size + sublanes
    row_base = pl.multiple_of((row // sublanes) * sublanes, sublanes)
    col_base = pl.multiple_of((col // lanes) * lanes, lanes)
    row_shift = row % sublanes
    col_shift = col % lanes
    rows = pl.ds(row_base, tall)
    cols = pl.ds(col_base, wide)

    def take(ref, channel):
        block = ref[channel, rows, cols]
        block = pltpu.roll(block, (tall - row_shift) % tall, 0)
        return pltpu.roll(block, (wide - col_shift) % wide, 1)[:size, :size]

    def put(ref, channel, values):
        block = jnp.concatenate([values, jnp.zeros((size, lanes), jnp.float32)], axis=1)
        block = jnp.concatenate([block, jnp.zeros((sublanes, wide), jnp.float32)], axis=0)
        block = pltpu.roll(pltpu.roll(block, col_shift, 1), row_shift, 0)
        ref[channel, rows, cols] += block

    return take, put


def split_bf16(values):
    scaled = values * 65537.0
    high = scaled - (scaled - values)
    return high.astype(jnp.bfloat16), (values - high).astype(jnp.bfloat16)


def dot_split(left_parts, right_parts):
    left_high, left_low = left_parts
    right_high, right_low = right_parts
    total = jnp.dot(left_high, right_high, preferred_element_type=jnp.float32)
    total += jnp.dot(left_high, right_low, preferred_element_type=jnp.float32)
    return total + jnp.dot(left_low, right_high, preferred_element_type=jnp.float32)


def gradient_kernel(spots_ref, count_ref, ext_hbm, probe_ref, amps_ref, tables_ref, out_ref, ext_ref, ext_sem):
    size = probe_ref.shape[1]
    fetch = pltpu.make_async_copy(ext_hbm, ext_ref, ext_sem)
    fetch.start()
    out_ref[...] = jnp.zeros(out_ref.shape, jnp.float32)
    fetch.wait()
    live = count_ref[lax.axis_index("sx")]
    with_power = out_ref.shape[0] > 2
    for slot in range(amps_ref.shape[0]):

        @pl.when(slot < live)
        def _():
            take, put = window_tools(size, spots_ref[slot, 0], spots_ref[slot, 1])
            probe_real = probe_ref[0]
            probe_imag = probe_ref[1]
            real_parts = (tables_ref[0], tables_ref[1])
            imag_parts = (tables_ref[2], tables_ref[3])

            def left(field_real, field_imag, sign):
                both = split_bf16(jnp.concatenate([field_real, field_imag], axis=1))
                by_real = dot_split(real_parts, both)
                by_imag = dot_split(imag_parts, both)
                out_real = by_real[:, :size] - sign * by_imag[:, size:]
                out_imag = by_real[:, size:] + sign * by_imag[:, :size]
                return out_real, out_imag

            def right(field_real, field_imag, sign):
                both = split_bf16(jnp.concatenate([field_real, field_imag], axis=0))
                by_real = dot_split(both, real_parts)
                by_imag = dot_split(both, imag_parts)
                out_real = by_real[:size] - sign * by_imag[size:]
                out_imag = by_imag[:size] * sign + by_real[size:]
                return out_real, out_imag

            obj_real = take(ext_ref, 0)
            obj_imag = take(ext_ref, 1)
            exit_real = probe_real * obj_real - probe_imag * obj_imag
            exit_imag = probe_real * obj_imag + probe_imag * obj_real
            half_real, half_imag = left(exit_real, exit_imag, 1.0)
            far_real, far_imag = right(half_real, half_imag, 1.0)
            factor = 1.0 - amps_ref[slot] / jnp.sqrt(far_real * far_real + far_imag * far_imag + SMOOTH)
            miss_real = far_real * factor
            miss_imag = far_imag * factor
            back_real, back_imag = left(miss_real, miss_imag, -1.0)
            near_real, near_imag = right(back_real, back_imag, -1.0)
            put(out_ref, 0, probe_real * near_real + probe_imag * near_imag)
            put(out_ref, 1, probe_real * near_imag - probe_imag * near_real)
            if with_power:
                put(out_ref, 2, probe_real * probe_real + probe_imag * probe_imag)


def power_kernel(spots_ref, count_ref, probe_ref, out_ref):
    size = probe_ref.shape[1]
    out_ref[...] = jnp.zeros(out_ref.shape, jnp.float32)
    power = probe_ref[0] * probe_ref[0] + probe_ref[1] * probe_ref[1]
    for slot in range(spots_ref.shape[0]):

        @pl.when(slot < count_ref[0])
        def _():
            _, put = window_tools(size, spots_ref[slot, 0], spots_ref[slot, 1])
            put(out_ref, 0, power)


VMEM_SPEC = pl.BlockSpec(memory_space=pltpu.VMEM)
SMEM_SPEC = pl.BlockSpec(memory_space=pltpu.SMEM)
KERNEL_PARAMS = pltpu.CompilerParams(vmem_limit_bytes=60 * 1024 * 1024)


def split_tables(length):
    index_values = np.arange(length, dtype=np.int32)
    product_mod = index_values[:, None] * index_values[None, :] % length
    angles = product_mod.astype(np.float32) * np.float32(2.0 * math.pi / length)
    scaling = np.float32(1.0 / math.sqrt(length))
    parts = []
    for table in (np.cos(angles) * scaling, -np.sin(angles) * scaling):
        table = table.astype(np.float32)
        scaled = table * np.float32(65537.0)
        high = scaled - (scaled - table)
        parts += [high.astype(ml_dtypes.bfloat16), (table - high).astype(ml_dtypes.bfloat16)]
    return jnp.asarray(np.stack(parts))


def gradient_canvas(channels, ext_shape, spots, count, extended, probe_field, own_amps, tables):
    return pl.pallas_call(
        gradient_kernel,
        out_shape=jax.ShapeDtypeStruct((channels,) + ext_shape, jnp.float32),
        in_specs=[SMEM_SPEC, SMEM_SPEC, pl.BlockSpec(memory_space=pl.ANY)] + [VMEM_SPEC] * 3,
        out_specs=VMEM_SPEC,
        scratch_shapes=[pltpu.VMEM(extended.shape, jnp.float32), pltpu.SemaphoreType.DMA(())],
        compiler_params=KERNEL_PARAMS,
    )(spots, count, extended, probe_field, own_amps, tables)


def power_canvas(ext_shape, spots, count, probe_field):
    return pl.pallas_call(
        power_kernel,
        out_shape=jax.ShapeDtypeStruct((1,) + ext_shape, jnp.float32),
        in_specs=[SMEM_SPEC, SMEM_SPEC, VMEM_SPEC],
        out_specs=VMEM_SPEC,
        compiler_params=KERNEL_PARAMS,
    )(spots, count.reshape(1), probe_field)


def mesh_place():
    return (
        lax.axis_index("sx"),
        lax.axis_index("sy"),
        lax.axis_size("sx"),
        lax.axis_size("sy"),
    )


def exists(row_dev, col_dev, row_count, col_count):
    return (row_dev >= 0) & (row_dev < row_count) & (col_dev >= 0) & (col_dev < col_count)


ROW_NEIGHBOURS = [(-1, 0), (1, 0)]
COL_NEIGHBOURS = [(0, -1), (0, 1)]


def neighbour_barrier(me_r, me_c, n_r, n_c):
    barrier = pltpu.get_barrier_semaphore()
    greeted = jnp.int32(0)
    for dr, dc in ROW_NEIGHBOURS + COL_NEIGHBOURS:
        present = exists(me_r + dr, me_c + dc, n_r, n_c)

        @pl.when(present)
        def _():
            pl.semaphore_signal(
                barrier, inc=1, device_id=(me_r + dr, me_c + dc), device_id_type=pl.DeviceIdType.MESH
            )

        greeted = greeted + present.astype(jnp.int32)
    pl.semaphore_wait(barrier, greeted)


def start_copies(place, pieces, send_sems, recv_sems):
    me_r, me_c, n_r, n_c = place
    copies = []
    for index, ((dr, dc), source, target) in enumerate(pieces):
        copy = pltpu.make_async_remote_copy(
            src_ref=source,
            dst_ref=target,
            send_sem=send_sems.at[index],
            recv_sem=recv_sems.at[index],
            device_id=(me_r + dr, me_c + dc),
            device_id_type=pl.DeviceIdType.MESH,
        )
        copies.append(((dr, dc), copy))

        @pl.when(exists(me_r + dr, me_c + dc, n_r, n_c))
        def _():
            copy.start()

    return copies


def wait_copies(place, copies):
    me_r, me_c, n_r, n_c = place
    for (dr, dc), copy in copies:

        @pl.when(exists(me_r + dr, me_c + dc, n_r, n_c))
        def _():
            copy.wait_send()

        @pl.when(exists(me_r - dr, me_c - dc, n_r, n_c))
        def _():
            copy.wait_recv()


def swap(place, pieces, send_sems, recv_sems):
    wait_copies(place, start_copies(place, pieces, send_sems, recv_sems))


def halo_kernel(cur_ref, ext_ref, zeros_ref, send_sems, recv_sems, local_sems):
    rows = cur_ref.shape[1]
    cols = cur_ref.shape[2]
    margin = (ext_ref.shape[2] - cols) // 2
    ext_cols = cols + 2 * margin
    place = mesh_place()
    me_r, me_c, n_r, n_c = place
    middle = slice(margin, margin + rows)
    own = pltpu.make_async_copy(cur_ref, ext_ref.at[:, middle, margin : margin + cols], local_sems.at[0])
    own.start()
    zeros_ref[...] = jnp.zeros(zeros_ref.shape, jnp.float32)
    unreached = [
        ((0, 1), ext_ref.at[:, middle, 0:margin], zeros_ref.at[:, :, 0:margin]),
        ((0, -1), ext_ref.at[:, middle, margin + cols : ext_cols], zeros_ref.at[:, :, 0:margin]),
        ((1, 0), ext_ref.at[:, 0:margin, :], zeros_ref),
        ((-1, 0), ext_ref.at[:, margin + rows : 2 * margin + rows, :], zeros_ref),
    ]
    blanks = []
    for index, ((dr, dc), target, source) in enumerate(unreached):
        blank = pltpu.make_async_copy(source, target, local_sems.at[index + 1])
        missing = jnp.logical_not(exists(me_r - dr, me_c - dc, n_r, n_c))
        blanks.append((blank, missing))

    neighbour_barrier(me_r, me_c, n_r, n_c)
    for blank, missing in blanks:

        @pl.when(missing)
        def _():
            blank.start()

    above = slice(0, margin)
    below = slice(margin + rows, 2 * margin + rows)
    inner = slice(margin, margin + cols)
    left = slice(0, margin)
    right = slice(margin + cols, ext_cols)
    bands = start_copies(
        place,
        [
            ((-1, 0), cur_ref, ext_ref.at[:, below, inner]),
            ((1, 0), cur_ref, ext_ref.at[:, above, inner]),
        ],
        send_sems.at[0:2],
        recv_sems.at[0:2],
    )
    swap(
        place,
        [
            ((0, -1), cur_ref.at[:, :, 0:margin], ext_ref.at[:, middle, right]),
            ((0, 1), cur_ref.at[:, :, cols - margin : cols], ext_ref.at[:, middle, left]),
        ],
        send_sems.at[2:4],
        recv_sems.at[2:4],
    )
    own.wait()
    for blank, missing in blanks:

        @pl.when(missing)
        def _():
            blank.wait()

    corners = start_copies(
        place,
        [
            ((-1, 0), ext_ref.at[:, middle, left], ext_ref.at[:, below, left]),
            ((-1, 0), ext_ref.at[:, middle, right], ext_ref.at[:, below, right]),
            ((1, 0), ext_ref.at[:, middle, left], ext_ref.at[:, above, left]),
            ((1, 0), ext_ref.at[:, middle, right], ext_ref.at[:, above, right]),
        ],
        send_sems.at[4:8],
        recv_sems.at[4:8],
    )
    wait_copies(place, bands)
    wait_copies(place, corners)


def fold_kernel(canvas_ref, cur_ref, *refs):
    if len(refs) == 10:
        light_in_ref, refs = None, refs
    else:
        light_in_ref, refs = refs[0], refs[1:]
    fold_body(canvas_ref, cur_ref, light_in_ref, *refs)


def fold_body(canvas_ref, cur_ref, light_in_ref, out_ref, light_ref, mid_bufs, corner_bufs, col_bufs, band_ref, total_ref, send_sems, recv_sems, band_sem):
    rows = out_ref.shape[1]
    cols = out_ref.shape[2]
    margin = (canvas_ref.shape[2] - cols) // 2
    ext_cols = cols + 2 * margin
    place = mesh_place()
    me_r, me_c, n_r, n_c = place
    own_band = pltpu.make_async_copy(canvas_ref.at[:, margin : margin + rows, :], band_ref, band_sem)
    own_band.start()
    neighbour_barrier(me_r, me_c, n_r, n_c)
    top = slice(0, margin)
    bottom = slice(margin + rows, 2 * margin + rows)
    left = slice(0, margin)
    inner = slice(margin, margin + cols)
    right = slice(margin + cols, ext_cols)
    corners = start_copies(
        place,
        [
            ((-1, 0), canvas_ref.at[:, top, left], corner_bufs.at[0, 0]),
            ((-1, 0), canvas_ref.at[:, top, right], corner_bufs.at[0, 1]),
            ((1, 0), canvas_ref.at[:, bottom, left], corner_bufs.at[1, 0]),
            ((1, 0), canvas_ref.at[:, bottom, right], corner_bufs.at[1, 1]),
        ],
        send_sems.at[0:4],
        recv_sems.at[0:4],
    )
    mids = start_copies(
        place,
        [
            ((-1, 0), canvas_ref.at[:, top, inner], mid_bufs.at[0]),
            ((1, 0), canvas_ref.at[:, bottom, inner], mid_bufs.at[1]),
        ],
        send_sems.at[4:6],
        recv_sems.at[4:6],
    )
    wait_copies(place, corners)
    own_band.wait()
    for slot, source_r in ((0, me_r + 1), (1, me_r - 1)):

        @pl.when(exists(source_r, me_c, n_r, n_c))
        def _():
            band_ref[:, :, left] += corner_bufs[slot, 0]
            band_ref[:, :, right] += corner_bufs[slot, 1]

    strips = start_copies(
        place,
        [
            ((0, -1), band_ref.at[:, :, left], col_bufs.at[0]),
            ((0, 1), band_ref.at[:, :, right], col_bufs.at[1]),
        ],
        send_sems.at[6:8],
        recv_sems.at[6:8],
    )
    wait_copies(place, mids)
    total_ref[...] = band_ref[:, :, inner]
    for slot, source_r in ((0, me_r + 1), (1, me_r - 1)):

        @pl.when(exists(source_r, me_c, n_r, n_c))
        def _():
            total_ref[...] += mid_bufs[slot]

    wait_copies(place, strips)

    @pl.when(exists(me_r, me_c + 1, n_r, n_c))
    def _():
        total_ref[:, :, cols - margin : cols] += col_bufs[0]

    @pl.when(exists(me_r, me_c - 1, n_r, n_c))
    def _():
        total_ref[:, :, 0:margin] += col_bufs[1]

    fields = cur_ref.shape[0]
    if total_ref.shape[0] > fields:
        light_ref[...] = total_ref[fields]
    else:
        light_ref[...] = light_in_ref[...]
    out_ref[...] = cur_ref[...] - total_ref[0:fields] / (light_ref[...] + DAMPING)


def exchange_halo(current, margin):
    depth, rows, cols = current.shape
    return pl.pallas_call(
        halo_kernel,
        out_shape=jax.ShapeDtypeStruct((depth, rows + 2 * margin, cols + 2 * margin), jnp.float32),
        in_specs=[VMEM_SPEC],
        out_specs=pl.BlockSpec(memory_space=pl.ANY),
        scratch_shapes=[
            pltpu.VMEM((depth, margin, cols + 2 * margin), jnp.float32),
            pltpu.SemaphoreType.DMA((8,)),
            pltpu.SemaphoreType.DMA((8,)),
            pltpu.SemaphoreType.DMA((5,)),
        ],
        compiler_params=pltpu.CompilerParams(
            vmem_limit_bytes=60 * 1024 * 1024, has_side_effects=True, collective_id=0
        ),
    )(current)


def fold_and_step(canvas, current, light, margin):
    depth, ext_rows, ext_cols = canvas.shape
    fields, rows, cols = current.shape
    return pl.pallas_call(
        fold_kernel,
        out_shape=(
            jax.ShapeDtypeStruct((fields, rows, cols), jnp.float32),
            jax.ShapeDtypeStruct((rows, cols), jnp.float32),
        ),
        in_specs=[pl.BlockSpec(memory_space=pl.ANY), VMEM_SPEC] + ([] if light is None else [VMEM_SPEC]),
        out_specs=(VMEM_SPEC, VMEM_SPEC),
        scratch_shapes=[
            pltpu.VMEM((2, depth, margin, cols), jnp.float32),
            pltpu.VMEM((2, 2, depth, margin, margin), jnp.float32),
            pltpu.VMEM((2, depth, rows, margin), jnp.float32),
            pltpu.VMEM((depth, rows, ext_cols), jnp.float32),
            pltpu.VMEM((depth, rows, cols), jnp.float32),
            pltpu.SemaphoreType.DMA((8,)),
            pltpu.SemaphoreType.DMA((8,)),
            pltpu.SemaphoreType.DMA(()),
        ],
        compiler_params=pltpu.CompilerParams(
            vmem_limit_bytes=60 * 1024 * 1024, has_side_effects=True, collective_id=depth
        ),
    )(canvas, current, *([] if light is None else [light]))


def on_device(object_field, probe_field, amplitudes, centres, counts):
    size_probe = probe_field.shape[1]
    margin = size_probe // 2
    block_rows = object_field.shape[1]
    block_cols = object_field.shape[2]
    tables = split_tables(size_probe)
    spots = centres[0, 0]
    own_amps = amplitudes[0, 0]
    column_counts = counts[:, 0]
    ext_shape = (block_rows + size_probe, block_cols + size_probe)

    current = object_field
    illumination = None
    for sweep_index in range(ITERS):
        extended = exchange_halo(current, margin)
        channels = 3 if sweep_index == 0 else 2
        canvas = gradient_canvas(
            channels, ext_shape, spots, column_counts, extended, probe_field, own_amps, tables
        )
        current, illumination = fold_and_step(canvas, current, illumination, margin)
    return current


def solution(mesh):
    return jax.shard_map(
        on_device,
        mesh=mesh,
        in_specs=(
            P(None, "sx", "sy"),
            P(),
            P("sx", "sy", None, None, None),
            P("sx", "sy", None, None),
            P(None, "sy"),
        ),
        out_specs=P(None, "sx", "sy"),
        check_vma=False,
    )
```

```python
import functools
import math

import jax
import ml_dtypes
import numpy as np
import jax.numpy as jnp
from jax import lax
from jax.sharding import PartitionSpec as P
from jax.experimental import pallas as pl
from jax.experimental.pallas import tpu as pltpu

ITERS = 2


SMOOTH = 1.0
DAMPING = 1.0


def with_halo(cells, sides, width):
    for axis, dim in sides:
        count = lax.axis_size(axis)
        ends = count - 1
        head = lax.slice_in_dim(cells, 0, width, axis=dim)
        tail = lax.slice_in_dim(cells, cells.shape[dim] - width, cells.shape[dim], axis=dim)
        cells = jnp.concatenate(
            [
                lax.ppermute(tail, axis, [(i, (i + 1) % count) for i in range(ends)]),
                cells,
                lax.ppermute(head, axis, [((i + 1) % count, i) for i in range(ends)]),
            ],
            axis=dim,
        )
    return cells


def dft_tables(length):
    index_values = jnp.arange(length, dtype=jnp.int32)
    product_mod = index_values[:, None] * index_values[None, :] % length
    angles = product_mod.astype(jnp.float32) * (2.0 * math.pi / length)
    scaling = 1.0 / math.sqrt(length)
    return (jnp.cos(angles) * scaling, -jnp.sin(angles) * scaling)


def matmul_exact(left_side, right_side):
    return jnp.dot(left_side, right_side, precision=lax.Precision.HIGHEST)


def complex_left(table_real, table_imag, field_real, field_imag):
    out_real = matmul_exact(table_real, field_real) - matmul_exact(table_imag, field_imag)
    out_imag = matmul_exact(table_real, field_imag) + matmul_exact(table_imag, field_real)
    return (out_real, out_imag)


def complex_right(field_real, field_imag, table_real, table_imag):
    out_real = matmul_exact(field_real, table_real) - matmul_exact(field_imag, table_imag)
    out_imag = matmul_exact(field_real, table_imag) + matmul_exact(field_imag, table_real)
    return (out_real, out_imag)


def position_gradient(object_patch, probe_field, amplitude, table_real, table_imag):
    probe_real = probe_field[0]
    probe_imag = probe_field[1]
    exit_real = probe_real * object_patch[0] - probe_imag * object_patch[1]
    exit_imag = probe_real * object_patch[1] + probe_imag * object_patch[0]
    half_real, half_imag = complex_left(table_real, table_imag, exit_real, exit_imag)
    far_real, far_imag = complex_right(half_real, half_imag, table_real, table_imag)
    factor = 1.0 - amplitude / jnp.sqrt(far_real * far_real + far_imag * far_imag + SMOOTH)
    miss_real = far_real * factor
    miss_imag = far_imag * factor
    back_real, back_imag = complex_left(table_real, -table_imag, miss_real, miss_imag)
    near_real, near_imag = complex_right(back_real, back_imag, table_real, -table_imag)
    return jnp.stack(
        [
            probe_real * near_real + probe_imag * near_imag,
            probe_real * near_imag - probe_imag * near_real,
        ]
    )


def add_patch(canvas, patch_values, corner_row, corner_col):
    zero_index = jnp.zeros((), jnp.int32)
    starts = (zero_index, corner_row, corner_col)
    present = lax.dynamic_slice(canvas, starts, patch_values.shape)
    return lax.dynamic_update_slice(canvas, present + patch_values, starts)


def fold_rows(extended, margin, length):
    middle_part = extended[:, 2 * margin : 2 * margin + length]
    upper_rim = extended[:, :margin]
    lower_rim = extended[:, extended.shape[1] - margin :]
    middle_part = middle_part.at[:, :margin].add(upper_rim)
    return middle_part.at[:, length - margin :].add(lower_rim)


def fold_cols(extended, margin, length):
    middle_part = extended[:, :, 2 * margin : 2 * margin + length]
    left_rim = extended[:, :, :margin]
    right_rim = extended[:, :, extended.shape[2] - margin :]
    middle_part = middle_part.at[:, :, :margin].add(left_rim)
    return middle_part.at[:, :, length - margin :].add(right_rim)


def settle(stacked, margin, block_rows, block_cols):
    full_ext = with_halo(stacked, (("sx", 1), ("sy", 2)), margin)
    return fold_cols(fold_rows(full_ext, margin, block_rows), margin, block_cols)


def local_pass(canvas, extended, spots, own_amps, probe_field, table_real, table_imag, upper_bound):
    size_probe = probe_field.shape[1]

    def local_step(slot_index, canvas_state):
        row_start = spots[slot_index, 0]
        col_start = spots[slot_index, 1]
        zero_index = jnp.zeros((), jnp.int32)
        object_patch = lax.dynamic_slice(
            extended, (zero_index, row_start, col_start), (2, size_probe, size_probe)
        )
        update = position_gradient(
            object_patch, probe_field, own_amps[slot_index], table_real, table_imag
        )
        return add_patch(canvas_state, update, row_start, col_start)

    return lax.fori_loop(0, upper_bound, local_step, canvas)


def dot_exact(left_side, right_side):
    return jnp.dot(
        left_side, right_side, precision=lax.Precision.HIGHEST, preferred_element_type=jnp.float32
    )


def window_tools(size, row, col):
    lanes = 128
    sublanes = 8
    wide = size + lanes
    tall = size + sublanes
    row_base = pl.multiple_of((row // sublanes) * sublanes, sublanes)
    col_base = pl.multiple_of((col // lanes) * lanes, lanes)
    row_shift = row % sublanes
    col_shift = col % lanes
    rows = pl.ds(row_base, tall)
    cols = pl.ds(col_base, wide)

    def take(ref, channel):
        block = ref[channel, rows, cols]
        block = pltpu.roll(block, (tall - row_shift) % tall, 0)
        return pltpu.roll(block, (wide - col_shift) % wide, 1)[:size, :size]

    def put(ref, channel, values):
        block = jnp.concatenate([values, jnp.zeros((size, lanes), jnp.float32)], axis=1)
        block = jnp.concatenate([block, jnp.zeros((sublanes, wide), jnp.float32)], axis=0)
        block = pltpu.roll(pltpu.roll(block, col_shift, 1), row_shift, 0)
        ref[channel, rows, cols] += block

    return take, put


def split_bf16(values):
    scaled = values * 65537.0
    high = scaled - (scaled - values)
    return high.astype(jnp.bfloat16), (values - high).astype(jnp.bfloat16)


def dot_split(left_parts, right_parts):
    left_high, left_low = left_parts
    right_high, right_low = right_parts
    total = jnp.dot(left_high, right_high, preferred_element_type=jnp.float32)
    total += jnp.dot(left_high, right_low, preferred_element_type=jnp.float32)
    return total + jnp.dot(left_low, right_high, preferred_element_type=jnp.float32)


def gradient_kernel(spots_ref, count_ref, ext_ref, probe_ref, amps_ref, tables_ref, out_ref):
    size = probe_ref.shape[1]
    out_ref[...] = jnp.zeros(out_ref.shape, jnp.float32)
    live = count_ref[lax.axis_index("sx")]
    with_power = out_ref.shape[0] > 2
    for slot in range(amps_ref.shape[0]):

        @pl.when(slot < live)
        def _():
            take, put = window_tools(size, spots_ref[slot, 0], spots_ref[slot, 1])
            probe_real = probe_ref[0]
            probe_imag = probe_ref[1]
            real_parts = (tables_ref[0], tables_ref[1])
            imag_parts = (tables_ref[2], tables_ref[3])

            def left(field_real, field_imag, sign):
                both = split_bf16(jnp.concatenate([field_real, field_imag], axis=1))
                by_real = dot_split(real_parts, both)
                by_imag = dot_split(imag_parts, both)
                out_real = by_real[:, :size] - sign * by_imag[:, size:]
                out_imag = by_real[:, size:] + sign * by_imag[:, :size]
                return out_real, out_imag

            def right(field_real, field_imag, sign):
                both = split_bf16(jnp.concatenate([field_real, field_imag], axis=0))
                by_real = dot_split(both, real_parts)
                by_imag = dot_split(both, imag_parts)
                out_real = by_real[:size] - sign * by_imag[size:]
                out_imag = by_imag[:size] * sign + by_real[size:]
                return out_real, out_imag

            obj_real = take(ext_ref, 0)
            obj_imag = take(ext_ref, 1)
            exit_real = probe_real * obj_real - probe_imag * obj_imag
            exit_imag = probe_real * obj_imag + probe_imag * obj_real
            half_real, half_imag = left(exit_real, exit_imag, 1.0)
            far_real, far_imag = right(half_real, half_imag, 1.0)
            factor = 1.0 - amps_ref[slot] / jnp.sqrt(far_real * far_real + far_imag * far_imag + SMOOTH)
            miss_real = far_real * factor
            miss_imag = far_imag * factor
            back_real, back_imag = left(miss_real, miss_imag, -1.0)
            near_real, near_imag = right(back_real, back_imag, -1.0)
            put(out_ref, 0, probe_real * near_real + probe_imag * near_imag)
            put(out_ref, 1, probe_real * near_imag - probe_imag * near_real)
            if with_power:
                put(out_ref, 2, probe_real * probe_real + probe_imag * probe_imag)


def power_kernel(spots_ref, count_ref, probe_ref, out_ref):
    size = probe_ref.shape[1]
    out_ref[...] = jnp.zeros(out_ref.shape, jnp.float32)
    power = probe_ref[0] * probe_ref[0] + probe_ref[1] * probe_ref[1]
    for slot in range(spots_ref.shape[0]):

        @pl.when(slot < count_ref[0])
        def _():
            _, put = window_tools(size, spots_ref[slot, 0], spots_ref[slot, 1])
            put(out_ref, 0, power)


VMEM_SPEC = pl.BlockSpec(memory_space=pltpu.VMEM)
SMEM_SPEC = pl.BlockSpec(memory_space=pltpu.SMEM)
KERNEL_PARAMS = pltpu.CompilerParams(vmem_limit_bytes=60 * 1024 * 1024)


def split_tables(length):
    index_values = np.arange(length, dtype=np.int32)
    product_mod = index_values[:, None] * index_values[None, :] % length
    angles = product_mod.astype(np.float32) * np.float32(2.0 * math.pi / length)
    scaling = np.float32(1.0 / math.sqrt(length))
    parts = []
    for table in (np.cos(angles) * scaling, -np.sin(angles) * scaling):
        table = table.astype(np.float32)
        scaled = table * np.float32(65537.0)
        high = scaled - (scaled - table)
        parts += [high.astype(ml_dtypes.bfloat16), (table - high).astype(ml_dtypes.bfloat16)]
    return jnp.asarray(np.stack(parts))


def gradient_canvas(channels, ext_shape, spots, count, extended, probe_field, own_amps, tables):
    return pl.pallas_call(
        gradient_kernel,
        out_shape=jax.ShapeDtypeStruct((channels,) + ext_shape, jnp.float32),
        in_specs=[SMEM_SPEC, SMEM_SPEC] + [VMEM_SPEC] * 4,
        out_specs=VMEM_SPEC,
        compiler_params=KERNEL_PARAMS,
    )(spots, count, extended, probe_field, own_amps, tables)


def power_canvas(ext_shape, spots, count, probe_field):
    return pl.pallas_call(
        power_kernel,
        out_shape=jax.ShapeDtypeStruct((1,) + ext_shape, jnp.float32),
        in_specs=[SMEM_SPEC, SMEM_SPEC, VMEM_SPEC],
        out_specs=VMEM_SPEC,
        compiler_params=KERNEL_PARAMS,
    )(spots, count.reshape(1), probe_field)


def mesh_place():
    return (
        lax.axis_index("sx"),
        lax.axis_index("sy"),
        lax.axis_size("sx"),
        lax.axis_size("sy"),
    )


def exists(row_dev, col_dev, row_count, col_count):
    return (row_dev >= 0) & (row_dev < row_count) & (col_dev >= 0) & (col_dev < col_count)


ROW_NEIGHBOURS = [(-1, 0), (1, 0)]
COL_NEIGHBOURS = [(0, -1), (0, 1)]


def neighbour_barrier(me_r, me_c, n_r, n_c):
    barrier = pltpu.get_barrier_semaphore()
    greeted = jnp.int32(0)
    for dr, dc in ROW_NEIGHBOURS + COL_NEIGHBOURS:
        present = exists(me_r + dr, me_c + dc, n_r, n_c)

        @pl.when(present)
        def _():
            pl.semaphore_signal(
                barrier, inc=1, device_id=(me_r + dr, me_c + dc), device_id_type=pl.DeviceIdType.MESH
            )

        greeted = greeted + present.astype(jnp.int32)
    pl.semaphore_wait(barrier, greeted)


def start_copies(place, pieces, send_sems, recv_sems):
    me_r, me_c, n_r, n_c = place
    copies = []
    for index, ((dr, dc), source, target) in enumerate(pieces):
        copy = pltpu.make_async_remote_copy(
            src_ref=source,
            dst_ref=target,
            send_sem=send_sems.at[index],
            recv_sem=recv_sems.at[index],
            device_id=(me_r + dr, me_c + dc),
            device_id_type=pl.DeviceIdType.MESH,
        )
        copies.append(((dr, dc), copy))

        @pl.when(exists(me_r + dr, me_c + dc, n_r, n_c))
        def _():
            copy.start()

    return copies


def wait_copies(place, copies):
    me_r, me_c, n_r, n_c = place
    for (dr, dc), copy in copies:

        @pl.when(exists(me_r + dr, me_c + dc, n_r, n_c))
        def _():
            copy.wait_send()

        @pl.when(exists(me_r - dr, me_c - dc, n_r, n_c))
        def _():
            copy.wait_recv()


def swap(place, pieces, send_sems, recv_sems):
    wait_copies(place, start_copies(place, pieces, send_sems, recv_sems))


def halo_kernel(cur_ref, ext_ref, zeros_ref, send_sems, recv_sems, local_sems):
    rows = cur_ref.shape[1]
    cols = cur_ref.shape[2]
    margin = (ext_ref.shape[2] - cols) // 2
    ext_cols = cols + 2 * margin
    place = mesh_place()
    me_r, me_c, n_r, n_c = place
    middle = slice(margin, margin + rows)
    own = pltpu.make_async_copy(cur_ref, ext_ref.at[:, middle, margin : margin + cols], local_sems.at[0])
    own.start()
    zeros_ref[...] = jnp.zeros(zeros_ref.shape, jnp.float32)
    unreached = [
        ((0, 1), ext_ref.at[:, middle, 0:margin], zeros_ref.at[:, :, 0:margin]),
        ((0, -1), ext_ref.at[:, middle, margin + cols : ext_cols], zeros_ref.at[:, :, 0:margin]),
        ((1, 0), ext_ref.at[:, 0:margin, :], zeros_ref),
        ((-1, 0), ext_ref.at[:, margin + rows : 2 * margin + rows, :], zeros_ref),
    ]
    blanks = []
    for index, ((dr, dc), target, source) in enumerate(unreached):
        blank = pltpu.make_async_copy(source, target, local_sems.at[index + 1])
        missing = jnp.logical_not(exists(me_r - dr, me_c - dc, n_r, n_c))
        blanks.append((blank, missing))

    neighbour_barrier(me_r, me_c, n_r, n_c)
    for blank, missing in blanks:

        @pl.when(missing)
        def _():
            blank.start()

    above = slice(0, margin)
    below = slice(margin + rows, 2 * margin + rows)
    inner = slice(margin, margin + cols)
    left = slice(0, margin)
    right = slice(margin + cols, ext_cols)
    bands = start_copies(
        place,
        [
            ((-1, 0), cur_ref, ext_ref.at[:, below, inner]),
            ((1, 0), cur_ref, ext_ref.at[:, above, inner]),
        ],
        send_sems.at[0:2],
        recv_sems.at[0:2],
    )
    swap(
        place,
        [
            ((0, -1), cur_ref.at[:, :, 0:margin], ext_ref.at[:, middle, right]),
            ((0, 1), cur_ref.at[:, :, cols - margin : cols], ext_ref.at[:, middle, left]),
        ],
        send_sems.at[2:4],
        recv_sems.at[2:4],
    )
    own.wait()
    for blank, missing in blanks:

        @pl.when(missing)
        def _():
            blank.wait()

    corners = start_copies(
        place,
        [
            ((-1, 0), ext_ref.at[:, middle, left], ext_ref.at[:, below, left]),
            ((-1, 0), ext_ref.at[:, middle, right], ext_ref.at[:, below, right]),
            ((1, 0), ext_ref.at[:, middle, left], ext_ref.at[:, above, left]),
            ((1, 0), ext_ref.at[:, middle, right], ext_ref.at[:, above, right]),
        ],
        send_sems.at[4:8],
        recv_sems.at[4:8],
    )
    wait_copies(place, bands)
    wait_copies(place, corners)


def fold_kernel(apply_step, canvas_ref, cur_ref, *refs):
    if len(refs) == 10:
        light_in_ref, refs = None, refs
    else:
        light_in_ref, refs = refs[0], refs[1:]
    fold_body(apply_step, canvas_ref, cur_ref, light_in_ref, *refs)


def step_kernel(cur_ref, grad_ref, light_ref, out_ref):
    out_ref[...] = cur_ref[...] - grad_ref[...] / (light_ref[...] + DAMPING)


def fold_body(apply_step, canvas_ref, cur_ref, light_in_ref, out_ref, light_ref, mid_bufs, corner_bufs, col_bufs, band_ref, total_ref, send_sems, recv_sems, band_sem):
    rows = out_ref.shape[1]
    cols = out_ref.shape[2]
    margin = (canvas_ref.shape[2] - cols) // 2
    ext_cols = cols + 2 * margin
    place = mesh_place()
    me_r, me_c, n_r, n_c = place
    own_band = pltpu.make_async_copy(canvas_ref.at[:, margin : margin + rows, :], band_ref, band_sem)
    own_band.start()
    neighbour_barrier(me_r, me_c, n_r, n_c)
    top = slice(0, margin)
    bottom = slice(margin + rows, 2 * margin + rows)
    left = slice(0, margin)
    inner = slice(margin, margin + cols)
    right = slice(margin + cols, ext_cols)
    corners = start_copies(
        place,
        [
            ((-1, 0), canvas_ref.at[:, top, left], corner_bufs.at[0, 0]),
            ((-1, 0), canvas_ref.at[:, top, right], corner_bufs.at[0, 1]),
            ((1, 0), canvas_ref.at[:, bottom, left], corner_bufs.at[1, 0]),
            ((1, 0), canvas_ref.at[:, bottom, right], corner_bufs.at[1, 1]),
        ],
        send_sems.at[0:4],
        recv_sems.at[0:4],
    )
    mids = start_copies(
        place,
        [
            ((-1, 0), canvas_ref.at[:, top, inner], mid_bufs.at[0]),
            ((1, 0), canvas_ref.at[:, bottom, inner], mid_bufs.at[1]),
        ],
        send_sems.at[4:6],
        recv_sems.at[4:6],
    )
    wait_copies(place, corners)
    own_band.wait()
    for slot, source_r in ((0, me_r + 1), (1, me_r - 1)):

        @pl.when(exists(source_r, me_c, n_r, n_c))
        def _():
            band_ref[:, :, left] += corner_bufs[slot, 0]
            band_ref[:, :, right] += corner_bufs[slot, 1]

    strips = start_copies(
        place,
        [
            ((0, -1), band_ref.at[:, :, left], col_bufs.at[0]),
            ((0, 1), band_ref.at[:, :, right], col_bufs.at[1]),
        ],
        send_sems.at[6:8],
        recv_sems.at[6:8],
    )
    wait_copies(place, mids)
    total_ref[...] = band_ref[:, :, inner]
    for slot, source_r in ((0, me_r + 1), (1, me_r - 1)):

        @pl.when(exists(source_r, me_c, n_r, n_c))
        def _():
            total_ref[...] += mid_bufs[slot]

    wait_copies(place, strips)

    @pl.when(exists(me_r, me_c + 1, n_r, n_c))
    def _():
        total_ref[:, :, cols - margin : cols] += col_bufs[0]

    @pl.when(exists(me_r, me_c - 1, n_r, n_c))
    def _():
        total_ref[:, :, 0:margin] += col_bufs[1]

    fields = cur_ref.shape[0]
    if total_ref.shape[0] > fields:
        light_ref[...] = total_ref[fields]
    else:
        light_ref[...] = light_in_ref[...]
    if apply_step:
        out_ref[...] = cur_ref[...] - total_ref[0:fields] / (light_ref[...] + DAMPING)
    else:
        out_ref[...] = total_ref[0:fields]


def exchange_halo(current, margin):
    depth, rows, cols = current.shape
    return pl.pallas_call(
        halo_kernel,
        out_shape=jax.ShapeDtypeStruct((depth, rows + 2 * margin, cols + 2 * margin), jnp.float32),
        in_specs=[VMEM_SPEC],
        out_specs=pl.BlockSpec(memory_space=pl.ANY),
        scratch_shapes=[
            pltpu.VMEM((depth, margin, cols + 2 * margin), jnp.float32),
            pltpu.SemaphoreType.DMA((8,)),
            pltpu.SemaphoreType.DMA((8,)),
            pltpu.SemaphoreType.DMA((5,)),
        ],
        compiler_params=pltpu.CompilerParams(
            vmem_limit_bytes=60 * 1024 * 1024, has_side_effects=True, collective_id=0
        ),
    )(current)


def fold_and_step(canvas, current, light, margin, apply_step=True):
    depth, ext_rows, ext_cols = canvas.shape
    fields, rows, cols = current.shape
    return pl.pallas_call(
        functools.partial(fold_kernel, apply_step),
        out_shape=(
            jax.ShapeDtypeStruct((fields, rows, cols), jnp.float32),
            jax.ShapeDtypeStruct((rows, cols), jnp.float32),
        ),
        in_specs=[pl.BlockSpec(memory_space=pl.ANY), VMEM_SPEC] + ([] if light is None else [VMEM_SPEC]),
        out_specs=(VMEM_SPEC, VMEM_SPEC),
        scratch_shapes=[
            pltpu.VMEM((2, depth, margin, cols), jnp.float32),
            pltpu.VMEM((2, 2, depth, margin, margin), jnp.float32),
            pltpu.VMEM((2, depth, rows, margin), jnp.float32),
            pltpu.VMEM((depth, rows, ext_cols), jnp.float32),
            pltpu.VMEM((depth, rows, cols), jnp.float32),
            pltpu.SemaphoreType.DMA((8,)),
            pltpu.SemaphoreType.DMA((8,)),
            pltpu.SemaphoreType.DMA(()),
        ],
        compiler_params=pltpu.CompilerParams(
            vmem_limit_bytes=60 * 1024 * 1024, has_side_effects=True, collective_id=depth
        ),
    )(canvas, current, *([] if light is None else [light]))


def on_device(object_field, probe_field, amplitudes, centres, counts):
    size_probe = probe_field.shape[1]
    margin = size_probe // 2
    block_rows = object_field.shape[1]
    block_cols = object_field.shape[2]
    tables = split_tables(size_probe)
    spots = centres[0, 0]
    own_amps = amplitudes[0, 0]
    column_counts = counts[:, 0]
    ext_shape = (block_rows + size_probe, block_cols + size_probe)

    current = object_field
    illumination = None
    for sweep_index in range(ITERS):
        extended = exchange_halo(current, margin)
        channels = 3 if sweep_index == 0 else 2
        canvas = gradient_canvas(
            channels, ext_shape, spots, column_counts, extended, probe_field, own_amps, tables
        )
        if sweep_index < ITERS - 1:
            current, illumination = fold_and_step(canvas, current, illumination, margin)
        else:
            gradient, _ = fold_and_step(canvas, current, illumination, margin, apply_step=False)
            current = pl.pallas_call(
                step_kernel,
                out_shape=jax.ShapeDtypeStruct(current.shape, jnp.float32),
                in_specs=[VMEM_SPEC] * 3,
                out_specs=VMEM_SPEC,
            )(current, gradient, illumination)
    return current


def solution(mesh):
    return jax.shard_map(
        on_device,
        mesh=mesh,
        in_specs=(
            P(None, "sx", "sy"),
            P(),
            P("sx", "sy", None, None, None),
            P("sx", "sy", None, None),
            P(None, "sy"),
        ),
        out_specs=P(None, "sx", "sy"),
        check_vma=False,
    )
```

```python
import math

import jax
import ml_dtypes
import numpy as np
import jax.numpy as jnp
from jax import lax
from jax.sharding import PartitionSpec as P
from jax.experimental import pallas as pl
from jax.experimental.pallas import tpu as pltpu

ITERS = 2


SMOOTH = 1.0
DAMPING = 1.0


def with_halo(cells, sides, width):
    for axis, dim in sides:
        count = lax.axis_size(axis)
        ends = count - 1
        head = lax.slice_in_dim(cells, 0, width, axis=dim)
        tail = lax.slice_in_dim(cells, cells.shape[dim] - width, cells.shape[dim], axis=dim)
        cells = jnp.concatenate(
            [
                lax.ppermute(tail, axis, [(i, (i + 1) % count) for i in range(ends)]),
                cells,
                lax.ppermute(head, axis, [((i + 1) % count, i) for i in range(ends)]),
            ],
            axis=dim,
        )
    return cells


def dft_tables(length):
    index_values = jnp.arange(length, dtype=jnp.int32)
    product_mod = index_values[:, None] * index_values[None, :] % length
    angles = product_mod.astype(jnp.float32) * (2.0 * math.pi / length)
    scaling = 1.0 / math.sqrt(length)
    return (jnp.cos(angles) * scaling, -jnp.sin(angles) * scaling)


def matmul_exact(left_side, right_side):
    return jnp.dot(left_side, right_side, precision=lax.Precision.HIGHEST)


def complex_left(table_real, table_imag, field_real, field_imag):
    out_real = matmul_exact(table_real, field_real) - matmul_exact(table_imag, field_imag)
    out_imag = matmul_exact(table_real, field_imag) + matmul_exact(table_imag, field_real)
    return (out_real, out_imag)


def complex_right(field_real, field_imag, table_real, table_imag):
    out_real = matmul_exact(field_real, table_real) - matmul_exact(field_imag, table_imag)
    out_imag = matmul_exact(field_real, table_imag) + matmul_exact(field_imag, table_real)
    return (out_real, out_imag)


def position_gradient(object_patch, probe_field, amplitude, table_real, table_imag):
    probe_real = probe_field[0]
    probe_imag = probe_field[1]
    exit_real = probe_real * object_patch[0] - probe_imag * object_patch[1]
    exit_imag = probe_real * object_patch[1] + probe_imag * object_patch[0]
    half_real, half_imag = complex_left(table_real, table_imag, exit_real, exit_imag)
    far_real, far_imag = complex_right(half_real, half_imag, table_real, table_imag)
    factor = 1.0 - amplitude / jnp.sqrt(far_real * far_real + far_imag * far_imag + SMOOTH)
    miss_real = far_real * factor
    miss_imag = far_imag * factor
    back_real, back_imag = complex_left(table_real, -table_imag, miss_real, miss_imag)
    near_real, near_imag = complex_right(back_real, back_imag, table_real, -table_imag)
    return jnp.stack(
        [
            probe_real * near_real + probe_imag * near_imag,
            probe_real * near_imag - probe_imag * near_real,
        ]
    )


def add_patch(canvas, patch_values, corner_row, corner_col):
    zero_index = jnp.zeros((), jnp.int32)
    starts = (zero_index, corner_row, corner_col)
    present = lax.dynamic_slice(canvas, starts, patch_values.shape)
    return lax.dynamic_update_slice(canvas, present + patch_values, starts)


def fold_rows(extended, margin, length):
    middle_part = extended[:, 2 * margin : 2 * margin + length]
    upper_rim = extended[:, :margin]
    lower_rim = extended[:, extended.shape[1] - margin :]
    middle_part = middle_part.at[:, :margin].add(upper_rim)
    return middle_part.at[:, length - margin :].add(lower_rim)


def fold_cols(extended, margin, length):
    middle_part = extended[:, :, 2 * margin : 2 * margin + length]
    left_rim = extended[:, :, :margin]
    right_rim = extended[:, :, extended.shape[2] - margin :]
    middle_part = middle_part.at[:, :, :margin].add(left_rim)
    return middle_part.at[:, :, length - margin :].add(right_rim)


def settle(stacked, margin, block_rows, block_cols):
    full_ext = with_halo(stacked, (("sx", 1), ("sy", 2)), margin)
    return fold_cols(fold_rows(full_ext, margin, block_rows), margin, block_cols)


def local_pass(canvas, extended, spots, own_amps, probe_field, table_real, table_imag, upper_bound):
    size_probe = probe_field.shape[1]

    def local_step(slot_index, canvas_state):
        row_start = spots[slot_index, 0]
        col_start = spots[slot_index, 1]
        zero_index = jnp.zeros((), jnp.int32)
        object_patch = lax.dynamic_slice(
            extended, (zero_index, row_start, col_start), (2, size_probe, size_probe)
        )
        update = position_gradient(
            object_patch, probe_field, own_amps[slot_index], table_real, table_imag
        )
        return add_patch(canvas_state, update, row_start, col_start)

    return lax.fori_loop(0, upper_bound, local_step, canvas)


def dot_exact(left_side, right_side):
    return jnp.dot(
        left_side, right_side, precision=lax.Precision.HIGHEST, preferred_element_type=jnp.float32
    )


def window_tools(size, row, col):
    lanes = 128
    sublanes = 8
    wide = size + lanes
    tall = size + sublanes
    row_base = pl.multiple_of((row // sublanes) * sublanes, sublanes)
    col_base = pl.multiple_of((col // lanes) * lanes, lanes)
    row_shift = row % sublanes
    col_shift = col % lanes
    rows = pl.ds(row_base, tall)
    cols = pl.ds(col_base, wide)

    def take(ref, channel):
        block = ref[channel, rows, cols]
        block = pltpu.roll(block, (tall - row_shift) % tall, 0)
        return pltpu.roll(block, (wide - col_shift) % wide, 1)[:size, :size]

    def put(ref, channel, values):
        block = jnp.concatenate([values, jnp.zeros((size, lanes), jnp.float32)], axis=1)
        block = jnp.concatenate([block, jnp.zeros((sublanes, wide), jnp.float32)], axis=0)
        block = pltpu.roll(pltpu.roll(block, col_shift, 1), row_shift, 0)
        ref[channel, rows, cols] += block

    return take, put


def split_bf16(values):
    scaled = values * 65537.0
    high = scaled - (scaled - values)
    return high.astype(jnp.bfloat16), (values - high).astype(jnp.bfloat16)


def dot_split(left_parts, right_parts):
    left_high, left_low = left_parts
    right_high, right_low = right_parts
    total = jnp.dot(left_high, right_high, preferred_element_type=jnp.float32)
    total += jnp.dot(left_high, right_low, preferred_element_type=jnp.float32)
    return total + jnp.dot(left_low, right_high, preferred_element_type=jnp.float32)


def light_block(size, infos_ref, probe_ref, light_ref, power_ref):
    rows, cols = light_ref.shape
    margin = size // 2
    power_ref[...] = jnp.zeros(power_ref.shape, jnp.float32)
    power = probe_ref[0] * probe_ref[0] + probe_ref[1] * probe_ref[1]
    for place in range(9):
        dr = place // 3 - 1
        dc = place % 3 - 1
        for slot in range(2):

            @pl.when(slot < infos_ref[place, 0, 4])
            def _():
                row = dr * rows + infos_ref[place, 0, 2 * slot] + margin
                col = dc * cols + infos_ref[place, 0, 2 * slot + 1] + cols
                _, put = window_tools(size, row, col)
                put(power_ref, 0, power)

    light_ref[...] = power_ref[0, size : size + rows, cols + margin : 2 * cols + margin]


def gradient_kernel(spots_ref, count_ref, ext_ref, probe_ref, amps_ref, tables_ref, *rest):
    size = probe_ref.shape[1]
    if len(rest) > 1:
        infos_ref, out_ref, light_ref, power_ref = rest
        light_block(size, infos_ref, probe_ref, light_ref, power_ref)
    else:
        (out_ref,) = rest
    out_ref[...] = jnp.zeros(out_ref.shape, jnp.float32)
    live = count_ref[lax.axis_index("sx")]
    with_power = out_ref.shape[0] > 2
    for slot in range(amps_ref.shape[0]):

        @pl.when(slot < live)
        def _():
            take, put = window_tools(size, spots_ref[slot, 0], spots_ref[slot, 1])
            probe_real = probe_ref[0]
            probe_imag = probe_ref[1]
            real_parts = (tables_ref[0], tables_ref[1])
            imag_parts = (tables_ref[2], tables_ref[3])

            def left(field_real, field_imag, sign):
                both = split_bf16(jnp.concatenate([field_real, field_imag], axis=1))
                by_real = dot_split(real_parts, both)
                by_imag = dot_split(imag_parts, both)
                out_real = by_real[:, :size] - sign * by_imag[:, size:]
                out_imag = by_real[:, size:] + sign * by_imag[:, :size]
                return out_real, out_imag

            def right(field_real, field_imag, sign):
                both = split_bf16(jnp.concatenate([field_real, field_imag], axis=0))
                by_real = dot_split(both, real_parts)
                by_imag = dot_split(both, imag_parts)
                out_real = by_real[:size] - sign * by_imag[size:]
                out_imag = by_imag[:size] * sign + by_real[size:]
                return out_real, out_imag

            obj_real = take(ext_ref, 0)
            obj_imag = take(ext_ref, 1)
            exit_real = probe_real * obj_real - probe_imag * obj_imag
            exit_imag = probe_real * obj_imag + probe_imag * obj_real
            half_real, half_imag = left(exit_real, exit_imag, 1.0)
            far_real, far_imag = right(half_real, half_imag, 1.0)
            factor = 1.0 - amps_ref[slot] / jnp.sqrt(far_real * far_real + far_imag * far_imag + SMOOTH)
            miss_real = far_real * factor
            miss_imag = far_imag * factor
            back_real, back_imag = left(miss_real, miss_imag, -1.0)
            near_real, near_imag = right(back_real, back_imag, -1.0)
            put(out_ref, 0, probe_real * near_real + probe_imag * near_imag)
            put(out_ref, 1, probe_real * near_imag - probe_imag * near_real)
            if with_power:
                put(out_ref, 2, probe_real * probe_real + probe_imag * probe_imag)


def power_kernel(spots_ref, count_ref, probe_ref, out_ref):
    size = probe_ref.shape[1]
    out_ref[...] = jnp.zeros(out_ref.shape, jnp.float32)
    power = probe_ref[0] * probe_ref[0] + probe_ref[1] * probe_ref[1]
    for slot in range(spots_ref.shape[0]):

        @pl.when(slot < count_ref[0])
        def _():
            _, put = window_tools(size, spots_ref[slot, 0], spots_ref[slot, 1])
            put(out_ref, 0, power)


VMEM_SPEC = pl.BlockSpec(memory_space=pltpu.VMEM)
SMEM_SPEC = pl.BlockSpec(memory_space=pltpu.SMEM)
KERNEL_PARAMS = pltpu.CompilerParams(vmem_limit_bytes=60 * 1024 * 1024)


def split_tables(length):
    index_values = np.arange(length, dtype=np.int32)
    product_mod = index_values[:, None] * index_values[None, :] % length
    angles = product_mod.astype(np.float32) * np.float32(2.0 * math.pi / length)
    scaling = np.float32(1.0 / math.sqrt(length))
    parts = []
    for table in (np.cos(angles) * scaling, -np.sin(angles) * scaling):
        table = table.astype(np.float32)
        scaled = table * np.float32(65537.0)
        high = scaled - (scaled - table)
        parts += [high.astype(ml_dtypes.bfloat16), (table - high).astype(ml_dtypes.bfloat16)]
    return jnp.asarray(np.stack(parts))


def gradient_canvas(channels, ext_shape, spots, count, extended, probe_field, own_amps, tables, infos=None):
    rows = ext_shape[0] - probe_field.shape[1]
    cols = ext_shape[1] - probe_field.shape[1]
    size = probe_field.shape[1]
    out_shape = jax.ShapeDtypeStruct((channels,) + ext_shape, jnp.float32)
    in_specs = [SMEM_SPEC, SMEM_SPEC] + [VMEM_SPEC] * 4
    args = [spots, count, extended, probe_field, own_amps, tables]
    scratch = []
    out_specs = VMEM_SPEC
    if infos is not None:
        out_shape = (out_shape, jax.ShapeDtypeStruct((rows, cols), jnp.float32))
        out_specs = (VMEM_SPEC, VMEM_SPEC)
        in_specs.append(SMEM_SPEC)
        args.append(infos)
        scratch = [pltpu.VMEM((1, 2 * rows + size // 2 + size + 8, 3 * cols + size), jnp.float32)]
    return pl.pallas_call(
        gradient_kernel,
        out_shape=out_shape,
        in_specs=in_specs,
        out_specs=out_specs,
        scratch_shapes=scratch,
        compiler_params=KERNEL_PARAMS,
    )(*args)


def power_canvas(ext_shape, spots, count, probe_field):
    return pl.pallas_call(
        power_kernel,
        out_shape=jax.ShapeDtypeStruct((1,) + ext_shape, jnp.float32),
        in_specs=[SMEM_SPEC, SMEM_SPEC, VMEM_SPEC],
        out_specs=VMEM_SPEC,
        compiler_params=KERNEL_PARAMS,
    )(spots, count.reshape(1), probe_field)


def mesh_place():
    return (
        lax.axis_index("sx"),
        lax.axis_index("sy"),
        lax.axis_size("sx"),
        lax.axis_size("sy"),
    )


def exists(row_dev, col_dev, row_count, col_count):
    return (row_dev >= 0) & (row_dev < row_count) & (col_dev >= 0) & (col_dev < col_count)


ROW_NEIGHBOURS = [(-1, 0), (1, 0)]
COL_NEIGHBOURS = [(0, -1), (0, 1)]


def neighbour_barrier(me_r, me_c, n_r, n_c):
    barrier = pltpu.get_barrier_semaphore()
    greeted = jnp.int32(0)
    for dr, dc in ROW_NEIGHBOURS + COL_NEIGHBOURS:
        present = exists(me_r + dr, me_c + dc, n_r, n_c)

        @pl.when(present)
        def _():
            pl.semaphore_signal(
                barrier, inc=1, device_id=(me_r + dr, me_c + dc), device_id_type=pl.DeviceIdType.MESH
            )

        greeted = greeted + present.astype(jnp.int32)
    pl.semaphore_wait(barrier, greeted)


def start_copies(place, pieces, send_sems, recv_sems):
    me_r, me_c, n_r, n_c = place
    copies = []
    for index, ((dr, dc), source, target) in enumerate(pieces):
        copy = pltpu.make_async_remote_copy(
            src_ref=source,
            dst_ref=target,
            send_sem=send_sems.at[index],
            recv_sem=recv_sems.at[index],
            device_id=(me_r + dr, me_c + dc),
            device_id_type=pl.DeviceIdType.MESH,
        )
        copies.append(((dr, dc), copy))

        @pl.when(exists(me_r + dr, me_c + dc, n_r, n_c))
        def _():
            copy.start()

    return copies


def wait_copies(place, copies):
    me_r, me_c, n_r, n_c = place
    for (dr, dc), copy in copies:

        @pl.when(exists(me_r + dr, me_c + dc, n_r, n_c))
        def _():
            copy.wait_send()

        @pl.when(exists(me_r - dr, me_c - dc, n_r, n_c))
        def _():
            copy.wait_recv()


def swap(place, pieces, send_sems, recv_sems):
    wait_copies(place, start_copies(place, pieces, send_sems, recv_sems))


def halo_kernel(cur_ref, info_ref, ext_ref, infos_ref, zeros_ref, send_sems, recv_sems, local_sems):
    rows = cur_ref.shape[1]
    cols = cur_ref.shape[2]
    margin = (ext_ref.shape[2] - cols) // 2
    ext_cols = cols + 2 * margin
    place = mesh_place()
    me_r, me_c, n_r, n_c = place
    middle = slice(margin, margin + rows)
    own = pltpu.make_async_copy(cur_ref, ext_ref.at[:, middle, margin : margin + cols], local_sems.at[0])
    own.start()
    infos_ref[...] = jnp.zeros(infos_ref.shape, jnp.int32)
    infos_ref[4] = info_ref[...]
    zeros_ref[...] = jnp.zeros(zeros_ref.shape, jnp.float32)
    unreached = [
        ((0, 1), ext_ref.at[:, middle, 0:margin], zeros_ref.at[:, :, 0:margin]),
        ((0, -1), ext_ref.at[:, middle, margin + cols : ext_cols], zeros_ref.at[:, :, 0:margin]),
        ((1, 0), ext_ref.at[:, 0:margin, :], zeros_ref),
        ((-1, 0), ext_ref.at[:, margin + rows : 2 * margin + rows, :], zeros_ref),
    ]
    blanks = []
    for index, ((dr, dc), target, source) in enumerate(unreached):
        blank = pltpu.make_async_copy(source, target, local_sems.at[index + 1])
        missing = jnp.logical_not(exists(me_r - dr, me_c - dc, n_r, n_c))
        blanks.append((blank, missing))

    neighbour_barrier(me_r, me_c, n_r, n_c)
    for blank, missing in blanks:

        @pl.when(missing)
        def _():
            blank.start()

    above = slice(0, margin)
    below = slice(margin + rows, 2 * margin + rows)
    inner = slice(margin, margin + cols)
    left = slice(0, margin)
    right = slice(margin + cols, ext_cols)
    bands = start_copies(
        place,
        [
            ((-1, 0), cur_ref, ext_ref.at[:, below, inner]),
            ((1, 0), cur_ref, ext_ref.at[:, above, inner]),
        ],
        send_sems.at[0:2],
        recv_sems.at[0:2],
    )
    swap(
        place,
        [
            ((0, -1), cur_ref.at[:, :, 0:margin], ext_ref.at[:, middle, right]),
            ((0, 1), cur_ref.at[:, :, cols - margin : cols], ext_ref.at[:, middle, left]),
            ((0, -1), info_ref, infos_ref.at[5]),
            ((0, 1), info_ref, infos_ref.at[3]),
        ],
        send_sems.at[8:12],
        recv_sems.at[8:12],
    )
    own.wait()
    for blank, missing in blanks:

        @pl.when(missing)
        def _():
            blank.wait()

    corners = start_copies(
        place,
        [
            ((-1, 0), ext_ref.at[:, middle, left], ext_ref.at[:, below, left]),
            ((-1, 0), ext_ref.at[:, middle, right], ext_ref.at[:, below, right]),
            ((1, 0), ext_ref.at[:, middle, left], ext_ref.at[:, above, left]),
            ((1, 0), ext_ref.at[:, middle, right], ext_ref.at[:, above, right]),
            ((-1, 0), infos_ref.at[3:6], infos_ref.at[6:9]),
            ((1, 0), infos_ref.at[3:6], infos_ref.at[0:3]),
        ],
        send_sems.at[2:8],
        recv_sems.at[2:8],
    )
    wait_copies(place, bands)
    wait_copies(place, corners)


def fold_kernel(canvas_ref, cur_ref, *refs):
    if len(refs) == 10:
        light_in_ref, refs = None, refs
    else:
        light_in_ref, refs = refs[0], refs[1:]
    fold_body(canvas_ref, cur_ref, light_in_ref, *refs)


def fold_body(canvas_ref, cur_ref, light_in_ref, out_ref, light_ref, mid_bufs, corner_bufs, col_bufs, band_ref, total_ref, send_sems, recv_sems, band_sem):
    rows = out_ref.shape[1]
    cols = out_ref.shape[2]
    margin = (canvas_ref.shape[2] - cols) // 2
    ext_cols = cols + 2 * margin
    place = mesh_place()
    me_r, me_c, n_r, n_c = place
    own_band = pltpu.make_async_copy(canvas_ref.at[:, margin : margin + rows, :], band_ref, band_sem)
    own_band.start()
    neighbour_barrier(me_r, me_c, n_r, n_c)
    top = slice(0, margin)
    bottom = slice(margin + rows, 2 * margin + rows)
    left = slice(0, margin)
    inner = slice(margin, margin + cols)
    right = slice(margin + cols, ext_cols)
    corners = start_copies(
        place,
        [
            ((-1, 0), canvas_ref.at[:, top, left], corner_bufs.at[0, 0]),
            ((-1, 0), canvas_ref.at[:, top, right], corner_bufs.at[0, 1]),
            ((1, 0), canvas_ref.at[:, bottom, left], corner_bufs.at[1, 0]),
            ((1, 0), canvas_ref.at[:, bottom, right], corner_bufs.at[1, 1]),
        ],
        send_sems.at[0:4],
        recv_sems.at[0:4],
    )
    mids = start_copies(
        place,
        [
            ((-1, 0), canvas_ref.at[:, top, inner], mid_bufs.at[0]),
            ((1, 0), canvas_ref.at[:, bottom, inner], mid_bufs.at[1]),
        ],
        send_sems.at[4:6],
        recv_sems.at[4:6],
    )
    wait_copies(place, corners)
    own_band.wait()
    for slot, source_r in ((0, me_r + 1), (1, me_r - 1)):

        @pl.when(exists(source_r, me_c, n_r, n_c))
        def _():
            band_ref[:, :, left] += corner_bufs[slot, 0]
            band_ref[:, :, right] += corner_bufs[slot, 1]

    strips = start_copies(
        place,
        [
            ((0, -1), band_ref.at[:, :, left], col_bufs.at[0]),
            ((0, 1), band_ref.at[:, :, right], col_bufs.at[1]),
        ],
        send_sems.at[6:8],
        recv_sems.at[6:8],
    )
    wait_copies(place, mids)
    total_ref[...] = band_ref[:, :, inner]
    for slot, source_r in ((0, me_r + 1), (1, me_r - 1)):

        @pl.when(exists(source_r, me_c, n_r, n_c))
        def _():
            total_ref[...] += mid_bufs[slot]

    wait_copies(place, strips)

    @pl.when(exists(me_r, me_c + 1, n_r, n_c))
    def _():
        total_ref[:, :, cols - margin : cols] += col_bufs[0]

    @pl.when(exists(me_r, me_c - 1, n_r, n_c))
    def _():
        total_ref[:, :, 0:margin] += col_bufs[1]

    fields = cur_ref.shape[0]
    if total_ref.shape[0] > fields:
        light_ref[...] = total_ref[fields]
    else:
        light_ref[...] = light_in_ref[...]
    out_ref[...] = cur_ref[...] - total_ref[0:fields] / (light_ref[...] + DAMPING)


def exchange_halo(current, info, margin):
    depth, rows, cols = current.shape
    return pl.pallas_call(
        halo_kernel,
        out_shape=(
            jax.ShapeDtypeStruct((depth, rows + 2 * margin, cols + 2 * margin), jnp.float32),
            jax.ShapeDtypeStruct((9,) + info.shape, jnp.int32),
        ),
        in_specs=[VMEM_SPEC, VMEM_SPEC],
        out_specs=(pl.BlockSpec(memory_space=pl.ANY), VMEM_SPEC),
        scratch_shapes=[
            pltpu.VMEM((depth, margin, cols + 2 * margin), jnp.float32),
            pltpu.SemaphoreType.DMA((12,)),
            pltpu.SemaphoreType.DMA((12,)),
            pltpu.SemaphoreType.DMA((5,)),
        ],
        compiler_params=pltpu.CompilerParams(
            vmem_limit_bytes=60 * 1024 * 1024, has_side_effects=True, collective_id=0
        ),
    )(current, info)


def fold_and_step(canvas, current, light, margin):
    depth, ext_rows, ext_cols = canvas.shape
    fields, rows, cols = current.shape
    return pl.pallas_call(
        fold_kernel,
        out_shape=(
            jax.ShapeDtypeStruct((fields, rows, cols), jnp.float32),
            jax.ShapeDtypeStruct((rows, cols), jnp.float32),
        ),
        in_specs=[pl.BlockSpec(memory_space=pl.ANY), VMEM_SPEC] + ([] if light is None else [VMEM_SPEC]),
        out_specs=(VMEM_SPEC, VMEM_SPEC),
        scratch_shapes=[
            pltpu.VMEM((2, depth, margin, cols), jnp.float32),
            pltpu.VMEM((2, 2, depth, margin, margin), jnp.float32),
            pltpu.VMEM((2, depth, rows, margin), jnp.float32),
            pltpu.VMEM((depth, rows, ext_cols), jnp.float32),
            pltpu.VMEM((depth, rows, cols), jnp.float32),
            pltpu.SemaphoreType.DMA((8,)),
            pltpu.SemaphoreType.DMA((8,)),
            pltpu.SemaphoreType.DMA(()),
        ],
        compiler_params=pltpu.CompilerParams(
            vmem_limit_bytes=60 * 1024 * 1024, has_side_effects=True, collective_id=depth
        ),
    )(canvas, current, *([] if light is None else [light]))


def on_device(object_field, probe_field, amplitudes, centres, counts):
    size_probe = probe_field.shape[1]
    margin = size_probe // 2
    block_rows = object_field.shape[1]
    block_cols = object_field.shape[2]
    tables = split_tables(size_probe)
    spots = centres[0, 0]
    own_amps = amplitudes[0, 0]
    column_counts = counts[:, 0]
    ext_shape = (block_rows + size_probe, block_cols + size_probe)

    live = jnp.sum(jnp.where(jnp.arange(column_counts.shape[0]) == lax.axis_index("sx"), column_counts, 0))
    info = jnp.zeros((8, 128), jnp.int32).at[0, 0:5].set(
        jnp.concatenate([spots.reshape(-1), live.reshape(1)]).astype(jnp.int32)
    )
    current = object_field
    extended, infos = exchange_halo(current, info, margin)
    canvas, illumination = gradient_canvas(
        2, ext_shape, spots, column_counts, extended, probe_field, own_amps, tables, infos
    )
    current, _ = fold_and_step(canvas, current, illumination, margin)
    for sweep_index in range(1, ITERS):
        extended, _ = exchange_halo(current, info, margin)
        canvas = gradient_canvas(
            2, ext_shape, spots, column_counts, extended, probe_field, own_amps, tables
        )
        current, _ = fold_and_step(canvas, current, illumination, margin)
    return current


def solution(mesh):
    return jax.shard_map(
        on_device,
        mesh=mesh,
        in_specs=(
            P(None, "sx", "sy"),
            P(),
            P("sx", "sy", None, None, None),
            P("sx", "sy", None, None),
            P(None, "sy"),
        ),
        out_specs=P(None, "sx", "sy"),
        check_vma=False,
    )
```

```python
import math

import jax
import ml_dtypes
import numpy as np
import jax.numpy as jnp
from jax import lax
from jax.sharding import PartitionSpec as P
from jax.experimental import pallas as pl
from jax.experimental.pallas import tpu as pltpu

ITERS = 2


SMOOTH = 1.0
DAMPING = 1.0


def with_halo(cells, sides, width):
    for axis, dim in sides:
        count = lax.axis_size(axis)
        ends = count - 1
        head = lax.slice_in_dim(cells, 0, width, axis=dim)
        tail = lax.slice_in_dim(cells, cells.shape[dim] - width, cells.shape[dim], axis=dim)
        cells = jnp.concatenate(
            [
                lax.ppermute(tail, axis, [(i, (i + 1) % count) for i in range(ends)]),
                cells,
                lax.ppermute(head, axis, [((i + 1) % count, i) for i in range(ends)]),
            ],
            axis=dim,
        )
    return cells


def dft_tables(length):
    index_values = jnp.arange(length, dtype=jnp.int32)
    product_mod = index_values[:, None] * index_values[None, :] % length
    angles = product_mod.astype(jnp.float32) * (2.0 * math.pi / length)
    scaling = 1.0 / math.sqrt(length)
    return (jnp.cos(angles) * scaling, -jnp.sin(angles) * scaling)


def matmul_exact(left_side, right_side):
    return jnp.dot(left_side, right_side, precision=lax.Precision.HIGHEST)


def complex_left(table_real, table_imag, field_real, field_imag):
    out_real = matmul_exact(table_real, field_real) - matmul_exact(table_imag, field_imag)
    out_imag = matmul_exact(table_real, field_imag) + matmul_exact(table_imag, field_real)
    return (out_real, out_imag)


def complex_right(field_real, field_imag, table_real, table_imag):
    out_real = matmul_exact(field_real, table_real) - matmul_exact(field_imag, table_imag)
    out_imag = matmul_exact(field_real, table_imag) + matmul_exact(field_imag, table_real)
    return (out_real, out_imag)


def position_gradient(object_patch, probe_field, amplitude, table_real, table_imag):
    probe_real = probe_field[0]
    probe_imag = probe_field[1]
    exit_real = probe_real * object_patch[0] - probe_imag * object_patch[1]
    exit_imag = probe_real * object_patch[1] + probe_imag * object_patch[0]
    half_real, half_imag = complex_left(table_real, table_imag, exit_real, exit_imag)
    far_real, far_imag = complex_right(half_real, half_imag, table_real, table_imag)
    factor = 1.0 - amplitude / jnp.sqrt(far_real * far_real + far_imag * far_imag + SMOOTH)
    miss_real = far_real * factor
    miss_imag = far_imag * factor
    back_real, back_imag = complex_left(table_real, -table_imag, miss_real, miss_imag)
    near_real, near_imag = complex_right(back_real, back_imag, table_real, -table_imag)
    return jnp.stack(
        [
            probe_real * near_real + probe_imag * near_imag,
            probe_real * near_imag - probe_imag * near_real,
        ]
    )


def add_patch(canvas, patch_values, corner_row, corner_col):
    zero_index = jnp.zeros((), jnp.int32)
    starts = (zero_index, corner_row, corner_col)
    present = lax.dynamic_slice(canvas, starts, patch_values.shape)
    return lax.dynamic_update_slice(canvas, present + patch_values, starts)


def fold_rows(extended, margin, length):
    middle_part = extended[:, 2 * margin : 2 * margin + length]
    upper_rim = extended[:, :margin]
    lower_rim = extended[:, extended.shape[1] - margin :]
    middle_part = middle_part.at[:, :margin].add(upper_rim)
    return middle_part.at[:, length - margin :].add(lower_rim)


def fold_cols(extended, margin, length):
    middle_part = extended[:, :, 2 * margin : 2 * margin + length]
    left_rim = extended[:, :, :margin]
    right_rim = extended[:, :, extended.shape[2] - margin :]
    middle_part = middle_part.at[:, :, :margin].add(left_rim)
    return middle_part.at[:, :, length - margin :].add(right_rim)


def settle(stacked, margin, block_rows, block_cols):
    full_ext = with_halo(stacked, (("sx", 1), ("sy", 2)), margin)
    return fold_cols(fold_rows(full_ext, margin, block_rows), margin, block_cols)


def local_pass(canvas, extended, spots, own_amps, probe_field, table_real, table_imag, upper_bound):
    size_probe = probe_field.shape[1]

    def local_step(slot_index, canvas_state):
        row_start = spots[slot_index, 0]
        col_start = spots[slot_index, 1]
        zero_index = jnp.zeros((), jnp.int32)
        object_patch = lax.dynamic_slice(
            extended, (zero_index, row_start, col_start), (2, size_probe, size_probe)
        )
        update = position_gradient(
            object_patch, probe_field, own_amps[slot_index], table_real, table_imag
        )
        return add_patch(canvas_state, update, row_start, col_start)

    return lax.fori_loop(0, upper_bound, local_step, canvas)


def dot_exact(left_side, right_side):
    return jnp.dot(
        left_side, right_side, precision=lax.Precision.HIGHEST, preferred_element_type=jnp.float32
    )


def window_tools(size, row, col):
    lanes = 128
    sublanes = 8
    wide = size + lanes
    tall = size + sublanes
    row_base = pl.multiple_of((row // sublanes) * sublanes, sublanes)
    col_base = pl.multiple_of((col // lanes) * lanes, lanes)
    row_shift = row % sublanes
    col_shift = col % lanes
    rows = pl.ds(row_base, tall)
    cols = pl.ds(col_base, wide)

    def take(ref, channel):
        block = ref[channel, rows, cols]
        block = pltpu.roll(block, (tall - row_shift) % tall, 0)
        return pltpu.roll(block, (wide - col_shift) % wide, 1)[:size, :size]

    def put(ref, channel, values):
        block = jnp.concatenate([values, jnp.zeros((size, lanes), jnp.float32)], axis=1)
        block = jnp.concatenate([block, jnp.zeros((sublanes, wide), jnp.float32)], axis=0)
        block = pltpu.roll(pltpu.roll(block, col_shift, 1), row_shift, 0)
        ref[channel, rows, cols] += block

    return take, put


def split_bf16(values):
    scaled = values * 65537.0
    high = scaled - (scaled - values)
    return high.astype(jnp.bfloat16), (values - high).astype(jnp.bfloat16)


def dot_split(left_parts, right_parts):
    left_high, left_low = left_parts
    right_high, right_low = right_parts
    total = jnp.dot(left_high, right_high, preferred_element_type=jnp.float32)
    total += jnp.dot(left_high, right_low, preferred_element_type=jnp.float32)
    return total + jnp.dot(left_low, right_high, preferred_element_type=jnp.float32)


def gradient_kernel(spots_ref, count_ref, ext_ref, probe_ref, amps_ref, tables_ref, out_ref):
    size = probe_ref.shape[1]
    out_ref[...] = jnp.zeros(out_ref.shape, jnp.float32)
    live = count_ref[lax.axis_index("sx")]
    with_power = out_ref.shape[0] > 2
    for slot in range(amps_ref.shape[0]):

        @pl.when(slot < live)
        def _():
            take, put = window_tools(size, spots_ref[slot, 0], spots_ref[slot, 1])
            probe_real = probe_ref[0]
            probe_imag = probe_ref[1]
            real_parts = (tables_ref[0], tables_ref[1])
            imag_parts = (tables_ref[2], tables_ref[3])

            def left(field_real, field_imag, sign):
                both = split_bf16(jnp.concatenate([field_real, field_imag], axis=1))
                by_real = dot_split(real_parts, both)
                by_imag = dot_split(imag_parts, both)
                out_real = by_real[:, :size] - sign * by_imag[:, size:]
                out_imag = by_real[:, size:] + sign * by_imag[:, :size]
                return out_real, out_imag

            def right(field_real, field_imag, sign):
                both = split_bf16(jnp.concatenate([field_real, field_imag], axis=0))
                by_real = dot_split(both, real_parts)
                by_imag = dot_split(both, imag_parts)
                out_real = by_real[:size] - sign * by_imag[size:]
                out_imag = by_imag[:size] * sign + by_real[size:]
                return out_real, out_imag

            obj_real = take(ext_ref, 0)
            obj_imag = take(ext_ref, 1)
            exit_real = probe_real * obj_real - probe_imag * obj_imag
            exit_imag = probe_real * obj_imag + probe_imag * obj_real
            half_real, half_imag = left(exit_real, exit_imag, 1.0)
            far_real, far_imag = right(half_real, half_imag, 1.0)
            factor = 1.0 - amps_ref[slot] / jnp.sqrt(far_real * far_real + far_imag * far_imag + SMOOTH)
            miss_real = far_real * factor
            miss_imag = far_imag * factor
            back_real, back_imag = left(miss_real, miss_imag, -1.0)
            near_real, near_imag = right(back_real, back_imag, -1.0)
            put(out_ref, 0, probe_real * near_real + probe_imag * near_imag)
            put(out_ref, 1, probe_real * near_imag - probe_imag * near_real)
            if with_power:
                put(out_ref, 2, probe_real * probe_real + probe_imag * probe_imag)


def power_kernel(spots_ref, count_ref, probe_ref, out_ref):
    size = probe_ref.shape[1]
    out_ref[...] = jnp.zeros(out_ref.shape, jnp.float32)
    power = probe_ref[0] * probe_ref[0] + probe_ref[1] * probe_ref[1]
    for slot in range(spots_ref.shape[0]):

        @pl.when(slot < count_ref[0])
        def _():
            _, put = window_tools(size, spots_ref[slot, 0], spots_ref[slot, 1])
            put(out_ref, 0, power)


VMEM_SPEC = pl.BlockSpec(memory_space=pltpu.VMEM)
SMEM_SPEC = pl.BlockSpec(memory_space=pltpu.SMEM)
KERNEL_PARAMS = pltpu.CompilerParams(vmem_limit_bytes=60 * 1024 * 1024)


def split_tables(length):
    index_values = np.arange(length, dtype=np.int32)
    product_mod = index_values[:, None] * index_values[None, :] % length
    angles = product_mod.astype(np.float32) * np.float32(2.0 * math.pi / length)
    scaling = np.float32(1.0 / math.sqrt(length))
    parts = []
    for table in (np.cos(angles) * scaling, -np.sin(angles) * scaling):
        table = table.astype(np.float32)
        scaled = table * np.float32(65537.0)
        high = scaled - (scaled - table)
        parts += [high.astype(ml_dtypes.bfloat16), (table - high).astype(ml_dtypes.bfloat16)]
    return jnp.asarray(np.stack(parts))


def gradient_canvas(channels, ext_shape, spots, count, extended, probe_field, own_amps, tables):
    return pl.pallas_call(
        gradient_kernel,
        out_shape=jax.ShapeDtypeStruct((channels,) + ext_shape, jnp.float32),
        in_specs=[SMEM_SPEC, SMEM_SPEC] + [VMEM_SPEC] * 4,
        out_specs=VMEM_SPEC,
        compiler_params=KERNEL_PARAMS,
    )(spots, count, extended, probe_field, own_amps, tables)


def power_canvas(ext_shape, spots, count, probe_field):
    return pl.pallas_call(
        power_kernel,
        out_shape=jax.ShapeDtypeStruct((1,) + ext_shape, jnp.float32),
        in_specs=[SMEM_SPEC, SMEM_SPEC, VMEM_SPEC],
        out_specs=VMEM_SPEC,
        compiler_params=KERNEL_PARAMS,
    )(spots, count.reshape(1), probe_field)


def mesh_place():
    return (
        lax.axis_index("sx"),
        lax.axis_index("sy"),
        lax.axis_size("sx"),
        lax.axis_size("sy"),
    )


def exists(row_dev, col_dev, row_count, col_count):
    return (row_dev >= 0) & (row_dev < row_count) & (col_dev >= 0) & (col_dev < col_count)


ROW_NEIGHBOURS = [(-1, 0), (1, 0)]
COL_NEIGHBOURS = [(0, -1), (0, 1)]


def neighbour_barrier(me_r, me_c, n_r, n_c):
    barrier = pltpu.get_barrier_semaphore()
    greeted = jnp.int32(0)
    for dr, dc in ROW_NEIGHBOURS + COL_NEIGHBOURS:
        present = exists(me_r + dr, me_c + dc, n_r, n_c)

        @pl.when(present)
        def _():
            pl.semaphore_signal(
                barrier, inc=1, device_id=(me_r + dr, me_c + dc), device_id_type=pl.DeviceIdType.MESH
            )

        greeted = greeted + present.astype(jnp.int32)
    pl.semaphore_wait(barrier, greeted)


def start_copies(place, pieces, send_sems, recv_sems):
    me_r, me_c, n_r, n_c = place
    copies = []
    for index, ((dr, dc), source, target) in enumerate(pieces):
        copy = pltpu.make_async_remote_copy(
            src_ref=source,
            dst_ref=target,
            send_sem=send_sems.at[index],
            recv_sem=recv_sems.at[index],
            device_id=(me_r + dr, me_c + dc),
            device_id_type=pl.DeviceIdType.MESH,
        )
        copies.append(((dr, dc), copy))

        @pl.when(exists(me_r + dr, me_c + dc, n_r, n_c))
        def _():
            copy.start()

    return copies


def wait_copies(place, copies):
    me_r, me_c, n_r, n_c = place
    for (dr, dc), copy in copies:

        @pl.when(exists(me_r + dr, me_c + dc, n_r, n_c))
        def _():
            copy.wait_send()

        @pl.when(exists(me_r - dr, me_c - dc, n_r, n_c))
        def _():
            copy.wait_recv()


def swap(place, pieces, send_sems, recv_sems):
    wait_copies(place, start_copies(place, pieces, send_sems, recv_sems))


def halo_kernel(cur_ref, ext_ref, zeros_ref, send_sems, recv_sems, local_sems):
    rows = cur_ref.shape[1]
    cols = cur_ref.shape[2]
    margin = (ext_ref.shape[2] - cols) // 2
    ext_cols = cols + 2 * margin
    place = mesh_place()
    me_r, me_c, n_r, n_c = place
    middle = slice(margin, margin + rows)
    own = pltpu.make_async_copy(cur_ref, ext_ref.at[:, middle, margin : margin + cols], local_sems.at[0])
    own.start()
    zeros_ref[...] = jnp.zeros(zeros_ref.shape, jnp.float32)
    unreached = [
        ((0, 1), ext_ref.at[:, middle, 0:margin], zeros_ref.at[:, :, 0:margin]),
        ((0, -1), ext_ref.at[:, middle, margin + cols : ext_cols], zeros_ref.at[:, :, 0:margin]),
        ((1, 0), ext_ref.at[:, 0:margin, :], zeros_ref),
        ((-1, 0), ext_ref.at[:, margin + rows : 2 * margin + rows, :], zeros_ref),
    ]
    blanks = []
    for index, ((dr, dc), target, source) in enumerate(unreached):
        blank = pltpu.make_async_copy(source, target, local_sems.at[index + 1])
        missing = jnp.logical_not(exists(me_r - dr, me_c - dc, n_r, n_c))
        blanks.append((blank, missing))

    neighbour_barrier(me_r, me_c, n_r, n_c)
    for blank, missing in blanks:

        @pl.when(missing)
        def _():
            blank.start()

    above = slice(0, margin)
    below = slice(margin + rows, 2 * margin + rows)
    inner = slice(margin, margin + cols)
    left = slice(0, margin)
    right = slice(margin + cols, ext_cols)
    strips = start_copies(
        place,
        [
            ((0, -1), cur_ref.at[:, :, 0:margin], ext_ref.at[:, middle, right]),
            ((0, 1), cur_ref.at[:, :, cols - margin : cols], ext_ref.at[:, middle, left]),
        ],
        send_sems.at[2:4],
        recv_sems.at[2:4],
    )
    bands = start_copies(
        place,
        [
            ((-1, 0), cur_ref, ext_ref.at[:, below, inner]),
            ((1, 0), cur_ref, ext_ref.at[:, above, inner]),
        ],
        send_sems.at[0:2],
        recv_sems.at[0:2],
    )
    wait_copies(place, strips)
    own.wait()
    for blank, missing in blanks:

        @pl.when(missing)
        def _():
            blank.wait()

    corners = start_copies(
        place,
        [
            ((-1, 0), ext_ref.at[:, middle, left], ext_ref.at[:, below, left]),
            ((-1, 0), ext_ref.at[:, middle, right], ext_ref.at[:, below, right]),
            ((1, 0), ext_ref.at[:, middle, left], ext_ref.at[:, above, left]),
            ((1, 0), ext_ref.at[:, middle, right], ext_ref.at[:, above, right]),
        ],
        send_sems.at[4:8],
        recv_sems.at[4:8],
    )
    wait_copies(place, bands)
    wait_copies(place, corners)


def fold_kernel(canvas_ref, cur_ref, *refs):
    if len(refs) == 10:
        light_in_ref, refs = None, refs
    else:
        light_in_ref, refs = refs[0], refs[1:]
    fold_body(canvas_ref, cur_ref, light_in_ref, *refs)


def fold_body(canvas_ref, cur_ref, light_in_ref, out_ref, light_ref, mid_bufs, corner_bufs, col_bufs, band_ref, total_ref, send_sems, recv_sems, band_sem):
    rows = out_ref.shape[1]
    cols = out_ref.shape[2]
    margin = (canvas_ref.shape[2] - cols) // 2
    ext_cols = cols + 2 * margin
    place = mesh_place()
    me_r, me_c, n_r, n_c = place
    own_band = pltpu.make_async_copy(canvas_ref.at[:, margin : margin + rows, :], band_ref, band_sem)
    own_band.start()
    neighbour_barrier(me_r, me_c, n_r, n_c)
    top = slice(0, margin)
    bottom = slice(margin + rows, 2 * margin + rows)
    left = slice(0, margin)
    inner = slice(margin, margin + cols)
    right = slice(margin + cols, ext_cols)
    corners = start_copies(
        place,
        [
            ((-1, 0), canvas_ref.at[:, top, left], corner_bufs.at[0, 0]),
            ((-1, 0), canvas_ref.at[:, top, right], corner_bufs.at[0, 1]),
            ((1, 0), canvas_ref.at[:, bottom, left], corner_bufs.at[1, 0]),
            ((1, 0), canvas_ref.at[:, bottom, right], corner_bufs.at[1, 1]),
        ],
        send_sems.at[0:4],
        recv_sems.at[0:4],
    )
    mids = start_copies(
        place,
        [
            ((-1, 0), canvas_ref.at[:, top, inner], mid_bufs.at[0]),
            ((1, 0), canvas_ref.at[:, bottom, inner], mid_bufs.at[1]),
        ],
        send_sems.at[4:6],
        recv_sems.at[4:6],
    )
    wait_copies(place, corners)
    own_band.wait()
    for slot, source_r in ((0, me_r + 1), (1, me_r - 1)):

        @pl.when(exists(source_r, me_c, n_r, n_c))
        def _():
            band_ref[:, :, left] += corner_bufs[slot, 0]
            band_ref[:, :, right] += corner_bufs[slot, 1]

    strips = start_copies(
        place,
        [
            ((0, -1), band_ref.at[:, :, left], col_bufs.at[0]),
            ((0, 1), band_ref.at[:, :, right], col_bufs.at[1]),
        ],
        send_sems.at[6:8],
        recv_sems.at[6:8],
    )
    wait_copies(place, mids)
    total_ref[...] = band_ref[:, :, inner]
    for slot, source_r in ((0, me_r + 1), (1, me_r - 1)):

        @pl.when(exists(source_r, me_c, n_r, n_c))
        def _():
            total_ref[...] += mid_bufs[slot]

    wait_copies(place, strips)

    @pl.when(exists(me_r, me_c + 1, n_r, n_c))
    def _():
        total_ref[:, :, cols - margin : cols] += col_bufs[0]

    @pl.when(exists(me_r, me_c - 1, n_r, n_c))
    def _():
        total_ref[:, :, 0:margin] += col_bufs[1]

    fields = cur_ref.shape[0]
    if total_ref.shape[0] > fields:
        light_ref[...] = total_ref[fields]
    else:
        light_ref[...] = light_in_ref[...]
    out_ref[...] = cur_ref[...] - total_ref[0:fields] / (light_ref[...] + DAMPING)


def exchange_halo(current, margin):
    depth, rows, cols = current.shape
    return pl.pallas_call(
        halo_kernel,
        out_shape=jax.ShapeDtypeStruct((depth, rows + 2 * margin, cols + 2 * margin), jnp.float32),
        in_specs=[VMEM_SPEC],
        out_specs=pl.BlockSpec(memory_space=pl.ANY),
        scratch_shapes=[
            pltpu.VMEM((depth, margin, cols + 2 * margin), jnp.float32),
            pltpu.SemaphoreType.DMA((8,)),
            pltpu.SemaphoreType.DMA((8,)),
            pltpu.SemaphoreType.DMA((5,)),
        ],
        compiler_params=pltpu.CompilerParams(
            vmem_limit_bytes=60 * 1024 * 1024, has_side_effects=True, collective_id=0
        ),
    )(current)


def fold_and_step(canvas, current, light, margin):
    depth, ext_rows, ext_cols = canvas.shape
    fields, rows, cols = current.shape
    return pl.pallas_call(
        fold_kernel,
        out_shape=(
            jax.ShapeDtypeStruct((fields, rows, cols), jnp.float32),
            jax.ShapeDtypeStruct((rows, cols), jnp.float32),
        ),
        in_specs=[pl.BlockSpec(memory_space=pl.ANY), VMEM_SPEC] + ([] if light is None else [VMEM_SPEC]),
        out_specs=(VMEM_SPEC, VMEM_SPEC),
        scratch_shapes=[
            pltpu.VMEM((2, depth, margin, cols), jnp.float32),
            pltpu.VMEM((2, 2, depth, margin, margin), jnp.float32),
            pltpu.VMEM((2, depth, rows, margin), jnp.float32),
            pltpu.VMEM((depth, rows, ext_cols), jnp.float32),
            pltpu.VMEM((depth, rows, cols), jnp.float32),
            pltpu.SemaphoreType.DMA((8,)),
            pltpu.SemaphoreType.DMA((8,)),
            pltpu.SemaphoreType.DMA(()),
        ],
        compiler_params=pltpu.CompilerParams(
            vmem_limit_bytes=60 * 1024 * 1024, has_side_effects=True, collective_id=depth
        ),
    )(canvas, current, *([] if light is None else [light]))


def on_device(object_field, probe_field, amplitudes, centres, counts):
    size_probe = probe_field.shape[1]
    margin = size_probe // 2
    block_rows = object_field.shape[1]
    block_cols = object_field.shape[2]
    tables = split_tables(size_probe)
    spots = centres[0, 0]
    own_amps = amplitudes[0, 0]
    column_counts = counts[:, 0]
    ext_shape = (block_rows + size_probe, block_cols + size_probe)

    current = object_field
    illumination = None
    for sweep_index in range(ITERS):
        extended = exchange_halo(current, margin)
        channels = 3 if sweep_index == 0 else 2
        canvas = gradient_canvas(
            channels, ext_shape, spots, column_counts, extended, probe_field, own_amps, tables
        )
        current, illumination = fold_and_step(canvas, current, illumination, margin)
    return current


def solution(mesh):
    return jax.shard_map(
        on_device,
        mesh=mesh,
        in_specs=(
            P(None, "sx", "sy"),
            P(),
            P("sx", "sy", None, None, None),
            P("sx", "sy", None, None),
            P(None, "sy"),
        ),
        out_specs=P(None, "sx", "sy"),
        check_vma=False,
    )
```

```python
import math

import jax
import ml_dtypes
import numpy as np
import jax.numpy as jnp
from jax import lax
from jax.sharding import PartitionSpec as P
from jax.experimental import pallas as pl
from jax.experimental.pallas import tpu as pltpu

ITERS = 2


SMOOTH = 1.0
DAMPING = 1.0


def with_halo(cells, sides, width):
    for axis, dim in sides:
        count = lax.axis_size(axis)
        ends = count - 1
        head = lax.slice_in_dim(cells, 0, width, axis=dim)
        tail = lax.slice_in_dim(cells, cells.shape[dim] - width, cells.shape[dim], axis=dim)
        cells = jnp.concatenate(
            [
                lax.ppermute(tail, axis, [(i, (i + 1) % count) for i in range(ends)]),
                cells,
                lax.ppermute(head, axis, [((i + 1) % count, i) for i in range(ends)]),
            ],
            axis=dim,
        )
    return cells


def dft_tables(length):
    index_values = jnp.arange(length, dtype=jnp.int32)
    product_mod = index_values[:, None] * index_values[None, :] % length
    angles = product_mod.astype(jnp.float32) * (2.0 * math.pi / length)
    scaling = 1.0 / math.sqrt(length)
    return (jnp.cos(angles) * scaling, -jnp.sin(angles) * scaling)


def matmul_exact(left_side, right_side):
    return jnp.dot(left_side, right_side, precision=lax.Precision.HIGHEST)


def complex_left(table_real, table_imag, field_real, field_imag):
    out_real = matmul_exact(table_real, field_real) - matmul_exact(table_imag, field_imag)
    out_imag = matmul_exact(table_real, field_imag) + matmul_exact(table_imag, field_real)
    return (out_real, out_imag)


def complex_right(field_real, field_imag, table_real, table_imag):
    out_real = matmul_exact(field_real, table_real) - matmul_exact(field_imag, table_imag)
    out_imag = matmul_exact(field_real, table_imag) + matmul_exact(field_imag, table_real)
    return (out_real, out_imag)


def position_gradient(object_patch, probe_field, amplitude, table_real, table_imag):
    probe_real = probe_field[0]
    probe_imag = probe_field[1]
    exit_real = probe_real * object_patch[0] - probe_imag * object_patch[1]
    exit_imag = probe_real * object_patch[1] + probe_imag * object_patch[0]
    half_real, half_imag = complex_left(table_real, table_imag, exit_real, exit_imag)
    far_real, far_imag = complex_right(half_real, half_imag, table_real, table_imag)
    factor = 1.0 - amplitude / jnp.sqrt(far_real * far_real + far_imag * far_imag + SMOOTH)
    miss_real = far_real * factor
    miss_imag = far_imag * factor
    back_real, back_imag = complex_left(table_real, -table_imag, miss_real, miss_imag)
    near_real, near_imag = complex_right(back_real, back_imag, table_real, -table_imag)
    return jnp.stack(
        [
            probe_real * near_real + probe_imag * near_imag,
            probe_real * near_imag - probe_imag * near_real,
        ]
    )


def add_patch(canvas, patch_values, corner_row, corner_col):
    zero_index = jnp.zeros((), jnp.int32)
    starts = (zero_index, corner_row, corner_col)
    present = lax.dynamic_slice(canvas, starts, patch_values.shape)
    return lax.dynamic_update_slice(canvas, present + patch_values, starts)


def fold_rows(extended, margin, length):
    middle_part = extended[:, 2 * margin : 2 * margin + length]
    upper_rim = extended[:, :margin]
    lower_rim = extended[:, extended.shape[1] - margin :]
    middle_part = middle_part.at[:, :margin].add(upper_rim)
    return middle_part.at[:, length - margin :].add(lower_rim)


def fold_cols(extended, margin, length):
    middle_part = extended[:, :, 2 * margin : 2 * margin + length]
    left_rim = extended[:, :, :margin]
    right_rim = extended[:, :, extended.shape[2] - margin :]
    middle_part = middle_part.at[:, :, :margin].add(left_rim)
    return middle_part.at[:, :, length - margin :].add(right_rim)


def settle(stacked, margin, block_rows, block_cols):
    full_ext = with_halo(stacked, (("sx", 1), ("sy", 2)), margin)
    return fold_cols(fold_rows(full_ext, margin, block_rows), margin, block_cols)


def local_pass(canvas, extended, spots, own_amps, probe_field, table_real, table_imag, upper_bound):
    size_probe = probe_field.shape[1]

    def local_step(slot_index, canvas_state):
        row_start = spots[slot_index, 0]
        col_start = spots[slot_index, 1]
        zero_index = jnp.zeros((), jnp.int32)
        object_patch = lax.dynamic_slice(
            extended, (zero_index, row_start, col_start), (2, size_probe, size_probe)
        )
        update = position_gradient(
            object_patch, probe_field, own_amps[slot_index], table_real, table_imag
        )
        return add_patch(canvas_state, update, row_start, col_start)

    return lax.fori_loop(0, upper_bound, local_step, canvas)


def dot_exact(left_side, right_side):
    return jnp.dot(
        left_side, right_side, precision=lax.Precision.HIGHEST, preferred_element_type=jnp.float32
    )


def window_tools(size, row, col):
    lanes = 128
    sublanes = 8
    wide = size + lanes
    tall = size + sublanes
    row_base = pl.multiple_of((row // sublanes) * sublanes, sublanes)
    col_base = pl.multiple_of((col // lanes) * lanes, lanes)
    row_shift = row % sublanes
    col_shift = col % lanes
    rows = pl.ds(row_base, tall)
    cols = pl.ds(col_base, wide)

    def take(ref, channel):
        block = ref[channel, rows, cols]
        block = pltpu.roll(block, (tall - row_shift) % tall, 0)
        return pltpu.roll(block, (wide - col_shift) % wide, 1)[:size, :size]

    def put(ref, channel, values):
        block = jnp.concatenate([values, jnp.zeros((size, lanes), jnp.float32)], axis=1)
        block = jnp.concatenate([block, jnp.zeros((sublanes, wide), jnp.float32)], axis=0)
        block = pltpu.roll(pltpu.roll(block, col_shift, 1), row_shift, 0)
        ref[channel, rows, cols] += block

    return take, put


def split_bf16(values):
    scaled = values * 65537.0
    high = scaled - (scaled - values)
    return high.astype(jnp.bfloat16), (values - high).astype(jnp.bfloat16)


def dot_split(left_parts, right_parts):
    left_high, left_low = left_parts
    right_high, right_low = right_parts
    total = jnp.dot(left_high, right_high, preferred_element_type=jnp.float32)
    total += jnp.dot(left_high, right_low, preferred_element_type=jnp.float32)
    return total + jnp.dot(left_low, right_high, preferred_element_type=jnp.float32)


def gradient_kernel(spots_ref, count_ref, ext_ref, probe_ref, amps_ref, tables_ref, out_ref):
    size = probe_ref.shape[1]
    out_ref[...] = jnp.zeros(out_ref.shape, jnp.float32)
    live = count_ref[lax.axis_index("sx")]
    with_power = out_ref.shape[0] > 2
    for slot in range(amps_ref.shape[0]):

        @pl.when(slot < live)
        def _():
            take, put = window_tools(size, spots_ref[slot, 0], spots_ref[slot, 1])
            probe_real = probe_ref[0]
            probe_imag = probe_ref[1]
            real_high, real_low, imag_high, imag_low = (tables_ref[k] for k in range(4))
            left_real = jnp.concatenate([real_high, real_high, real_low], axis=1)
            left_imag = jnp.concatenate([imag_high, imag_high, imag_low], axis=1)
            right_real = jnp.concatenate([real_high, real_low, real_high], axis=0)
            right_imag = jnp.concatenate([imag_high, imag_low, imag_high], axis=0)

            def product(left_side, right_side):
                return jnp.dot(left_side, right_side, preferred_element_type=jnp.float32)

            def left(field_real, field_imag, sign):
                high, low = split_bf16(jnp.concatenate([field_real, field_imag], axis=1))
                both = jnp.concatenate([high, low, high], axis=0)
                by_real = product(left_real, both)
                by_imag = product(left_imag, both)
                out_real = by_real[:, :size] - sign * by_imag[:, size:]
                out_imag = by_real[:, size:] + sign * by_imag[:, :size]
                return out_real, out_imag

            def right(field_real, field_imag, sign):
                high, low = split_bf16(jnp.concatenate([field_real, field_imag], axis=0))
                both = jnp.concatenate([high, high, low], axis=1)
                by_real = product(both, right_real)
                by_imag = product(both, right_imag)
                out_real = by_real[:size] - sign * by_imag[size:]
                out_imag = by_imag[:size] * sign + by_real[size:]
                return out_real, out_imag

            obj_real = take(ext_ref, 0)
            obj_imag = take(ext_ref, 1)
            exit_real = probe_real * obj_real - probe_imag * obj_imag
            exit_imag = probe_real * obj_imag + probe_imag * obj_real
            half_real, half_imag = left(exit_real, exit_imag, 1.0)
            far_real, far_imag = right(half_real, half_imag, 1.0)
            factor = 1.0 - amps_ref[slot] / jnp.sqrt(far_real * far_real + far_imag * far_imag + SMOOTH)
            miss_real = far_real * factor
            miss_imag = far_imag * factor
            back_real, back_imag = left(miss_real, miss_imag, -1.0)
            near_real, near_imag = right(back_real, back_imag, -1.0)
            put(out_ref, 0, probe_real * near_real + probe_imag * near_imag)
            put(out_ref, 1, probe_real * near_imag - probe_imag * near_real)
            if with_power:
                put(out_ref, 2, probe_real * probe_real + probe_imag * probe_imag)


def power_kernel(spots_ref, count_ref, probe_ref, out_ref):
    size = probe_ref.shape[1]
    out_ref[...] = jnp.zeros(out_ref.shape, jnp.float32)
    power = probe_ref[0] * probe_ref[0] + probe_ref[1] * probe_ref[1]
    for slot in range(spots_ref.shape[0]):

        @pl.when(slot < count_ref[0])
        def _():
            _, put = window_tools(size, spots_ref[slot, 0], spots_ref[slot, 1])
            put(out_ref, 0, power)


VMEM_SPEC = pl.BlockSpec(memory_space=pltpu.VMEM)
SMEM_SPEC = pl.BlockSpec(memory_space=pltpu.SMEM)
KERNEL_PARAMS = pltpu.CompilerParams(vmem_limit_bytes=60 * 1024 * 1024)


def split_tables(length):
    index_values = np.arange(length, dtype=np.int32)
    product_mod = index_values[:, None] * index_values[None, :] % length
    angles = product_mod.astype(np.float32) * np.float32(2.0 * math.pi / length)
    scaling = np.float32(1.0 / math.sqrt(length))
    parts = []
    for table in (np.cos(angles) * scaling, -np.sin(angles) * scaling):
        table = table.astype(np.float32)
        scaled = table * np.float32(65537.0)
        high = scaled - (scaled - table)
        parts += [high.astype(ml_dtypes.bfloat16), (table - high).astype(ml_dtypes.bfloat16)]
    return jnp.asarray(np.stack(parts))


def gradient_canvas(channels, ext_shape, spots, count, extended, probe_field, own_amps, tables):
    return pl.pallas_call(
        gradient_kernel,
        out_shape=jax.ShapeDtypeStruct((channels,) + ext_shape, jnp.float32),
        in_specs=[SMEM_SPEC, SMEM_SPEC] + [VMEM_SPEC] * 4,
        out_specs=VMEM_SPEC,
        compiler_params=KERNEL_PARAMS,
    )(spots, count, extended, probe_field, own_amps, tables)


def power_canvas(ext_shape, spots, count, probe_field):
    return pl.pallas_call(
        power_kernel,
        out_shape=jax.ShapeDtypeStruct((1,) + ext_shape, jnp.float32),
        in_specs=[SMEM_SPEC, SMEM_SPEC, VMEM_SPEC],
        out_specs=VMEM_SPEC,
        compiler_params=KERNEL_PARAMS,
    )(spots, count.reshape(1), probe_field)


def mesh_place():
    return (
        lax.axis_index("sx"),
        lax.axis_index("sy"),
        lax.axis_size("sx"),
        lax.axis_size("sy"),
    )


def exists(row_dev, col_dev, row_count, col_count):
    return (row_dev >= 0) & (row_dev < row_count) & (col_dev >= 0) & (col_dev < col_count)


ROW_NEIGHBOURS = [(-1, 0), (1, 0)]
COL_NEIGHBOURS = [(0, -1), (0, 1)]


def neighbour_barrier(me_r, me_c, n_r, n_c):
    barrier = pltpu.get_barrier_semaphore()
    greeted = jnp.int32(0)
    for dr, dc in ROW_NEIGHBOURS + COL_NEIGHBOURS:
        present = exists(me_r + dr, me_c + dc, n_r, n_c)

        @pl.when(present)
        def _():
            pl.semaphore_signal(
                barrier, inc=1, device_id=(me_r + dr, me_c + dc), device_id_type=pl.DeviceIdType.MESH
            )

        greeted = greeted + present.astype(jnp.int32)
    pl.semaphore_wait(barrier, greeted)


def start_copies(place, pieces, send_sems, recv_sems):
    me_r, me_c, n_r, n_c = place
    copies = []
    for index, ((dr, dc), source, target) in enumerate(pieces):
        copy = pltpu.make_async_remote_copy(
            src_ref=source,
            dst_ref=target,
            send_sem=send_sems.at[index],
            recv_sem=recv_sems.at[index],
            device_id=(me_r + dr, me_c + dc),
            device_id_type=pl.DeviceIdType.MESH,
        )
        copies.append(((dr, dc), copy))

        @pl.when(exists(me_r + dr, me_c + dc, n_r, n_c))
        def _():
            copy.start()

    return copies


def wait_copies(place, copies):
    me_r, me_c, n_r, n_c = place
    for (dr, dc), copy in copies:

        @pl.when(exists(me_r + dr, me_c + dc, n_r, n_c))
        def _():
            copy.wait_send()

        @pl.when(exists(me_r - dr, me_c - dc, n_r, n_c))
        def _():
            copy.wait_recv()


def swap(place, pieces, send_sems, recv_sems):
    wait_copies(place, start_copies(place, pieces, send_sems, recv_sems))


def halo_kernel(cur_ref, ext_ref, zeros_ref, send_sems, recv_sems, local_sems):
    rows = cur_ref.shape[1]
    cols = cur_ref.shape[2]
    margin = (ext_ref.shape[2] - cols) // 2
    ext_cols = cols + 2 * margin
    place = mesh_place()
    me_r, me_c, n_r, n_c = place
    middle = slice(margin, margin + rows)
    own = pltpu.make_async_copy(cur_ref, ext_ref.at[:, middle, margin : margin + cols], local_sems.at[0])
    own.start()
    zeros_ref[...] = jnp.zeros(zeros_ref.shape, jnp.float32)
    unreached = [
        ((0, 1), ext_ref.at[:, middle, 0:margin], zeros_ref.at[:, :, 0:margin]),
        ((0, -1), ext_ref.at[:, middle, margin + cols : ext_cols], zeros_ref.at[:, :, 0:margin]),
        ((1, 0), ext_ref.at[:, 0:margin, :], zeros_ref),
        ((-1, 0), ext_ref.at[:, margin + rows : 2 * margin + rows, :], zeros_ref),
    ]
    blanks = []
    for index, ((dr, dc), target, source) in enumerate(unreached):
        blank = pltpu.make_async_copy(source, target, local_sems.at[index + 1])
        missing = jnp.logical_not(exists(me_r - dr, me_c - dc, n_r, n_c))
        blanks.append((blank, missing))

    neighbour_barrier(me_r, me_c, n_r, n_c)
    for blank, missing in blanks:

        @pl.when(missing)
        def _():
            blank.start()

    above = slice(0, margin)
    below = slice(margin + rows, 2 * margin + rows)
    inner = slice(margin, margin + cols)
    left = slice(0, margin)
    right = slice(margin + cols, ext_cols)
    bands = start_copies(
        place,
        [
            ((-1, 0), cur_ref, ext_ref.at[:, below, inner]),
            ((1, 0), cur_ref, ext_ref.at[:, above, inner]),
        ],
        send_sems.at[0:2],
        recv_sems.at[0:2],
    )
    swap(
        place,
        [
            ((0, -1), cur_ref.at[:, :, 0:margin], ext_ref.at[:, middle, right]),
            ((0, 1), cur_ref.at[:, :, cols - margin : cols], ext_ref.at[:, middle, left]),
        ],
        send_sems.at[2:4],
        recv_sems.at[2:4],
    )
    own.wait()
    for blank, missing in blanks:

        @pl.when(missing)
        def _():
            blank.wait()

    corners = start_copies(
        place,
        [
            ((-1, 0), ext_ref.at[:, middle, left], ext_ref.at[:, below, left]),
            ((-1, 0), ext_ref.at[:, middle, right], ext_ref.at[:, below, right]),
            ((1, 0), ext_ref.at[:, middle, left], ext_ref.at[:, above, left]),
            ((1, 0), ext_ref.at[:, middle, right], ext_ref.at[:, above, right]),
        ],
        send_sems.at[4:8],
        recv_sems.at[4:8],
    )
    wait_copies(place, bands)
    wait_copies(place, corners)


def fold_kernel(canvas_ref, cur_ref, *refs):
    if len(refs) == 10:
        light_in_ref, refs = None, refs
    else:
        light_in_ref, refs = refs[0], refs[1:]
    fold_body(canvas_ref, cur_ref, light_in_ref, *refs)


def fold_body(canvas_ref, cur_ref, light_in_ref, out_ref, light_ref, mid_bufs, corner_bufs, col_bufs, band_ref, total_ref, send_sems, recv_sems, band_sem):
    rows = out_ref.shape[1]
    cols = out_ref.shape[2]
    margin = (canvas_ref.shape[2] - cols) // 2
    ext_cols = cols + 2 * margin
    place = mesh_place()
    me_r, me_c, n_r, n_c = place
    own_band = pltpu.make_async_copy(canvas_ref.at[:, margin : margin + rows, :], band_ref, band_sem)
    own_band.start()
    neighbour_barrier(me_r, me_c, n_r, n_c)
    top = slice(0, margin)
    bottom = slice(margin + rows, 2 * margin + rows)
    left = slice(0, margin)
    inner = slice(margin, margin + cols)
    right = slice(margin + cols, ext_cols)
    corners = start_copies(
        place,
        [
            ((-1, 0), canvas_ref.at[:, top, left], corner_bufs.at[0, 0]),
            ((-1, 0), canvas_ref.at[:, top, right], corner_bufs.at[0, 1]),
            ((1, 0), canvas_ref.at[:, bottom, left], corner_bufs.at[1, 0]),
            ((1, 0), canvas_ref.at[:, bottom, right], corner_bufs.at[1, 1]),
        ],
        send_sems.at[0:4],
        recv_sems.at[0:4],
    )
    mids = start_copies(
        place,
        [
            ((-1, 0), canvas_ref.at[:, top, inner], mid_bufs.at[0]),
            ((1, 0), canvas_ref.at[:, bottom, inner], mid_bufs.at[1]),
        ],
        send_sems.at[4:6],
        recv_sems.at[4:6],
    )
    wait_copies(place, corners)
    own_band.wait()
    for slot, source_r in ((0, me_r + 1), (1, me_r - 1)):

        @pl.when(exists(source_r, me_c, n_r, n_c))
        def _():
            band_ref[:, :, left] += corner_bufs[slot, 0]
            band_ref[:, :, right] += corner_bufs[slot, 1]

    strips = start_copies(
        place,
        [
            ((0, -1), band_ref.at[:, :, left], col_bufs.at[0]),
            ((0, 1), band_ref.at[:, :, right], col_bufs.at[1]),
        ],
        send_sems.at[6:8],
        recv_sems.at[6:8],
    )
    wait_copies(place, mids)
    total_ref[...] = band_ref[:, :, inner]
    for slot, source_r in ((0, me_r + 1), (1, me_r - 1)):

        @pl.when(exists(source_r, me_c, n_r, n_c))
        def _():
            total_ref[...] += mid_bufs[slot]

    wait_copies(place, strips)

    @pl.when(exists(me_r, me_c + 1, n_r, n_c))
    def _():
        total_ref[:, :, cols - margin : cols] += col_bufs[0]

    @pl.when(exists(me_r, me_c - 1, n_r, n_c))
    def _():
        total_ref[:, :, 0:margin] += col_bufs[1]

    fields = cur_ref.shape[0]
    if total_ref.shape[0] > fields:
        light_ref[...] = total_ref[fields]
    else:
        light_ref[...] = light_in_ref[...]
    out_ref[...] = cur_ref[...] - total_ref[0:fields] / (light_ref[...] + DAMPING)


def exchange_halo(current, margin):
    depth, rows, cols = current.shape
    return pl.pallas_call(
        halo_kernel,
        out_shape=jax.ShapeDtypeStruct((depth, rows + 2 * margin, cols + 2 * margin), jnp.float32),
        in_specs=[VMEM_SPEC],
        out_specs=pl.BlockSpec(memory_space=pl.ANY),
        scratch_shapes=[
            pltpu.VMEM((depth, margin, cols + 2 * margin), jnp.float32),
            pltpu.SemaphoreType.DMA((8,)),
            pltpu.SemaphoreType.DMA((8,)),
            pltpu.SemaphoreType.DMA((5,)),
        ],
        compiler_params=pltpu.CompilerParams(
            vmem_limit_bytes=60 * 1024 * 1024, has_side_effects=True, collective_id=0
        ),
    )(current)


def fold_and_step(canvas, current, light, margin):
    depth, ext_rows, ext_cols = canvas.shape
    fields, rows, cols = current.shape
    return pl.pallas_call(
        fold_kernel,
        out_shape=(
            jax.ShapeDtypeStruct((fields, rows, cols), jnp.float32),
            jax.ShapeDtypeStruct((rows, cols), jnp.float32),
        ),
        in_specs=[pl.BlockSpec(memory_space=pl.ANY), VMEM_SPEC] + ([] if light is None else [VMEM_SPEC]),
        out_specs=(VMEM_SPEC, VMEM_SPEC),
        scratch_shapes=[
            pltpu.VMEM((2, depth, margin, cols), jnp.float32),
            pltpu.VMEM((2, 2, depth, margin, margin), jnp.float32),
            pltpu.VMEM((2, depth, rows, margin), jnp.float32),
            pltpu.VMEM((depth, rows, ext_cols), jnp.float32),
            pltpu.VMEM((depth, rows, cols), jnp.float32),
            pltpu.SemaphoreType.DMA((8,)),
            pltpu.SemaphoreType.DMA((8,)),
            pltpu.SemaphoreType.DMA(()),
        ],
        compiler_params=pltpu.CompilerParams(
            vmem_limit_bytes=60 * 1024 * 1024, has_side_effects=True, collective_id=depth
        ),
    )(canvas, current, *([] if light is None else [light]))


def on_device(object_field, probe_field, amplitudes, centres, counts):
    size_probe = probe_field.shape[1]
    margin = size_probe // 2
    block_rows = object_field.shape[1]
    block_cols = object_field.shape[2]
    tables = split_tables(size_probe)
    spots = centres[0, 0]
    own_amps = amplitudes[0, 0]
    column_counts = counts[:, 0]
    ext_shape = (block_rows + size_probe, block_cols + size_probe)

    current = object_field
    illumination = None
    for sweep_index in range(ITERS):
        extended = exchange_halo(current, margin)
        channels = 3 if sweep_index == 0 else 2
        canvas = gradient_canvas(
            channels, ext_shape, spots, column_counts, extended, probe_field, own_amps, tables
        )
        current, illumination = fold_and_step(canvas, current, illumination, margin)
    return current


def solution(mesh):
    return jax.shard_map(
        on_device,
        mesh=mesh,
        in_specs=(
            P(None, "sx", "sy"),
            P(),
            P("sx", "sy", None, None, None),
            P("sx", "sy", None, None),
            P(None, "sy"),
        ),
        out_specs=P(None, "sx", "sy"),
        check_vma=False,
    )
```

```python
import math

import jax
import ml_dtypes
import numpy as np
import jax.numpy as jnp
from jax import lax
from jax.sharding import PartitionSpec as P
from jax.experimental import pallas as pl
from jax.experimental.pallas import tpu as pltpu

ITERS = 2


SMOOTH = 1.0
DAMPING = 1.0


def with_halo(cells, sides, width):
    for axis, dim in sides:
        count = lax.axis_size(axis)
        ends = count - 1
        head = lax.slice_in_dim(cells, 0, width, axis=dim)
        tail = lax.slice_in_dim(cells, cells.shape[dim] - width, cells.shape[dim], axis=dim)
        cells = jnp.concatenate(
            [
                lax.ppermute(tail, axis, [(i, (i + 1) % count) for i in range(ends)]),
                cells,
                lax.ppermute(head, axis, [((i + 1) % count, i) for i in range(ends)]),
            ],
            axis=dim,
        )
    return cells


def dft_tables(length):
    index_values = jnp.arange(length, dtype=jnp.int32)
    product_mod = index_values[:, None] * index_values[None, :] % length
    angles = product_mod.astype(jnp.float32) * (2.0 * math.pi / length)
    scaling = 1.0 / math.sqrt(length)
    return (jnp.cos(angles) * scaling, -jnp.sin(angles) * scaling)


def matmul_exact(left_side, right_side):
    return jnp.dot(left_side, right_side, precision=lax.Precision.HIGHEST)


def complex_left(table_real, table_imag, field_real, field_imag):
    out_real = matmul_exact(table_real, field_real) - matmul_exact(table_imag, field_imag)
    out_imag = matmul_exact(table_real, field_imag) + matmul_exact(table_imag, field_real)
    return (out_real, out_imag)


def complex_right(field_real, field_imag, table_real, table_imag):
    out_real = matmul_exact(field_real, table_real) - matmul_exact(field_imag, table_imag)
    out_imag = matmul_exact(field_real, table_imag) + matmul_exact(field_imag, table_real)
    return (out_real, out_imag)


def position_gradient(object_patch, probe_field, amplitude, table_real, table_imag):
    probe_real = probe_field[0]
    probe_imag = probe_field[1]
    exit_real = probe_real * object_patch[0] - probe_imag * object_patch[1]
    exit_imag = probe_real * object_patch[1] + probe_imag * object_patch[0]
    half_real, half_imag = complex_left(table_real, table_imag, exit_real, exit_imag)
    far_real, far_imag = complex_right(half_real, half_imag, table_real, table_imag)
    factor = 1.0 - amplitude / jnp.sqrt(far_real * far_real + far_imag * far_imag + SMOOTH)
    miss_real = far_real * factor
    miss_imag = far_imag * factor
    back_real, back_imag = complex_left(table_real, -table_imag, miss_real, miss_imag)
    near_real, near_imag = complex_right(back_real, back_imag, table_real, -table_imag)
    return jnp.stack(
        [
            probe_real * near_real + probe_imag * near_imag,
            probe_real * near_imag - probe_imag * near_real,
        ]
    )


def add_patch(canvas, patch_values, corner_row, corner_col):
    zero_index = jnp.zeros((), jnp.int32)
    starts = (zero_index, corner_row, corner_col)
    present = lax.dynamic_slice(canvas, starts, patch_values.shape)
    return lax.dynamic_update_slice(canvas, present + patch_values, starts)


def fold_rows(extended, margin, length):
    middle_part = extended[:, 2 * margin : 2 * margin + length]
    upper_rim = extended[:, :margin]
    lower_rim = extended[:, extended.shape[1] - margin :]
    middle_part = middle_part.at[:, :margin].add(upper_rim)
    return middle_part.at[:, length - margin :].add(lower_rim)


def fold_cols(extended, margin, length):
    middle_part = extended[:, :, 2 * margin : 2 * margin + length]
    left_rim = extended[:, :, :margin]
    right_rim = extended[:, :, extended.shape[2] - margin :]
    middle_part = middle_part.at[:, :, :margin].add(left_rim)
    return middle_part.at[:, :, length - margin :].add(right_rim)


def settle(stacked, margin, block_rows, block_cols):
    full_ext = with_halo(stacked, (("sx", 1), ("sy", 2)), margin)
    return fold_cols(fold_rows(full_ext, margin, block_rows), margin, block_cols)


def local_pass(canvas, extended, spots, own_amps, probe_field, table_real, table_imag, upper_bound):
    size_probe = probe_field.shape[1]

    def local_step(slot_index, canvas_state):
        row_start = spots[slot_index, 0]
        col_start = spots[slot_index, 1]
        zero_index = jnp.zeros((), jnp.int32)
        object_patch = lax.dynamic_slice(
            extended, (zero_index, row_start, col_start), (2, size_probe, size_probe)
        )
        update = position_gradient(
            object_patch, probe_field, own_amps[slot_index], table_real, table_imag
        )
        return add_patch(canvas_state, update, row_start, col_start)

    return lax.fori_loop(0, upper_bound, local_step, canvas)


def dot_exact(left_side, right_side):
    return jnp.dot(
        left_side, right_side, precision=lax.Precision.HIGHEST, preferred_element_type=jnp.float32
    )


def window_tools(size, row, col):
    lanes = 128
    sublanes = 8
    wide = size + lanes
    tall = size + sublanes
    row_base = pl.multiple_of((row // sublanes) * sublanes, sublanes)
    col_base = pl.multiple_of((col // lanes) * lanes, lanes)
    row_shift = row % sublanes
    col_shift = col % lanes
    rows = pl.ds(row_base, tall)
    cols = pl.ds(col_base, wide)

    def take(ref, channel):
        block = ref[channel, rows, cols]
        block = pltpu.roll(block, (tall - row_shift) % tall, 0)
        return pltpu.roll(block, (wide - col_shift) % wide, 1)[:size, :size]

    def put(ref, channel, values):
        block = jnp.concatenate([values, jnp.zeros((size, lanes), jnp.float32)], axis=1)
        block = jnp.concatenate([block, jnp.zeros((sublanes, wide), jnp.float32)], axis=0)
        block = pltpu.roll(pltpu.roll(block, col_shift, 1), row_shift, 0)
        ref[channel, rows, cols] += block

    return take, put


def split_bf16(values):
    scaled = values * 65537.0
    high = scaled - (scaled - values)
    return high.astype(jnp.bfloat16), (values - high).astype(jnp.bfloat16)


def dot_split(left_parts, right_parts):
    left_high, left_low = left_parts
    right_high, right_low = right_parts
    total = jnp.dot(left_high, right_high, preferred_element_type=jnp.float32)
    total += jnp.dot(left_high, right_low, preferred_element_type=jnp.float32)
    return total + jnp.dot(left_low, right_high, preferred_element_type=jnp.float32)


def gradient_kernel(spots_ref, count_ref, ext_ref, probe_ref, amps_ref, tables_ref, out_ref):
    size = probe_ref.shape[1]
    out_ref[...] = jnp.zeros(out_ref.shape, jnp.float32)
    live = count_ref[lax.axis_index("sx")]
    with_power = out_ref.shape[0] > 2
    for slot in range(amps_ref.shape[0]):

        @pl.when(slot < live)
        def _():
            take, put = window_tools(size, spots_ref[slot, 0], spots_ref[slot, 1])
            probe_real = probe_ref[0]
            probe_imag = probe_ref[1]
            real_parts = (tables_ref[0], tables_ref[1])
            imag_parts = (tables_ref[2], tables_ref[3])

            def left(field_real, field_imag, sign):
                both = split_bf16(jnp.concatenate([field_real, field_imag], axis=1))
                by_real = dot_split(real_parts, both)
                by_imag = dot_split(imag_parts, both)
                out_real = by_real[:, :size] - sign * by_imag[:, size:]
                out_imag = by_real[:, size:] + sign * by_imag[:, :size]
                return out_real, out_imag

            def right(field_real, field_imag, sign):
                both = split_bf16(jnp.concatenate([field_real, field_imag], axis=0))
                by_real = dot_split(both, real_parts)
                by_imag = dot_split(both, imag_parts)
                out_real = by_real[:size] - sign * by_imag[size:]
                out_imag = by_imag[:size] * sign + by_real[size:]
                return out_real, out_imag

            obj_real = take(ext_ref, 0)
            obj_imag = take(ext_ref, 1)
            exit_real = probe_real * obj_real - probe_imag * obj_imag
            exit_imag = probe_real * obj_imag + probe_imag * obj_real
            half_real, half_imag = left(exit_real, exit_imag, 1.0)
            far_real, far_imag = right(half_real, half_imag, 1.0)
            factor = 1.0 - amps_ref[slot] / jnp.sqrt(far_real * far_real + far_imag * far_imag + SMOOTH)
            miss_real = far_real * factor
            miss_imag = far_imag * factor
            back_real, back_imag = left(miss_real, miss_imag, -1.0)
            near_real, near_imag = right(back_real, back_imag, -1.0)
            put(out_ref, 0, probe_real * near_real + probe_imag * near_imag)
            put(out_ref, 1, probe_real * near_imag - probe_imag * near_real)
            if with_power:
                put(out_ref, 2, probe_real * probe_real + probe_imag * probe_imag)


def power_kernel(spots_ref, count_ref, probe_ref, out_ref):
    size = probe_ref.shape[1]
    out_ref[...] = jnp.zeros(out_ref.shape, jnp.float32)
    power = probe_ref[0] * probe_ref[0] + probe_ref[1] * probe_ref[1]
    for slot in range(spots_ref.shape[0]):

        @pl.when(slot < count_ref[0])
        def _():
            _, put = window_tools(size, spots_ref[slot, 0], spots_ref[slot, 1])
            put(out_ref, 0, power)


VMEM_SPEC = pl.BlockSpec(memory_space=pltpu.VMEM)
SMEM_SPEC = pl.BlockSpec(memory_space=pltpu.SMEM)
KERNEL_PARAMS = pltpu.CompilerParams(vmem_limit_bytes=60 * 1024 * 1024)


def split_tables(length):
    index_values = np.arange(length, dtype=np.int32)
    product_mod = index_values[:, None] * index_values[None, :] % length
    angles = product_mod.astype(np.float32) * np.float32(2.0 * math.pi / length)
    scaling = np.float32(1.0 / math.sqrt(length))
    parts = []
    for table in (np.cos(angles) * scaling, -np.sin(angles) * scaling):
        table = table.astype(np.float32)
        scaled = table * np.float32(65537.0)
        high = scaled - (scaled - table)
        parts += [high.astype(ml_dtypes.bfloat16), (table - high).astype(ml_dtypes.bfloat16)]
    return jnp.asarray(np.stack(parts))


def gradient_canvas(channels, ext_shape, spots, count, extended, probe_field, own_amps, tables):
    return pl.pallas_call(
        gradient_kernel,
        out_shape=jax.ShapeDtypeStruct((channels,) + ext_shape, jnp.float32),
        in_specs=[SMEM_SPEC, SMEM_SPEC] + [VMEM_SPEC] * 4,
        out_specs=VMEM_SPEC,
        compiler_params=KERNEL_PARAMS,
    )(spots, count, extended, probe_field, own_amps, tables)


def power_canvas(ext_shape, spots, count, probe_field):
    return pl.pallas_call(
        power_kernel,
        out_shape=jax.ShapeDtypeStruct((1,) + ext_shape, jnp.float32),
        in_specs=[SMEM_SPEC, SMEM_SPEC, VMEM_SPEC],
        out_specs=VMEM_SPEC,
        compiler_params=KERNEL_PARAMS,
    )(spots, count.reshape(1), probe_field)


def mesh_place():
    return (
        lax.axis_index("sx"),
        lax.axis_index("sy"),
        lax.axis_size("sx"),
        lax.axis_size("sy"),
    )


def exists(row_dev, col_dev, row_count, col_count):
    return (row_dev >= 0) & (row_dev < row_count) & (col_dev >= 0) & (col_dev < col_count)


ROW_NEIGHBOURS = [(-1, 0), (1, 0)]
COL_NEIGHBOURS = [(0, -1), (0, 1)]


def neighbour_barrier(me_r, me_c, n_r, n_c):
    barrier = pltpu.get_barrier_semaphore()
    greeted = jnp.int32(0)
    for dr, dc in ROW_NEIGHBOURS + COL_NEIGHBOURS:
        present = exists(me_r + dr, me_c + dc, n_r, n_c)

        @pl.when(present)
        def _():
            pl.semaphore_signal(
                barrier, inc=1, device_id=(me_r + dr, me_c + dc), device_id_type=pl.DeviceIdType.MESH
            )

        greeted = greeted + present.astype(jnp.int32)
    pl.semaphore_wait(barrier, greeted)


def start_copies(place, pieces, send_sems, recv_sems):
    me_r, me_c, n_r, n_c = place
    copies = []
    for index, ((dr, dc), source, target) in enumerate(pieces):
        copy = pltpu.make_async_remote_copy(
            src_ref=source,
            dst_ref=target,
            send_sem=send_sems.at[index],
            recv_sem=recv_sems.at[index],
            device_id=(me_r + dr, me_c + dc),
            device_id_type=pl.DeviceIdType.MESH,
        )
        copies.append(((dr, dc), copy))

        @pl.when(exists(me_r + dr, me_c + dc, n_r, n_c))
        def _():
            copy.start()

    return copies


def wait_copies(place, copies):
    me_r, me_c, n_r, n_c = place
    for (dr, dc), copy in copies:

        @pl.when(exists(me_r + dr, me_c + dc, n_r, n_c))
        def _():
            copy.wait_send()

        @pl.when(exists(me_r - dr, me_c - dc, n_r, n_c))
        def _():
            copy.wait_recv()


def swap(place, pieces, send_sems, recv_sems):
    wait_copies(place, start_copies(place, pieces, send_sems, recv_sems))


def halo_kernel(cur_ref, ext_ref, zeros_ref, send_sems, recv_sems, local_sems):
    rows = cur_ref.shape[1]
    cols = cur_ref.shape[2]
    margin = (ext_ref.shape[2] - cols) // 2
    ext_cols = cols + 2 * margin
    place = mesh_place()
    me_r, me_c, n_r, n_c = place
    middle = slice(margin, margin + rows)
    own = pltpu.make_async_copy(cur_ref, ext_ref.at[:, middle, margin : margin + cols], local_sems.at[0])
    own.start()
    edge_device = jnp.logical_not(
        exists(me_r - 1, me_c, n_r, n_c)
        & exists(me_r + 1, me_c, n_r, n_c)
        & exists(me_r, me_c - 1, n_r, n_c)
        & exists(me_r, me_c + 1, n_r, n_c)
    )

    @pl.when(edge_device)
    def _():
        zeros_ref[...] = jnp.zeros(zeros_ref.shape, jnp.float32)

    unreached = [
        ((0, 1), ext_ref.at[:, middle, 0:margin], zeros_ref.at[:, :, 0:margin]),
        ((0, -1), ext_ref.at[:, middle, margin + cols : ext_cols], zeros_ref.at[:, :, 0:margin]),
        ((1, 0), ext_ref.at[:, 0:margin, :], zeros_ref),
        ((-1, 0), ext_ref.at[:, margin + rows : 2 * margin + rows, :], zeros_ref),
    ]
    blanks = []
    for index, ((dr, dc), target, source) in enumerate(unreached):
        blank = pltpu.make_async_copy(source, target, local_sems.at[index + 1])
        missing = jnp.logical_not(exists(me_r - dr, me_c - dc, n_r, n_c))
        blanks.append((blank, missing))

    neighbour_barrier(me_r, me_c, n_r, n_c)
    for blank, missing in blanks:

        @pl.when(missing)
        def _():
            blank.start()

    above = slice(0, margin)
    below = slice(margin + rows, 2 * margin + rows)
    inner = slice(margin, margin + cols)
    left = slice(0, margin)
    right = slice(margin + cols, ext_cols)
    bands = start_copies(
        place,
        [
            ((-1, 0), cur_ref, ext_ref.at[:, below, inner]),
            ((1, 0), cur_ref, ext_ref.at[:, above, inner]),
        ],
        send_sems.at[0:2],
        recv_sems.at[0:2],
    )
    swap(
        place,
        [
            ((0, -1), cur_ref.at[:, :, 0:margin], ext_ref.at[:, middle, right]),
            ((0, 1), cur_ref.at[:, :, cols - margin : cols], ext_ref.at[:, middle, left]),
        ],
        send_sems.at[2:4],
        recv_sems.at[2:4],
    )
    own.wait()
    for blank, missing in blanks:

        @pl.when(missing)
        def _():
            blank.wait()

    corners = start_copies(
        place,
        [
            ((-1, 0), ext_ref.at[:, middle, left], ext_ref.at[:, below, left]),
            ((-1, 0), ext_ref.at[:, middle, right], ext_ref.at[:, below, right]),
            ((1, 0), ext_ref.at[:, middle, left], ext_ref.at[:, above, left]),
            ((1, 0), ext_ref.at[:, middle, right], ext_ref.at[:, above, right]),
        ],
        send_sems.at[4:8],
        recv_sems.at[4:8],
    )
    wait_copies(place, bands)
    wait_copies(place, corners)


def fold_kernel(canvas_ref, cur_ref, *refs):
    if len(refs) == 10:
        light_in_ref, refs = None, refs
    else:
        light_in_ref, refs = refs[0], refs[1:]
    fold_body(canvas_ref, cur_ref, light_in_ref, *refs)


def fold_body(canvas_ref, cur_ref, light_in_ref, out_ref, light_ref, mid_bufs, corner_bufs, col_bufs, band_ref, total_ref, send_sems, recv_sems, band_sem):
    rows = out_ref.shape[1]
    cols = out_ref.shape[2]
    margin = (canvas_ref.shape[2] - cols) // 2
    ext_cols = cols + 2 * margin
    place = mesh_place()
    me_r, me_c, n_r, n_c = place
    own_band = pltpu.make_async_copy(canvas_ref.at[:, margin : margin + rows, :], band_ref, band_sem)
    neighbour_barrier(me_r, me_c, n_r, n_c)
    top = slice(0, margin)
    bottom = slice(margin + rows, 2 * margin + rows)
    left = slice(0, margin)
    inner = slice(margin, margin + cols)
    right = slice(margin + cols, ext_cols)
    corners = start_copies(
        place,
        [
            ((-1, 0), canvas_ref.at[:, top, left], corner_bufs.at[0, 0]),
            ((-1, 0), canvas_ref.at[:, top, right], corner_bufs.at[0, 1]),
            ((1, 0), canvas_ref.at[:, bottom, left], corner_bufs.at[1, 0]),
            ((1, 0), canvas_ref.at[:, bottom, right], corner_bufs.at[1, 1]),
        ],
        send_sems.at[0:4],
        recv_sems.at[0:4],
    )
    mids = start_copies(
        place,
        [
            ((-1, 0), canvas_ref.at[:, top, inner], mid_bufs.at[0]),
            ((1, 0), canvas_ref.at[:, bottom, inner], mid_bufs.at[1]),
        ],
        send_sems.at[4:6],
        recv_sems.at[4:6],
    )
    own_band.start()
    wait_copies(place, corners)
    own_band.wait()
    for slot, source_r in ((0, me_r + 1), (1, me_r - 1)):

        @pl.when(exists(source_r, me_c, n_r, n_c))
        def _():
            band_ref[:, :, left] += corner_bufs[slot, 0]
            band_ref[:, :, right] += corner_bufs[slot, 1]

    strips = start_copies(
        place,
        [
            ((0, -1), band_ref.at[:, :, left], col_bufs.at[0]),
            ((0, 1), band_ref.at[:, :, right], col_bufs.at[1]),
        ],
        send_sems.at[6:8],
        recv_sems.at[6:8],
    )
    wait_copies(place, mids)
    total_ref[...] = band_ref[:, :, inner]
    for slot, source_r in ((0, me_r + 1), (1, me_r - 1)):

        @pl.when(exists(source_r, me_c, n_r, n_c))
        def _():
            total_ref[...] += mid_bufs[slot]

    wait_copies(place, strips)

    @pl.when(exists(me_r, me_c + 1, n_r, n_c))
    def _():
        total_ref[:, :, cols - margin : cols] += col_bufs[0]

    @pl.when(exists(me_r, me_c - 1, n_r, n_c))
    def _():
        total_ref[:, :, 0:margin] += col_bufs[1]

    fields = cur_ref.shape[0]
    if total_ref.shape[0] > fields:
        light_ref[...] = total_ref[fields]
    else:
        light_ref[...] = light_in_ref[...]
    out_ref[...] = cur_ref[...] - total_ref[0:fields] / (light_ref[...] + DAMPING)


def exchange_halo(current, margin):
    depth, rows, cols = current.shape
    return pl.pallas_call(
        halo_kernel,
        out_shape=jax.ShapeDtypeStruct((depth, rows + 2 * margin, cols + 2 * margin), jnp.float32),
        in_specs=[VMEM_SPEC],
        out_specs=pl.BlockSpec(memory_space=pl.ANY),
        scratch_shapes=[
            pltpu.VMEM((depth, margin, cols + 2 * margin), jnp.float32),
            pltpu.SemaphoreType.DMA((8,)),
            pltpu.SemaphoreType.DMA((8,)),
            pltpu.SemaphoreType.DMA((5,)),
        ],
        compiler_params=pltpu.CompilerParams(
            vmem_limit_bytes=60 * 1024 * 1024, has_side_effects=True, collective_id=0
        ),
    )(current)


def fold_and_step(canvas, current, light, margin):
    depth, ext_rows, ext_cols = canvas.shape
    fields, rows, cols = current.shape
    return pl.pallas_call(
        fold_kernel,
        out_shape=(
            jax.ShapeDtypeStruct((fields, rows, cols), jnp.float32),
            jax.ShapeDtypeStruct((rows, cols), jnp.float32),
        ),
        in_specs=[pl.BlockSpec(memory_space=pl.ANY), VMEM_SPEC] + ([] if light is None else [VMEM_SPEC]),
        out_specs=(VMEM_SPEC, VMEM_SPEC),
        scratch_shapes=[
            pltpu.VMEM((2, depth, margin, cols), jnp.float32),
            pltpu.VMEM((2, 2, depth, margin, margin), jnp.float32),
            pltpu.VMEM((2, depth, rows, margin), jnp.float32),
            pltpu.VMEM((depth, rows, ext_cols), jnp.float32),
            pltpu.VMEM((depth, rows, cols), jnp.float32),
            pltpu.SemaphoreType.DMA((8,)),
            pltpu.SemaphoreType.DMA((8,)),
            pltpu.SemaphoreType.DMA(()),
        ],
        compiler_params=pltpu.CompilerParams(
            vmem_limit_bytes=60 * 1024 * 1024, has_side_effects=True, collective_id=depth
        ),
    )(canvas, current, *([] if light is None else [light]))


def on_device(object_field, probe_field, amplitudes, centres, counts):
    size_probe = probe_field.shape[1]
    margin = size_probe // 2
    block_rows = object_field.shape[1]
    block_cols = object_field.shape[2]
    tables = split_tables(size_probe)
    spots = centres[0, 0]
    own_amps = amplitudes[0, 0]
    column_counts = counts[:, 0]
    ext_shape = (block_rows + size_probe, block_cols + size_probe)

    current = object_field
    illumination = None
    for sweep_index in range(ITERS):
        extended = exchange_halo(current, margin)
        channels = 3 if sweep_index == 0 else 2
        canvas = gradient_canvas(
            channels, ext_shape, spots, column_counts, extended, probe_field, own_amps, tables
        )
        current, illumination = fold_and_step(canvas, current, illumination, margin)
    return current


def solution(mesh):
    return jax.shard_map(
        on_device,
        mesh=mesh,
        in_specs=(
            P(None, "sx", "sy"),
            P(),
            P("sx", "sy", None, None, None),
            P("sx", "sy", None, None),
            P(None, "sy"),
        ),
        out_specs=P(None, "sx", "sy"),
        check_vma=False,
    )
```

```python
import math

import jax
import ml_dtypes
import numpy as np
import jax.numpy as jnp
from jax import lax
from jax.sharding import PartitionSpec as P
from jax.experimental import pallas as pl
from jax.experimental.pallas import tpu as pltpu

ITERS = 2


SMOOTH = 1.0
DAMPING = 1.0


def with_halo(cells, sides, width):
    for axis, dim in sides:
        count = lax.axis_size(axis)
        ends = count - 1
        head = lax.slice_in_dim(cells, 0, width, axis=dim)
        tail = lax.slice_in_dim(cells, cells.shape[dim] - width, cells.shape[dim], axis=dim)
        cells = jnp.concatenate(
            [
                lax.ppermute(tail, axis, [(i, (i + 1) % count) for i in range(ends)]),
                cells,
                lax.ppermute(head, axis, [((i + 1) % count, i) for i in range(ends)]),
            ],
            axis=dim,
        )
    return cells


def dft_tables(length):
    index_values = jnp.arange(length, dtype=jnp.int32)
    product_mod = index_values[:, None] * index_values[None, :] % length
    angles = product_mod.astype(jnp.float32) * (2.0 * math.pi / length)
    scaling = 1.0 / math.sqrt(length)
    return (jnp.cos(angles) * scaling, -jnp.sin(angles) * scaling)


def matmul_exact(left_side, right_side):
    return jnp.dot(left_side, right_side, precision=lax.Precision.HIGHEST)


def complex_left(table_real, table_imag, field_real, field_imag):
    out_real = matmul_exact(table_real, field_real) - matmul_exact(table_imag, field_imag)
    out_imag = matmul_exact(table_real, field_imag) + matmul_exact(table_imag, field_real)
    return (out_real, out_imag)


def complex_right(field_real, field_imag, table_real, table_imag):
    out_real = matmul_exact(field_real, table_real) - matmul_exact(field_imag, table_imag)
    out_imag = matmul_exact(field_real, table_imag) + matmul_exact(field_imag, table_real)
    return (out_real, out_imag)


def position_gradient(object_patch, probe_field, amplitude, table_real, table_imag):
    probe_real = probe_field[0]
    probe_imag = probe_field[1]
    exit_real = probe_real * object_patch[0] - probe_imag * object_patch[1]
    exit_imag = probe_real * object_patch[1] + probe_imag * object_patch[0]
    half_real, half_imag = complex_left(table_real, table_imag, exit_real, exit_imag)
    far_real, far_imag = complex_right(half_real, half_imag, table_real, table_imag)
    factor = 1.0 - amplitude / jnp.sqrt(far_real * far_real + far_imag * far_imag + SMOOTH)
    miss_real = far_real * factor
    miss_imag = far_imag * factor
    back_real, back_imag = complex_left(table_real, -table_imag, miss_real, miss_imag)
    near_real, near_imag = complex_right(back_real, back_imag, table_real, -table_imag)
    return jnp.stack(
        [
            probe_real * near_real + probe_imag * near_imag,
            probe_real * near_imag - probe_imag * near_real,
        ]
    )


def add_patch(canvas, patch_values, corner_row, corner_col):
    zero_index = jnp.zeros((), jnp.int32)
    starts = (zero_index, corner_row, corner_col)
    present = lax.dynamic_slice(canvas, starts, patch_values.shape)
    return lax.dynamic_update_slice(canvas, present + patch_values, starts)


def fold_rows(extended, margin, length):
    middle_part = extended[:, 2 * margin : 2 * margin + length]
    upper_rim = extended[:, :margin]
    lower_rim = extended[:, extended.shape[1] - margin :]
    middle_part = middle_part.at[:, :margin].add(upper_rim)
    return middle_part.at[:, length - margin :].add(lower_rim)


def fold_cols(extended, margin, length):
    middle_part = extended[:, :, 2 * margin : 2 * margin + length]
    left_rim = extended[:, :, :margin]
    right_rim = extended[:, :, extended.shape[2] - margin :]
    middle_part = middle_part.at[:, :, :margin].add(left_rim)
    return middle_part.at[:, :, length - margin :].add(right_rim)


def settle(stacked, margin, block_rows, block_cols):
    full_ext = with_halo(stacked, (("sx", 1), ("sy", 2)), margin)
    return fold_cols(fold_rows(full_ext, margin, block_rows), margin, block_cols)


def local_pass(canvas, extended, spots, own_amps, probe_field, table_real, table_imag, upper_bound):
    size_probe = probe_field.shape[1]

    def local_step(slot_index, canvas_state):
        row_start = spots[slot_index, 0]
        col_start = spots[slot_index, 1]
        zero_index = jnp.zeros((), jnp.int32)
        object_patch = lax.dynamic_slice(
            extended, (zero_index, row_start, col_start), (2, size_probe, size_probe)
        )
        update = position_gradient(
            object_patch, probe_field, own_amps[slot_index], table_real, table_imag
        )
        return add_patch(canvas_state, update, row_start, col_start)

    return lax.fori_loop(0, upper_bound, local_step, canvas)


def dot_exact(left_side, right_side):
    return jnp.dot(
        left_side, right_side, precision=lax.Precision.HIGHEST, preferred_element_type=jnp.float32
    )


def window_tools(size, row, col):
    lanes = 128
    sublanes = 8
    wide = size + lanes
    tall = size + sublanes
    row_base = pl.multiple_of((row // sublanes) * sublanes, sublanes)
    col_base = pl.multiple_of((col // lanes) * lanes, lanes)
    row_shift = row % sublanes
    col_shift = col % lanes
    rows = pl.ds(row_base, tall)
    cols = pl.ds(col_base, wide)

    def take(ref, channel):
        block = ref[channel, rows, cols]
        block = pltpu.roll(block, (tall - row_shift) % tall, 0)
        return pltpu.roll(block, (wide - col_shift) % wide, 1)[:size, :size]

    def put(ref, channel, values):
        block = jnp.concatenate([values, jnp.zeros((size, lanes), jnp.float32)], axis=1)
        block = jnp.concatenate([block, jnp.zeros((sublanes, wide), jnp.float32)], axis=0)
        block = pltpu.roll(pltpu.roll(block, col_shift, 1), row_shift, 0)
        ref[channel, rows, cols] += block

    return take, put


def split_bf16(values):
    scaled = values * 65537.0
    high = scaled - (scaled - values)
    return high.astype(jnp.bfloat16), (values - high).astype(jnp.bfloat16)


def dot_split(left_parts, right_parts):
    left_high, left_low = left_parts
    right_high, right_low = right_parts
    total = jnp.dot(left_high, right_high, preferred_element_type=jnp.float32)
    total += jnp.dot(left_high, right_low, preferred_element_type=jnp.float32)
    return total + jnp.dot(left_low, right_high, preferred_element_type=jnp.float32)


def gradient_kernel(spots_ref, count_ref, ext_ref, probe_ref, amps_ref, tables_ref, out_ref):
    size = probe_ref.shape[1]
    out_ref[...] = jnp.zeros(out_ref.shape, jnp.float32)
    live = count_ref[lax.axis_index("sx")]
    with_power = out_ref.shape[0] > 2
    for slot in range(amps_ref.shape[0]):

        @pl.when(slot < live)
        def _():
            take, put = window_tools(size, spots_ref[slot, 0], spots_ref[slot, 1])
            probe_real = probe_ref[0]
            probe_imag = probe_ref[1]
            real_parts = (tables_ref[0], tables_ref[1])
            imag_parts = (tables_ref[2], tables_ref[3])

            def left(field_real, field_imag, sign):
                both = split_bf16(jnp.concatenate([field_real, field_imag], axis=1))
                by_real = dot_split(real_parts, both)
                by_imag = dot_split(imag_parts, both)
                out_real = by_real[:, :size] - sign * by_imag[:, size:]
                out_imag = by_real[:, size:] + sign * by_imag[:, :size]
                return out_real, out_imag

            def right(field_real, field_imag, sign):
                both = split_bf16(jnp.concatenate([field_real, field_imag], axis=0))
                by_real = dot_split(both, real_parts)
                by_imag = dot_split(both, imag_parts)
                out_real = by_real[:size] - sign * by_imag[size:]
                out_imag = by_imag[:size] * sign + by_real[size:]
                return out_real, out_imag

            obj_real = take(ext_ref, 0)
            obj_imag = take(ext_ref, 1)
            exit_real = probe_real * obj_real - probe_imag * obj_imag
            exit_imag = probe_real * obj_imag + probe_imag * obj_real
            half_real, half_imag = left(exit_real, exit_imag, 1.0)
            far_real, far_imag = right(half_real, half_imag, 1.0)
            factor = 1.0 - amps_ref[slot] / jnp.sqrt(far_real * far_real + far_imag * far_imag + SMOOTH)
            miss_real = far_real * factor
            miss_imag = far_imag * factor
            back_real, back_imag = left(miss_real, miss_imag, -1.0)
            near_real, near_imag = right(back_real, back_imag, -1.0)
            put(out_ref, 0, probe_real * near_real + probe_imag * near_imag)
            put(out_ref, 1, probe_real * near_imag - probe_imag * near_real)
            if with_power:
                put(out_ref, 2, probe_real * probe_real + probe_imag * probe_imag)


def power_kernel(spots_ref, count_ref, probe_ref, out_ref):
    size = probe_ref.shape[1]
    out_ref[...] = jnp.zeros(out_ref.shape, jnp.float32)
    power = probe_ref[0] * probe_ref[0] + probe_ref[1] * probe_ref[1]
    for slot in range(spots_ref.shape[0]):

        @pl.when(slot < count_ref[0])
        def _():
            _, put = window_tools(size, spots_ref[slot, 0], spots_ref[slot, 1])
            put(out_ref, 0, power)


VMEM_SPEC = pl.BlockSpec(memory_space=pltpu.VMEM)
SMEM_SPEC = pl.BlockSpec(memory_space=pltpu.SMEM)
KERNEL_PARAMS = pltpu.CompilerParams(vmem_limit_bytes=60 * 1024 * 1024)


def split_tables(length):
    index_values = np.arange(length, dtype=np.int32)
    product_mod = index_values[:, None] * index_values[None, :] % length
    angles = product_mod.astype(np.float32) * np.float32(2.0 * math.pi / length)
    scaling = np.float32(1.0 / math.sqrt(length))
    parts = []
    for table in (np.cos(angles) * scaling, -np.sin(angles) * scaling):
        table = table.astype(np.float32)
        scaled = table * np.float32(65537.0)
        high = scaled - (scaled - table)
        parts += [high.astype(ml_dtypes.bfloat16), (table - high).astype(ml_dtypes.bfloat16)]
    return jnp.asarray(np.stack(parts))


def gradient_canvas(channels, ext_shape, spots, count, extended, probe_field, own_amps, tables):
    return pl.pallas_call(
        gradient_kernel,
        out_shape=jax.ShapeDtypeStruct((channels,) + ext_shape, jnp.float32),
        in_specs=[SMEM_SPEC, SMEM_SPEC] + [VMEM_SPEC] * 4,
        out_specs=VMEM_SPEC,
        compiler_params=KERNEL_PARAMS,
    )(spots, count, extended, probe_field, own_amps, tables)


def power_canvas(ext_shape, spots, count, probe_field):
    return pl.pallas_call(
        power_kernel,
        out_shape=jax.ShapeDtypeStruct((1,) + ext_shape, jnp.float32),
        in_specs=[SMEM_SPEC, SMEM_SPEC, VMEM_SPEC],
        out_specs=VMEM_SPEC,
        compiler_params=KERNEL_PARAMS,
    )(spots, count.reshape(1), probe_field)


def mesh_place():
    return (
        lax.axis_index("sx"),
        lax.axis_index("sy"),
        lax.axis_size("sx"),
        lax.axis_size("sy"),
    )


def exists(row_dev, col_dev, row_count, col_count):
    return (row_dev >= 0) & (row_dev < row_count) & (col_dev >= 0) & (col_dev < col_count)


ROW_NEIGHBOURS = [(-1, 0), (1, 0)]
COL_NEIGHBOURS = [(0, -1), (0, 1)]


def neighbour_barrier(me_r, me_c, n_r, n_c):
    barrier = pltpu.get_barrier_semaphore()
    greeted = jnp.int32(0)
    for dr, dc in ROW_NEIGHBOURS + COL_NEIGHBOURS:
        present = exists(me_r + dr, me_c + dc, n_r, n_c)

        @pl.when(present)
        def _():
            pl.semaphore_signal(
                barrier, inc=1, device_id=(me_r + dr, me_c + dc), device_id_type=pl.DeviceIdType.MESH
            )

        greeted = greeted + present.astype(jnp.int32)
    pl.semaphore_wait(barrier, greeted)


def start_copies(place, pieces, send_sems, recv_sems):
    me_r, me_c, n_r, n_c = place
    copies = []
    for index, ((dr, dc), source, target) in enumerate(pieces):
        copy = pltpu.make_async_remote_copy(
            src_ref=source,
            dst_ref=target,
            send_sem=send_sems.at[index],
            recv_sem=recv_sems.at[index],
            device_id=(me_r + dr, me_c + dc),
            device_id_type=pl.DeviceIdType.MESH,
        )
        copies.append(((dr, dc), copy))

        @pl.when(exists(me_r + dr, me_c + dc, n_r, n_c))
        def _():
            copy.start()

    return copies


def wait_copies(place, copies):
    me_r, me_c, n_r, n_c = place
    for (dr, dc), copy in copies:

        @pl.when(exists(me_r + dr, me_c + dc, n_r, n_c))
        def _():
            copy.wait_send()

        @pl.when(exists(me_r - dr, me_c - dc, n_r, n_c))
        def _():
            copy.wait_recv()


def swap(place, pieces, send_sems, recv_sems):
    wait_copies(place, start_copies(place, pieces, send_sems, recv_sems))


def halo_kernel(cur_ref, ext_ref, zeros_ref, send_sems, recv_sems, local_sems):
    rows = cur_ref.shape[1]
    cols = cur_ref.shape[2]
    margin = (ext_ref.shape[2] - cols) // 2
    ext_cols = cols + 2 * margin
    place = mesh_place()
    me_r, me_c, n_r, n_c = place
    middle = slice(margin, margin + rows)
    own = pltpu.make_async_copy(cur_ref, ext_ref.at[:, middle, margin : margin + cols], local_sems.at[0])
    own.start()
    zeros_ref[...] = jnp.zeros(zeros_ref.shape, jnp.float32)
    unreached = [
        ((0, 1), ext_ref.at[:, middle, 0:margin], zeros_ref.at[:, :, 0:margin]),
        ((0, -1), ext_ref.at[:, middle, margin + cols : ext_cols], zeros_ref.at[:, :, 0:margin]),
        ((1, 0), ext_ref.at[:, 0:margin, :], zeros_ref),
        ((-1, 0), ext_ref.at[:, margin + rows : 2 * margin + rows, :], zeros_ref),
    ]
    blanks = []
    for index, ((dr, dc), target, source) in enumerate(unreached):
        blank = pltpu.make_async_copy(source, target, local_sems.at[index + 1])
        missing = jnp.logical_not(exists(me_r - dr, me_c - dc, n_r, n_c))
        blanks.append((blank, missing))

    neighbour_barrier(me_r, me_c, n_r, n_c)
    for blank, missing in blanks:

        @pl.when(missing)
        def _():
            blank.start()

    above = slice(0, margin)
    below = slice(margin + rows, 2 * margin + rows)
    inner = slice(margin, margin + cols)
    left = slice(0, margin)
    right = slice(margin + cols, ext_cols)
    bands = start_copies(
        place,
        [
            ((-1, 0), cur_ref, ext_ref.at[:, below, inner]),
            ((1, 0), cur_ref, ext_ref.at[:, above, inner]),
        ],
        send_sems.at[0:2],
        recv_sems.at[0:2],
    )
    swap(
        place,
        [
            ((0, -1), cur_ref.at[:, :, 0:margin], ext_ref.at[:, middle, right]),
            ((0, 1), cur_ref.at[:, :, cols - margin : cols], ext_ref.at[:, middle, left]),
        ],
        send_sems.at[2:4],
        recv_sems.at[2:4],
    )
    own.wait()
    for blank, missing in blanks:

        @pl.when(missing)
        def _():
            blank.wait()

    corners = start_copies(
        place,
        [
            ((-1, 0), ext_ref.at[:, middle, left], ext_ref.at[:, below, left]),
            ((-1, 0), ext_ref.at[:, middle, right], ext_ref.at[:, below, right]),
            ((1, 0), ext_ref.at[:, middle, left], ext_ref.at[:, above, left]),
            ((1, 0), ext_ref.at[:, middle, right], ext_ref.at[:, above, right]),
        ],
        send_sems.at[4:8],
        recv_sems.at[4:8],
    )
    wait_copies(place, bands)
    wait_copies(place, corners)


def fold_kernel(canvas_ref, cur_ref, *refs):
    if len(refs) == 10:
        light_in_ref, refs = None, refs
    else:
        light_in_ref, refs = refs[0], refs[1:]
    fold_body(canvas_ref, cur_ref, light_in_ref, *refs)


def fold_body(canvas_ref, cur_ref, light_in_ref, out_ref, light_ref, mid_bufs, corner_bufs, col_bufs, band_ref, total_ref, send_sems, recv_sems, band_sem):
    rows = out_ref.shape[1]
    cols = out_ref.shape[2]
    margin = (canvas_ref.shape[2] - cols) // 2
    ext_cols = cols + 2 * margin
    place = mesh_place()
    me_r, me_c, n_r, n_c = place
    own_band = pltpu.make_async_copy(canvas_ref.at[:, margin : margin + rows, :], band_ref, band_sem)
    own_band.start()
    neighbour_barrier(me_r, me_c, n_r, n_c)
    top = slice(0, margin)
    bottom = slice(margin + rows, 2 * margin + rows)
    left = slice(0, margin)
    inner = slice(margin, margin + cols)
    right = slice(margin + cols, ext_cols)
    corners = start_copies(
        place,
        [
            ((-1, 0), canvas_ref.at[:, top, left], corner_bufs.at[0, 0]),
            ((-1, 0), canvas_ref.at[:, top, right], corner_bufs.at[0, 1]),
            ((1, 0), canvas_ref.at[:, bottom, left], corner_bufs.at[1, 0]),
            ((1, 0), canvas_ref.at[:, bottom, right], corner_bufs.at[1, 1]),
        ],
        send_sems.at[0:4],
        recv_sems.at[0:4],
    )
    mids = start_copies(
        place,
        [
            ((-1, 0), canvas_ref.at[:, top, inner], mid_bufs.at[0]),
            ((1, 0), canvas_ref.at[:, bottom, inner], mid_bufs.at[1]),
        ],
        send_sems.at[4:6],
        recv_sems.at[4:6],
    )
    own_band.wait()
    strips = []
    for side, columns, (dr, dc), buffer in ((0, left, (0, -1), col_bufs.at[0]), (1, right, (0, 1), col_bufs.at[1])):
        wait_copies(place, [corners[side], corners[side + 2]])
        for slot, source_r in ((0, me_r + 1), (1, me_r - 1)):

            @pl.when(exists(source_r, me_c, n_r, n_c))
            def _():
                band_ref[:, :, columns] += corner_bufs[slot, side]

        strips += start_copies(
            place, [((dr, dc), band_ref.at[:, :, columns], buffer)], send_sems.at[6 + side : 7 + side], recv_sems.at[6 + side : 7 + side]
        )
    wait_copies(place, mids)
    total_ref[...] = band_ref[:, :, inner]
    for slot, source_r in ((0, me_r + 1), (1, me_r - 1)):

        @pl.when(exists(source_r, me_c, n_r, n_c))
        def _():
            total_ref[...] += mid_bufs[slot]

    wait_copies(place, strips)

    @pl.when(exists(me_r, me_c + 1, n_r, n_c))
    def _():
        total_ref[:, :, cols - margin : cols] += col_bufs[0]

    @pl.when(exists(me_r, me_c - 1, n_r, n_c))
    def _():
        total_ref[:, :, 0:margin] += col_bufs[1]

    fields = cur_ref.shape[0]
    if total_ref.shape[0] > fields:
        light_ref[...] = total_ref[fields]
    else:
        light_ref[...] = light_in_ref[...]
    out_ref[...] = cur_ref[...] - total_ref[0:fields] / (light_ref[...] + DAMPING)


def exchange_halo(current, margin):
    depth, rows, cols = current.shape
    return pl.pallas_call(
        halo_kernel,
        out_shape=jax.ShapeDtypeStruct((depth, rows + 2 * margin, cols + 2 * margin), jnp.float32),
        in_specs=[VMEM_SPEC],
        out_specs=pl.BlockSpec(memory_space=pl.ANY),
        scratch_shapes=[
            pltpu.VMEM((depth, margin, cols + 2 * margin), jnp.float32),
            pltpu.SemaphoreType.DMA((8,)),
            pltpu.SemaphoreType.DMA((8,)),
            pltpu.SemaphoreType.DMA((5,)),
        ],
        compiler_params=pltpu.CompilerParams(
            vmem_limit_bytes=60 * 1024 * 1024, has_side_effects=True, collective_id=0
        ),
    )(current)


def fold_and_step(canvas, current, light, margin):
    depth, ext_rows, ext_cols = canvas.shape
    fields, rows, cols = current.shape
    return pl.pallas_call(
        fold_kernel,
        out_shape=(
            jax.ShapeDtypeStruct((fields, rows, cols), jnp.float32),
            jax.ShapeDtypeStruct((rows, cols), jnp.float32),
        ),
        in_specs=[pl.BlockSpec(memory_space=pl.ANY), VMEM_SPEC] + ([] if light is None else [VMEM_SPEC]),
        out_specs=(VMEM_SPEC, VMEM_SPEC),
        scratch_shapes=[
            pltpu.VMEM((2, depth, margin, cols), jnp.float32),
            pltpu.VMEM((2, 2, depth, margin, margin), jnp.float32),
            pltpu.VMEM((2, depth, rows, margin), jnp.float32),
            pltpu.VMEM((depth, rows, ext_cols), jnp.float32),
            pltpu.VMEM((depth, rows, cols), jnp.float32),
            pltpu.SemaphoreType.DMA((8,)),
            pltpu.SemaphoreType.DMA((8,)),
            pltpu.SemaphoreType.DMA(()),
        ],
        compiler_params=pltpu.CompilerParams(
            vmem_limit_bytes=60 * 1024 * 1024, has_side_effects=True, collective_id=depth
        ),
    )(canvas, current, *([] if light is None else [light]))


def on_device(object_field, probe_field, amplitudes, centres, counts):
    size_probe = probe_field.shape[1]
    margin = size_probe // 2
    block_rows = object_field.shape[1]
    block_cols = object_field.shape[2]
    tables = split_tables(size_probe)
    spots = centres[0, 0]
    own_amps = amplitudes[0, 0]
    column_counts = counts[:, 0]
    ext_shape = (block_rows + size_probe, block_cols + size_probe)

    current = object_field
    illumination = None
    for sweep_index in range(ITERS):
        extended = exchange_halo(current, margin)
        channels = 3 if sweep_index == 0 else 2
        canvas = gradient_canvas(
            channels, ext_shape, spots, column_counts, extended, probe_field, own_amps, tables
        )
        current, illumination = fold_and_step(canvas, current, illumination, margin)
    return current


def solution(mesh):
    return jax.shard_map(
        on_device,
        mesh=mesh,
        in_specs=(
            P(None, "sx", "sy"),
            P(),
            P("sx", "sy", None, None, None),
            P("sx", "sy", None, None),
            P(None, "sy"),
        ),
        out_specs=P(None, "sx", "sy"),
        check_vma=False,
    )
```

```python
import functools
import math

import jax
import ml_dtypes
import numpy as np
import jax.numpy as jnp
from jax import lax
from jax.sharding import PartitionSpec as P
from jax.experimental import pallas as pl
from jax.experimental.pallas import tpu as pltpu

ITERS = 2


SMOOTH = 1.0
DAMPING = 1.0


def with_halo(cells, sides, width):
    for axis, dim in sides:
        count = lax.axis_size(axis)
        ends = count - 1
        head = lax.slice_in_dim(cells, 0, width, axis=dim)
        tail = lax.slice_in_dim(cells, cells.shape[dim] - width, cells.shape[dim], axis=dim)
        cells = jnp.concatenate(
            [
                lax.ppermute(tail, axis, [(i, (i + 1) % count) for i in range(ends)]),
                cells,
                lax.ppermute(head, axis, [((i + 1) % count, i) for i in range(ends)]),
            ],
            axis=dim,
        )
    return cells


def dft_tables(length):
    index_values = jnp.arange(length, dtype=jnp.int32)
    product_mod = index_values[:, None] * index_values[None, :] % length
    angles = product_mod.astype(jnp.float32) * (2.0 * math.pi / length)
    scaling = 1.0 / math.sqrt(length)
    return (jnp.cos(angles) * scaling, -jnp.sin(angles) * scaling)


def matmul_exact(left_side, right_side):
    return jnp.dot(left_side, right_side, precision=lax.Precision.HIGHEST)


def complex_left(table_real, table_imag, field_real, field_imag):
    out_real = matmul_exact(table_real, field_real) - matmul_exact(table_imag, field_imag)
    out_imag = matmul_exact(table_real, field_imag) + matmul_exact(table_imag, field_real)
    return (out_real, out_imag)


def complex_right(field_real, field_imag, table_real, table_imag):
    out_real = matmul_exact(field_real, table_real) - matmul_exact(field_imag, table_imag)
    out_imag = matmul_exact(field_real, table_imag) + matmul_exact(field_imag, table_real)
    return (out_real, out_imag)


def position_gradient(object_patch, probe_field, amplitude, table_real, table_imag):
    probe_real = probe_field[0]
    probe_imag = probe_field[1]
    exit_real = probe_real * object_patch[0] - probe_imag * object_patch[1]
    exit_imag = probe_real * object_patch[1] + probe_imag * object_patch[0]
    half_real, half_imag = complex_left(table_real, table_imag, exit_real, exit_imag)
    far_real, far_imag = complex_right(half_real, half_imag, table_real, table_imag)
    factor = 1.0 - amplitude / jnp.sqrt(far_real * far_real + far_imag * far_imag + SMOOTH)
    miss_real = far_real * factor
    miss_imag = far_imag * factor
    back_real, back_imag = complex_left(table_real, -table_imag, miss_real, miss_imag)
    near_real, near_imag = complex_right(back_real, back_imag, table_real, -table_imag)
    return jnp.stack(
        [
            probe_real * near_real + probe_imag * near_imag,
            probe_real * near_imag - probe_imag * near_real,
        ]
    )


def add_patch(canvas, patch_values, corner_row, corner_col):
    zero_index = jnp.zeros((), jnp.int32)
    starts = (zero_index, corner_row, corner_col)
    present = lax.dynamic_slice(canvas, starts, patch_values.shape)
    return lax.dynamic_update_slice(canvas, present + patch_values, starts)


def fold_rows(extended, margin, length):
    middle_part = extended[:, 2 * margin : 2 * margin + length]
    upper_rim = extended[:, :margin]
    lower_rim = extended[:, extended.shape[1] - margin :]
    middle_part = middle_part.at[:, :margin].add(upper_rim)
    return middle_part.at[:, length - margin :].add(lower_rim)


def fold_cols(extended, margin, length):
    middle_part = extended[:, :, 2 * margin : 2 * margin + length]
    left_rim = extended[:, :, :margin]
    right_rim = extended[:, :, extended.shape[2] - margin :]
    middle_part = middle_part.at[:, :, :margin].add(left_rim)
    return middle_part.at[:, :, length - margin :].add(right_rim)


def settle(stacked, margin, block_rows, block_cols):
    full_ext = with_halo(stacked, (("sx", 1), ("sy", 2)), margin)
    return fold_cols(fold_rows(full_ext, margin, block_rows), margin, block_cols)


def local_pass(canvas, extended, spots, own_amps, probe_field, table_real, table_imag, upper_bound):
    size_probe = probe_field.shape[1]

    def local_step(slot_index, canvas_state):
        row_start = spots[slot_index, 0]
        col_start = spots[slot_index, 1]
        zero_index = jnp.zeros((), jnp.int32)
        object_patch = lax.dynamic_slice(
            extended, (zero_index, row_start, col_start), (2, size_probe, size_probe)
        )
        update = position_gradient(
            object_patch, probe_field, own_amps[slot_index], table_real, table_imag
        )
        return add_patch(canvas_state, update, row_start, col_start)

    return lax.fori_loop(0, upper_bound, local_step, canvas)


def dot_exact(left_side, right_side):
    return jnp.dot(
        left_side, right_side, precision=lax.Precision.HIGHEST, preferred_element_type=jnp.float32
    )


def window_tools(size, row, col):
    lanes = 128
    sublanes = 8
    wide = size + lanes
    tall = size + sublanes
    row_base = pl.multiple_of((row // sublanes) * sublanes, sublanes)
    col_base = pl.multiple_of((col // lanes) * lanes, lanes)
    row_shift = row % sublanes
    col_shift = col % lanes
    rows = pl.ds(row_base, tall)
    cols = pl.ds(col_base, wide)

    def take(ref, channel):
        block = ref[channel, rows, cols]
        block = pltpu.roll(block, (tall - row_shift) % tall, 0)
        return pltpu.roll(block, (wide - col_shift) % wide, 1)[:size, :size]

    def put(ref, channel, values):
        block = jnp.concatenate([values, jnp.zeros((size, lanes), jnp.float32)], axis=1)
        block = jnp.concatenate([block, jnp.zeros((sublanes, wide), jnp.float32)], axis=0)
        block = pltpu.roll(pltpu.roll(block, col_shift, 1), row_shift, 0)
        ref[channel, rows, cols] += block

    return take, put


def split_bf16(values):
    scaled = values * 65537.0
    high = scaled - (scaled - values)
    return high.astype(jnp.bfloat16), (values - high).astype(jnp.bfloat16)


def dot_split(left_parts, right_parts):
    left_high, left_low = left_parts
    right_high, right_low = right_parts
    total = jnp.dot(left_high, right_high, preferred_element_type=jnp.float32)
    total += jnp.dot(left_high, right_low, preferred_element_type=jnp.float32)
    return total + jnp.dot(left_low, right_high, preferred_element_type=jnp.float32)


def gradient_kernel(spots_ref, count_ref, ext_ref, probe_ref, amps_ref, tables_ref, out_ref):
    size = probe_ref.shape[1]
    out_ref[...] = jnp.zeros(out_ref.shape, jnp.float32)
    live = count_ref[lax.axis_index("sx")]
    with_power = out_ref.shape[0] > 2
    for slot in range(amps_ref.shape[0]):

        @pl.when(slot < live)
        def _():
            take, put = window_tools(size, spots_ref[slot, 0], spots_ref[slot, 1])
            probe_real = probe_ref[0]
            probe_imag = probe_ref[1]
            real_parts = (tables_ref[0], tables_ref[1])
            imag_parts = (tables_ref[2], tables_ref[3])

            def left(field_real, field_imag, sign):
                both = split_bf16(jnp.concatenate([field_real, field_imag], axis=1))
                by_real = dot_split(real_parts, both)
                by_imag = dot_split(imag_parts, both)
                out_real = by_real[:, :size] - sign * by_imag[:, size:]
                out_imag = by_real[:, size:] + sign * by_imag[:, :size]
                return out_real, out_imag

            def right(field_real, field_imag, sign):
                both = split_bf16(jnp.concatenate([field_real, field_imag], axis=0))
                by_real = dot_split(both, real_parts)
                by_imag = dot_split(both, imag_parts)
                out_real = by_real[:size] - sign * by_imag[size:]
                out_imag = by_imag[:size] * sign + by_real[size:]
                return out_real, out_imag

            obj_real = take(ext_ref, 0)
            obj_imag = take(ext_ref, 1)
            exit_real = probe_real * obj_real - probe_imag * obj_imag
            exit_imag = probe_real * obj_imag + probe_imag * obj_real
            half_real, half_imag = left(exit_real, exit_imag, 1.0)
            far_real, far_imag = right(half_real, half_imag, 1.0)
            factor = 1.0 - amps_ref[slot] / jnp.sqrt(far_real * far_real + far_imag * far_imag + SMOOTH)
            miss_real = far_real * factor
            miss_imag = far_imag * factor
            back_real, back_imag = left(miss_real, miss_imag, -1.0)
            near_real, near_imag = right(back_real, back_imag, -1.0)
            put(out_ref, 0, probe_real * near_real + probe_imag * near_imag)
            put(out_ref, 1, probe_real * near_imag - probe_imag * near_real)
            if with_power:
                put(out_ref, 2, probe_real * probe_real + probe_imag * probe_imag)


def power_kernel(spots_ref, count_ref, probe_ref, out_ref):
    size = probe_ref.shape[1]
    out_ref[...] = jnp.zeros(out_ref.shape, jnp.float32)
    power = probe_ref[0] * probe_ref[0] + probe_ref[1] * probe_ref[1]
    for slot in range(spots_ref.shape[0]):

        @pl.when(slot < count_ref[0])
        def _():
            _, put = window_tools(size, spots_ref[slot, 0], spots_ref[slot, 1])
            put(out_ref, 0, power)


VMEM_SPEC = pl.BlockSpec(memory_space=pltpu.VMEM)
SMEM_SPEC = pl.BlockSpec(memory_space=pltpu.SMEM)
KERNEL_PARAMS = pltpu.CompilerParams(vmem_limit_bytes=60 * 1024 * 1024)


def split_tables(length):
    index_values = np.arange(length, dtype=np.int32)
    product_mod = index_values[:, None] * index_values[None, :] % length
    angles = product_mod.astype(np.float32) * np.float32(2.0 * math.pi / length)
    scaling = np.float32(1.0 / math.sqrt(length))
    parts = []
    for table in (np.cos(angles) * scaling, -np.sin(angles) * scaling):
        table = table.astype(np.float32)
        scaled = table * np.float32(65537.0)
        high = scaled - (scaled - table)
        parts += [high.astype(ml_dtypes.bfloat16), (table - high).astype(ml_dtypes.bfloat16)]
    return jnp.asarray(np.stack(parts))


def gradient_canvas(channels, ext_shape, spots, count, extended, probe_field, own_amps, tables):
    return pl.pallas_call(
        gradient_kernel,
        out_shape=jax.ShapeDtypeStruct((channels,) + ext_shape, jnp.float32),
        in_specs=[SMEM_SPEC, SMEM_SPEC] + [VMEM_SPEC] * 4,
        out_specs=VMEM_SPEC,
        compiler_params=KERNEL_PARAMS,
    )(spots, count, extended, probe_field, own_amps, tables)


def power_canvas(ext_shape, spots, count, probe_field):
    return pl.pallas_call(
        power_kernel,
        out_shape=jax.ShapeDtypeStruct((1,) + ext_shape, jnp.float32),
        in_specs=[SMEM_SPEC, SMEM_SPEC, VMEM_SPEC],
        out_specs=VMEM_SPEC,
        compiler_params=KERNEL_PARAMS,
    )(spots, count.reshape(1), probe_field)


def mesh_place():
    return (
        lax.axis_index("sx"),
        lax.axis_index("sy"),
        lax.axis_size("sx"),
        lax.axis_size("sy"),
    )


def exists(row_dev, col_dev, row_count, col_count):
    return (row_dev >= 0) & (row_dev < row_count) & (col_dev >= 0) & (col_dev < col_count)


ROW_NEIGHBOURS = [(-1, 0), (1, 0)]
COL_NEIGHBOURS = [(0, -1), (0, 1)]


def neighbour_barrier(me_r, me_c, n_r, n_c):
    barrier = pltpu.get_barrier_semaphore()
    greeted = jnp.int32(0)
    for dr, dc in ROW_NEIGHBOURS + COL_NEIGHBOURS:
        present = exists(me_r + dr, me_c + dc, n_r, n_c)

        @pl.when(present)
        def _():
            pl.semaphore_signal(
                barrier, inc=1, device_id=(me_r + dr, me_c + dc), device_id_type=pl.DeviceIdType.MESH
            )

        greeted = greeted + present.astype(jnp.int32)
    pl.semaphore_wait(barrier, greeted)


def start_copies(place, pieces, send_sems, recv_sems):
    me_r, me_c, n_r, n_c = place
    copies = []
    for index, ((dr, dc), source, target) in enumerate(pieces):
        copy = pltpu.make_async_remote_copy(
            src_ref=source,
            dst_ref=target,
            send_sem=send_sems.at[index],
            recv_sem=recv_sems.at[index],
            device_id=(me_r + dr, me_c + dc),
            device_id_type=pl.DeviceIdType.MESH,
        )
        copies.append(((dr, dc), copy))

        @pl.when(exists(me_r + dr, me_c + dc, n_r, n_c))
        def _():
            copy.start()

    return copies


def wait_copies(place, copies):
    me_r, me_c, n_r, n_c = place
    for (dr, dc), copy in copies:

        @pl.when(exists(me_r + dr, me_c + dc, n_r, n_c))
        def _():
            copy.wait_send()

        @pl.when(exists(me_r - dr, me_c - dc, n_r, n_c))
        def _():
            copy.wait_recv()


def swap(place, pieces, send_sems, recv_sems):
    wait_copies(place, start_copies(place, pieces, send_sems, recv_sems))


def halo_kernel(cur_ref, ext_ref, zeros_ref, send_sems, recv_sems, local_sems):
    rows = cur_ref.shape[1]
    cols = cur_ref.shape[2]
    margin = (ext_ref.shape[2] - cols) // 2
    ext_cols = cols + 2 * margin
    place = mesh_place()
    me_r, me_c, n_r, n_c = place
    middle = slice(margin, margin + rows)
    own = pltpu.make_async_copy(cur_ref, ext_ref.at[:, middle, margin : margin + cols], local_sems.at[0])
    own.start()
    zeros_ref[...] = jnp.zeros(zeros_ref.shape, jnp.float32)
    unreached = [
        ((0, 1), ext_ref.at[:, middle, 0:margin], zeros_ref.at[:, :, 0:margin]),
        ((0, -1), ext_ref.at[:, middle, margin + cols : ext_cols], zeros_ref.at[:, :, 0:margin]),
        ((1, 0), ext_ref.at[:, 0:margin, :], zeros_ref),
        ((-1, 0), ext_ref.at[:, margin + rows : 2 * margin + rows, :], zeros_ref),
    ]
    blanks = []
    for index, ((dr, dc), target, source) in enumerate(unreached):
        blank = pltpu.make_async_copy(source, target, local_sems.at[index + 1])
        missing = jnp.logical_not(exists(me_r - dr, me_c - dc, n_r, n_c))
        blanks.append((blank, missing))

    neighbour_barrier(me_r, me_c, n_r, n_c)
    for blank, missing in blanks:

        @pl.when(missing)
        def _():
            blank.start()

    above = slice(0, margin)
    below = slice(margin + rows, 2 * margin + rows)
    inner = slice(margin, margin + cols)
    left = slice(0, margin)
    right = slice(margin + cols, ext_cols)
    bands = start_copies(
        place,
        [
            ((-1, 0), cur_ref, ext_ref.at[:, below, inner]),
            ((1, 0), cur_ref, ext_ref.at[:, above, inner]),
        ],
        send_sems.at[0:2],
        recv_sems.at[0:2],
    )
    swap(
        place,
        [
            ((0, -1), cur_ref.at[:, :, 0:margin], ext_ref.at[:, middle, right]),
            ((0, 1), cur_ref.at[:, :, cols - margin : cols], ext_ref.at[:, middle, left]),
        ],
        send_sems.at[2:4],
        recv_sems.at[2:4],
    )
    own.wait()
    for blank, missing in blanks:

        @pl.when(missing)
        def _():
            blank.wait()

    corners = start_copies(
        place,
        [
            ((-1, 0), ext_ref.at[:, middle, left], ext_ref.at[:, below, left]),
            ((-1, 0), ext_ref.at[:, middle, right], ext_ref.at[:, below, right]),
            ((1, 0), ext_ref.at[:, middle, left], ext_ref.at[:, above, left]),
            ((1, 0), ext_ref.at[:, middle, right], ext_ref.at[:, above, right]),
        ],
        send_sems.at[4:8],
        recv_sems.at[4:8],
    )
    wait_copies(place, bands)
    wait_copies(place, corners)


def fold_kernel(light_given, canvas_ref, cur_ref, *refs):
    if light_given:
        light_in_ref, out_ref, refs = refs[0], refs[1], refs[2:]
        fold_body(canvas_ref, cur_ref, light_in_ref, out_ref, None, *refs)
    else:
        fold_body(canvas_ref, cur_ref, None, *refs)


def fold_body(canvas_ref, cur_ref, light_in_ref, out_ref, light_ref, mid_bufs, corner_bufs, col_bufs, band_ref, total_ref, send_sems, recv_sems, band_sem):
    rows = out_ref.shape[1]
    cols = out_ref.shape[2]
    margin = (canvas_ref.shape[2] - cols) // 2
    ext_cols = cols + 2 * margin
    place = mesh_place()
    me_r, me_c, n_r, n_c = place
    own_band = pltpu.make_async_copy(canvas_ref.at[:, margin : margin + rows, :], band_ref, band_sem)
    own_band.start()
    neighbour_barrier(me_r, me_c, n_r, n_c)
    top = slice(0, margin)
    bottom = slice(margin + rows, 2 * margin + rows)
    left = slice(0, margin)
    inner = slice(margin, margin + cols)
    right = slice(margin + cols, ext_cols)
    corners = start_copies(
        place,
        [
            ((-1, 0), canvas_ref.at[:, top, left], corner_bufs.at[0, 0]),
            ((-1, 0), canvas_ref.at[:, top, right], corner_bufs.at[0, 1]),
            ((1, 0), canvas_ref.at[:, bottom, left], corner_bufs.at[1, 0]),
            ((1, 0), canvas_ref.at[:, bottom, right], corner_bufs.at[1, 1]),
        ],
        send_sems.at[0:4],
        recv_sems.at[0:4],
    )
    mids = start_copies(
        place,
        [
            ((-1, 0), canvas_ref.at[:, top, inner], mid_bufs.at[0]),
            ((1, 0), canvas_ref.at[:, bottom, inner], mid_bufs.at[1]),
        ],
        send_sems.at[4:6],
        recv_sems.at[4:6],
    )
    wait_copies(place, corners)
    own_band.wait()
    for slot, source_r in ((0, me_r + 1), (1, me_r - 1)):

        @pl.when(exists(source_r, me_c, n_r, n_c))
        def _():
            band_ref[:, :, left] += corner_bufs[slot, 0]
            band_ref[:, :, right] += corner_bufs[slot, 1]

    strips = start_copies(
        place,
        [
            ((0, -1), band_ref.at[:, :, left], col_bufs.at[0]),
            ((0, 1), band_ref.at[:, :, right], col_bufs.at[1]),
        ],
        send_sems.at[6:8],
        recv_sems.at[6:8],
    )
    wait_copies(place, mids)
    total_ref[...] = band_ref[:, :, inner]
    for slot, source_r in ((0, me_r + 1), (1, me_r - 1)):

        @pl.when(exists(source_r, me_c, n_r, n_c))
        def _():
            total_ref[...] += mid_bufs[slot]

    wait_copies(place, strips)

    @pl.when(exists(me_r, me_c + 1, n_r, n_c))
    def _():
        total_ref[:, :, cols - margin : cols] += col_bufs[0]

    @pl.when(exists(me_r, me_c - 1, n_r, n_c))
    def _():
        total_ref[:, :, 0:margin] += col_bufs[1]

    fields = cur_ref.shape[0]
    if light_in_ref is None:
        light_ref[...] = total_ref[fields]
        light = light_ref[...]
    else:
        light = light_in_ref[...]
    out_ref[...] = cur_ref[...] - total_ref[0:fields] / (light + DAMPING)


def exchange_halo(current, margin):
    depth, rows, cols = current.shape
    return pl.pallas_call(
        halo_kernel,
        out_shape=jax.ShapeDtypeStruct((depth, rows + 2 * margin, cols + 2 * margin), jnp.float32),
        in_specs=[VMEM_SPEC],
        out_specs=pl.BlockSpec(memory_space=pl.ANY),
        scratch_shapes=[
            pltpu.VMEM((depth, margin, cols + 2 * margin), jnp.float32),
            pltpu.SemaphoreType.DMA((8,)),
            pltpu.SemaphoreType.DMA((8,)),
            pltpu.SemaphoreType.DMA((5,)),
        ],
        compiler_params=pltpu.CompilerParams(
            vmem_limit_bytes=60 * 1024 * 1024, has_side_effects=True, collective_id=0
        ),
    )(current)


def fold_and_step(canvas, current, light, margin):
    depth, ext_rows, ext_cols = canvas.shape
    fields, rows, cols = current.shape
    results = pl.pallas_call(
        functools.partial(fold_kernel, light is not None),
        out_shape=(jax.ShapeDtypeStruct((fields, rows, cols), jnp.float32),)
        + (() if light is not None else (jax.ShapeDtypeStruct((rows, cols), jnp.float32),)),
        in_specs=[pl.BlockSpec(memory_space=pl.ANY), VMEM_SPEC] + ([] if light is None else [VMEM_SPEC]),
        out_specs=(VMEM_SPEC,) + (() if light is not None else (VMEM_SPEC,)),
        scratch_shapes=[
            pltpu.VMEM((2, depth, margin, cols), jnp.float32),
            pltpu.VMEM((2, 2, depth, margin, margin), jnp.float32),
            pltpu.VMEM((2, depth, rows, margin), jnp.float32),
            pltpu.VMEM((depth, rows, ext_cols), jnp.float32),
            pltpu.VMEM((depth, rows, cols), jnp.float32),
            pltpu.SemaphoreType.DMA((8,)),
            pltpu.SemaphoreType.DMA((8,)),
            pltpu.SemaphoreType.DMA(()),
        ],
        compiler_params=pltpu.CompilerParams(
            vmem_limit_bytes=60 * 1024 * 1024, has_side_effects=True, collective_id=depth
        ),
    )(canvas, current, *([] if light is None else [light]))
    return (results[0], light) if light is not None else tuple(results)


def on_device(object_field, probe_field, amplitudes, centres, counts):
    size_probe = probe_field.shape[1]
    margin = size_probe // 2
    block_rows = object_field.shape[1]
    block_cols = object_field.shape[2]
    tables = split_tables(size_probe)
    spots = centres[0, 0]
    own_amps = amplitudes[0, 0]
    column_counts = counts[:, 0]
    ext_shape = (block_rows + size_probe, block_cols + size_probe)

    current = object_field
    illumination = None
    for sweep_index in range(ITERS):
        extended = exchange_halo(current, margin)
        channels = 3 if sweep_index == 0 else 2
        canvas = gradient_canvas(
            channels, ext_shape, spots, column_counts, extended, probe_field, own_amps, tables
        )
        current, illumination = fold_and_step(canvas, current, illumination, margin)
    return current


def solution(mesh):
    return jax.shard_map(
        on_device,
        mesh=mesh,
        in_specs=(
            P(None, "sx", "sy"),
            P(),
            P("sx", "sy", None, None, None),
            P("sx", "sy", None, None),
            P(None, "sy"),
        ),
        out_specs=P(None, "sx", "sy"),
        check_vma=False,
    )
```
